32 devices in a mesh: dp: 4 (over z), fsdp: 8 (over y, x, core).
Axes of the slice: x: 2, y: 2, z: 4, core: 2. Of those that a mesh axis runs over, the one named last changes fastest.
Arguments:
- frames: bfloat16 [256, 256, 512], P(('dp', 'fsdp')), may hold values from -6 to 6
- group: int32 [256], P(('dp', 'fsdp')), may hold values from 0 to 1
- lengths: int32 [256], P(('dp', 'fsdp')), may hold values from 128 to 256, as said below
- conv_weight: bfloat16 [2, 7, 512], P(None, None, ('dp', 'fsdp')), may hold values from -2 to 2
- conv_bias: bfloat16 [2, 512], P(None, ('dp', 'fsdp')), may hold values from -3 to 3
- ada_scale: bfloat16 [2, 2, 512], P(None, None, ('dp', 'fsdp')), may hold values from 0.5 to 1.5
- ada_shift: bfloat16 [2, 2, 512], P(None, None, ('dp', 'fsdp')), may hold values from -3 to 3
- up_weight: bfloat16 [2, 512, 1536], P(None, ('dp', 'fsdp')), may hold values from -0.25 to 0.25
- up_bias: bfloat16 [2, 1536], P(None, ('dp', 'fsdp')), may hold values from -3 to 3
- down_weight: bfloat16 [2, 1536, 512], P(None, ('dp', 'fsdp')), may hold values from -0.15625 to 0.15625
- down_bias: bfloat16 [2, 512], P(None, ('dp', 'fsdp')), may hold values from -3 to 3
- layer_scale: bfloat16 [2, 512], P(None, ('dp', 'fsdp')), may hold values from 0.5 to 1.5
- out_grad: bfloat16 [256, 256, 512], P(('dp', 'fsdp')), may hold values from -6 to 6
Outputs:
- output: bfloat16 [256, 256, 512], P(('dp', 'fsdp'))
- input_grad: float32 [256, 256, 512], P(('dp', 'fsdp'))
- conv_weight_grad: float32 [2, 7, 512], P(None, None, ('dp', 'fsdp'))
- conv_bias_grad: float32 [2, 512], P(None, ('dp', 'fsdp'))
- ada_scale_grad: float32 [2, 2, 512], P(None, None, ('dp', 'fsdp'))
- ada_shift_grad: float32 [2, 2, 512], P(None, None, ('dp', 'fsdp'))
- up_weight_grad: float32 [2, 512, 1536], P(None, ('dp', 'fsdp'))
- up_bias_grad: float32 [2, 1536], P(None, ('dp', 'fsdp'))
- down_weight_grad: float32 [2, 1536, 512], P(None, ('dp', 'fsdp'))
- down_bias_grad: float32 [2, 512], P(None, ('dp', 'fsdp'))
- layer_scale_grad: float32 [2, 512], P(None, ('dp', 'fsdp'))
The draws below stay inside these ranges and needn't reach their ends.
Inputs may be any that keep to these rules, and one draw needn't show every extreme that they name: `lengths`: A clip of group 0 has at most 256 valid frames, one of group 1 at most 236; clip 0 has 256 and clip 1 has 236.
All inputs are finite; a program needn't handle non-finite values.
Results may differ from the reference program's by a relative error of at most 0.0066.
Values may be sent and summed in bfloat16 or wider, within the bound.
A program may use at most 192 MiB of HBM per device.

```python
import math
import jax
import jax.numpy as jnp
from jax import lax

D = 512
H = 1536
KERNEL = 7
GROUPS = 2
BLOCKS = 2
FRAMES = 256
SHORT = 236
CLIPS = 256


def clip_plan(key):
    base_key = jax.random.fold_in(key, 31)
    key_group, key_whole, key_part = jax.random.split(base_key, 3)
    group_ids = jax.random.randint(key_group, (CLIPS,), 0, GROUPS).astype(jnp.int32)
    group_ids = group_ids.at[0].set(0).at[1].set(1)
    limit_len = jnp.where(group_ids == 0, FRAMES, SHORT).astype(jnp.int32)
    whole_clip = jax.random.randint(key_whole, (CLIPS,), 0, 2)
    partial_len = jax.random.randint(key_part, (CLIPS,), FRAMES // 2, FRAMES + 1).astype(jnp.int32)
    valid_len = jnp.where(whole_clip == 1, limit_len, jnp.minimum(partial_len, limit_len)).astype(jnp.int32)
    valid_len = valid_len.at[0].set(FRAMES).at[1].set(SHORT)
    return (group_ids, valid_len)


def draw_group(key, part):
    return clip_plan(key)[0]


def draw_lengths(key, part):
    return clip_plan(key)[1]


def shard_levels(rng, shape, cuts, low, largest):
    level = 1.0
    for position, blocks in cuts:
        heights = jax.random.uniform(jax.random.fold_in(jax.random.fold_in(rng, 6), position), (blocks,), jnp.float32, low / len(cuts), largest / len(cuts))
        level = level * jnp.repeat(jnp.exp(heights), shape[position] // blocks).reshape((-1,) + (1,) * (len(shape) - 1 - position))
    return level


def bell_draw(key, shape, scale, limit, pieces=(), kind=jnp.bfloat16):
    level = shard_levels(key, shape, pieces, -0.22, 0.18) if pieces else 1.0
    drawn = jax.random.normal(key, shape, jnp.float32) * scale * level
    return jnp.minimum(jnp.maximum(drawn, -limit), limit).astype(kind)


def setup_inputs(seed: int = 0) -> dict:
    key_of = jax.random.split(jax.random.key(seed), 14)
    frames = bell_draw(key_of[0], (CLIPS, FRAMES, D), 1.0, 6.0, ((0, 32),))
    group = draw_group(jax.random.fold_in(key_of[13], 71), 0)
    lengths = draw_lengths(jax.random.fold_in(key_of[13], 71), 0)
    conv_weight = bell_draw(key_of[3], (BLOCKS, KERNEL, D), KERNEL ** -0.5, 2.0, ((2, 32),))
    conv_bias = bell_draw(key_of[4], (BLOCKS, D), 0.5, 3.0, ((1, 32),))
    ada_scale = jnp.clip(0.5 + 1.0 * jax.random.uniform(key_of[5], (BLOCKS, GROUPS, D), jnp.float32) ** shard_levels(key_of[5], (BLOCKS, GROUPS, D), ((2, 32),), -0.2, 0.2), 0.5, 1.5).astype(jnp.bfloat16)
    ada_shift = bell_draw(key_of[6], (BLOCKS, GROUPS, D), 0.5, 3.0, ((2, 32),))
    up_weight = bell_draw(key_of[7], (BLOCKS, D, H), D ** -0.5, 0.25, ((1, 32),))
    up_bias = bell_draw(key_of[8], (BLOCKS, H), 0.5, 3.0, ((1, 32),))
    down_weight = bell_draw(key_of[9], (BLOCKS, H, D), H ** -0.5, 0.15625, ((1, 32),))
    down_bias = bell_draw(key_of[10], (BLOCKS, D), 0.5, 3.0, ((1, 32),))
    layer_scale = jnp.clip(0.5 + 1.0 * jax.random.uniform(key_of[11], (BLOCKS, D), jnp.float32) ** shard_levels(key_of[11], (BLOCKS, D), ((1, 32),), -0.2, 0.2), 0.5, 1.5).astype(jnp.bfloat16)
    out_grad = bell_draw(key_of[12], (CLIPS, FRAMES, D), 1.0, 6.0, ((0, 32),))
    return {"frames": frames, "group": group, "lengths": lengths, "conv_weight": conv_weight, "conv_bias": conv_bias, "ada_scale": ada_scale, "ada_shift": ada_shift, "up_weight": up_weight, "up_bias": up_bias, "down_weight": down_weight, "down_bias": down_bias, "layer_scale": layer_scale, "out_grad": out_grad}


@jax.custom_vjp
def low(v):
    return lax.optimization_barrier(v.astype(jnp.bfloat16)).astype(jnp.float32)

@jax.custom_vjp
def low_back(v):
    return v

def low_keep(v):
    return (low(v), None)

def low_pass(kept, grad):
    return (grad,)

def back_keep(v):
    return (v, None)

def back_low(kept, grad):
    return (low(grad),)
low.defvjp(low_keep, low_pass)
low_back.defvjp(back_keep, back_low)
EPSILON = 1e-06

def conv_block(weights, stream, valid_rows, group_ids):
    conv_kernel, conv_shift, scale_table, shift_table, up_matrix, up_offset, down_matrix, down_offset, layer_gain = weights
    half_kernel = KERNEL // 2
    masked = stream * valid_rows
    padded = jnp.pad(masked, ((0, 0), (half_kernel, half_kernel), (0, 0)))
    mixed = conv_shift
    for offset in range(KERNEL):
        mixed = mixed + conv_kernel[offset] * padded[:, offset:offset + FRAMES, :]
    center = mixed - lax.optimization_barrier(jnp.mean(mixed, axis=-1, keepdims=True))
    spread = lax.optimization_barrier(jnp.mean(center * center, axis=-1, keepdims=True))
    normed = center * lax.rsqrt(spread + EPSILON)
    gain_rows = jnp.take(scale_table, group_ids, axis=0)
    shift_rows = jnp.take(shift_table, group_ids, axis=0)
    shaped = normed * gain_rows[:, None, :] + shift_rows[:, None, :]
    before = low_back(jnp.einsum('ctd,dh->cth', low(shaped), up_matrix, precision=lax.Precision.HIGHEST) + up_offset)
    activated = low(jax.nn.gelu(before, approximate=False))
    branch = low_back(jnp.einsum('cth,hd->ctd', activated, down_matrix, precision=lax.Precision.HIGHEST) + down_offset)
    return stream + valid_rows * layer_gain * branch

def reference(frames, group, lengths, conv_weight, conv_bias, ada_scale, ada_shift, up_weight, up_bias, down_weight, down_bias, layer_scale, out_grad):
    params = (conv_weight.astype(jnp.float32), conv_bias.astype(jnp.float32), ada_scale.astype(jnp.float32), ada_shift.astype(jnp.float32), up_weight.astype(jnp.float32), up_bias.astype(jnp.float32), down_weight.astype(jnp.float32), down_bias.astype(jnp.float32), layer_scale.astype(jnp.float32))
    per_step = math.gcd(CLIPS, max(1, 4096 // FRAMES))
    steps_count = CLIPS // per_step

    def network(weights, features):

        def one_step(bundle):
            clip_rows, clip_groups, clip_lengths = bundle
            valid_rows = (jnp.arange(FRAMES, dtype=jnp.int32)[None, :] < clip_lengths[:, None]).astype(jnp.float32)[:, :, None]
            for block_index in range(BLOCKS):
                chosen = tuple((entry[block_index] for entry in weights))
                clip_rows = conv_block(chosen, clip_rows, valid_rows, clip_groups)
            return clip_rows
        result = lax.map(jax.checkpoint(one_step), (features.reshape(steps_count, per_step, FRAMES, D), group.reshape(steps_count, per_step), lengths.reshape(steps_count, per_step)))
        return result.reshape(CLIPS, FRAMES, D)
    final, pullback = jax.vjp(network, params, frames.astype(jnp.float32))
    grads, input_grad = pullback(out_grad.astype(jnp.float32))
    return (final.astype(jnp.bfloat16), input_grad, grads[0], grads[1], grads[2], grads[3], grads[4], grads[5], grads[6], grads[7], grads[8])
```

```python
import functools
import math
import jax
import jax.numpy as jnp
from jax import lax
from jax.experimental import pallas as pl
from jax.experimental.pallas import tpu as pltpu
from jax.sharding import PartitionSpec as P

F32 = jnp.float32
BF16 = jnp.bfloat16
EPSILON = 1e-06
TAPS, CONV_BIAS, SCALE, SHIFT, DOWN_BIAS, GAIN, ROWS = 0, 7, 8, 10, 12, 13, 16
A_TAPS, A_BIAS, A_SCALE, A_SHIFT, A_DOWN, A_GAIN = 0, 7, 8, 9, 10, 11
HALO = 3
LANES = 128
VMEM_LIMIT = 64 * 1024 * 1024 - 128 * 1024
NN = (((1,), (0,)), ((), ()))
NT = (((1,), (1,)), ((), ()))
TN = (((0,), (0,)), ((), ()))
DMA = pltpu.SemaphoreType.DMA


def mm(a, b, dims):
    return lax.dot_general(a, b, dims, preferred_element_type=F32)


def gelu_pair(before):
    u = before * math.sqrt(0.5)
    phi = 0.5 + 0.5 * lax.erf(u)
    bell = jnp.exp2(u * u * (-math.log2(math.e))) * (1.0 / math.sqrt(math.pi))
    return before * phi, phi + u * bell


def per_clip(values, clips, width):
    rows = lax.broadcasted_iota(jnp.int32, (clips, width), 0)
    out = jnp.zeros((clips, width), jnp.int32)
    for c in range(clips):
        out = jnp.where(rows == c, values[c], out)
    return out


def prepare(small, lens, groups, s8, len8, group_count):
    clips, width = len8.shape
    for r in range(14):
        s8[r] = jnp.broadcast_to(small[r : r + 1, :], (clips, width))
    member = per_clip(groups, clips, width)
    len8[...] = per_clip(lens, clips, width)
    gain = jnp.zeros((clips, width), F32)
    shift = jnp.zeros((clips, width), F32)
    for g in range(group_count):
        chosen = jnp.where(member == g, 1.0, 0.0)
        gain = gain + chosen * s8[SCALE + g]
        shift = shift + chosen * s8[SHIFT + g]
    s8[SCALE] = gain
    s8[SHIFT] = shift


def keep_frames(v, t0, len8, other=0.0):
    t = lax.broadcasted_iota(jnp.int32, v.shape, 0) + t0
    return jnp.where(t < len8[...][None], v, other)


def spread_clips(block, t0, dst, d0, frames):
    clips = block.shape[0]
    for c in range(clips):
        for t in range(0, frames, 16):
            v = block[c, pl.ds(t0 + t, 16), :].astype(F32)
            for l in range(dst.shape[0]):
                dst[l, pl.ds((d0 + t) * clips + c, 16, stride=clips), :] = v[:, l * LANES : (l + 1) * LANES]


def collect_clips(src, block, frames):
    clips = block.shape[0]
    for c in range(clips):
        for t in range(0, frames, 16):
            for l in range(src.shape[0]):
                v = src[l, pl.ds(t * clips + c, 16, stride=clips), :]
                block[c, t : t + 16, l * LANES : (l + 1) * LANES] = v.astype(block.dtype)


def rows_of(src, start, n):
    return jnp.concatenate([src[l, pl.ds(start, n), :] for l in range(src.shape[0])], axis=-1)


def put_rows(dst, start, v):
    for l in range(dst.shape[0]):
        dst[l, pl.ds(start, v.shape[0]), :] = v[:, l * LANES : (l + 1) * LANES]


def fold(v):
    return jnp.sum(v, axis=0)


def smem():
    return pl.BlockSpec(memory_space=pltpu.SMEM)


def vmem():
    return pl.BlockSpec(memory_space=pltpu.VMEM)


def hbm():
    return pl.BlockSpec(memory_space=pl.ANY)


def whole(*dims):
    return pl.BlockSpec(dims, lambda i: (0,) * len(dims), pipeline_mode=pl.Buffered(1))


def shape(dims, dtype=F32):
    return jax.ShapeDtypeStruct(dims, dtype)


MESH = pl.DeviceIdType.MESH
PACK = 20


class Place:
    def __init__(self, deep, side):
        self.deep, self.side = deep, side
        self.z = lax.axis_index("dp")
        f = lax.axis_index("fsdp")
        self.f = f
        self.core = lax.rem(f, 2)
        chip = f // 2
        self.low = lax.rem(chip, side)
        self.high = chip // side
        self.first = jnp.where(self.core == 0, self.high, self.low)
        self.second = jnp.where(self.core == 0, self.low, self.high)

    def chip_of(self, first, second):
        high = jnp.where(self.core == 0, first, second)
        low = jnp.where(self.core == 0, second, first)
        return high, low

    def fsdp_of(self, first, second):
        high, low = self.chip_of(first, second)
        return (high * self.side + low) * 2 + self.core

    def z_peer(self, p):
        return {"dp": lax.rem(self.z + p, self.deep)}

    def first_peer(self, p):
        return {"fsdp": self.fsdp_of(lax.rem(self.first + p, self.side), self.second)}

    def second_peer(self, p):
        return {"fsdp": self.fsdp_of(self.first, lax.rem(self.second + p, self.side))}

    def core_peer(self):
        return {"fsdp": self.f + 1 - 2 * self.core}

    def greet(self):
        barrier = pltpu.get_barrier_semaphore()
        peers = [self.z_peer(p) for p in range(1, self.deep)]
        peers += [self.first_peer(p) for p in range(1, self.side)]
        peers += [self.second_peer(p) for p in range(1, self.side)]
        peers.append(self.core_peer())
        for peer in peers:
            pl.semaphore_signal(barrier, inc=1, device_id=peer, device_id_type=MESH)
        pl.semaphore_wait(barrier, len(peers))


def send(src, dst, send_sem, recv_sem, peer):
    return pltpu.make_async_remote_copy(
        src_ref=src, dst_ref=dst, send_sem=send_sem, recv_sem=recv_sem, device_id=peer, device_id_type=MESH
    )


def run(copies):
    for c in copies:
        c.start()


def done(copies):
    for c in copies:
        c.wait()


def weight_route(place, own, full, sems):
    zs, zr, fs, fr, ss, sr, cs, cr = sems
    deep, side, core = place.deep, place.side, place.core

    def held(p, q):
        high, low = place.chip_of(lax.rem(place.first + p, side), lax.rem(place.second + q, side))
        return full.at[:, high, low, core]

    mine = full.at[place.z, place.high, place.low, core]
    along_z = [send(own, mine, zs.at[p - 1], zr.at[p - 1], place.z_peer(p)) for p in range(1, deep)]
    along_first = [
        send(held(0, 0), held(0, 0), fs.at[p - 1], fr.at[p - 1], place.first_peer(p)) for p in range(1, side)
    ]
    along_second = []
    for j in range(side):
        high, low = place.chip_of(j, place.second)
        line = full.at[:, high, low, core]
        for p in range(1, side):
            n = j * (side - 1) + p - 1
            along_second.append(send(line, line, ss.at[n], sr.at[n], place.second_peer(p)))
    across = lambda p, q: send(held(p, q), held(p, q), cs.at[p * side + q], cr.at[p * side + q], place.core_peer())
    over = [[across(0, 0)], [across(p, 0) for p in range(1, side)],
            [across(p, q) for q in range(1, side) for p in range(side)]]
    return [along_z, along_first, along_second], over


def gather_sems(count, deep, side):
    one = [deep - 1, deep - 1, side - 1, side - 1, side * (side - 1), side * (side - 1), side * side, side * side]
    return [DMA((count, n)) for n in one]


def place_small(place, shards, pack, group_count, taps):
    conv_w, conv_b, scale, shift, up_b, down_b, gain = shards
    width = conv_b.shape[1]
    lane = lax.broadcasted_iota(jnp.int32, (width, LANES), 1)
    row = lax.broadcasted_iota(jnp.int32, (width, LANES), 0)
    spot = jnp.where(lane == row + place.f * width, 1.0, 0.0).astype(BF16)
    wide = up_b.shape[1]
    span = wide * LANES // width
    lane = lax.broadcasted_iota(jnp.int32, (wide, span), 1)
    row = lax.broadcasted_iota(jnp.int32, (wide, span), 0)
    spread = jnp.where(lane == row + place.f * wide, 1.0, 0.0).astype(BF16)
    pack[...] = jnp.zeros(pack.shape, F32)
    for b in range(2):
        o = b * PACK
        for k in range(taps):
            pack[o + k : o + k + 1, :] = mm(conv_w[k, b : b + 1, :], spot, NN)
        pack[o + SCALE : o + SCALE + group_count, :] = mm(scale[b], spot, NN)
        pack[o + SHIFT : o + SHIFT + group_count, :] = mm(shift[b], spot, NN)
        for src, at in ((conv_b, CONV_BIAS), (down_b, DOWN_BIAS), (gain, GAIN)):
            pack[o + at : o + at + 1, :] = mm(src[b : b + 1, :], spot, NN)
        bias = mm(up_b[b : b + 1, :], spread, NN)
        for q in range(span // LANES):
            pack[o + 14 + q : o + 15 + q, :] = bias[:, q * LANES : (q + 1) * LANES]


class Gather:
    def __init__(self, shards, up_full, down_full, small_full, upb_full, refs, deep, side, group_count, taps):
        (self.pack, self.zbuf, self.first_in, self.first_sum, self.second_in, self.second_sum, self.core_in,
         self.local_sems, self.out_sems, self.small_s, self.small_r) = refs[:11]
        sems = refs[11:]
        self.place = place = Place(deep, side)
        self.small_full, self.upb_full, self.shards = small_full, upb_full, shards
        self.group_count, self.taps = group_count, taps
        up_w, down_w = shards[4], shards[6]
        self.full = (up_full, down_full)
        self.routes, self.local = [], []
        for n, (own, full) in enumerate(
            ((up_w.at[0], up_full.at[0]), (down_w.at[0], down_full.at[0]), (up_w.at[1], up_full.at[1]), (down_w.at[1], down_full.at[1]))
        ):
            self.routes.append(weight_route(place, own, full, [s.at[n] for s in sems]))
            spot = full.at[place.z, place.high, place.low, place.core]
            self.local.append(pltpu.make_async_copy(own, spot, self.local_sems.at[n]))
        stages = [
            [(self.zbuf.at[place.z], self.zbuf.at[place.z], place.z_peer(p)) for p in range(1, deep)],
            [(self.zbuf, self.first_in.at[p - 1], place.first_peer(p)) for p in range(1, side)],
            [(self.first_sum, self.second_in.at[p - 1], place.second_peer(p)) for p in range(1, side)],
            [(self.second_sum, self.core_in, place.core_peer())],
        ]
        n = 0
        self.small = []
        for stage in stages:
            copies = []
            for src, dst, peer in stage:
                copies.append(send(src, dst, self.small_s.at[n], self.small_r.at[n], peer))
                n += 1
            self.small.append(copies)

    def begin(self, n):
        run(self.routes[n][0][0])
        self.local[n].start()

    def after_z(self, n):
        along, over = self.routes[n]
        self.local[n].wait()
        done(along[0])
        run(along[1])
        run(over[0])

    def after_first(self, n):
        along, over = self.routes[n]
        done(along[1])
        run(along[2])
        run(over[1])

    def after_second(self, n):
        along, over = self.routes[n]
        done(along[2])
        run(over[2])

    def end(self, n):
        for copies in self.routes[n][1]:
            done(copies)

    def early(self, spread, ready, conv, tiles):
        place = self.place
        place.greet()
        self.begin(0)
        conv_w, conv_b, scale, shift, _, up_b, _, down_b, gain = self.shards
        place_small(place, (conv_w, conv_b, scale, shift, up_b, down_b, gain), self.pack, self.group_count, self.taps)
        self.zbuf[place.z] = self.pack[...]
        run(self.small[0])
        self.begin(1)
        spread()
        done(self.small[0])
        run(self.small[1])
        self.after_z(0)
        done(self.small[1])
        total = self.zbuf[...]
        for p in range(1, place.side):
            total = total + self.first_in[p - 1]
        self.first_sum[...] = total
        run(self.small[2])
        self.after_z(1)
        self.begin(2)
        self.begin(3)
        done(self.small[2])
        total = self.first_sum[...]
        for p in range(1, place.side):
            total = total + self.second_in[p - 1]
        self.second_sum[...] = total
        run(self.small[3])
        self.after_first(0)
        done(self.small[3])
        self.finish_small()
        ready()
        conv(0, tiles // 4)
        self.after_first(1)
        conv(tiles // 4, tiles // 2)
        self.after_second(0)
        conv(tiles // 2, tiles)
        self.after_second(1)
        self.end(0)

    def finish_small(self):
        total = self.second_sum[...] + self.core_in[...]
        deep = self.place.deep
        per = self.upb_full.shape[2] // deep
        self.small_full[...] = jnp.zeros(self.small_full.shape, F32)
        for b in range(2):
            o = b * PACK
            for z in range(deep):
                self.small_full[b, 0:14, z * LANES : (z + 1) * LANES] = total[z, o : o + 14, :]
                for q in range(per // LANES):
                    at = z * per + q * LANES
                    self.upb_full[b, :, at : at + LANES] = total[z, o + 14 + q : o + 15 + q, :]

    def late(self, i, tiles, up_out, down_out):
        outs = (up_out, down_out)
        keep = lambda n: pltpu.make_async_copy(self.full[n % 2].at[n // 2], outs[n % 2].at[n // 2], self.out_sems.at[n])

        @pl.when(i == 1)
        def _():
            keep(0).start()
            self.after_z(2)
            self.after_z(3)

        @pl.when(i == tiles // 2 + 1)
        def _():
            self.after_first(2)
            self.after_first(3)

        @pl.when(i == tiles)
        def _():
            self.end(1)
            keep(1).start()

        @pl.when(i == 2 * tiles - tiles // 4)
        def _():
            self.after_second(2)
            self.after_second(3)

        @pl.when(i == 2 * tiles)
        def _():
            for n in (2, 3):
                self.end(n)
                keep(n).start()

        @pl.when(i == 3 * tiles - 1)
        def _():
            for n in range(4):
                keep(n).wait()


def gather_scratch(deep, side):
    buf = pltpu.VMEM((deep, 2 * PACK, LANES), F32)
    many = pltpu.VMEM((side - 1, deep, 2 * PACK, LANES), F32)
    n = deep - 1 + 2 * (side - 1) + 1
    return [pltpu.VMEM((2 * PACK, LANES), F32), buf, many, buf, many, buf, buf, DMA((4,)), DMA((4,)), DMA((n,)), DMA((n,))] + gather_sems(
        4, deep, side
    )


def conv_norm(masked, f0, frames, s8, normed, inv, shaped, taps, step=4):
    clips, width = s8.shape[1:]
    for j in range(0, frames, step):
        mixed = s8[CONV_BIAS][None]
        for k in range(taps):
            mixed = mixed + s8[TAPS + k][None] * masked[pl.ds(f0 + j + k, step)]
        center = mixed - jnp.mean(mixed, axis=-1, keepdims=True)
        inv_std = lax.rsqrt(jnp.mean(center * center, axis=-1, keepdims=True) + EPSILON)
        norm = center * inv_std
        normed[pl.ds(f0 + j, step)] = norm
        inv[pl.ds(f0 + j, step)] = jnp.broadcast_to(inv_std, (step, clips, LANES))
        rows = norm * s8[SCALE][None] + s8[SHIFT][None]
        at = pl.multiple_of((f0 + j) * clips, step * clips)
        shaped[pl.ds(at, step * clips), :] = rows.reshape(step * clips, width).astype(BF16)


def up_gelu(shaped, up_cols, u8, act, r0, slope, rows, hidden, cols=256, sub=16):
    left = shaped[pl.ds(r0, rows), :]
    for n in range(0, hidden, cols):
        before = mm(left, up_cols(n, n + cols), NN)
        for r in range(0, rows, sub):
            piece = before[r : r + sub].reshape(sub // 8, 8, cols) + u8[:, n : n + cols][None]
            a, s = gelu_pair(piece.reshape(sub, cols))
            act[pl.ds(r0 + r, sub), n : n + cols] = a.astype(BF16)
            slope[r : r + sub, n : n + cols] = s.astype(slope.dtype)


def forward_kernel(*refs, near, deep, side, ft, taps, group_count):
    lens, groups, frames = refs[:3]
    if near:
        shards, refs = refs[3:12], refs[12:]
        (out, act_out, slope, normed_out, inv_out, shaped_out, masked_out, up_out, down_out, small_full, upb_full) = refs[:11]
        refs = refs[11:]
    else:
        small_full, upb_full, up_full, down_full = refs[3:7]
        (out, act_out, slope, normed_out, inv_out, shaped_out, masked_out) = refs[7:14]
        refs = refs[14:]
    (stream, masked0, masked1, normed, inv, shaped, first_rows, act, s8, u8, len8, save_sem, act_sem, row_sem) = refs[:14]
    refs = refs[14:]
    if near:
        up_full, down_full = refs[:2]
        gather_refs = refs[2:]

    i = pl.program_id(0)
    clips, frame_count, width = frames.shape
    hidden = act.shape[1]
    tiles = frame_count // ft
    rows = ft * clips

    def up_cols(b):
        if near:
            return lambda lo, hi: up_full[b, :, :, :, :, :, lo:hi].reshape(width, hi - lo)
        return lambda lo, hi: up_full[b, :, lo:hi]

    def down_rows(b):
        return down_full[b].reshape(hidden, width)

    body = pl.ds(HALO, frame_count)
    save = lambda n, src, dst: pltpu.make_async_copy(src, dst, save_sem.at[n])
    saves0 = [
        save(0, masked0.at[body], masked_out.at[0]), save(1, normed, normed_out.at[0]),
        save(2, inv, inv_out.at[0]), save(3, shaped, shaped_out.at[0]),
    ]
    save_masked1 = save(4, masked1.at[body], masked_out.at[1])
    tail = lambda b, j: pltpu.make_async_copy(
        act.at[pl.ds(pl.multiple_of(j * rows, rows), rows)],
        act_out.at[b, pl.ds(pl.multiple_of(j * rows, rows), rows)], act_sem.at[j])

    def row_saves(j):
        f = pl.ds(j * ft, ft)
        r = pl.ds(pl.multiple_of(j * rows, rows), rows)
        return [
            pltpu.make_async_copy(normed.at[f], normed_out.at[1, f], row_sem.at[0, j]),
            pltpu.make_async_copy(inv.at[f], inv_out.at[1, f], row_sem.at[1, j]),
            pltpu.make_async_copy(shaped.at[r], shaped_out.at[1, r], row_sem.at[2, j]),
        ]

    def spread():
        def one(n, carry):
            t0 = pl.multiple_of(n * 16, 16)
            spread_clips(frames, t0, stream, 0, 16)
            v = rows_of(stream, 0, 16 * clips)
            at = pl.multiple_of(t0 * clips, 16 * clips)
            first_rows[pl.ds(at, 16 * clips), :] = v.astype(BF16)
            masked0[pl.ds(HALO + t0, 16)] = keep_frames(v.reshape(16, clips, width), t0, len8)
            return carry
        lax.fori_loop(0, frame_count // 16, one, 0)

    def conv0(lo, hi):
        def one(n, carry):
            conv_norm(masked0, n * ft, ft, s8.at[0], normed, inv, shaped, taps)
            return carry
        lax.fori_loop(lo, hi, one, 0)

    @pl.when(i == 0)
    def _():
        zeros = jnp.zeros((HALO, clips, width), F32)
        for m in (masked0, masked1):
            m[0:HALO] = zeros
            m[HALO + frame_count :] = zeros
        len8[...] = per_clip(lens, clips, width)

        def ready():
            for b in range(2):
                prepare(small_full.at[b], lens, groups, s8.at[b], len8, group_count)
                u8[b] = jnp.broadcast_to(upb_full[b, 0:1, :], u8.shape[1:])

        if near:
            Gather(shards, up_full, down_full, small_full, upb_full, gather_refs, deep, side, group_count, taps).early(
                spread, ready, conv0, tiles)
        else:
            spread()
            ready()
            conv0(0, tiles)
        for c in saves0:
            c.start()

    if near:
        Gather(shards, up_full, down_full, small_full, upb_full, gather_refs, deep, side, group_count, taps).late(
            i, tiles, up_out, down_out)

    @pl.when(i < tiles)
    def _():
        r0 = pl.multiple_of(i * rows, rows)
        up_gelu(shaped, up_cols(0), u8.at[0], act, r0, slope, rows, hidden)
        tail(0, i).start()

    @pl.when((i >= tiles) & (i < 2 * tiles))
    def _():
        j = i - tiles
        f0 = j * ft
        r0 = pl.multiple_of(j * rows, rows)
        branch = mm(act[pl.ds(r0, rows), :], down_rows(0), NN)
        for t in range(0, ft, 4):
            b = branch[t * clips : (t + 4) * clips].reshape(4, clips, width) + s8[0, DOWN_BIAS][None]
            total = masked0[pl.ds(HALO + f0 + t, 4)] + s8[0, GAIN][None] * b
            masked1[pl.ds(HALO + f0 + t, 4)] = keep_frames(total, f0 + t, len8)
        tail(0, j).wait()

    @pl.when(i == 2 * tiles)
    def _():
        for c in saves0:
            c.wait()
        save_masked1.start()

    @pl.when(i >= 2 * tiles)
    def _():
        j = i - 2 * tiles
        f0 = j * ft
        r0 = pl.multiple_of(j * rows, rows)
        conv_norm(masked1, f0, ft, s8.at[1], normed, inv, shaped, taps)
        for c in row_saves(j):
            c.start()
        up_gelu(shaped, up_cols(1), u8.at[1], act, r0, slope, rows, hidden)
        tail(1, j).start()
        branch = mm(act[pl.ds(r0, rows), :], down_rows(1), NN)
        for t in range(0, ft, 4):
            b = branch[t * clips : (t + 4) * clips].reshape(4, clips, width) + s8[1, DOWN_BIAS][None]
            total = masked1[pl.ds(HALO + f0 + t, 4)] + s8[1, GAIN][None] * b
            at = pl.multiple_of(r0 + t * clips, 4 * clips)
            first = first_rows[pl.ds(at, 4 * clips), :].astype(F32).reshape(4, clips, width)
            put_rows(stream, t * clips, keep_frames(total, f0 + t, len8, first).reshape(4 * clips, width))
        collect_clips(stream, out, ft)

    @pl.when(i == 3 * tiles - 1)
    def _():
        save_masked1.wait()
        for j in range(tiles):
            tail(1, j).wait()
            for c in row_saves(j):
                c.wait()


def forward(near, deep, side, lens, groups, frames, weights, hidden, ft, taps, group_count):
    clips, fc, d = frames.shape
    h = hidden
    n, r = fc // ft, ft * clips
    R = fc * clips
    slope_at = lambda i: jnp.where(i < n, i, jnp.where(i < 2 * n, n - 1, i - n))
    out_specs = [
        pl.BlockSpec((clips, ft, d), lambda i: (0, jnp.maximum(i - 2 * n, 0), 0)), hbm(),
        pl.BlockSpec((r, h), lambda i: (slope_at(i), 0)), hbm(), hbm(), hbm(), hbm(),
    ]
    out_shape = [
        shape((clips, fc, d), BF16), shape((2, R, h), BF16), shape((2 * R, h), BF16), shape((2, fc, clips, d)),
        shape((2, fc, clips, LANES)), shape((2, R, d), BF16), shape((2, fc, clips, d)),
    ]
    scratch = [
        pltpu.VMEM((d // LANES, max(r, 16 * clips), LANES), F32),
        pltpu.VMEM((fc + 2 * HALO, clips, d), F32), pltpu.VMEM((fc + 2 * HALO, clips, d), F32),
        pltpu.VMEM((fc, clips, d), F32), pltpu.VMEM((fc, clips, LANES), F32), pltpu.VMEM((R, d), BF16),
        pltpu.VMEM((R, d), BF16), pltpu.VMEM((R, h), BF16),
        pltpu.VMEM((2, 14, clips, d), F32), pltpu.VMEM((2, clips, h), F32), pltpu.VMEM((clips, d), jnp.int32),
        DMA((5,)), DMA((n,)), DMA((3, n)),
    ]
    params = dict(vmem_limit_bytes=VMEM_LIMIT)
    if near:
        urows, drows = weights[4].shape[1], weights[6].shape[1]
        dims = (2, deep, side, side, 2)
        full = [dims + (urows, h), dims + (drows, d)]
        in_specs = [smem(), smem(), whole(clips, fc, d)] + [vmem()] * 9
        out_specs += [hbm(), hbm(), vmem(), vmem()]
        out_shape += [shape(full[0], BF16), shape(full[1], BF16), shape((2, ROWS, d)), shape((2, 1, h))]
        scratch += [pltpu.VMEM(f, BF16) for f in full] + gather_scratch(deep, side)
        params.update(collective_id=0, has_side_effects=True)
    else:
        in_specs = [smem(), smem(), whole(clips, fc, d)] + [vmem()] * 4
    return pl.pallas_call(
        functools.partial(forward_kernel, near=near, deep=deep, side=side, ft=ft, taps=taps, group_count=group_count),
        name="forward",
        grid=(3 * n,),
        in_specs=in_specs,
        out_specs=out_specs,
        out_shape=out_shape,
        scratch_shapes=scratch,
        compiler_params=pltpu.CompilerParams(**params),
    )(lens, groups, frames, *weights)


class Scatter:
    def __init__(self, place, term, bufs, sems):
        self.place, self.term = place, term
        self.core_out, self.core_in, self.second_in, self.first_in, self.z_in = bufs
        self.sems = sems

    def entry(self, z, first, second):
        high, low = self.place.chip_of(first, second)
        return (z * self.place.side + high) * self.place.side + low

    def own(self, e, core):
        rows = self.core_in.shape[1]
        return self.term[pl.ds(pl.multiple_of((e * 2 + core) * rows, 8), rows), :]

    def fill(self, count, write):
        def one(n, carry):
            write(n)
            return carry
        lax.fori_loop(0, count, one, 0)


    def second_at(self, p):
        return (p - 1) * self.place.side * self.place.deep

    def first_at(self, p):
        return self.second_at(self.place.side) + (p - 1) * self.place.deep

    def z_at(self, p):
        return self.first_at(self.place.side) + p - 1

    def core_copies(self):
        return [send(self.core_out, self.core_in, self.sems[0].at[0], self.sems[1].at[0], self.place.core_peer())]

    def second_copies(self):
        return [
            send(self.core_out.at[pl.ds(self.second_at(p), self.place.side * self.place.deep)], self.second_in.at[p - 1], self.sems[2].at[p - 1], self.sems[3].at[p - 1], self.place.second_peer(p))
            for p in range(1, self.place.side)
        ]

    def first_copies(self):
        return [
            send(self.core_out.at[pl.ds(self.first_at(p), self.place.deep)], self.first_in.at[p - 1], self.sems[4].at[p - 1], self.sems[5].at[p - 1], self.place.first_peer(p))
            for p in range(1, self.place.side)
        ]

    def z_copies(self):
        return [
            send(self.core_out.at[self.z_at(p)], self.z_in.at[p - 1], self.sems[6].at[p - 1], self.sems[7].at[p - 1], self.place.z_peer(p))
            for p in range(1, self.place.deep)
        ]

    def core_start(self):
        def write(n):
            self.core_out[n] = self.own(n, 1 - self.place.core).astype(BF16)
        self.fill(self.core_out.shape[0], write)
        run(self.core_copies())

    def part1(self, z, first, second):
        e = self.entry(z, first, second)
        return self.own(e, self.place.core) + self.core_in[e].astype(F32)

    def part2(self, z, first):
        total = self.part1(z, first, self.place.second)
        for p in range(1, self.place.side):
            total = total + self.second_in[p - 1, first * self.place.deep + z].astype(F32)
        return total

    def part3(self, z):
        total = self.part2(z, self.place.first)
        for p in range(1, self.place.side):
            total = total + self.first_in[p - 1, z].astype(F32)
        return total

    def second_start(self):
        at = self.place
        done(self.core_copies())
        copies = self.second_copies()
        for p in range(1, at.side):
            to = lax.rem(at.second + p, at.side)
            def write(n):
                first, z = n // at.deep, lax.rem(n, at.deep)
                self.core_out[self.second_at(p) + n] = self.part1(z, first, to).astype(BF16)
            self.fill(at.side * at.deep, write)
            copies[p - 1].start()

    def first_start(self):
        at = self.place
        done(self.second_copies())
        copies = self.first_copies()
        for p in range(1, at.side):
            to = lax.rem(at.first + p, at.side)
            def write(z):
                self.core_out[self.first_at(p) + z] = self.part2(z, to).astype(BF16)
            self.fill(at.deep, write)
            copies[p - 1].start()

    def z_start(self):
        at = self.place
        done(self.first_copies())
        copies = self.z_copies()
        for p in range(1, at.deep):
            self.core_out[self.z_at(p)] = self.part3(lax.rem(at.z + p, at.deep)).astype(BF16)
            copies[p - 1].start()

    def finish(self, out):
        done(self.z_copies())
        total = self.part3(self.place.z)
        for p in range(1, self.place.deep):
            total = total + self.z_in[p - 1].astype(F32)
        out[...] = total


def scatter_bufs(deep, side, rows, cols):
    v = lambda *lead: pltpu.VMEM(lead + (rows, cols), BF16)
    e = deep * side * side
    return [v(e), v(e), v(side - 1, side * deep), v(side - 1, deep), v(deep - 1)]


def scatter_sems(count, deep, side):
    return [DMA((count, n)) for n in (1, 1, side - 1, side - 1, side - 1, side - 1, deep - 1, deep - 1)]


def pack_small(small, upb, b, terms, deep):
    per = upb.shape[1] // deep
    o = b * PACK
    for z in range(deep):
        terms[z, o : o + 14, :] = small[0:14, z * LANES : (z + 1) * LANES]
        for q in range(per // LANES):
            at = z * per + q * LANES
            terms[z, o + 14 + q : o + 15 + q, :] = upb[:, at : at + LANES]


def sum_small(place, terms, bufs, z_in, out, s, r):
    stages = [[place.core_peer()], [place.second_peer(p) for p in range(1, place.side)],
              [place.first_peer(p) for p in range(1, place.side)]]
    n = 0
    here = terms
    for stage, peers in enumerate(stages):
        into, total_ref = bufs[stage]
        copies = []
        for p, peer in enumerate(peers):
            copies.append(send(here, into.at[p], s.at[n], r.at[n], peer))
            n += 1
        run(copies)
        yield
        done(copies)
        total = here[...]
        for p in range(len(peers)):
            total = total + into[p]
        total_ref[...] = total
        here = total_ref
    copies = []
    for p in range(1, place.deep):
        to = lax.rem(place.z + p, place.deep)
        copies.append(send(here.at[to], z_in.at[p - 1], s.at[n], r.at[n], place.z_peer(p)))
        n += 1
    run(copies)
    yield
    done(copies)
    total = here[place.z]
    for p in range(1, place.deep):
        total = total + z_in[p - 1]
    out[...] = total


def small_bufs(deep, side):
    buf = pltpu.VMEM((deep, 2 * PACK, LANES), F32)
    many = lambda n: pltpu.VMEM((n, deep, 2 * PACK, LANES), F32)
    n = deep - 1 + 2 * (side - 1) + 1
    return [buf, many(1), buf, many(side - 1), buf, many(side - 1), buf, pltpu.VMEM((deep - 1, 2 * PACK, LANES), F32), DMA((n,)), DMA((n,))]


class Sums:
    def __init__(self, refs, dup, ddown, up_part, down_part, small_part, small_grad, upb_grad, deep, side):
        self.place = Place(deep, side)
        (self.terms, c_in, c_sum, s_in, s_sum, f_in, f_sum, self.z_in, self.small_s, self.small_r) = refs[:10]
        self.bufs = ((c_in, c_sum), (s_in, s_sum), (f_in, f_sum))
        refs = refs[10:]
        sems = refs[-8:]
        self.small_part, self.small_grad, self.upb_grad = small_part, small_grad, upb_grad
        self.jobs = {}
        self.outs = {}
        for n, (b, term, out) in enumerate(
            ((1, ddown, down_part), (1, dup, up_part), (0, ddown, down_part), (0, dup, up_part))
        ):
            job = Scatter(self.place, term.at[b], refs[5 * n : 5 * n + 5], [s.at[n] for s in sems])
            self.jobs.setdefault(b, []).append((job, out.at[b]))

    def each(self, b, what):
        for job, out in self.jobs[b]:
            if what == "finish":
                job.finish(out)
            else:
                getattr(job, what)()

    def before(self, i, span, parts, tiles):
        @pl.when(i == 0)
        def _():
            self.place.greet()

        plan = [
            (parts, 1, "core_start"), (parts + 3, 1, "second_start"), (span, 1, "first_start"),
            (span + 3, 1, "z_start"), (span + parts - 1, 1, "finish"),
            (span + parts, 0, "core_start"), (span + parts + 3, 0, "second_start"), (2 * span - 1, 0, "first_start"),
        ]
        for at, b, what in plan:
            @pl.when(i == at)
            def _():
                self.each(b, what)

    def after(self, i, span):
        @pl.when(i == 2 * span - 1)
        def _():
            self.terms[...] = jnp.zeros(self.terms.shape, F32)
            for b in range(2):
                pack_small(self.small_grad.at[b], self.upb_grad.at[b], b, self.terms, self.place.deep)
            steps = sum_small(self.place, self.terms, self.bufs, self.z_in, self.small_part, self.small_s, self.small_r)
            next(steps)
            next(steps)
            self.each(0, "z_start")
            for _ in steps:
                pass
            self.each(0, "finish")


def sums_scratch(deep, side, urows, drows, d, h):
    ub, db = scatter_bufs(deep, side, urows, h), scatter_bufs(deep, side, drows, d)
    return small_bufs(deep, side) + db + ub + db + ub + scatter_sems(4, deep, side)


def norm_back(gs, normed, inv, s8, gm, gm0, acc, frames, step=4):
    clips, width = s8.shape[1:]
    a_scale, a_shift, a_bias = acc[A_SCALE], acc[A_SHIFT], acc[A_BIAS]
    for j in range(0, frames, step):
        g = gs[j * clips : (j + step) * clips].reshape(step, clips, width)
        norm = normed[j : j + step]
        gn = g * norm
        a_scale = a_scale + fold(gn)
        a_shift = a_shift + fold(g)
        gg = g * s8[SCALE][None]
        mean = jnp.mean(gg, axis=-1, keepdims=True)
        mean_norm = jnp.mean(gn * s8[SCALE][None], axis=-1, keepdims=True)
        inv_std = jnp.concatenate([inv[j : j + step]] * (width // LANES), axis=-1)
        grad = inv_std * (gg - mean - norm * mean_norm)
        a_bias = a_bias + fold(grad)
        gm[pl.ds(gm0 + j, step)] = grad
    acc[A_SCALE], acc[A_SHIFT], acc[A_BIAS] = a_scale, a_shift, a_bias


def conv_back(gm, gm0, s8, masked, gs, t0, out, acc, frames, len8, taps, step=8):
    clips, width = len8.shape
    half = taps // 2
    for l in range(width // LANES):
        cols = slice(l * LANES, (l + 1) * LANES)
        sums = [acc[A_TAPS + k, :, cols] for k in range(taps)]
        for j in range(0, frames, step):
            here = masked[j : j + step, :, cols]
            total = None
            for k in range(taps):
                piece = gm[pl.ds(gm0 + j + half - k, step), :, cols]
                term = s8[TAPS + k, :, cols][None] * piece
                total = term if total is None else total + term
                sums[k] = sums[k] + fold(piece * here)
            t = lax.broadcasted_iota(jnp.int32, total.shape, 0) + (t0 + j)
            total = jnp.where(t < len8[:, cols][None], total, 0.0)
            total = gs[pl.ds(t0 + j, step), :, cols] + total
            gs[pl.ds(t0 + j, step), :, cols] = total
            out[l, j * clips : (j + step) * clips, :] = total.reshape(step * clips, LANES)
        for k in range(taps):
            acc[A_TAPS + k, :, cols] = sums[k]


def finish_small(acc, upb_acc, groups, s8, small_grad, upb_grad, group_count):
    clips, width = acc.shape[1:]
    member = per_clip(groups, clips, width)
    line = lambda v: jnp.sum(v, axis=0, keepdims=True)
    rows = [line(acc[A_TAPS + k]) for k in range(7)]
    rows.append(line(acc[A_BIAS]))
    for base in (A_SCALE, A_SHIFT):
        for g in range(group_count):
            rows.append(line(jnp.where(member == g, acc[base], 0.0)))
    rows.append(line(acc[A_DOWN]))
    rows.append(line((acc[A_GAIN] + s8[DOWN_BIAS] * acc[A_DOWN]) / s8[GAIN]))
    for r, row in enumerate(rows):
        small_grad[r : r + 1, :] = row
    for r in range(len(rows), small_grad.shape[0]):
        small_grad[r : r + 1, :] = jnp.zeros((1, width), F32)
    upb_grad[...] = line(upb_acc[...])


def backward_kernel(*refs, near, deep, side, ft, tiles, parts, taps, group_count):
    lens, groups, og, act, slope, normed, inv, shaped, masked, up, down, small = refs[:12]
    refs = refs[12:]
    if near:
        gs_out, up_part, down_part, small_part = refs[:4]
        dup, ddown, small_grad, upb_grad = refs[4:8]
        refs = refs[8:]
    else:
        gs_out, dup, ddown, small_grad, upb_grad = refs[:5]
        refs = refs[5:]
    gs, gb, gbef, gm, lanes, s8, len8, acc, upb_acc = refs[:9]
    refs = refs[9:]

    i = pl.program_id(0)
    frame_count, clips, width = gs.shape
    hidden = gbef.shape[1]
    cols = hidden // parts
    rows = ft * clips
    total_rows = frame_count * clips
    base = 2 * ft
    span = parts + tiles + 2
    step = lax.rem(i, span)
    b = 1 - i // span

    @pl.when(step == 0)
    def _():
        prepare(small.at[b], lens, groups, s8, len8, group_count)
        acc[...] = jnp.zeros(acc.shape, F32)

    @pl.when(i == 0)
    def _():
        gm[pl.ds(0, base)] = jnp.zeros((base, clips, width), F32)
        gm[pl.ds(base + frame_count, HALO)] = jnp.zeros((HALO, clips, width), F32)

        def one(n, carry):
            t0 = pl.multiple_of(n * 16, 16)
            spread_clips(og, t0, lanes, 0, 16)
            gs[pl.ds(t0, 16)] = rows_of(lanes, 0, 16 * clips).reshape(16, clips, width)
            return carry
        lax.fori_loop(0, frame_count // 16, one, 0)

    @pl.when(step == 0)
    def _():
        def one(n, a_down):
            t0 = n * 4
            gvb = s8[GAIN][None] * keep_frames(gs[pl.ds(t0, 4)], t0, len8)
            at = pl.multiple_of(t0 * clips, 4 * clips)
            gb[pl.ds(at, 4 * clips), :] = gvb.reshape(4 * clips, width).astype(BF16)
            return a_down + fold(gvb)
        acc[A_DOWN] = lax.fori_loop(0, frame_count // 4, one, jnp.zeros((clips, width), F32), unroll=4)

    if near:
        sums = Sums(refs, dup, ddown, up_part, down_part, small_part, small_grad, upb_grad, deep, side)
        sums.before(i, span, parts, tiles)

    @pl.when(step < parts)
    def _():
        c0 = pl.multiple_of(step * cols, cols)
        at = pl.ds(c0, cols)
        grads = gb[...]
        lower = down[0, at, :]
        term = mm(act[0], grads, TN)
        ddown[b, at, :] = term
        acc[A_GAIN] += fold((term * lower.astype(F32)).reshape(cols // 8, 8, width))
        ga = mm(grads, lower, NT)
        total = jnp.zeros((8, cols), F32)
        sub = 16
        for r in range(0, total_rows, sub):
            gr = ga[r : r + sub] * slope[0, r : r + sub, :].astype(F32)
            total = total + fold(gr.reshape(sub // 8, 8, cols))
            gbef[r : r + sub, at] = gr.astype(BF16)
        upb_acc[:, at] = total
        dup[b, :, at] = mm(shaped[0], gbef[:, at], TN)

    j = step - parts

    @pl.when((j >= 0) & (j < tiles))
    def _():
        r0 = pl.multiple_of(j * rows, rows)
        grad = mm(gbef[pl.ds(r0, rows), :], up[0], NT)
        norm_back(grad, normed.at[0], inv.at[0], s8, gm, base + j * ft, acc, ft)

    @pl.when(j >= 2)
    def _():
        conv_back(gm, base + (j - 2) * ft, s8, masked.at[0], gs, (j - 2) * ft, gs_out, acc, ft, len8, taps)

    @pl.when(step == span - 1)
    def _():
        finish_small(acc, upb_acc, groups, s8, small_grad.at[b], upb_grad.at[b], group_count)

    if near:
        sums.after(i, span)


def backward(near, deep, side, lens, groups, og, saved, ups, downs, small, ft, taps, group_count):
    act, slope, normed, inv, shaped, masked = saved
    clips, fc, d = og.shape
    h = ups.shape[2]
    R, r, n = fc * clips, ft * clips, fc // ft
    parts = 6
    cols = h // parts
    span = parts + n + 2
    block = lambda i: 1 - i // span
    part = lambda i: jnp.minimum(lax.rem(i, span), parts - 1)
    tile = lambda i: jnp.clip(lax.rem(i, span) - parts, 0, n - 1)
    late = lambda i: jnp.clip(lax.rem(i, span) - parts - 2, 0, n - 1)
    last = lambda i: jnp.clip(i - span - parts - 2, 0, n - 1)
    in_specs = [
        smem(), smem(), whole(clips, fc, d),
        pl.BlockSpec((1, R, cols), lambda i: (block(i), 0, part(i))),
        pl.BlockSpec((1, R, cols), lambda i: (block(i), 0, part(i))),
        pl.BlockSpec((1, ft, clips, d), lambda i: (block(i), tile(i), 0, 0)),
        pl.BlockSpec((1, ft, clips, LANES), lambda i: (block(i), tile(i), 0, 0)),
        pl.BlockSpec((1, R, d), lambda i: (block(i), 0, 0), pipeline_mode=pl.Buffered(1)),
        pl.BlockSpec((1, ft, clips, d), lambda i: (block(i), late(i), 0, 0)),
        pl.BlockSpec((1, d, h), lambda i: (block(i), 0, 0)),
        pl.BlockSpec((1, h, d), lambda i: (block(i), 0, 0)),
        whole(2, ROWS, d),
    ]
    out_specs = [pl.BlockSpec((d // LANES, r, LANES), lambda i: (0, last(i), 0))]
    out_shape = [shape((d // LANES, R, LANES))]
    sums = [(2, d, h), (2, h, d), (2, ROWS, d), (2, 1, h)]
    scratch = []
    params = dict(vmem_limit_bytes=VMEM_LIMIT)
    if near:
        e = deep * side * side * 2
        urows, drows = d // e, h // e
        out_specs += [vmem()] * 3
        out_shape += [shape((2, urows, h)), shape((2, drows, d)), shape((2 * PACK, LANES))]
        scratch += [pltpu.VMEM(v, F32) for v in sums]
        params.update(collective_id=1, has_side_effects=True)
    else:
        out_specs += [whole(*v) for v in sums]
        out_shape += [shape(v) for v in sums]
    scratch += [
        pltpu.VMEM((fc, clips, d), F32), pltpu.VMEM((R, d), BF16), pltpu.VMEM((R, h), BF16),
        pltpu.VMEM((fc + 2 * ft + HALO, clips, d), F32), pltpu.VMEM((d // LANES, 16 * clips, LANES), F32),
        pltpu.VMEM((14, clips, d), F32), pltpu.VMEM((clips, d), jnp.int32),
        pltpu.VMEM((12, clips, d), F32), pltpu.VMEM((clips, h), F32),
    ]
    if near:
        scratch += sums_scratch(deep, side, urows, drows, d, h)
    return pl.pallas_call(
        functools.partial(backward_kernel, near=near, deep=deep, side=side, ft=ft, tiles=n, parts=parts, taps=taps, group_count=group_count),
        name="backward",
        grid=(2 * span,),
        in_specs=in_specs,
        out_specs=out_specs,
        out_shape=out_shape,
        scratch_shapes=scratch,
        compiler_params=pltpu.CompilerParams(**params),
    )(lens, groups, og, act, slope, normed, inv, shaped, masked, ups, downs, small)


def unpack_kernel(gs, up_in, down_in, small, gin, conv_w, conv_b, scale, shift, up_w, up_b, down_w, down_b, gain):
    collect_clips(gs, gin, gin.shape[1])

    @pl.when(pl.program_id(0) == 0)
    def _():
        unpack_parts(up_in, down_in, small, conv_w, conv_b, scale, shift, up_w, up_b, down_w, down_b, gain)


def unpack_parts(up_in, down_in, small, conv_w, conv_b, scale, shift, up_w, up_b, down_w, down_b, gain):
    f = lax.axis_index("fsdp")
    width = conv_b.shape[1]
    wide = up_b.shape[1]
    span = wide * LANES // width
    turned = pltpu.roll(small[...], lax.rem(LANES - f * width, LANES), 1)
    for b in range(2):
        o = b * PACK
        for k in range(conv_w.shape[0]):
            conv_w[k, b : b + 1, :] = turned[o + k : o + k + 1, :width]
        conv_b[b : b + 1, :] = turned[o + CONV_BIAS : o + CONV_BIAS + 1, :width]
        scale[b] = turned[o + SCALE : o + SCALE + scale.shape[1], :width]
        shift[b] = turned[o + SHIFT : o + SHIFT + shift.shape[1], :width]
        down_b[b : b + 1, :] = turned[o + DOWN_BIAS : o + DOWN_BIAS + 1, :width]
        gain[b : b + 1, :] = turned[o + GAIN : o + GAIN + 1, :width]
        bias = jnp.concatenate([small[o + 14 + q : o + 15 + q, :] for q in range(span // LANES)], axis=1)
        bias = pltpu.roll(jnp.broadcast_to(bias, (8, span)), lax.rem(span - f * wide, span), 1)
        up_b[b : b + 1, :] = bias[0:1, :wide]
    up_w[...] = up_in[...]
    down_w[...] = down_in[...]


def unpack(gs, parts, clips, taps, group_count, width, wide):
    split, R, lanes = gs.shape
    fc = R // clips
    ft = 32
    if parts is None:
        return pl.pallas_call(
            lambda src, dst: collect_clips(src, dst, ft),
            name="unpack",
            grid=(fc // ft,),
            in_specs=[pl.BlockSpec((split, ft * clips, lanes), lambda i: (0, i, 0))],
            out_specs=pl.BlockSpec((clips, ft, split * lanes), lambda i: (0, i, 0)),
            out_shape=shape((clips, fc, split * lanes)),
        )(gs)
    up_in, down_in, small = parts
    outs = [(taps, 2, width), (2, width), (2, group_count, width), (2, group_count, width), up_in.shape, (2, wide),
            down_in.shape, (2, width), (2, width)]
    return pl.pallas_call(
        unpack_kernel,
        name="unpack",
        grid=(fc // ft,),
        in_specs=[pl.BlockSpec((split, ft * clips, lanes), lambda i: (0, i, 0))] + [whole(*v.shape) for v in parts],
        out_specs=[pl.BlockSpec((clips, ft, split * lanes), lambda i: (0, i, 0))] + [whole(*v) for v in outs],
        out_shape=[shape((clips, fc, split * lanes))] + [shape(v) for v in outs],
    )(gs, up_in, down_in, small)


def body(deep, fan, frames, group, lengths, conv_w, conv_b, scale, shift, up_w, up_b, down_w, down_b, gain, out_grad):
    side = math.isqrt(fan // 2)
    clips = frames.shape[0]
    taps, group_count, hidden = conv_w.shape[1], scale.shape[1], up_w.shape[2]
    width, wide = conv_b.shape[1], up_b.shape[1]
    axes = ("dp", "fsdp")
    near = width * fan == LANES and up_w.shape[1] % 16 == 0 and down_w.shape[1] % 16 == 0
    ft = 32
    if near:
        weights = (conv_w.transpose(1, 0, 2), conv_b, scale, shift, up_w, up_b, down_w, down_b, gain)
    else:
        whole_of = lambda v, axis: lax.all_gather(v, axes, axis=axis, tiled=True)
        ups, downs = whole_of(up_w, 1), whole_of(down_w, 1)
        lines = jnp.concatenate(
            [conv_w, conv_b[:, None], scale, shift, down_b[:, None], gain[:, None], jnp.zeros((2, 2, width), BF16)], axis=1
        )
        small = whole_of(lines, 2).astype(F32)
        upb = whole_of(up_b, 1).astype(F32)[:, None]
        weights = (small, upb, ups, downs)
    out, act, slope, normed, inv, shaped, masked, *full = forward(
        near, deep, side, lengths, group, frames, weights, hidden, ft, taps, group_count
    )
    if near:
        ups, downs, small, _ = full
        ups, downs = ups.reshape(2, -1, hidden), downs.reshape(2, hidden, -1)
    saved = (act, slope.reshape(act.shape), normed, inv, shaped, masked)
    gs, *parts = backward(near, deep, side, lengths, group, out_grad, saved, ups, downs, small, ft, taps, group_count)
    if near:
        gin, conv_grad, *grads = unpack(gs, parts, clips, taps, group_count, width, wide)
        return (out, gin, conv_grad.transpose(1, 0, 2), *grads)
    gin = unpack(gs, None, clips, taps, group_count, width, wide)
    dup, ddown, lines, ug = parts
    owner = lambda v, axis: lax.psum_scatter(v, axes, scatter_dimension=axis, tiled=True)
    lines = owner(lines, 2)
    return (
        out, gin, lines[:, :taps], lines[:, CONV_BIAS], lines[:, SCALE : SCALE + group_count],
        lines[:, SHIFT : SHIFT + group_count], owner(dup, 1), owner(ug[:, 0], 1), owner(ddown, 1),
        lines[:, DOWN_BIAS], lines[:, GAIN],
    )


def solution(mesh):
    split = ("dp", "fsdp")
    clip = P(split, None, None)
    first, middle, last = P(None, split), P(None, split, None), P(None, None, split)
    in_specs = (clip, P(split), P(split), last, first, last, last, middle, first, middle, first, first, clip)
    out_specs = (clip, clip, last, first, last, last, middle, first, middle, first, first)
    run = functools.partial(body, mesh.shape["dp"], mesh.shape["fsdp"])
    return jax.shard_map(run, mesh=mesh, in_specs=in_specs, out_specs=out_specs, check_vma=False)
```

```python
import functools
import math
import jax
import jax.numpy as jnp
from jax import lax
from jax.experimental import pallas as pl
from jax.experimental.pallas import tpu as pltpu
from jax.sharding import PartitionSpec as P

F32 = jnp.float32
BF16 = jnp.bfloat16
EPSILON = 1e-06
TAPS, CONV_BIAS, SCALE, SHIFT, DOWN_BIAS, GAIN, ROWS = 0, 7, 8, 10, 12, 13, 16
A_TAPS, A_BIAS, A_SCALE, A_SHIFT, A_DOWN, A_GAIN = 0, 7, 8, 9, 10, 11
HALO = 3
LANES = 128
VMEM_LIMIT = 64 * 1024 * 1024 - 128 * 1024
NN = (((1,), (0,)), ((), ()))
NT = (((1,), (1,)), ((), ()))
TN = (((0,), (0,)), ((), ()))
DMA = pltpu.SemaphoreType.DMA


def mm(a, b, dims):
    return lax.dot_general(a, b, dims, preferred_element_type=F32)


def gelu_pair(before):
    u = before * math.sqrt(0.5)
    phi = 0.5 + 0.5 * lax.erf(u)
    bell = jnp.exp2(u * u * (-math.log2(math.e))) * (1.0 / math.sqrt(math.pi))
    return before * phi, phi + u * bell


def per_clip(values, clips, width):
    rows = lax.broadcasted_iota(jnp.int32, (clips, width), 0)
    out = jnp.zeros((clips, width), jnp.int32)
    for c in range(clips):
        out = jnp.where(rows == c, values[c], out)
    return out


def prepare(small, lens, groups, s8, len8, group_count):
    clips, width = len8.shape
    for r in range(14):
        s8[r] = jnp.broadcast_to(small[r : r + 1, :], (clips, width))
    member = per_clip(groups, clips, width)
    len8[...] = per_clip(lens, clips, width)
    gain = jnp.zeros((clips, width), F32)
    shift = jnp.zeros((clips, width), F32)
    for g in range(group_count):
        chosen = jnp.where(member == g, 1.0, 0.0)
        gain = gain + chosen * s8[SCALE + g]
        shift = shift + chosen * s8[SHIFT + g]
    s8[SCALE] = gain
    s8[SHIFT] = shift


def keep_frames(v, t0, len8, other=0.0):
    t = lax.broadcasted_iota(jnp.int32, v.shape, 0) + t0
    return jnp.where(t < len8[...][None], v, other)


def spread_clips(block, t0, dst, d0, frames):
    clips = block.shape[0]
    for c in range(clips):
        for t in range(0, frames, 16):
            v = block[c, pl.ds(t0 + t, 16), :].astype(F32)
            for l in range(dst.shape[0]):
                dst[l, pl.ds((d0 + t) * clips + c, 16, stride=clips), :] = v[:, l * LANES : (l + 1) * LANES]


def collect_clips(src, block, frames):
    clips = block.shape[0]
    for c in range(clips):
        for t in range(0, frames, 16):
            for l in range(src.shape[0]):
                v = src[l, pl.ds(t * clips + c, 16, stride=clips), :]
                block[c, t : t + 16, l * LANES : (l + 1) * LANES] = v.astype(block.dtype)


def rows_of(src, start, n):
    return jnp.concatenate([src[l, pl.ds(start, n), :] for l in range(src.shape[0])], axis=-1)


def put_rows(dst, start, v):
    for l in range(dst.shape[0]):
        dst[l, pl.ds(start, v.shape[0]), :] = v[:, l * LANES : (l + 1) * LANES]


def fold(v):
    return jnp.sum(v, axis=0)


def smem():
    return pl.BlockSpec(memory_space=pltpu.SMEM)


def vmem():
    return pl.BlockSpec(memory_space=pltpu.VMEM)


def hbm():
    return pl.BlockSpec(memory_space=pl.ANY)


def whole(*dims):
    return pl.BlockSpec(dims, lambda i: (0,) * len(dims), pipeline_mode=pl.Buffered(1))


def shape(dims, dtype=F32):
    return jax.ShapeDtypeStruct(dims, dtype)


MESH = pl.DeviceIdType.MESH
PACK = 20


class Place:
    def __init__(self, deep, side):
        self.deep, self.side = deep, side
        self.z = lax.axis_index("dp")
        f = lax.axis_index("fsdp")
        self.f = f
        self.core = lax.rem(f, 2)
        chip = f // 2
        self.low = lax.rem(chip, side)
        self.high = chip // side
        self.first = jnp.where(self.core == 0, self.high, self.low)
        self.second = jnp.where(self.core == 0, self.low, self.high)

    def chip_of(self, first, second):
        high = jnp.where(self.core == 0, first, second)
        low = jnp.where(self.core == 0, second, first)
        return high, low

    def fsdp_of(self, first, second):
        high, low = self.chip_of(first, second)
        return (high * self.side + low) * 2 + self.core

    def z_peer(self, p):
        return {"dp": lax.rem(self.z + p, self.deep)}

    def first_peer(self, p):
        return {"fsdp": self.fsdp_of(lax.rem(self.first + p, self.side), self.second)}

    def second_peer(self, p):
        return {"fsdp": self.fsdp_of(self.first, lax.rem(self.second + p, self.side))}

    def core_peer(self):
        return {"fsdp": self.f + 1 - 2 * self.core}

    def greet(self):
        barrier = pltpu.get_barrier_semaphore()
        peers = [self.z_peer(p) for p in range(1, self.deep)]
        peers += [self.first_peer(p) for p in range(1, self.side)]
        peers += [self.second_peer(p) for p in range(1, self.side)]
        peers.append(self.core_peer())
        for peer in peers:
            pl.semaphore_signal(barrier, inc=1, device_id=peer, device_id_type=MESH)
        pl.semaphore_wait(barrier, len(peers))


def send(src, dst, send_sem, recv_sem, peer):
    return pltpu.make_async_remote_copy(
        src_ref=src, dst_ref=dst, send_sem=send_sem, recv_sem=recv_sem, device_id=peer, device_id_type=MESH
    )


def run(copies):
    for c in copies:
        c.start()


def done(copies):
    for c in copies:
        c.wait()


def weight_route(place, own, full, sems):
    zs, zr, fs, fr, ss, sr, cs, cr = sems
    deep, side, core = place.deep, place.side, place.core

    def held(p, q):
        high, low = place.chip_of(lax.rem(place.first + p, side), lax.rem(place.second + q, side))
        return full.at[:, high, low, core]

    mine = full.at[place.z, place.high, place.low, core]
    along_z = [send(own, mine, zs.at[p - 1], zr.at[p - 1], place.z_peer(p)) for p in range(1, deep)]
    along_first = [
        send(held(0, 0), held(0, 0), fs.at[p - 1], fr.at[p - 1], place.first_peer(p)) for p in range(1, side)
    ]
    along_second = []
    for j in range(side):
        high, low = place.chip_of(j, place.second)
        line = full.at[:, high, low, core]
        for p in range(1, side):
            n = j * (side - 1) + p - 1
            along_second.append(send(line, line, ss.at[n], sr.at[n], place.second_peer(p)))
    across = lambda p, q: send(held(p, q), held(p, q), cs.at[p * side + q], cr.at[p * side + q], place.core_peer())
    over = [[across(0, 0)], [across(p, 0) for p in range(1, side)],
            [across(p, q) for q in range(1, side) for p in range(side)]]
    return [along_z, along_first, along_second], over


def gather_sems(count, deep, side):
    one = [deep - 1, deep - 1, side - 1, side - 1, side * (side - 1), side * (side - 1), side * side, side * side]
    return [DMA((count, n)) for n in one]


def place_small(place, shards, pack, group_count, taps):
    conv_w, conv_b, scale, shift, up_b, down_b, gain = shards
    width = conv_b.shape[1]
    lane = lax.broadcasted_iota(jnp.int32, (width, LANES), 1)
    row = lax.broadcasted_iota(jnp.int32, (width, LANES), 0)
    spot = jnp.where(lane == row + place.f * width, 1.0, 0.0).astype(BF16)
    wide = up_b.shape[1]
    span = wide * LANES // width
    lane = lax.broadcasted_iota(jnp.int32, (wide, span), 1)
    row = lax.broadcasted_iota(jnp.int32, (wide, span), 0)
    spread = jnp.where(lane == row + place.f * wide, 1.0, 0.0).astype(BF16)
    pack[...] = jnp.zeros(pack.shape, F32)
    for b in range(2):
        o = b * PACK
        for k in range(taps):
            pack[o + k : o + k + 1, :] = mm(conv_w[k, b : b + 1, :], spot, NN)
        pack[o + SCALE : o + SCALE + group_count, :] = mm(scale[b], spot, NN)
        pack[o + SHIFT : o + SHIFT + group_count, :] = mm(shift[b], spot, NN)
        for src, at in ((conv_b, CONV_BIAS), (down_b, DOWN_BIAS), (gain, GAIN)):
            pack[o + at : o + at + 1, :] = mm(src[b : b + 1, :], spot, NN)
        bias = mm(up_b[b : b + 1, :], spread, NN)
        for q in range(span // LANES):
            pack[o + 14 + q : o + 15 + q, :] = bias[:, q * LANES : (q + 1) * LANES]


class Gather:
    def __init__(self, shards, up_full, down_full, small_full, upb_full, refs, deep, side, group_count, taps):
        (self.pack, self.zbuf, self.first_in, self.first_sum, self.second_in, self.second_sum, self.core_in,
         self.local_sems, self.small_s, self.small_r) = refs[:10]
        sems = refs[10:]
        self.place = place = Place(deep, side)
        self.small_full, self.upb_full, self.shards = small_full, upb_full, shards
        self.group_count, self.taps = group_count, taps
        up_w, down_w = shards[4], shards[6]
        self.full = (up_full, down_full)
        self.routes, self.local = [], []
        for n, (own, full) in enumerate(
            ((up_w.at[0], up_full.at[0]), (down_w.at[0], down_full.at[0]), (up_w.at[1], up_full.at[1]), (down_w.at[1], down_full.at[1]))
        ):
            self.routes.append(weight_route(place, own, full, [s.at[n] for s in sems]))
            spot = full.at[place.z, place.high, place.low, place.core]
            self.local.append(pltpu.make_async_copy(own, spot, self.local_sems.at[n]))
        stages = [
            [(self.zbuf.at[place.z], self.zbuf.at[place.z], place.z_peer(p)) for p in range(1, deep)],
            [(self.zbuf, self.first_in.at[p - 1], place.first_peer(p)) for p in range(1, side)],
            [(self.first_sum, self.second_in.at[p - 1], place.second_peer(p)) for p in range(1, side)],
            [(self.second_sum, self.core_in, place.core_peer())],
        ]
        n = 0
        self.small = []
        for stage in stages:
            copies = []
            for src, dst, peer in stage:
                copies.append(send(src, dst, self.small_s.at[n], self.small_r.at[n], peer))
                n += 1
            self.small.append(copies)

    def begin(self, n):
        run(self.routes[n][0][0])
        self.local[n].start()

    def after_z(self, n):
        along, over = self.routes[n]
        self.local[n].wait()
        done(along[0])
        run(along[1])
        run(over[0])

    def after_first(self, n):
        along, over = self.routes[n]
        done(along[1])
        run(along[2])
        run(over[1])

    def after_second(self, n):
        along, over = self.routes[n]
        done(along[2])
        run(over[2])

    def end(self, n):
        for copies in self.routes[n][1]:
            done(copies)

    def early(self, spread, ready, conv, tiles):
        place = self.place
        place.greet()
        self.begin(0)
        conv_w, conv_b, scale, shift, _, up_b, _, down_b, gain = self.shards
        place_small(place, (conv_w, conv_b, scale, shift, up_b, down_b, gain), self.pack, self.group_count, self.taps)
        self.zbuf[place.z] = self.pack[...]
        run(self.small[0])
        self.begin(1)
        spread()
        done(self.small[0])
        run(self.small[1])
        self.after_z(0)
        done(self.small[1])
        total = self.zbuf[...]
        for p in range(1, place.side):
            total = total + self.first_in[p - 1]
        self.first_sum[...] = total
        run(self.small[2])
        self.after_z(1)
        self.begin(2)
        self.begin(3)
        done(self.small[2])
        total = self.first_sum[...]
        for p in range(1, place.side):
            total = total + self.second_in[p - 1]
        self.second_sum[...] = total
        run(self.small[3])
        self.after_first(0)
        done(self.small[3])
        self.finish_small()
        ready()
        conv(0, tiles // 4)
        self.after_first(1)
        conv(tiles // 4, tiles // 2)
        self.after_second(0)
        conv(tiles // 2, tiles)
        self.after_second(1)
        self.end(0)

    def finish_small(self):
        total = self.second_sum[...] + self.core_in[...]
        deep = self.place.deep
        per = self.upb_full.shape[2] // deep
        self.small_full[...] = jnp.zeros(self.small_full.shape, F32)
        for b in range(2):
            o = b * PACK
            for z in range(deep):
                self.small_full[b, 0:14, z * LANES : (z + 1) * LANES] = total[z, o : o + 14, :]
                for q in range(per // LANES):
                    at = z * per + q * LANES
                    self.upb_full[b, :, at : at + LANES] = total[z, o + 14 + q : o + 15 + q, :]

    def late(self, i, tiles):
        @pl.when(i == 1)
        def _():
            self.after_z(2)
            self.after_z(3)

        @pl.when(i == tiles // 2 + 1)
        def _():
            self.after_first(2)
            self.after_first(3)

        @pl.when(i == tiles)
        def _():
            self.end(1)

        @pl.when(i == 2 * tiles - tiles // 4)
        def _():
            self.after_second(2)
            self.after_second(3)

        @pl.when(i == 2 * tiles)
        def _():
            for n in (2, 3):
                self.end(n)


def gather_scratch(deep, side):
    buf = pltpu.VMEM((deep, 2 * PACK, LANES), F32)
    many = pltpu.VMEM((side - 1, deep, 2 * PACK, LANES), F32)
    n = deep - 1 + 2 * (side - 1) + 1
    return [pltpu.VMEM((2 * PACK, LANES), F32), buf, many, buf, many, buf, buf, DMA((4,)), DMA((n,)), DMA((n,))] + gather_sems(
        4, deep, side
    )


def conv_norm(masked, f0, frames, s8, normed, inv, shaped, taps, n0=0, step=4):
    clips, width = s8.shape[1:]
    for j in range(0, frames, step):
        mixed = s8[CONV_BIAS][None]
        for k in range(taps):
            mixed = mixed + s8[TAPS + k][None] * masked[pl.ds(f0 + j + k, step)]
        center = mixed - jnp.mean(mixed, axis=-1, keepdims=True)
        inv_std = lax.rsqrt(jnp.mean(center * center, axis=-1, keepdims=True) + EPSILON)
        norm = center * inv_std
        normed[pl.ds(n0 + f0 + j, step)] = norm
        inv[pl.ds(f0 + j, step)] = jnp.broadcast_to(inv_std, (step, clips, LANES))
        rows = norm * s8[SCALE][None] + s8[SHIFT][None]
        at = pl.multiple_of((f0 + j) * clips, step * clips)
        shaped[pl.ds(at, step * clips), :] = rows.reshape(step * clips, width).astype(BF16)


def up_gelu(shaped, up_cols, u8, act, r0, slope, s0, rows, hidden, cols=256, sub=16):
    left = shaped[pl.ds(r0, rows), :]
    for n in range(0, hidden, cols):
        before = mm(left, up_cols(n, n + cols), NN)
        for r in range(0, rows, sub):
            piece = before[r : r + sub].reshape(sub // 8, 8, cols) + u8[:, n : n + cols][None]
            a, s = gelu_pair(piece.reshape(sub, cols))
            act[pl.ds(r0 + r, sub), n : n + cols] = a.astype(BF16)
            slope[pl.ds(s0 + r, sub), n : n + cols] = s.astype(slope.dtype)


def forward_kernel(
    lens, groups, frames, small_full, upb_full, up_full, down_full, out, act_out, slope, normed_out, inv_out, shaped_out, masked_out,
    stream, masked0, masked1, normed, inv, shaped, first_rows, act, s8, u8, len8, save_sem, act_sem, row_sem, *, ft, taps, group_count,
):
    i = pl.program_id(0)
    clips, frame_count, width = frames.shape
    hidden = act.shape[1]
    tiles = frame_count // ft
    rows = ft * clips

    def up_cols(b):
        return lambda lo, hi: up_full[b, :, lo:hi]

    body = pl.ds(HALO, frame_count)
    save = lambda n, src, dst: pltpu.make_async_copy(src, dst, save_sem.at[n])
    saves0 = [
        save(0, masked0.at[body], masked_out.at[0]), save(1, normed, normed_out.at[0]),
        save(2, inv, inv_out.at[0]), save(3, shaped, shaped_out.at[0]),
    ]
    save_masked1 = save(4, masked1.at[body], masked_out.at[1])
    tail = lambda b, j: pltpu.make_async_copy(
        act.at[pl.ds(pl.multiple_of(j * rows, rows), rows)],
        act_out.at[b, pl.ds(pl.multiple_of(j * rows, rows), rows)], act_sem.at[j])

    def row_saves(j):
        f = pl.ds(j * ft, ft)
        r = pl.ds(pl.multiple_of(j * rows, rows), rows)
        return [
            pltpu.make_async_copy(normed.at[f], normed_out.at[1, f], row_sem.at[0, j]),
            pltpu.make_async_copy(inv.at[f], inv_out.at[1, f], row_sem.at[1, j]),
            pltpu.make_async_copy(shaped.at[r], shaped_out.at[1, r], row_sem.at[2, j]),
        ]

    @pl.when(i == 0)
    def _():
        zeros = jnp.zeros((HALO, clips, width), F32)
        for m in (masked0, masked1):
            m[0:HALO] = zeros
            m[HALO + frame_count :] = zeros
        len8[...] = per_clip(lens, clips, width)

        def spread(n, carry):
            t0 = pl.multiple_of(n * 16, 16)
            spread_clips(frames, t0, stream, 0, 16)
            v = rows_of(stream, 0, 16 * clips)
            at = pl.multiple_of(t0 * clips, 16 * clips)
            first_rows[pl.ds(at, 16 * clips), :] = v.astype(BF16)
            masked0[pl.ds(HALO + t0, 16)] = keep_frames(v.reshape(16, clips, width), t0, len8)
            return carry
        lax.fori_loop(0, frame_count // 16, spread, 0)
        for b in range(2):
            prepare(small_full.at[b], lens, groups, s8.at[b], len8, group_count)
            u8[b] = jnp.broadcast_to(upb_full[b, 0:1, :], u8.shape[1:])

        def conv0(n, carry):
            conv_norm(masked0, n * ft, ft, s8.at[0], normed, inv, shaped, taps)
            return carry
        lax.fori_loop(0, tiles, conv0, 0)
        for c in saves0:
            c.start()

    @pl.when(i < tiles)
    def _():
        r0 = pl.multiple_of(i * rows, rows)
        up_gelu(shaped, up_cols(0), u8.at[0], act, r0, slope, 0, rows, hidden)
        tail(0, i).start()

    @pl.when((i >= tiles) & (i < 2 * tiles))
    def _():
        j = i - tiles
        f0 = j * ft
        r0 = pl.multiple_of(j * rows, rows)
        branch = mm(act[pl.ds(r0, rows), :], down_full[0], NN)
        for t in range(0, ft, 4):
            b = branch[t * clips : (t + 4) * clips].reshape(4, clips, width) + s8[0, DOWN_BIAS][None]
            total = masked0[pl.ds(HALO + f0 + t, 4)] + s8[0, GAIN][None] * b
            masked1[pl.ds(HALO + f0 + t, 4)] = keep_frames(total, f0 + t, len8)
        tail(0, j).wait()

    @pl.when(i == 2 * tiles)
    def _():
        for c in saves0:
            c.wait()
        save_masked1.start()

    @pl.when(i >= 2 * tiles)
    def _():
        j = i - 2 * tiles
        f0 = j * ft
        r0 = pl.multiple_of(j * rows, rows)
        conv_norm(masked1, f0, ft, s8.at[1], normed, inv, shaped, taps)
        for c in row_saves(j):
            c.start()
        up_gelu(shaped, up_cols(1), u8.at[1], act, r0, slope, 0, rows, hidden)
        tail(1, j).start()
        branch = mm(act[pl.ds(r0, rows), :], down_full[1], NN)
        last_block(branch, masked1, f0, r0, ft, s8.at[1], len8, first_rows, stream, out)

    @pl.when(i == 3 * tiles - 1)
    def _():
        save_masked1.wait()
        for j in range(tiles):
            tail(1, j).wait()
            for c in row_saves(j):
                c.wait()


def last_block(branch, masked1, f0, r0, ft, s8, len8, first_rows, stream, out):
    clips, width = len8.shape
    for t in range(0, ft, 4):
        b = branch[t * clips : (t + 4) * clips].reshape(4, clips, width) + s8[DOWN_BIAS][None]
        total = masked1[pl.ds(HALO + f0 + t, 4)] + s8[GAIN][None] * b
        at = pl.multiple_of(r0 + t * clips, 4 * clips)
        first = first_rows[pl.ds(at, 4 * clips), :].astype(F32).reshape(4, clips, width)
        put_rows(stream, t * clips, keep_frames(total, f0 + t, len8, first).reshape(4 * clips, width))
    collect_clips(stream, out, ft)


def forward(lens, groups, frames, weights, hidden, ft, taps, group_count):
    clips, fc, d = frames.shape
    h = hidden
    n, r = fc // ft, ft * clips
    R = fc * clips
    slope_at = lambda i: jnp.where(i < n, i, jnp.where(i < 2 * n, n - 1, i - n))
    return pl.pallas_call(
        functools.partial(forward_kernel, ft=ft, taps=taps, group_count=group_count),
        name="forward",
        grid=(3 * n,),
        in_specs=[smem(), smem(), whole(clips, fc, d)] + [vmem()] * 4,
        out_specs=[
            pl.BlockSpec((clips, ft, d), lambda i: (0, jnp.maximum(i - 2 * n, 0), 0)), hbm(),
            pl.BlockSpec((r, h), lambda i: (slope_at(i), 0)), hbm(), hbm(), hbm(), hbm(),
        ],
        out_shape=[
            shape((clips, fc, d), BF16), shape((2, R, h), BF16), shape((2 * R, h), BF16), shape((2, fc, clips, d)),
            shape((2, fc, clips, LANES)), shape((2, R, d), BF16), shape((2, fc, clips, d)),
        ],
        scratch_shapes=[
            pltpu.VMEM((d // LANES, max(r, 16 * clips), LANES), F32),
            pltpu.VMEM((fc + 2 * HALO, clips, d), F32), pltpu.VMEM((fc + 2 * HALO, clips, d), F32),
            pltpu.VMEM((fc, clips, d), F32), pltpu.VMEM((fc, clips, LANES), F32), pltpu.VMEM((R, d), BF16),
            pltpu.VMEM((R, d), BF16), pltpu.VMEM((R, h), BF16),
            pltpu.VMEM((2, 14, clips, d), F32), pltpu.VMEM((2, clips, h), F32), pltpu.VMEM((clips, d), jnp.int32),
            DMA((5,)), DMA((n,)), DMA((3, n)),
        ],
        compiler_params=pltpu.CompilerParams(vmem_limit_bytes=VMEM_LIMIT),
    )(lens, groups, frames, *weights)


class Scatter:
    def __init__(self, place, term, bufs, sems):
        self.place, self.term = place, term
        self.core_in, self.second_in, self.first_in, self.z_in = bufs
        self.sems = sems

    def line(self, first, second):
        high, low = self.place.chip_of(first, second)
        return self.term.at[:, high, low, self.place.core]

    def spot(self, z, first, second):
        high, low = self.place.chip_of(first, second)
        return (z, high, low)

    def core_copies(self):
        at = self.place
        return [send(self.term.at[:, :, :, 1 - at.core], self.core_in, self.sems[0].at[0], self.sems[1].at[0], at.core_peer())]

    def second_copies(self, p):
        at = self.place
        to = lax.rem(at.second + p, at.side)
        n = (p - 1) * at.side
        return [
            send(self.line(f, to), self.second_in.at[p - 1, f], self.sems[2].at[n + f], self.sems[3].at[n + f], at.second_peer(p))
            for f in range(at.side)
        ]

    def first_copy(self, p):
        at = self.place
        to = lax.rem(at.first + p, at.side)
        return send(self.line(to, at.second), self.first_in.at[p - 1], self.sems[4].at[p - 1], self.sems[5].at[p - 1], at.first_peer(p))

    def z_copy(self, p):
        at = self.place
        to = lax.rem(at.z + p, at.deep)
        high, low = at.chip_of(at.first, at.second)
        return send(self.term.at[to, high, low, at.core], self.z_in.at[p - 1], self.sems[6].at[p - 1], self.sems[7].at[p - 1], at.z_peer(p))

    def part1(self, z, first, second):
        z, high, low = self.spot(z, first, second)
        return self.term[z, high, low, self.place.core].astype(F32) + self.core_in[z, high, low].astype(F32)

    def part2(self, z, first):
        total = self.part1(z, first, self.place.second)
        for p in range(1, self.place.side):
            total = total + self.second_in[p - 1, first, z].astype(F32)
        return total

    def part3(self, z):
        total = self.part2(z, self.place.first)
        for p in range(1, self.place.side):
            total = total + self.first_in[p - 1, z].astype(F32)
        return total

    def put(self, z, first, second, total):
        z, high, low = self.spot(z, first, second)
        self.term[z, high, low, self.place.core] = total.astype(BF16)

    def core_start(self):
        run(self.core_copies())

    def second_start(self):
        at = self.place
        done(self.core_copies())
        for p in range(1, at.side):
            to = lax.rem(at.second + p, at.side)
            copies = self.second_copies(p)
            for first in range(at.side):
                def one(z, carry):
                    self.put(z, first, to, self.part1(z, first, to))
                    return carry
                lax.fori_loop(0, at.deep, one, 0)
                copies[first].start()

    def first_start(self):
        at = self.place
        for p in range(1, at.side):
            done(self.second_copies(p))
        for p in range(1, at.side):
            to = lax.rem(at.first + p, at.side)
            def one(z, carry):
                self.put(z, to, at.second, self.part2(z, to))
                return carry
            lax.fori_loop(0, at.deep, one, 0)
            self.first_copy(p).start()

    def z_start(self):
        at = self.place
        done([self.first_copy(p) for p in range(1, at.side)])
        for p in range(1, at.deep):
            to = lax.rem(at.z + p, at.deep)
            self.put(to, at.first, at.second, self.part3(to))
            self.z_copy(p).start()

    def finish(self, out):
        at = self.place
        done([self.z_copy(p) for p in range(1, at.deep)])
        total = self.part3(at.z)
        for p in range(1, at.deep):
            total = total + self.z_in[p - 1].astype(F32)
        out[...] = total


def scatter_bufs(deep, side, rows, cols):
    v = lambda *lead: pltpu.VMEM(lead + (rows, cols), BF16)
    return [v(deep, side, side), v(side - 1, side, deep), v(side - 1, deep), v(deep - 1)]


def scatter_sems(count, deep, side):
    return [DMA((count, n)) for n in (1, 1, side * (side - 1), side * (side - 1), side - 1, side - 1, deep - 1, deep - 1)]


def pack_small(small, upb, b, terms, deep):
    per = upb.shape[1] // deep
    o = b * PACK
    for z in range(deep):
        terms[z, o : o + 14, :] = small[0:14, z * LANES : (z + 1) * LANES]
        for q in range(per // LANES):
            at = z * per + q * LANES
            terms[z, o + 14 + q : o + 15 + q, :] = upb[:, at : at + LANES]


def sum_small(place, terms, bufs, z_in, out, s, r):
    stages = [[place.core_peer()], [place.second_peer(p) for p in range(1, place.side)],
              [place.first_peer(p) for p in range(1, place.side)]]
    n = 0
    here = terms
    for stage, peers in enumerate(stages):
        into, total_ref = bufs[stage]
        copies = []
        for p, peer in enumerate(peers):
            copies.append(send(here, into.at[p], s.at[n], r.at[n], peer))
            n += 1
        run(copies)
        yield
        done(copies)
        total = here[...]
        for p in range(len(peers)):
            total = total + into[p]
        total_ref[...] = total
        here = total_ref
    copies = []
    for p in range(1, place.deep):
        to = lax.rem(place.z + p, place.deep)
        copies.append(send(here.at[to], z_in.at[p - 1], s.at[n], r.at[n], place.z_peer(p)))
        n += 1
    run(copies)
    yield
    done(copies)
    total = here[place.z]
    for p in range(1, place.deep):
        total = total + z_in[p - 1]
    out[...] = total


def small_bufs(deep, side):
    buf = pltpu.VMEM((deep, 2 * PACK, LANES), F32)
    many = lambda n: pltpu.VMEM((n, deep, 2 * PACK, LANES), F32)
    n = deep - 1 + 2 * (side - 1) + 1
    return [buf, many(1), buf, many(side - 1), buf, many(side - 1), buf, pltpu.VMEM((deep - 1, 2 * PACK, LANES), F32), DMA((n,)), DMA((n,))]


class Sums:
    def __init__(self, refs, dup, ddown, up_part, down_part, small_part, small_grad, upb_grad, deep, side):
        self.place = Place(deep, side)
        (self.terms, c_in, c_sum, s_in, s_sum, f_in, f_sum, self.z_in, self.small_s, self.small_r) = refs[:10]
        self.bufs = ((c_in, c_sum), (s_in, s_sum), (f_in, f_sum))
        refs = refs[10:]
        sems = refs[-8:]
        self.small_part, self.small_grad, self.upb_grad = small_part, small_grad, upb_grad
        self.jobs = {}
        self.outs = {}
        for n, (b, term, out) in enumerate(
            ((1, ddown, down_part), (1, dup, up_part), (0, ddown, down_part), (0, dup, up_part))
        ):
            job = Scatter(self.place, term.at[b], refs[4 * n : 4 * n + 4], [s.at[n] for s in sems])
            self.jobs.setdefault(b, []).append((job, out.at[b]))

    def each(self, b, what):
        for job, out in self.jobs[b]:
            if what == "finish":
                job.finish(out)
            else:
                getattr(job, what)()

    def before(self, i, span, parts, tiles):
        plan = [
            (parts, 1, "core_start"), (parts + 3, 1, "second_start"), (span, 1, "first_start"),
            (span + 3, 1, "z_start"), (span + parts - 1, 1, "finish"),
            (span + parts, 0, "core_start"), (span + parts + 3, 0, "second_start"), (2 * span - 1, 0, "first_start"),
        ]
        for at, b, what in plan:
            @pl.when(i == at)
            def _():
                self.each(b, what)

    def after(self, i, span):
        @pl.when(i == 2 * span - 1)
        def _():
            self.terms[...] = jnp.zeros(self.terms.shape, F32)
            for b in range(2):
                pack_small(self.small_grad.at[b], self.upb_grad.at[b], b, self.terms, self.place.deep)
            steps = sum_small(self.place, self.terms, self.bufs, self.z_in, self.small_part, self.small_s, self.small_r)
            next(steps)
            next(steps)
            self.each(0, "z_start")
            for _ in steps:
                pass
            self.each(0, "finish")


def sums_scratch(deep, side, urows, drows, d, h):
    ub, db = scatter_bufs(deep, side, urows, h), scatter_bufs(deep, side, drows, d)
    return small_bufs(deep, side) + db + ub + db + ub + scatter_sems(4, deep, side)


def norm_back(gs, normed, n0, inv, i0, s8, gm, gm0, acc, frames, step=4):
    clips, width = s8.shape[1:]
    a_scale, a_shift, a_bias = acc[A_SCALE], acc[A_SHIFT], acc[A_BIAS]
    for j in range(0, frames, step):
        g = gs[j * clips : (j + step) * clips].reshape(step, clips, width)
        norm = normed[pl.ds(n0 + j, step)]
        gn = g * norm
        a_scale = a_scale + fold(gn)
        a_shift = a_shift + fold(g)
        gg = g * s8[SCALE][None]
        mean = jnp.mean(gg, axis=-1, keepdims=True)
        mean_norm = jnp.mean(gn * s8[SCALE][None], axis=-1, keepdims=True)
        inv_std = jnp.concatenate([inv[pl.ds(i0 + j, step)]] * (width // LANES), axis=-1)
        grad = inv_std * (gg - mean - norm * mean_norm)
        a_bias = a_bias + fold(grad)
        gm[pl.ds(gm0 + j, step)] = grad
    acc[A_SCALE], acc[A_SHIFT], acc[A_BIAS] = a_scale, a_shift, a_bias


def conv_back(gm, gm0, s8, masked, m0, gs, g0, t0, out, acc, frames, len8, taps, step=8):
    clips, width = len8.shape
    half = taps // 2
    for l in range(width // LANES):
        cols = slice(l * LANES, (l + 1) * LANES)
        sums = [acc[A_TAPS + k, :, cols] for k in range(taps)]
        for j in range(0, frames, step):
            here = masked[pl.ds(m0 + j, step), :, cols]
            total = None
            for k in range(taps):
                piece = gm[pl.ds(gm0 + j + half - k, step), :, cols]
                term = s8[TAPS + k, :, cols][None] * piece
                total = term if total is None else total + term
                sums[k] = sums[k] + fold(piece * here)
            t = lax.broadcasted_iota(jnp.int32, total.shape, 0) + (t0 + j)
            total = jnp.where(t < len8[:, cols][None], total, 0.0)
            total = gs[pl.ds(g0 + j, step), :, cols] + total
            gs[pl.ds(g0 + j, step), :, cols] = total
            out[l, j * clips : (j + step) * clips, :] = total.reshape(step * clips, LANES)
        for k in range(taps):
            acc[A_TAPS + k, :, cols] = sums[k]


def finish_small(acc, upb_acc, groups, s8, small_grad, upb_grad, group_count):
    clips, width = acc.shape[1:]
    member = per_clip(groups, clips, width)
    line = lambda v: jnp.sum(v, axis=0, keepdims=True)
    rows = [line(acc[A_TAPS + k]) for k in range(7)]
    rows.append(line(acc[A_BIAS]))
    for base in (A_SCALE, A_SHIFT):
        for g in range(group_count):
            rows.append(line(jnp.where(member == g, acc[base], 0.0)))
    rows.append(line(acc[A_DOWN]))
    rows.append(line((acc[A_GAIN] + s8[DOWN_BIAS] * acc[A_DOWN]) / s8[GAIN]))
    for r, row in enumerate(rows):
        small_grad[r : r + 1, :] = row
    for r in range(len(rows), small_grad.shape[0]):
        small_grad[r : r + 1, :] = jnp.zeros((1, width), F32)
    upb_grad[...] = line(upb_acc[...])


def backward_kernel(
    lens, groups, og, act, slope, normed, inv, shaped, masked, up, down, small, gs_out, dup, ddown, small_grad, upb_grad,
    gs, gb, gbef, gm, lanes, s8, len8, acc, upb_acc, *, ft, tiles, parts, taps, group_count,
):
    i = pl.program_id(0)
    frame_count, clips, width = gs.shape
    hidden = gbef.shape[1]
    cols = hidden // parts
    rows = ft * clips
    total_rows = frame_count * clips
    base = 2 * ft
    span = parts + tiles + 2
    step = lax.rem(i, span)
    b = 1 - i // span

    @pl.when(step == 0)
    def _():
        prepare(small.at[b], lens, groups, s8, len8, group_count)
        acc[...] = jnp.zeros(acc.shape, F32)

    @pl.when(i == 0)
    def _():
        gm[pl.ds(0, base)] = jnp.zeros((base, clips, width), F32)
        gm[pl.ds(base + frame_count, HALO)] = jnp.zeros((HALO, clips, width), F32)
        spread_grad(og, lanes, gs, 0)

    @pl.when(step == 0)
    def _():
        acc[A_DOWN] = branch_grad(gs, 0, s8, len8, gb)

    @pl.when(step < parts)
    def _():
        c0 = pl.multiple_of(step * cols, cols)
        at = pl.ds(c0, cols)
        lower = down[0, at, :]
        term = mm(act[0], gb[...], TN)
        ddown[b, at, :] = term
        acc[A_GAIN] += fold((term * lower.astype(F32)).reshape(cols // 8, 8, width))
        before_grad(gb, lower, slope.at[0], slice(None), gbef, at, upb_acc, total_rows)
        dup[b, :, at] = mm(shaped[0], gbef[:, at], TN)

    j = step - parts

    @pl.when((j >= 0) & (j < tiles))
    def _():
        r0 = pl.multiple_of(j * rows, rows)
        grad = mm(gbef[pl.ds(r0, rows), :], up[0], NT)
        norm_back(grad, normed.at[0], 0, inv.at[0], 0, s8, gm, base + j * ft, acc, ft)

    @pl.when(j >= 2)
    def _():
        f0 = (j - 2) * ft
        conv_back(gm, base + f0, s8, masked.at[0], 0, gs, f0, f0, gs_out, acc, ft, len8, taps)

    @pl.when(step == span - 1)
    def _():
        finish_small(acc, upb_acc, groups, s8, small_grad.at[b], upb_grad.at[b], group_count)


def spread_grad(og, lanes, gs, g0):
    clips, frame_count, width = og.shape

    def one(n, carry):
        t0 = pl.multiple_of(n * 16, 16)
        spread_clips(og, t0, lanes, 0, 16)
        gs[pl.ds(g0 + t0, 16)] = rows_of(lanes, 0, 16 * clips).reshape(16, clips, width)
        return carry
    lax.fori_loop(0, frame_count // 16, one, 0)


def branch_grad(gs, g0, s8, len8, gb):
    clips, width = len8.shape
    frame_count = gb.shape[0] // clips

    def one(n, a_down):
        t0 = n * 4
        gvb = s8[GAIN][None] * keep_frames(gs[pl.ds(g0 + t0, 4)], t0, len8)
        at = pl.multiple_of(t0 * clips, 4 * clips)
        gb[pl.ds(at, 4 * clips), :] = gvb.reshape(4 * clips, width).astype(BF16)
        return a_down + fold(gvb)
    return lax.fori_loop(0, frame_count // 4, one, jnp.zeros((clips, width), F32), unroll=4)


def before_grad(gb, lower, slope, slope_cols, gbef, at, upb_acc, rows, sub=16):
    cols = lower.shape[0]
    ga = mm(gb[...], lower, NT)
    total = jnp.zeros((8, cols), F32)
    for r in range(0, rows, sub):
        gr = ga[r : r + sub] * slope[r : r + sub, slope_cols].astype(F32)
        total = total + fold(gr.reshape(sub // 8, 8, cols))
        gbef[r : r + sub, at] = gr.astype(BF16)
    upb_acc[:, at] = total


def backward(lens, groups, og, saved, ups, downs, small, ft, taps, group_count):
    act, slope, normed, inv, shaped, masked = saved
    clips, fc, d = og.shape
    h = ups.shape[2]
    R, r, n = fc * clips, ft * clips, fc // ft
    parts = 6
    cols = h // parts
    span = parts + n + 2
    block = lambda i: 1 - i // span
    part = lambda i: jnp.minimum(lax.rem(i, span), parts - 1)
    tile = lambda i: jnp.clip(lax.rem(i, span) - parts, 0, n - 1)
    late = lambda i: jnp.clip(lax.rem(i, span) - parts - 2, 0, n - 1)
    last = lambda i: jnp.clip(i - span - parts - 2, 0, n - 1)
    sums = [(2, d, h), (2, h, d), (2, ROWS, d), (2, 1, h)]
    return pl.pallas_call(
        functools.partial(backward_kernel, ft=ft, tiles=n, parts=parts, taps=taps, group_count=group_count),
        name="backward",
        grid=(2 * span,),
        in_specs=[
            smem(), smem(), whole(clips, fc, d),
            pl.BlockSpec((1, R, cols), lambda i: (block(i), 0, part(i))),
            pl.BlockSpec((1, R, cols), lambda i: (block(i), 0, part(i))),
            pl.BlockSpec((1, ft, clips, d), lambda i: (block(i), tile(i), 0, 0)),
            pl.BlockSpec((1, ft, clips, LANES), lambda i: (block(i), tile(i), 0, 0)),
            pl.BlockSpec((1, R, d), lambda i: (block(i), 0, 0), pipeline_mode=pl.Buffered(1)),
            pl.BlockSpec((1, ft, clips, d), lambda i: (block(i), late(i), 0, 0)),
            pl.BlockSpec((1, d, h), lambda i: (block(i), 0, 0)),
            pl.BlockSpec((1, h, d), lambda i: (block(i), 0, 0)),
            whole(2, ROWS, d),
        ],
        out_specs=[pl.BlockSpec((d // LANES, r, LANES), lambda i: (0, last(i), 0))] + [whole(*v) for v in sums],
        out_shape=[shape((d // LANES, R, LANES))] + [shape(v) for v in sums],
        scratch_shapes=[
            pltpu.VMEM((fc, clips, d), F32), pltpu.VMEM((R, d), BF16), pltpu.VMEM((R, h), BF16),
            pltpu.VMEM((fc + 2 * ft + HALO, clips, d), F32), pltpu.VMEM((d // LANES, 16 * clips, LANES), F32),
            pltpu.VMEM((14, clips, d), F32), pltpu.VMEM((clips, d), jnp.int32),
            pltpu.VMEM((12, clips, d), F32), pltpu.VMEM((clips, h), F32),
        ],
        compiler_params=pltpu.CompilerParams(vmem_limit_bytes=VMEM_LIMIT),
    )(lens, groups, og, act, slope, normed, inv, shaped, masked, ups, downs, small)


def step_kernel(*refs, deep, side, ft, parts, taps, group_count):
    lens, groups, frames, og = refs[:4]
    shards = refs[4:13]
    out, gs_out, up_part, down_part, small_part, act_far, slope_far = refs[13:20]
    (io, stream, masked0, masked1, normed, inv, shaped, first_rows, act, slope, gb, s8, u8, len8, acc, upb_acc) = refs[20:36]
    small_full, upb_full, small_grad, upb_grad, up_full, down_full, up_term, down_term = refs[36:44]
    io_sem, act_sem, slope_sem, act_back_sem, slope_back_sem = refs[44:49]
    gather_refs, sum_refs = refs[49:67], refs[67:]

    i = pl.program_id(0)
    clips, frame_count, width = io.shape
    hidden = act.shape[1]
    tiles = frame_count // ft
    rows = ft * clips
    cols = hidden // parts
    span = parts + tiles + 1
    body = pl.ds(HALO, frame_count)

    load = lambda n, src: pltpu.make_async_copy(src, io, io_sem.at[n])
    tile_rows = lambda j: pl.ds(pl.multiple_of(j * rows, rows), rows)
    part_at = lambda p: pl.ds(pl.multiple_of(p * cols, cols), cols)

    def spills(j):
        r = tile_rows(j)
        return [
            pltpu.make_async_copy(act.at[r], act_far.at[r], act_sem.at[j]),
            pltpu.make_async_copy(slope.at[r], slope_far.at[r], slope_sem.at[j]),
        ]

    def act_back(p):
        return pltpu.make_async_copy(act_far.at[:, part_at(p)], act.at[:, part_at(p)], act_back_sem.at[p])

    def slope_back(j):
        return pltpu.make_async_copy(slope_far.at[tile_rows(j)], slope.at[tile_rows(j)], slope_back_sem.at[j])

    def up_cols(b):
        return lambda lo, hi: up_full[b, :, :, :, :, :, lo:hi].reshape(width, hi - lo)

    def spread():
        load(0, frames).wait()

        def one(n, carry):
            t0 = pl.multiple_of(n * 16, 16)
            spread_clips(io, t0, stream, 0, 16)
            v = rows_of(stream, 0, 16 * clips)
            at = pl.multiple_of(t0 * clips, 16 * clips)
            first_rows[pl.ds(at, 16 * clips), :] = v.astype(BF16)
            masked0[pl.ds(HALO + t0, 16)] = keep_frames(v.reshape(16, clips, width), t0, len8)
            return carry
        lax.fori_loop(0, frame_count // 16, one, 0)
        load(1, og).start()

    def conv0(lo, hi):
        def one(n, carry):
            conv_norm(masked0, n * ft, ft, s8.at[0], normed.at[0], inv.at[0], shaped, taps, HALO)
            return carry
        lax.fori_loop(lo, hi, one, 0)

    def ready():
        for b in range(2):
            prepare(small_full.at[b], lens, groups, s8.at[b], len8, group_count)
            u8[b] = jnp.broadcast_to(upb_full[b, 0:1, :], u8.shape[1:])

    @pl.when(i == 0)
    def _():
        load(0, frames).start()
        zeros = jnp.zeros((HALO, clips, width), F32)
        for m in (masked0, masked1, normed.at[0], normed.at[1]):
            m[0:HALO] = zeros
            m[HALO + frame_count : HALO + frame_count + HALO] = zeros
        len8[...] = per_clip(lens, clips, width)
        Gather(shards, up_full, down_full, small_full, upb_full, gather_refs, deep, side, group_count, taps).early(
            spread, ready, conv0, tiles)

    Gather(shards, up_full, down_full, small_full, upb_full, gather_refs, deep, side, group_count, taps).late(i, tiles)

    @pl.when(i < tiles)
    def _():
        r0 = pl.multiple_of(i * rows, rows)
        up_gelu(shaped, up_cols(0), u8.at[0], act, r0, slope, r0, rows, hidden)
        run(spills(i))

    @pl.when((i >= tiles) & (i < 2 * tiles))
    def _():
        j = i - tiles
        f0 = j * ft
        r0 = pl.multiple_of(j * rows, rows)
        branch = mm(act[pl.ds(r0, rows), :], down_full[0].reshape(hidden, width), NN)
        for t in range(0, ft, 4):
            b = branch[t * clips : (t + 4) * clips].reshape(4, clips, width) + s8[0, DOWN_BIAS][None]
            total = masked0[pl.ds(HALO + f0 + t, 4)] + s8[0, GAIN][None] * b
            masked1[pl.ds(HALO + f0 + t, 4)] = keep_frames(total, f0 + t, len8)

    @pl.when((i >= 2 * tiles) & (i < 3 * tiles))
    def _():
        j = i - 2 * tiles
        f0 = j * ft
        r0 = pl.multiple_of(j * rows, rows)
        done(spills(j))
        conv_norm(masked1, f0, ft, s8.at[1], normed.at[1], inv.at[1], shaped, taps, HALO)
        up_gelu(shaped, up_cols(1), u8.at[1], act, r0, slope, r0, rows, hidden)
        branch = mm(act[pl.ds(r0, rows), :], down_full[1].reshape(hidden, width), NN)
        last_block(branch, masked1, f0, r0, ft, s8.at[1], len8, first_rows, stream, out)

    k = i - 3 * tiles
    step = lax.rem(jnp.maximum(k, 0), span)
    b = jnp.where(k < span, 1, 0)

    @pl.when(k == 0)
    def _():
        load(1, og).wait()
        spread_grad(io, stream, masked0, HALO)

    @pl.when(k == span)
    def _():
        def one(n, carry):
            t0 = n * 4
            at = pl.multiple_of(t0 * clips, 4 * clips)
            v = normed[0, pl.ds(HALO + t0, 4)] * s8[0, SCALE][None] + s8[0, SHIFT][None]
            shaped[pl.ds(at, 4 * clips), :] = v.reshape(4 * clips, width).astype(BF16)
            first = first_rows[pl.ds(at, 4 * clips), :].astype(F32).reshape(4, clips, width)
            masked1[pl.ds(HALO + t0, 4)] = keep_frames(first, t0, len8)
            return carry
        lax.fori_loop(0, frame_count // 4, one, 0, unroll=4)
        for j in range(tiles):
            slope_back(j).wait()

    @pl.when((k >= 0) & (step == 0))
    def _():
        acc[...] = jnp.zeros(acc.shape, F32)
        acc[A_DOWN] = branch_grad(masked0, HALO, s8.at[b], len8, gb)

    sums = Sums(sum_refs, up_term, down_term, up_part, down_part, small_part, small_grad, upb_grad, deep, side)
    sums.before(k, span, parts, tiles)

    @pl.when((k >= span) & (step < parts))
    def _():
        act_back(step).wait()

    @pl.when((k >= 0) & (step < parts))
    def _():
        at = part_at(step)
        drows, urows = down_full.shape[5], up_full.shape[5]
        per = drows // 16
        spots = []
        for m in range(cols // 16):
            row = step * (cols // 16) + m
            e = row // per
            z, chip = e // (2 * side * side), e // 2
            sub = pl.ds(pl.multiple_of((row - e * per) * 16, 16), 16)
            spots.append((b, z, lax.rem(chip // side, side), lax.rem(chip, side), lax.rem(e, 2), sub))
        lower = jnp.concatenate([down_full[spot] for spot in spots], axis=0)
        term = mm(act[:, at], gb[...], TN)
        for m, spot in enumerate(spots):
            down_term[spot] = term[m * 16 : (m + 1) * 16].astype(BF16)
        acc[A_GAIN] += fold((term * lower.astype(F32)).reshape(cols // 8, 8, width))
        before_grad(gb, lower, slope, at, slope, at, upb_acc, frame_count * clips)
        term = mm(shaped[...], slope[:, at], TN).astype(BF16)
        up_term[b, :, :, :, :, :, at] = term.reshape(deep, side, side, 2, urows, cols)

    @pl.when((k >= 0) & (k < parts))
    def _():
        act_back(step).start()

    j = step - parts

    @pl.when((j >= 0) & (j < tiles))
    def _():
        r0 = pl.multiple_of(j * rows, rows)
        grad = mm(slope[pl.ds(r0, rows), :], up_full[b].reshape(width, hidden), NT)
        norm_back(grad, normed.at[b], HALO + j * ft, inv.at[b], j * ft, s8.at[b], normed.at[b], HALO + j * ft, acc, ft)

    @pl.when((k < span) & (j >= 0) & (j < tiles))
    def _():
        slope_back(j).start()

    @pl.when(j >= 1)
    def _():
        f0 = (j - 1) * ft
        conv_back(
            normed.at[b], HALO + f0, s8.at[b], masked1, HALO + f0, masked0, HALO + f0, f0, gs_out, acc, ft, len8, taps)

    @pl.when((k >= 0) & (step == span - 1))
    def _():
        finish_small(acc, upb_acc, groups, s8.at[b], small_grad.at[b], upb_grad.at[b], group_count)

    sums.after(k, span)


def whole_step(deep, side, lens, groups, frames, og, weights, ft, taps, group_count):
    clips, fc, d = frames.shape
    h = weights[4].shape[2]
    urows, drows = weights[4].shape[1], weights[6].shape[1]
    R, r, n = fc * clips, ft * clips, fc // ft
    parts = 6
    span = parts + n + 1
    last = lambda i: jnp.clip(i - 3 * n - span - parts - 1, 0, n - 1)
    dims = (2, deep, side, side, 2)
    rows = lambda dtype, *lead: pltpu.VMEM(lead + (d,), dtype)
    halo = fc + 2 * HALO
    return pl.pallas_call(
        functools.partial(step_kernel, deep=deep, side=side, ft=ft, parts=parts, taps=taps, group_count=group_count),
        name="step",
        grid=(3 * n + 2 * span,),
        in_specs=[smem(), smem(), hbm(), hbm()] + [vmem()] * 9,
        out_specs=[
            pl.BlockSpec((clips, ft, d), lambda i: (0, jnp.clip(i - 2 * n, 0, n - 1), 0)),
            pl.BlockSpec((d // LANES, r, LANES), lambda i: (0, last(i), 0)), vmem(), vmem(), vmem(), hbm(), hbm(),
        ],
        out_shape=[
            shape((clips, fc, d), BF16), shape((d // LANES, R, LANES)), shape((2, urows, h)), shape((2, drows, d)),
            shape((2 * PACK, LANES)), shape((R, h), BF16), shape((R, h), BF16),
        ],
        scratch_shapes=[
            rows(BF16, clips, fc), pltpu.VMEM((d // LANES, max(r, 16 * clips), LANES), F32),
            rows(F32, halo, clips), rows(F32, halo, clips), rows(F32, 2, halo, clips), pltpu.VMEM((2, fc, clips, LANES), F32),
            rows(BF16, R), rows(BF16, R), pltpu.VMEM((R, h), BF16), pltpu.VMEM((R, h), BF16), rows(BF16, R),
            rows(F32, 2, 14, clips), pltpu.VMEM((2, clips, h), F32), rows(jnp.int32, clips), rows(F32, 12, clips),
            pltpu.VMEM((clips, h), F32),
            rows(F32, 2, ROWS), pltpu.VMEM((2, 1, h), F32), rows(F32, 2, ROWS), pltpu.VMEM((2, 1, h), F32),
            pltpu.VMEM(dims + (urows, h), BF16), rows(BF16, *dims, drows), pltpu.VMEM(dims + (urows, h), BF16), rows(BF16, *dims, drows),
            DMA((2,)), DMA((n,)), DMA((n,)), DMA((parts,)), DMA((n,)),
        ] + gather_scratch(deep, side) + sums_scratch(deep, side, urows, drows, d, h),
        compiler_params=pltpu.CompilerParams(vmem_limit_bytes=VMEM_LIMIT, collective_id=0, has_side_effects=True),
    )(lens, groups, frames, og, *weights)


def unpack_kernel(gs, up_in, down_in, small, gin, conv_w, conv_b, scale, shift, up_w, up_b, down_w, down_b, gain):
    collect_clips(gs, gin, gin.shape[1])

    @pl.when(pl.program_id(0) == 0)
    def _():
        unpack_parts(up_in, down_in, small, conv_w, conv_b, scale, shift, up_w, up_b, down_w, down_b, gain)


def unpack_parts(up_in, down_in, small, conv_w, conv_b, scale, shift, up_w, up_b, down_w, down_b, gain):
    f = lax.axis_index("fsdp")
    width = conv_b.shape[1]
    wide = up_b.shape[1]
    span = wide * LANES // width
    turned = pltpu.roll(small[...], lax.rem(LANES - f * width, LANES), 1)
    for b in range(2):
        o = b * PACK
        for k in range(conv_w.shape[0]):
            conv_w[k, b : b + 1, :] = turned[o + k : o + k + 1, :width]
        conv_b[b : b + 1, :] = turned[o + CONV_BIAS : o + CONV_BIAS + 1, :width]
        scale[b] = turned[o + SCALE : o + SCALE + scale.shape[1], :width]
        shift[b] = turned[o + SHIFT : o + SHIFT + shift.shape[1], :width]
        down_b[b : b + 1, :] = turned[o + DOWN_BIAS : o + DOWN_BIAS + 1, :width]
        gain[b : b + 1, :] = turned[o + GAIN : o + GAIN + 1, :width]
        bias = jnp.concatenate([small[o + 14 + q : o + 15 + q, :] for q in range(span // LANES)], axis=1)
        bias = pltpu.roll(jnp.broadcast_to(bias, (8, span)), lax.rem(span - f * wide, span), 1)
        up_b[b : b + 1, :] = bias[0:1, :wide]
    up_w[...] = up_in[...]
    down_w[...] = down_in[...]


def unpack(gs, parts, clips, taps, group_count, width, wide):
    split, R, lanes = gs.shape
    fc = R // clips
    ft = 32
    if parts is None:
        return pl.pallas_call(
            lambda src, dst: collect_clips(src, dst, ft),
            name="unpack",
            grid=(fc // ft,),
            in_specs=[pl.BlockSpec((split, ft * clips, lanes), lambda i: (0, i, 0))],
            out_specs=pl.BlockSpec((clips, ft, split * lanes), lambda i: (0, i, 0)),
            out_shape=shape((clips, fc, split * lanes)),
        )(gs)
    up_in, down_in, small = parts
    outs = [(taps, 2, width), (2, width), (2, group_count, width), (2, group_count, width), up_in.shape, (2, wide),
            down_in.shape, (2, width), (2, width)]
    return pl.pallas_call(
        unpack_kernel,
        name="unpack",
        grid=(fc // ft,),
        in_specs=[pl.BlockSpec((split, ft * clips, lanes), lambda i: (0, i, 0))] + [whole(*v.shape) for v in parts],
        out_specs=[pl.BlockSpec((clips, ft, split * lanes), lambda i: (0, i, 0))] + [whole(*v) for v in outs],
        out_shape=[shape((clips, fc, split * lanes))] + [shape(v) for v in outs],
    )(gs, up_in, down_in, small)


def body(deep, fan, frames, group, lengths, conv_w, conv_b, scale, shift, up_w, up_b, down_w, down_b, gain, out_grad):
    side = math.isqrt(fan // 2)
    clips = frames.shape[0]
    taps, group_count, hidden = conv_w.shape[1], scale.shape[1], up_w.shape[2]
    width, wide = conv_b.shape[1], up_b.shape[1]
    axes = ("dp", "fsdp")
    near = width * fan == LANES and up_w.shape[1] % 16 == 0 and down_w.shape[1] % 16 == 0
    ft = 32
    if near:
        weights = (conv_w.transpose(1, 0, 2), conv_b, scale, shift, up_w, up_b, down_w, down_b, gain)
    else:
        whole_of = lambda v, axis: lax.all_gather(v, axes, axis=axis, tiled=True)
        ups, downs = whole_of(up_w, 1), whole_of(down_w, 1)
        lines = jnp.concatenate(
            [conv_w, conv_b[:, None], scale, shift, down_b[:, None], gain[:, None], jnp.zeros((2, 2, width), BF16)], axis=1
        )
        small = whole_of(lines, 2).astype(F32)
        upb = whole_of(up_b, 1).astype(F32)[:, None]
        weights = (small, upb, ups, downs)
    if near:
        out, gs, *parts, _, _ = whole_step(deep, side, lengths, group, frames, out_grad, weights, ft, taps, group_count)
        gin, conv_grad, *grads = unpack(gs, parts, clips, taps, group_count, width, wide)
        return (out, gin, conv_grad.transpose(1, 0, 2), *grads)
    out, act, slope, *rest = forward(lengths, group, frames, weights, hidden, ft, taps, group_count)
    saved = (act, slope.reshape(act.shape), *rest)
    gs, *parts = backward(lengths, group, out_grad, saved, ups, downs, small, ft, taps, group_count)
    gin = unpack(gs, None, clips, taps, group_count, width, wide)
    dup, ddown, lines, ug = parts
    owner = lambda v, axis: lax.psum_scatter(v, axes, scatter_dimension=axis, tiled=True)
    lines = owner(lines, 2)
    return (
        out, gin, lines[:, :taps], lines[:, CONV_BIAS], lines[:, SCALE : SCALE + group_count],
        lines[:, SHIFT : SHIFT + group_count], owner(dup, 1), owner(ug[:, 0], 1), owner(ddown, 1),
        lines[:, DOWN_BIAS], lines[:, GAIN],
    )


def solution(mesh):
    split = ("dp", "fsdp")
    clip = P(split, None, None)
    first, middle, last = P(None, split), P(None, split, None), P(None, None, split)
    in_specs = (clip, P(split), P(split), last, first, last, last, middle, first, middle, first, first, clip)
    out_specs = (clip, clip, last, first, last, last, middle, first, middle, first, first)
    run = functools.partial(body, mesh.shape["dp"], mesh.shape["fsdp"])
    return jax.shard_map(run, mesh=mesh, in_specs=in_specs, out_specs=out_specs, check_vma=False)
```

```python
import functools
import math
import jax
import jax.numpy as jnp
from jax import lax
from jax.experimental import pallas as pl
from jax.experimental.pallas import tpu as pltpu
from jax.sharding import PartitionSpec as P

F32 = jnp.float32
BF16 = jnp.bfloat16
EPSILON = 1e-06
TAPS, CONV_BIAS, SCALE, SHIFT, DOWN_BIAS, GAIN, ROWS = 0, 7, 8, 10, 12, 13, 16
A_TAPS, A_BIAS, A_SCALE, A_SHIFT, A_DOWN, A_GAIN = 0, 7, 8, 9, 10, 11
HALO = 3
LANES = 128
VMEM_LIMIT = 64 * 1024 * 1024 - 128 * 1024
NN = (((1,), (0,)), ((), ()))
NT = (((1,), (1,)), ((), ()))
TN = (((0,), (0,)), ((), ()))
DMA = pltpu.SemaphoreType.DMA


def mm(a, b, dims):
    return lax.dot_general(a, b, dims, preferred_element_type=F32)


def gelu_pair(before):
    u = before * math.sqrt(0.5)
    phi = 0.5 + 0.5 * lax.erf(u)
    bell = jnp.exp2(u * u * (-math.log2(math.e))) * (1.0 / math.sqrt(math.pi))
    return before * phi, phi + u * bell


def per_clip(values, clips, width):
    rows = lax.broadcasted_iota(jnp.int32, (clips, width), 0)
    out = jnp.zeros((clips, width), jnp.int32)
    for c in range(clips):
        out = jnp.where(rows == c, values[c], out)
    return out


def prepare(small, lens, groups, s8, len8, group_count):
    clips, width = len8.shape
    for r in range(14):
        s8[r] = jnp.broadcast_to(small[r : r + 1, :], (clips, width))
    member = per_clip(groups, clips, width)
    len8[...] = per_clip(lens, clips, width)
    gain = jnp.zeros((clips, width), F32)
    shift = jnp.zeros((clips, width), F32)
    for g in range(group_count):
        chosen = jnp.where(member == g, 1.0, 0.0)
        gain = gain + chosen * s8[SCALE + g]
        shift = shift + chosen * s8[SHIFT + g]
    s8[SCALE] = gain
    s8[SHIFT] = shift


def keep_frames(v, t0, len8, other=0.0):
    t = lax.broadcasted_iota(jnp.int32, v.shape, 0) + t0
    return jnp.where(t < len8[...][None], v, other)


def spread_clips(block, t0, dst, d0, frames):
    clips = block.shape[0]
    for c in range(clips):
        for t in range(0, frames, 16):
            v = block[c, pl.ds(t0 + t, 16), :].astype(F32)
            for l in range(dst.shape[0]):
                dst[l, pl.ds((d0 + t) * clips + c, 16, stride=clips), :] = v[:, l * LANES : (l + 1) * LANES]


def collect_clips(src, block, frames):
    clips = block.shape[0]
    for c in range(clips):
        for t in range(0, frames, 16):
            for l in range(src.shape[0]):
                v = src[l, pl.ds(t * clips + c, 16, stride=clips), :]
                block[c, t : t + 16, l * LANES : (l + 1) * LANES] = v.astype(block.dtype)


def rows_of(src, start, n):
    return jnp.concatenate([src[l, pl.ds(start, n), :] for l in range(src.shape[0])], axis=-1)


def put_rows(dst, start, v):
    for l in range(dst.shape[0]):
        dst[l, pl.ds(start, v.shape[0]), :] = v[:, l * LANES : (l + 1) * LANES]


def fold(v):
    return jnp.sum(v, axis=0)


def smem():
    return pl.BlockSpec(memory_space=pltpu.SMEM)


def vmem():
    return pl.BlockSpec(memory_space=pltpu.VMEM)


def hbm():
    return pl.BlockSpec(memory_space=pl.ANY)


def whole(*dims):
    return pl.BlockSpec(dims, lambda i: (0,) * len(dims), pipeline_mode=pl.Buffered(1))


def shape(dims, dtype=F32):
    return jax.ShapeDtypeStruct(dims, dtype)


MESH = pl.DeviceIdType.MESH
PACK = 20


class Place:
    def __init__(self, deep, side):
        self.deep, self.side = deep, side
        self.z = lax.axis_index("dp")
        f = lax.axis_index("fsdp")
        self.f = f
        self.core = lax.rem(f, 2)
        chip = f // 2
        self.low = lax.rem(chip, side)
        self.high = chip // side
        self.first = jnp.where(self.core == 0, self.high, self.low)
        self.second = jnp.where(self.core == 0, self.low, self.high)

    def chip_of(self, first, second):
        high = jnp.where(self.core == 0, first, second)
        low = jnp.where(self.core == 0, second, first)
        return high, low

    def fsdp_of(self, first, second):
        high, low = self.chip_of(first, second)
        return (high * self.side + low) * 2 + self.core

    def z_peer(self, p):
        return {"dp": lax.rem(self.z + p, self.deep)}

    def first_peer(self, p):
        return {"fsdp": self.fsdp_of(lax.rem(self.first + p, self.side), self.second)}

    def second_peer(self, p):
        return {"fsdp": self.fsdp_of(self.first, lax.rem(self.second + p, self.side))}

    def core_peer(self):
        return {"fsdp": self.f + 1 - 2 * self.core}

    def greet(self):
        barrier = pltpu.get_barrier_semaphore()
        peers = [self.z_peer(p) for p in range(1, self.deep)]
        peers += [self.first_peer(p) for p in range(1, self.side)]
        peers += [self.second_peer(p) for p in range(1, self.side)]
        peers.append(self.core_peer())
        for peer in peers:
            pl.semaphore_signal(barrier, inc=1, device_id=peer, device_id_type=MESH)
        pl.semaphore_wait(barrier, len(peers))


def send(src, dst, send_sem, recv_sem, peer):
    return pltpu.make_async_remote_copy(
        src_ref=src, dst_ref=dst, send_sem=send_sem, recv_sem=recv_sem, device_id=peer, device_id_type=MESH
    )


def run(copies):
    for c in copies:
        c.start()


def done(copies):
    for c in copies:
        c.wait()


def weight_route(place, own, full, sems):
    zs, zr, fs, fr, ss, sr, cs, cr = sems
    deep, side, core = place.deep, place.side, place.core

    def held(p, q):
        high, low = place.chip_of(lax.rem(place.first + p, side), lax.rem(place.second + q, side))
        return full.at[:, high, low, core]

    mine = full.at[place.z, place.high, place.low, core]
    along_z = [send(own, mine, zs.at[p - 1], zr.at[p - 1], place.z_peer(p)) for p in range(1, deep)]
    along_first = [
        send(held(0, 0), held(0, 0), fs.at[p - 1], fr.at[p - 1], place.first_peer(p)) for p in range(1, side)
    ]
    along_second = []
    for j in range(side):
        high, low = place.chip_of(j, place.second)
        line = full.at[:, high, low, core]
        for p in range(1, side):
            n = j * (side - 1) + p - 1
            along_second.append(send(line, line, ss.at[n], sr.at[n], place.second_peer(p)))
    across = lambda p, q: send(held(p, q), held(p, q), cs.at[p * side + q], cr.at[p * side + q], place.core_peer())
    over = [[across(0, 0)], [across(p, 0) for p in range(1, side)],
            [across(p, q) for q in range(1, side) for p in range(side)]]
    return [along_z, along_first, along_second], over


def gather_sems(count, deep, side):
    one = [deep - 1, deep - 1, side - 1, side - 1, side * (side - 1), side * (side - 1), side * side, side * side]
    return [DMA((count, n)) for n in one]


def place_small(place, shards, pack, group_count, taps):
    conv_w, conv_b, scale, shift, up_b, down_b, gain = shards
    width = conv_b.shape[1]
    lane = lax.broadcasted_iota(jnp.int32, (width, LANES), 1)
    row = lax.broadcasted_iota(jnp.int32, (width, LANES), 0)
    spot = jnp.where(lane == row + place.f * width, 1.0, 0.0).astype(BF16)
    wide = up_b.shape[1]
    span = wide * LANES // width
    lane = lax.broadcasted_iota(jnp.int32, (wide, span), 1)
    row = lax.broadcasted_iota(jnp.int32, (wide, span), 0)
    spread = jnp.where(lane == row + place.f * wide, 1.0, 0.0).astype(BF16)
    pack[...] = jnp.zeros(pack.shape, F32)
    for b in range(2):
        o = b * PACK
        for k in range(taps):
            pack[o + k : o + k + 1, :] = mm(conv_w[k, b : b + 1, :], spot, NN)
        pack[o + SCALE : o + SCALE + group_count, :] = mm(scale[b], spot, NN)
        pack[o + SHIFT : o + SHIFT + group_count, :] = mm(shift[b], spot, NN)
        for src, at in ((conv_b, CONV_BIAS), (down_b, DOWN_BIAS), (gain, GAIN)):
            pack[o + at : o + at + 1, :] = mm(src[b : b + 1, :], spot, NN)
        bias = mm(up_b[b : b + 1, :], spread, NN)
        for q in range(span // LANES):
            pack[o + 14 + q : o + 15 + q, :] = bias[:, q * LANES : (q + 1) * LANES]


class Gather:
    def __init__(self, shards, up_full, down_full, small_full, upb_full, refs, deep, side, group_count, taps):
        (self.pack, self.zbuf, self.first_in, self.first_sum, self.second_in, self.second_sum, self.core_in,
         self.local_sems, self.small_s, self.small_r) = refs[:10]
        sems = refs[10:]
        self.place = place = Place(deep, side)
        self.small_full, self.upb_full, self.shards = small_full, upb_full, shards
        self.group_count, self.taps = group_count, taps
        up_w, down_w = shards[4], shards[6]
        self.full = (up_full, down_full)
        self.routes, self.local = [], []
        for n, (own, full) in enumerate(
            ((up_w.at[0], up_full.at[0]), (down_w.at[0], down_full.at[0]), (up_w.at[1], up_full.at[1]), (down_w.at[1], down_full.at[1]))
        ):
            self.routes.append(weight_route(place, own, full, [s.at[n] for s in sems]))
            spot = full.at[place.z, place.high, place.low, place.core]
            self.local.append(pltpu.make_async_copy(own, spot, self.local_sems.at[n]))
        stages = [
            [(self.zbuf.at[place.z], self.zbuf.at[place.z], place.z_peer(p)) for p in range(1, deep)],
            [(self.zbuf, self.first_in.at[p - 1], place.first_peer(p)) for p in range(1, side)],
            [(self.first_sum, self.second_in.at[p - 1], place.second_peer(p)) for p in range(1, side)],
            [(self.second_sum, self.core_in, place.core_peer())],
        ]
        n = 0
        self.small = []
        for stage in stages:
            copies = []
            for src, dst, peer in stage:
                copies.append(send(src, dst, self.small_s.at[n], self.small_r.at[n], peer))
                n += 1
            self.small.append(copies)

    def begin(self, n):
        run(self.routes[n][0][0])
        self.local[n].start()

    def after_z(self, n):
        along, over = self.routes[n]
        self.local[n].wait()
        done(along[0])
        run(along[1])
        run(over[0])

    def after_first(self, n):
        along, over = self.routes[n]
        done(along[1])
        run(along[2])
        run(over[1])

    def after_second(self, n):
        along, over = self.routes[n]
        done(along[2])
        run(over[2])

    def end(self, n):
        for copies in self.routes[n][1]:
            done(copies)

    def early(self, spread, ready, conv, tiles):
        place = self.place
        place.greet()
        self.begin(0)
        conv_w, conv_b, scale, shift, _, up_b, _, down_b, gain = self.shards
        place_small(place, (conv_w, conv_b, scale, shift, up_b, down_b, gain), self.pack, self.group_count, self.taps)
        self.zbuf[place.z] = self.pack[...]
        run(self.small[0])
        self.begin(1)
        self.begin(2)
        self.begin(3)
        spread()
        done(self.small[0])
        run(self.small[1])
        self.after_z(0)
        done(self.small[1])
        total = self.zbuf[...]
        for p in range(1, place.side):
            total = total + self.first_in[p - 1]
        self.first_sum[...] = total
        run(self.small[2])
        self.after_z(1)
        done(self.small[2])
        total = self.first_sum[...]
        for p in range(1, place.side):
            total = total + self.second_in[p - 1]
        self.second_sum[...] = total
        run(self.small[3])
        self.after_first(0)
        done(self.small[3])
        self.finish_small()
        ready()
        self.after_first(1)
        conv(0, tiles // 2)
        self.after_second(0)
        self.after_z(2)
        self.after_z(3)
        conv(tiles // 2, 3 * tiles // 4)
        self.after_second(1)
        conv(3 * tiles // 4, tiles)
        self.end(0)

    def finish_small(self):
        total = self.second_sum[...] + self.core_in[...]
        deep = self.place.deep
        per = self.upb_full.shape[2] // deep
        self.small_full[...] = jnp.zeros(self.small_full.shape, F32)
        for b in range(2):
            o = b * PACK
            for z in range(deep):
                self.small_full[b, 0:14, z * LANES : (z + 1) * LANES] = total[z, o : o + 14, :]
                for q in range(per // LANES):
                    at = z * per + q * LANES
                    self.upb_full[b, :, at : at + LANES] = total[z, o + 14 + q : o + 15 + q, :]

    def late(self, i, tiles):
        @pl.when(i == tiles // 4)
        def _():
            self.after_first(2)

        @pl.when(i == tiles // 2)
        def _():
            self.after_first(3)

        @pl.when(i == tiles)
        def _():
            self.end(1)

        @pl.when(i == tiles + tiles // 2)
        def _():
            self.after_second(2)

        @pl.when(i == 2 * tiles - 1)
        def _():
            self.after_second(3)

        @pl.when(i == 2 * tiles)
        def _():
            for n in (2, 3):
                self.end(n)


def gather_scratch(deep, side):
    buf = pltpu.VMEM((deep, 2 * PACK, LANES), F32)
    many = pltpu.VMEM((side - 1, deep, 2 * PACK, LANES), F32)
    n = deep - 1 + 2 * (side - 1) + 1
    return [pltpu.VMEM((2 * PACK, LANES), F32), buf, many, buf, many, buf, buf, DMA((4,)), DMA((n,)), DMA((n,))] + gather_sems(
        4, deep, side
    )


def conv_norm(masked, f0, frames, s8, normed, inv, shaped, taps, n0=0, step=4):
    clips, width = s8.shape[1:]
    for j in range(0, frames, step):
        mixed = s8[CONV_BIAS][None]
        for k in range(taps):
            mixed = mixed + s8[TAPS + k][None] * masked[pl.ds(f0 + j + k, step)]
        center = mixed - jnp.mean(mixed, axis=-1, keepdims=True)
        inv_std = lax.rsqrt(jnp.mean(center * center, axis=-1, keepdims=True) + EPSILON)
        norm = center * inv_std
        normed[pl.ds(n0 + f0 + j, step)] = norm
        inv[pl.ds(f0 + j, step)] = jnp.broadcast_to(inv_std, (step, clips, LANES))
        rows = norm * s8[SCALE][None] + s8[SHIFT][None]
        at = pl.multiple_of((f0 + j) * clips, step * clips)
        shaped[pl.ds(at, step * clips), :] = rows.reshape(step * clips, width).astype(BF16)


def up_gelu(shaped, up_cols, u8, act, r0, slope, s0, rows, hidden, cols=256, sub=16):
    left = shaped[pl.ds(r0, rows), :]
    for n in range(0, hidden, cols):
        before = mm(left, up_cols(n, n + cols), NN)
        for r in range(0, rows, sub):
            piece = before[r : r + sub].reshape(sub // 8, 8, cols) + u8[:, n : n + cols][None]
            a, s = gelu_pair(piece.reshape(sub, cols))
            act[pl.ds(r0 + r, sub), n : n + cols] = a.astype(BF16)
            slope[pl.ds(s0 + r, sub), n : n + cols] = s.astype(slope.dtype)


def forward_kernel(
    lens, groups, frames, small_full, upb_full, up_full, down_full, out, act_out, slope, normed_out, inv_out, shaped_out, masked_out,
    stream, masked0, masked1, normed, inv, shaped, first_rows, act, s8, u8, len8, save_sem, act_sem, row_sem, *, ft, taps, group_count,
):
    i = pl.program_id(0)
    clips, frame_count, width = frames.shape
    hidden = act.shape[1]
    tiles = frame_count // ft
    rows = ft * clips

    def up_cols(b):
        return lambda lo, hi: up_full[b, :, lo:hi]

    body = pl.ds(HALO, frame_count)
    save = lambda n, src, dst: pltpu.make_async_copy(src, dst, save_sem.at[n])
    saves0 = [
        save(0, masked0.at[body], masked_out.at[0]), save(1, normed, normed_out.at[0]),
        save(2, inv, inv_out.at[0]), save(3, shaped, shaped_out.at[0]),
    ]
    save_masked1 = save(4, masked1.at[body], masked_out.at[1])
    tail = lambda b, j: pltpu.make_async_copy(
        act.at[pl.ds(pl.multiple_of(j * rows, rows), rows)],
        act_out.at[b, pl.ds(pl.multiple_of(j * rows, rows), rows)], act_sem.at[j])

    def row_saves(j):
        f = pl.ds(j * ft, ft)
        r = pl.ds(pl.multiple_of(j * rows, rows), rows)
        return [
            pltpu.make_async_copy(normed.at[f], normed_out.at[1, f], row_sem.at[0, j]),
            pltpu.make_async_copy(inv.at[f], inv_out.at[1, f], row_sem.at[1, j]),
            pltpu.make_async_copy(shaped.at[r], shaped_out.at[1, r], row_sem.at[2, j]),
        ]

    @pl.when(i == 0)
    def _():
        zeros = jnp.zeros((HALO, clips, width), F32)
        for m in (masked0, masked1):
            m[0:HALO] = zeros
            m[HALO + frame_count :] = zeros
        len8[...] = per_clip(lens, clips, width)

        def spread(n, carry):
            t0 = pl.multiple_of(n * 16, 16)
            spread_clips(frames, t0, stream, 0, 16)
            v = rows_of(stream, 0, 16 * clips)
            at = pl.multiple_of(t0 * clips, 16 * clips)
            first_rows[pl.ds(at, 16 * clips), :] = v.astype(BF16)
            masked0[pl.ds(HALO + t0, 16)] = keep_frames(v.reshape(16, clips, width), t0, len8)
            return carry
        lax.fori_loop(0, frame_count // 16, spread, 0)
        for b in range(2):
            prepare(small_full.at[b], lens, groups, s8.at[b], len8, group_count)
            u8[b] = jnp.broadcast_to(upb_full[b, 0:1, :], u8.shape[1:])

        def conv0(n, carry):
            conv_norm(masked0, n * ft, ft, s8.at[0], normed, inv, shaped, taps)
            return carry
        lax.fori_loop(0, tiles, conv0, 0)
        for c in saves0:
            c.start()

    @pl.when(i < tiles)
    def _():
        r0 = pl.multiple_of(i * rows, rows)
        up_gelu(shaped, up_cols(0), u8.at[0], act, r0, slope, 0, rows, hidden)
        tail(0, i).start()

    @pl.when((i >= tiles) & (i < 2 * tiles))
    def _():
        j = i - tiles
        f0 = j * ft
        r0 = pl.multiple_of(j * rows, rows)
        branch = mm(act[pl.ds(r0, rows), :], down_full[0], NN)
        for t in range(0, ft, 4):
            b = branch[t * clips : (t + 4) * clips].reshape(4, clips, width) + s8[0, DOWN_BIAS][None]
            total = masked0[pl.ds(HALO + f0 + t, 4)] + s8[0, GAIN][None] * b
            masked1[pl.ds(HALO + f0 + t, 4)] = keep_frames(total, f0 + t, len8)
        tail(0, j).wait()

    @pl.when(i == 2 * tiles)
    def _():
        for c in saves0:
            c.wait()
        save_masked1.start()

    @pl.when(i >= 2 * tiles)
    def _():
        j = i - 2 * tiles
        f0 = j * ft
        r0 = pl.multiple_of(j * rows, rows)
        conv_norm(masked1, f0, ft, s8.at[1], normed, inv, shaped, taps)
        for c in row_saves(j):
            c.start()
        up_gelu(shaped, up_cols(1), u8.at[1], act, r0, slope, 0, rows, hidden)
        tail(1, j).start()
        branch = mm(act[pl.ds(r0, rows), :], down_full[1], NN)
        last_block(branch, masked1, f0, r0, ft, s8.at[1], len8, first_rows, stream, out)

    @pl.when(i == 3 * tiles - 1)
    def _():
        save_masked1.wait()
        for j in range(tiles):
            tail(1, j).wait()
            for c in row_saves(j):
                c.wait()


def last_block(branch, masked1, f0, r0, ft, s8, len8, first_rows, stream, out):
    clips, width = len8.shape
    for t in range(0, ft, 4):
        b = branch[t * clips : (t + 4) * clips].reshape(4, clips, width) + s8[DOWN_BIAS][None]
        total = masked1[pl.ds(HALO + f0 + t, 4)] + s8[GAIN][None] * b
        at = pl.multiple_of(r0 + t * clips, 4 * clips)
        first = first_rows[pl.ds(at, 4 * clips), :].astype(F32).reshape(4, clips, width)
        put_rows(stream, t * clips, keep_frames(total, f0 + t, len8, first).reshape(4 * clips, width))
    collect_clips(stream, out, ft)


def forward(lens, groups, frames, weights, hidden, ft, taps, group_count):
    clips, fc, d = frames.shape
    h = hidden
    n, r = fc // ft, ft * clips
    R = fc * clips
    slope_at = lambda i: jnp.where(i < n, i, jnp.where(i < 2 * n, n - 1, i - n))
    return pl.pallas_call(
        functools.partial(forward_kernel, ft=ft, taps=taps, group_count=group_count),
        name="forward",
        grid=(3 * n,),
        in_specs=[smem(), smem(), whole(clips, fc, d)] + [vmem()] * 4,
        out_specs=[
            pl.BlockSpec((clips, ft, d), lambda i: (0, jnp.maximum(i - 2 * n, 0), 0)), hbm(),
            pl.BlockSpec((r, h), lambda i: (slope_at(i), 0)), hbm(), hbm(), hbm(), hbm(),
        ],
        out_shape=[
            shape((clips, fc, d), BF16), shape((2, R, h), BF16), shape((2 * R, h), BF16), shape((2, fc, clips, d)),
            shape((2, fc, clips, LANES)), shape((2, R, d), BF16), shape((2, fc, clips, d)),
        ],
        scratch_shapes=[
            pltpu.VMEM((d // LANES, max(r, 16 * clips), LANES), F32),
            pltpu.VMEM((fc + 2 * HALO, clips, d), F32), pltpu.VMEM((fc + 2 * HALO, clips, d), F32),
            pltpu.VMEM((fc, clips, d), F32), pltpu.VMEM((fc, clips, LANES), F32), pltpu.VMEM((R, d), BF16),
            pltpu.VMEM((R, d), BF16), pltpu.VMEM((R, h), BF16),
            pltpu.VMEM((2, 14, clips, d), F32), pltpu.VMEM((2, clips, h), F32), pltpu.VMEM((clips, d), jnp.int32),
            DMA((5,)), DMA((n,)), DMA((3, n)),
        ],
        compiler_params=pltpu.CompilerParams(vmem_limit_bytes=VMEM_LIMIT),
    )(lens, groups, frames, *weights)


class Scatter:
    def __init__(self, place, term, bufs, sems):
        self.place, self.term = place, term
        self.core_in, self.second_in, self.first_in, self.z_in = bufs
        self.sems = sems

    def line(self, first, second):
        high, low = self.place.chip_of(first, second)
        return self.term.at[:, high, low, self.place.core]

    def spot(self, z, first, second):
        high, low = self.place.chip_of(first, second)
        return (z, high, low)

    def core_copies(self):
        at = self.place
        return [send(self.term.at[:, :, :, 1 - at.core], self.core_in, self.sems[0].at[0], self.sems[1].at[0], at.core_peer())]

    def second_copies(self, p):
        at = self.place
        to = lax.rem(at.second + p, at.side)
        n = (p - 1) * at.side
        return [
            send(self.line(f, to), self.second_in.at[p - 1, f], self.sems[2].at[n + f], self.sems[3].at[n + f], at.second_peer(p))
            for f in range(at.side)
        ]

    def first_copy(self, p):
        at = self.place
        to = lax.rem(at.first + p, at.side)
        return send(self.line(to, at.second), self.first_in.at[p - 1], self.sems[4].at[p - 1], self.sems[5].at[p - 1], at.first_peer(p))

    def z_copy(self, p):
        at = self.place
        to = lax.rem(at.z + p, at.deep)
        high, low = at.chip_of(at.first, at.second)
        return send(self.term.at[to, high, low, at.core], self.z_in.at[p - 1], self.sems[6].at[p - 1], self.sems[7].at[p - 1], at.z_peer(p))

    def part1(self, z, first, second):
        z, high, low = self.spot(z, first, second)
        return self.term[z, high, low, self.place.core].astype(F32) + self.core_in[z, high, low].astype(F32)

    def part2(self, z, first):
        total = self.part1(z, first, self.place.second)
        for p in range(1, self.place.side):
            total = total + self.second_in[p - 1, first, z].astype(F32)
        return total

    def part3(self, z):
        total = self.part2(z, self.place.first)
        for p in range(1, self.place.side):
            total = total + self.first_in[p - 1, z].astype(F32)
        return total

    def put(self, z, first, second, total):
        z, high, low = self.spot(z, first, second)
        self.term[z, high, low, self.place.core] = total.astype(BF16)

    def core_start(self):
        run(self.core_copies())

    def second_start(self):
        at = self.place
        done(self.core_copies())
        for p in range(1, at.side):
            to = lax.rem(at.second + p, at.side)
            copies = self.second_copies(p)
            for first in range(at.side):
                def one(z, carry):
                    self.put(z, first, to, self.part1(z, first, to))
                    return carry
                lax.fori_loop(0, at.deep, one, 0)
                copies[first].start()

    def first_start(self):
        at = self.place
        for p in range(1, at.side):
            done(self.second_copies(p))
        for p in range(1, at.side):
            to = lax.rem(at.first + p, at.side)
            def one(z, carry):
                self.put(z, to, at.second, self.part2(z, to))
                return carry
            lax.fori_loop(0, at.deep, one, 0)
            self.first_copy(p).start()

    def z_start(self):
        at = self.place
        done([self.first_copy(p) for p in range(1, at.side)])
        for p in range(1, at.deep):
            to = lax.rem(at.z + p, at.deep)
            self.put(to, at.first, at.second, self.part3(to))
            self.z_copy(p).start()

    def finish(self, out):
        at = self.place
        done([self.z_copy(p) for p in range(1, at.deep)])
        total = self.part3(at.z)
        for p in range(1, at.deep):
            total = total + self.z_in[p - 1].astype(F32)
        out[...] = total


def scatter_bufs(deep, side, rows, cols):
    v = lambda *lead: pltpu.VMEM(lead + (rows, cols), BF16)
    return [v(deep, side, side), v(side - 1, side, deep), v(side - 1, deep), v(deep - 1)]


def scatter_sems(count, deep, side):
    return [DMA((count, n)) for n in (1, 1, side * (side - 1), side * (side - 1), side - 1, side - 1, deep - 1, deep - 1)]


def pack_small(small, upb, b, terms, deep):
    per = upb.shape[1] // deep
    o = b * PACK
    for z in range(deep):
        terms[z, o : o + 14, :] = small[0:14, z * LANES : (z + 1) * LANES]
        for q in range(per // LANES):
            at = z * per + q * LANES
            terms[z, o + 14 + q : o + 15 + q, :] = upb[:, at : at + LANES]


def sum_small(place, terms, z_in, bufs, out, s, r):
    n = 0
    copies = []
    for p in range(1, place.deep):
        to = lax.rem(place.z + p, place.deep)
        copies.append(send(terms.at[to], z_in.at[p - 1], s.at[n], r.at[n], place.z_peer(p)))
        n += 1
    run(copies)
    yield
    done(copies)
    total = terms[place.z]
    for p in range(1, place.deep):
        total = total + z_in[p - 1]
    stages = [[place.core_peer()], [place.second_peer(p) for p in range(1, place.side)],
              [place.first_peer(p) for p in range(1, place.side)]]
    for (here, into), peers in zip(bufs, stages):
        here[...] = total
        copies = []
        for p, peer in enumerate(peers):
            copies.append(send(here, into.at[p], s.at[n], r.at[n], peer))
            n += 1
        run(copies)
        yield
        done(copies)
        for p in range(len(peers)):
            total = total + into[p]
    out[...] = total


def small_bufs(deep, side):
    many = lambda *n: pltpu.VMEM(n + (2 * PACK, LANES), F32)
    n = deep - 1 + 2 * (side - 1) + 1
    return [many(deep), many(deep - 1), many(), many(1), many(), many(side - 1), many(), many(side - 1), DMA((n,)), DMA((n,))]


class Sums:
    def __init__(self, refs, up_term, down_term, up_part, down_part, small_part, small_grad, upb_grad, deep, side):
        self.place = Place(deep, side)
        self.terms, self.z_in = refs[:2]
        self.bufs = [refs[2:4], refs[4:6], refs[6:8]]
        self.small_s, self.small_r = refs[8:10]
        refs = refs[10:]
        sems = refs[-8:]
        self.small_part, self.small_grad, self.upb_grad = small_part, small_grad, upb_grad
        half = up_part.shape[2] // 2
        self.jobs = []
        for b in (1, 0):
            views = [(down_term.at[b], down_part.at[b])]
            for lo in (0, half):
                views.append((up_term.at[b, :, :, :, :, :, pl.ds(lo, half)], up_part.at[b, :, pl.ds(lo, half)]))
            for term, out in views:
                n = len(self.jobs)
                self.jobs.append((Scatter(self.place, term, refs[4 * n : 4 * n + 4], [s.at[n] for s in sems]), out))

    def do(self, n, what):
        job, out = self.jobs[n]
        if what == "finish":
            job.finish(out)
        else:
            getattr(job, what)()

    def before(self, i, span, parts):
        times = [
            {"core_start": parts, "second_start": parts + 2, "first_start": 2 * parts, "z_start": 2 * parts + 3, "finish": span - 1},
            {"core_start": parts + 3, "second_start": parts + 5, "first_start": 2 * parts + 2, "z_start": 2 * parts + 5, "finish": span - 1},
            {"core_start": 2 * parts, "second_start": 2 * parts + 2, "first_start": 2 * parts + 5, "z_start": span - 1, "finish": span + 2},
        ]
        plan = []
        for order, what in enumerate(("core_start", "second_start", "first_start", "z_start", "finish")):
            for n in range(6):
                at = times[n % 3][what] + (n // 3) * span
                if at < 2 * span:
                    plan.append((at, order, n, what))
        for at in sorted({p[0] for p in plan}):
            @pl.when(i == at)
            def _():
                for now, _, n, what in plan:
                    if now == at:
                        self.do(n, what)

    def after(self, i, span):
        @pl.when(i == 2 * span - 1)
        def _():
            self.terms[...] = jnp.zeros(self.terms.shape, F32)
            for b in range(2):
                pack_small(self.small_grad.at[b], self.upb_grad.at[b], b, self.terms, self.place.deep)
            steps = sum_small(self.place, self.terms, self.z_in, self.bufs, self.small_part, self.small_s, self.small_r)
            next(steps)
            self.do(5, "finish")
            for _ in steps:
                pass


def sums_scratch(deep, side, urows, drows, d, h):
    ub, db = scatter_bufs(deep, side, urows, h // 2), scatter_bufs(deep, side, drows, d)
    return small_bufs(deep, side) + 2 * (db + ub + ub) + scatter_sems(6, deep, side)


def norm_back(gs, normed, n0, inv, i0, s8, gm, gm0, acc, frames, step=4):
    clips, width = s8.shape[1:]
    a_scale, a_shift, a_bias = acc[A_SCALE], acc[A_SHIFT], acc[A_BIAS]
    for j in range(0, frames, step):
        g = gs[j * clips : (j + step) * clips].reshape(step, clips, width)
        norm = normed[pl.ds(n0 + j, step)]
        gn = g * norm
        a_scale = a_scale + fold(gn)
        a_shift = a_shift + fold(g)
        gg = g * s8[SCALE][None]
        mean = jnp.mean(gg, axis=-1, keepdims=True)
        mean_norm = jnp.mean(gn * s8[SCALE][None], axis=-1, keepdims=True)
        inv_std = jnp.concatenate([inv[pl.ds(i0 + j, step)]] * (width // LANES), axis=-1)
        grad = inv_std * (gg - mean - norm * mean_norm)
        a_bias = a_bias + fold(grad)
        gm[pl.ds(gm0 + j, step)] = grad
    acc[A_SCALE], acc[A_SHIFT], acc[A_BIAS] = a_scale, a_shift, a_bias


def conv_back(gm, gm0, s8, masked, m0, gs, g0, t0, out, acc, frames, len8, taps, step=8):
    clips, width = len8.shape
    half = taps // 2
    for l in range(width // LANES):
        cols = slice(l * LANES, (l + 1) * LANES)
        sums = [acc[A_TAPS + k, :, cols] for k in range(taps)]
        for j in range(0, frames, step):
            here = masked[pl.ds(m0 + j, step), :, cols]
            total = None
            for k in range(taps):
                piece = gm[pl.ds(gm0 + j + half - k, step), :, cols]
                term = s8[TAPS + k, :, cols][None] * piece
                total = term if total is None else total + term
                sums[k] = sums[k] + fold(piece * here)
            t = lax.broadcasted_iota(jnp.int32, total.shape, 0) + (t0 + j)
            total = jnp.where(t < len8[:, cols][None], total, 0.0)
            total = gs[pl.ds(g0 + j, step), :, cols] + total
            gs[pl.ds(g0 + j, step), :, cols] = total
            out[l, j * clips : (j + step) * clips, :] = total.reshape(step * clips, LANES)
        for k in range(taps):
            acc[A_TAPS + k, :, cols] = sums[k]


def finish_small(acc, upb_acc, groups, s8, small_grad, upb_grad, group_count):
    clips, width = acc.shape[1:]
    member = per_clip(groups, clips, width)
    line = lambda v: jnp.sum(v, axis=0, keepdims=True)
    rows = [line(acc[A_TAPS + k]) for k in range(7)]
    rows.append(line(acc[A_BIAS]))
    for base in (A_SCALE, A_SHIFT):
        for g in range(group_count):
            rows.append(line(jnp.where(member == g, acc[base], 0.0)))
    rows.append(line(acc[A_DOWN]))
    rows.append(line((acc[A_GAIN] + s8[DOWN_BIAS] * acc[A_DOWN]) / s8[GAIN]))
    for r, row in enumerate(rows):
        small_grad[r : r + 1, :] = row
    for r in range(len(rows), small_grad.shape[0]):
        small_grad[r : r + 1, :] = jnp.zeros((1, width), F32)
    upb_grad[...] = line(upb_acc[...])


def backward_kernel(
    lens, groups, og, act, slope, normed, inv, shaped, masked, up, down, small, gs_out, dup, ddown, small_grad, upb_grad,
    gs, gb, gbef, gm, lanes, s8, len8, acc, upb_acc, *, ft, tiles, parts, taps, group_count,
):
    i = pl.program_id(0)
    frame_count, clips, width = gs.shape
    hidden = gbef.shape[1]
    cols = hidden // parts
    rows = ft * clips
    total_rows = frame_count * clips
    base = 2 * ft
    span = parts + tiles + 2
    step = lax.rem(i, span)
    b = 1 - i // span

    @pl.when(step == 0)
    def _():
        prepare(small.at[b], lens, groups, s8, len8, group_count)
        acc[...] = jnp.zeros(acc.shape, F32)

    @pl.when(i == 0)
    def _():
        gm[pl.ds(0, base)] = jnp.zeros((base, clips, width), F32)
        gm[pl.ds(base + frame_count, HALO)] = jnp.zeros((HALO, clips, width), F32)
        spread_grad(og, lanes, gs, 0)

    @pl.when(step == 0)
    def _():
        acc[A_DOWN] = branch_grad(gs, 0, s8, len8, gb)

    @pl.when(step < parts)
    def _():
        c0 = pl.multiple_of(step * cols, cols)
        at = pl.ds(c0, cols)
        lower = down[0, at, :]
        term = mm(act[0], gb[...], TN)
        ddown[b, at, :] = term
        acc[A_GAIN] += fold((term * lower.astype(F32)).reshape(cols // 8, 8, width))
        before_grad(gb, lower, slope.at[0], slice(None), gbef, at, upb_acc, total_rows)
        dup[b, :, at] = mm(shaped[0], gbef[:, at], TN)

    j = step - parts

    @pl.when((j >= 0) & (j < tiles))
    def _():
        r0 = pl.multiple_of(j * rows, rows)
        grad = mm(gbef[pl.ds(r0, rows), :], up[0], NT)
        norm_back(grad, normed.at[0], 0, inv.at[0], 0, s8, gm, base + j * ft, acc, ft)

    @pl.when(j >= 2)
    def _():
        f0 = (j - 2) * ft
        conv_back(gm, base + f0, s8, masked.at[0], 0, gs, f0, f0, gs_out, acc, ft, len8, taps)

    @pl.when(step == span - 1)
    def _():
        finish_small(acc, upb_acc, groups, s8, small_grad.at[b], upb_grad.at[b], group_count)


def spread_grad(og, lanes, gs, g0):
    clips, frame_count, width = og.shape

    def one(n, carry):
        t0 = pl.multiple_of(n * 16, 16)
        spread_clips(og, t0, lanes, 0, 16)
        gs[pl.ds(g0 + t0, 16)] = rows_of(lanes, 0, 16 * clips).reshape(16, clips, width)
        return carry
    lax.fori_loop(0, frame_count // 16, one, 0)


def branch_grad(gs, g0, s8, len8, gb):
    clips, width = len8.shape
    frame_count = gb.shape[0] // clips

    def one(n, a_down):
        t0 = n * 4
        gvb = s8[GAIN][None] * keep_frames(gs[pl.ds(g0 + t0, 4)], t0, len8)
        at = pl.multiple_of(t0 * clips, 4 * clips)
        gb[pl.ds(at, 4 * clips), :] = gvb.reshape(4 * clips, width).astype(BF16)
        return a_down + fold(gvb)
    return lax.fori_loop(0, frame_count // 4, one, jnp.zeros((clips, width), F32), unroll=4)


def before_grad(gb, lower, slope, slope_cols, gbef, at, upb_acc, rows, sub=16):
    cols = lower.shape[0]
    ga = mm(gb[...], lower, NT)
    total = jnp.zeros((8, cols), F32)
    for r in range(0, rows, sub):
        gr = ga[r : r + sub] * slope[r : r + sub, slope_cols].astype(F32)
        total = total + fold(gr.reshape(sub // 8, 8, cols))
        gbef[r : r + sub, at] = gr.astype(BF16)
    upb_acc[:, at] = total


def backward(lens, groups, og, saved, ups, downs, small, ft, taps, group_count):
    act, slope, normed, inv, shaped, masked = saved
    clips, fc, d = og.shape
    h = ups.shape[2]
    R, r, n = fc * clips, ft * clips, fc // ft
    parts = 6
    cols = h // parts
    span = parts + n + 2
    block = lambda i: 1 - i // span
    part = lambda i: jnp.minimum(lax.rem(i, span), parts - 1)
    tile = lambda i: jnp.clip(lax.rem(i, span) - parts, 0, n - 1)
    late = lambda i: jnp.clip(lax.rem(i, span) - parts - 2, 0, n - 1)
    last = lambda i: jnp.clip(i - span - parts - 2, 0, n - 1)
    sums = [(2, d, h), (2, h, d), (2, ROWS, d), (2, 1, h)]
    return pl.pallas_call(
        functools.partial(backward_kernel, ft=ft, tiles=n, parts=parts, taps=taps, group_count=group_count),
        name="backward",
        grid=(2 * span,),
        in_specs=[
            smem(), smem(), whole(clips, fc, d),
            pl.BlockSpec((1, R, cols), lambda i: (block(i), 0, part(i))),
            pl.BlockSpec((1, R, cols), lambda i: (block(i), 0, part(i))),
            pl.BlockSpec((1, ft, clips, d), lambda i: (block(i), tile(i), 0, 0)),
            pl.BlockSpec((1, ft, clips, LANES), lambda i: (block(i), tile(i), 0, 0)),
            pl.BlockSpec((1, R, d), lambda i: (block(i), 0, 0), pipeline_mode=pl.Buffered(1)),
            pl.BlockSpec((1, ft, clips, d), lambda i: (block(i), late(i), 0, 0)),
            pl.BlockSpec((1, d, h), lambda i: (block(i), 0, 0)),
            pl.BlockSpec((1, h, d), lambda i: (block(i), 0, 0)),
            whole(2, ROWS, d),
        ],
        out_specs=[pl.BlockSpec((d // LANES, r, LANES), lambda i: (0, last(i), 0))] + [whole(*v) for v in sums],
        out_shape=[shape((d // LANES, R, LANES))] + [shape(v) for v in sums],
        scratch_shapes=[
            pltpu.VMEM((fc, clips, d), F32), pltpu.VMEM((R, d), BF16), pltpu.VMEM((R, h), BF16),
            pltpu.VMEM((fc + 2 * ft + HALO, clips, d), F32), pltpu.VMEM((d // LANES, 16 * clips, LANES), F32),
            pltpu.VMEM((14, clips, d), F32), pltpu.VMEM((clips, d), jnp.int32),
            pltpu.VMEM((12, clips, d), F32), pltpu.VMEM((clips, h), F32),
        ],
        compiler_params=pltpu.CompilerParams(vmem_limit_bytes=VMEM_LIMIT),
    )(lens, groups, og, act, slope, normed, inv, shaped, masked, ups, downs, small)


def step_kernel(*refs, deep, side, ft, parts, taps, group_count):
    lens, groups, frames, og = refs[:4]
    shards = refs[4:13]
    out, gs_out, up_part, down_part, small_part, act_far, slope_far = refs[13:20]
    (io, stream, masked0, masked1, normed, inv, shaped, first_rows, act, slope, gb, s8, u8, len8, acc, upb_acc) = refs[20:36]
    small_full, upb_full, small_grad, upb_grad, up_full, down_full, up_term, down_term = refs[36:44]
    io_sem, act_sem, slope_sem, act_back_sem, slope_back_sem = refs[44:49]
    gather_refs, sum_refs = refs[49:67], refs[67:]

    i = pl.program_id(0)
    clips, frame_count, width = io.shape
    hidden = act.shape[1]
    tiles = frame_count // ft
    rows = ft * clips
    cols = hidden // parts
    span = 2 * parts + tiles + 1

    load = lambda n, src: pltpu.make_async_copy(src, io, io_sem.at[n])
    tile_rows = lambda j: pl.ds(pl.multiple_of(j * rows, rows), rows)
    part_at = lambda p: pl.ds(pl.multiple_of(p * cols, cols), cols)

    def spills(j):
        r = tile_rows(j)
        return [
            pltpu.make_async_copy(act.at[r], act_far.at[r], act_sem.at[j]),
            pltpu.make_async_copy(slope.at[r], slope_far.at[r], slope_sem.at[j]),
        ]

    def act_back(p):
        return pltpu.make_async_copy(act_far.at[:, part_at(p)], act.at[:, part_at(p)], act_back_sem.at[p])

    def slope_back(j):
        return pltpu.make_async_copy(slope_far.at[tile_rows(j)], slope.at[tile_rows(j)], slope_back_sem.at[j])

    def up_cols(b):
        return lambda lo, hi: up_full[b, :, :, :, :, :, lo:hi].reshape(width, hi - lo)

    def spread():
        load(0, frames).wait()

        def one(n, carry):
            t0 = pl.multiple_of(n * 16, 16)
            spread_clips(io, t0, stream, 0, 16)
            v = rows_of(stream, 0, 16 * clips)
            at = pl.multiple_of(t0 * clips, 16 * clips)
            first_rows[pl.ds(at, 16 * clips), :] = v.astype(BF16)
            masked0[pl.ds(HALO + t0, 16)] = keep_frames(v.reshape(16, clips, width), t0, len8)
            return carry
        lax.fori_loop(0, frame_count // 16, one, 0)
        load(1, og).start()

    def conv0(lo, hi):
        def one(n, carry):
            conv_norm(masked0, n * ft, ft, s8.at[0], normed.at[0], inv.at[0], shaped, taps, HALO)
            return carry
        lax.fori_loop(lo, hi, one, 0)

    def ready():
        for b in range(2):
            prepare(small_full.at[b], lens, groups, s8.at[b], len8, group_count)
            u8[b] = jnp.broadcast_to(upb_full[b, 0:1, :], u8.shape[1:])

    @pl.when(i == 0)
    def _():
        load(0, frames).start()
        zeros = jnp.zeros((HALO, clips, width), F32)
        for m in (masked0, masked1, normed.at[0], normed.at[1]):
            m[0:HALO] = zeros
            m[HALO + frame_count : HALO + frame_count + HALO] = zeros
        len8[...] = per_clip(lens, clips, width)
        Gather(shards, up_full, down_full, small_full, upb_full, gather_refs, deep, side, group_count, taps).early(
            spread, ready, conv0, tiles)

    Gather(shards, up_full, down_full, small_full, upb_full, gather_refs, deep, side, group_count, taps).late(i, tiles)

    @pl.when(i < tiles)
    def _():
        r0 = pl.multiple_of(i * rows, rows)
        up_gelu(shaped, up_cols(0), u8.at[0], act, r0, slope, r0, rows, hidden)
        run(spills(i))

    @pl.when((i >= tiles) & (i < 2 * tiles))
    def _():
        j = i - tiles
        f0 = j * ft
        r0 = pl.multiple_of(j * rows, rows)
        branch = mm(act[pl.ds(r0, rows), :], down_full[0].reshape(hidden, width), NN)
        for t in range(0, ft, 4):
            b = branch[t * clips : (t + 4) * clips].reshape(4, clips, width) + s8[0, DOWN_BIAS][None]
            total = masked0[pl.ds(HALO + f0 + t, 4)] + s8[0, GAIN][None] * b
            masked1[pl.ds(HALO + f0 + t, 4)] = keep_frames(total, f0 + t, len8)

    @pl.when((i >= 2 * tiles) & (i < 3 * tiles))
    def _():
        j = i - 2 * tiles
        f0 = j * ft
        r0 = pl.multiple_of(j * rows, rows)
        done(spills(j))
        conv_norm(masked1, f0, ft, s8.at[1], normed.at[1], inv.at[1], shaped, taps, HALO)
        up_gelu(shaped, up_cols(1), u8.at[1], act, r0, slope, r0, rows, hidden)
        branch = mm(act[pl.ds(r0, rows), :], down_full[1].reshape(hidden, width), NN)
        last_block(branch, masked1, f0, r0, ft, s8.at[1], len8, first_rows, stream, out)

    k = i - 3 * tiles
    step = lax.rem(jnp.maximum(k, 0), span)
    b = jnp.where(k < span, 1, 0)

    @pl.when(k == 0)
    def _():
        load(1, og).wait()
        spread_grad(io, stream, masked0, HALO)

    @pl.when(k == span)
    def _():
        def one(n, carry):
            t0 = n * 4
            at = pl.multiple_of(t0 * clips, 4 * clips)
            v = normed[0, pl.ds(HALO + t0, 4)] * s8[0, SCALE][None] + s8[0, SHIFT][None]
            shaped[pl.ds(at, 4 * clips), :] = v.reshape(4 * clips, width).astype(BF16)
            first = first_rows[pl.ds(at, 4 * clips), :].astype(F32).reshape(4, clips, width)
            masked1[pl.ds(HALO + t0, 4)] = keep_frames(first, t0, len8)
            return carry
        lax.fori_loop(0, frame_count // 4, one, 0, unroll=4)
        for j in range(tiles):
            slope_back(j).wait()

    @pl.when((k >= 0) & (step == 0))
    def _():
        acc[...] = jnp.zeros(acc.shape, F32)
        acc[A_DOWN] = branch_grad(masked0, HALO, s8.at[b], len8, gb)

    sums = Sums(sum_refs, up_term, down_term, up_part, down_part, small_part, small_grad, upb_grad, deep, side)
    sums.before(k, span, parts)

    @pl.when((k >= span) & (step < parts))
    def _():
        act_back(step).wait()

    def spots(p):
        per = down_full.shape[5] // 16
        for m in range(cols // 16):
            row = p * (cols // 16) + m
            e = row // per
            z, chip = e // (2 * side * side), e // 2
            sub = pl.ds(pl.multiple_of((row - e * per) * 16, 16), 16)
            yield (b, z, lax.rem(chip // side, side), lax.rem(chip, side), lax.rem(e, 2), sub)

    @pl.when((k >= 0) & (step < parts))
    def _():
        term = mm(act[:, part_at(step)], gb[...], TN)
        total = jnp.zeros((clips, width), F32)
        for m, spot in enumerate(spots(step)):
            piece = term[m * 16 : (m + 1) * 16]
            down_term[spot] = piece.astype(BF16)
            total = total + fold((piece * down_full[spot].astype(F32)).reshape(2, 8, width))
        acc[A_GAIN] += total

    @pl.when((k >= 0) & (k < parts))
    def _():
        act_back(step).start()

    @pl.when((k >= 0) & (step >= parts) & (step < 2 * parts))
    def _():
        at = part_at(step - parts)
        lower = jnp.concatenate([down_full[spot] for spot in spots(step - parts)], axis=0)
        before_grad(gb, lower, slope, at, slope, at, upb_acc, frame_count * clips)
        term = mm(shaped[...], slope[:, at], TN).astype(BF16)
        up_term[b, :, :, :, :, :, at] = term.reshape(deep, side, side, 2, up_full.shape[5], cols)

    j = step - 2 * parts

    @pl.when((j >= 0) & (j < tiles))
    def _():
        r0 = pl.multiple_of(j * rows, rows)
        grad = mm(slope[pl.ds(r0, rows), :], up_full[b].reshape(width, hidden), NT)
        norm_back(grad, normed.at[b], HALO + j * ft, inv.at[b], j * ft, s8.at[b], normed.at[b], HALO + j * ft, acc, ft)

    @pl.when((k < span) & (j >= 0) & (j < tiles))
    def _():
        slope_back(j).start()

    @pl.when(j >= 1)
    def _():
        f0 = (j - 1) * ft
        conv_back(
            normed.at[b], HALO + f0, s8.at[b], masked1, HALO + f0, masked0, HALO + f0, f0, gs_out, acc, ft, len8, taps)

    @pl.when((k >= 0) & (step == span - 1))
    def _():
        finish_small(acc, upb_acc, groups, s8.at[b], small_grad.at[b], upb_grad.at[b], group_count)

    sums.after(k, span)


def whole_step(deep, side, lens, groups, frames, og, weights, ft, taps, group_count):
    clips, fc, d = frames.shape
    h = weights[4].shape[2]
    urows, drows = weights[4].shape[1], weights[6].shape[1]
    R, r, n = fc * clips, ft * clips, fc // ft
    parts = 6
    span = 2 * parts + n + 1
    last = lambda i: jnp.clip(i - 3 * n - span - 2 * parts - 1, 0, n - 1)
    dims = (2, deep, side, side, 2)
    rows = lambda dtype, *lead: pltpu.VMEM(lead + (d,), dtype)
    halo = fc + 2 * HALO
    return pl.pallas_call(
        functools.partial(step_kernel, deep=deep, side=side, ft=ft, parts=parts, taps=taps, group_count=group_count),
        name="step",
        grid=(3 * n + 2 * span,),
        in_specs=[smem(), smem(), hbm(), hbm()] + [vmem()] * 9,
        out_specs=[
            pl.BlockSpec((clips, ft, d), lambda i: (0, jnp.clip(i - 2 * n, 0, n - 1), 0)),
            pl.BlockSpec((d // LANES, r, LANES), lambda i: (0, last(i), 0)), vmem(), vmem(), vmem(), hbm(), hbm(),
        ],
        out_shape=[
            shape((clips, fc, d), BF16), shape((d // LANES, R, LANES)), shape((2, urows, h)), shape((2, drows, d)),
            shape((2 * PACK, LANES)), shape((R, h), BF16), shape((R, h), BF16),
        ],
        scratch_shapes=[
            rows(BF16, clips, fc), pltpu.VMEM((d // LANES, max(r, 16 * clips), LANES), F32),
            rows(F32, halo, clips), rows(F32, halo, clips), rows(F32, 2, halo, clips), pltpu.VMEM((2, fc, clips, LANES), F32),
            rows(BF16, R), rows(BF16, R), pltpu.VMEM((R, h), BF16), pltpu.VMEM((R, h), BF16), rows(BF16, R),
            rows(F32, 2, 14, clips), pltpu.VMEM((2, clips, h), F32), rows(jnp.int32, clips), rows(F32, 12, clips),
            pltpu.VMEM((clips, h), F32),
            rows(F32, 2, ROWS), pltpu.VMEM((2, 1, h), F32), rows(F32, 2, ROWS), pltpu.VMEM((2, 1, h), F32),
            pltpu.VMEM(dims + (urows, h), BF16), rows(BF16, *dims, drows), pltpu.VMEM(dims + (urows, h), BF16), rows(BF16, *dims, drows),
            DMA((2,)), DMA((n,)), DMA((n,)), DMA((parts,)), DMA((n,)),
        ] + gather_scratch(deep, side) + sums_scratch(deep, side, urows, drows, d, h),
        compiler_params=pltpu.CompilerParams(vmem_limit_bytes=VMEM_LIMIT, collective_id=0, has_side_effects=True),
    )(lens, groups, frames, og, *weights)


def unpack_kernel(gs, up_in, down_in, small, gin, conv_w, conv_b, scale, shift, up_w, up_b, down_w, down_b, gain):
    collect_clips(gs, gin, gin.shape[1])

    @pl.when(pl.program_id(0) == 0)
    def _():
        unpack_parts(up_in, down_in, small, conv_w, conv_b, scale, shift, up_w, up_b, down_w, down_b, gain)


def unpack_parts(up_in, down_in, small, conv_w, conv_b, scale, shift, up_w, up_b, down_w, down_b, gain):
    f = lax.axis_index("fsdp")
    width = conv_b.shape[1]
    wide = up_b.shape[1]
    span = wide * LANES // width
    turned = pltpu.roll(small[...], lax.rem(LANES - f * width, LANES), 1)
    for b in range(2):
        o = b * PACK
        for k in range(conv_w.shape[0]):
            conv_w[k, b : b + 1, :] = turned[o + k : o + k + 1, :width]
        conv_b[b : b + 1, :] = turned[o + CONV_BIAS : o + CONV_BIAS + 1, :width]
        scale[b] = turned[o + SCALE : o + SCALE + scale.shape[1], :width]
        shift[b] = turned[o + SHIFT : o + SHIFT + shift.shape[1], :width]
        down_b[b : b + 1, :] = turned[o + DOWN_BIAS : o + DOWN_BIAS + 1, :width]
        gain[b : b + 1, :] = turned[o + GAIN : o + GAIN + 1, :width]
        bias = jnp.concatenate([small[o + 14 + q : o + 15 + q, :] for q in range(span // LANES)], axis=1)
        bias = pltpu.roll(jnp.broadcast_to(bias, (8, span)), lax.rem(span - f * wide, span), 1)
        up_b[b : b + 1, :] = bias[0:1, :wide]
    up_w[...] = up_in[...]
    down_w[...] = down_in[...]


def unpack(gs, parts, clips, taps, group_count, width, wide):
    split, R, lanes = gs.shape
    fc = R // clips
    ft = 32
    if parts is None:
        return pl.pallas_call(
            lambda src, dst: collect_clips(src, dst, ft),
            name="unpack",
            grid=(fc // ft,),
            in_specs=[pl.BlockSpec((split, ft * clips, lanes), lambda i: (0, i, 0))],
            out_specs=pl.BlockSpec((clips, ft, split * lanes), lambda i: (0, i, 0)),
            out_shape=shape((clips, fc, split * lanes)),
        )(gs)
    up_in, down_in, small = parts
    outs = [(taps, 2, width), (2, width), (2, group_count, width), (2, group_count, width), up_in.shape, (2, wide),
            down_in.shape, (2, width), (2, width)]
    return pl.pallas_call(
        unpack_kernel,
        name="unpack",
        grid=(fc // ft,),
        in_specs=[pl.BlockSpec((split, ft * clips, lanes), lambda i: (0, i, 0))] + [whole(*v.shape) for v in parts],
        out_specs=[pl.BlockSpec((clips, ft, split * lanes), lambda i: (0, i, 0))] + [whole(*v) for v in outs],
        out_shape=[shape((clips, fc, split * lanes))] + [shape(v) for v in outs],
    )(gs, up_in, down_in, small)


def body(deep, fan, frames, group, lengths, conv_w, conv_b, scale, shift, up_w, up_b, down_w, down_b, gain, out_grad):
    side = math.isqrt(fan // 2)
    clips = frames.shape[0]
    taps, group_count, hidden = conv_w.shape[1], scale.shape[1], up_w.shape[2]
    width, wide = conv_b.shape[1], up_b.shape[1]
    axes = ("dp", "fsdp")
    near = width * fan == LANES and up_w.shape[1] % 16 == 0 and down_w.shape[1] % 16 == 0
    ft = 32
    if near:
        weights = (conv_w.transpose(1, 0, 2), conv_b, scale, shift, up_w, up_b, down_w, down_b, gain)
    else:
        whole_of = lambda v, axis: lax.all_gather(v, axes, axis=axis, tiled=True)
        ups, downs = whole_of(up_w, 1), whole_of(down_w, 1)
        lines = jnp.concatenate(
            [conv_w, conv_b[:, None], scale, shift, down_b[:, None], gain[:, None], jnp.zeros((2, 2, width), BF16)], axis=1
        )
        small = whole_of(lines, 2).astype(F32)
        upb = whole_of(up_b, 1).astype(F32)[:, None]
        weights = (small, upb, ups, downs)
    if near:
        out, gs, *parts, _, _ = whole_step(deep, side, lengths, group, frames, out_grad, weights, ft, taps, group_count)
        gin, conv_grad, *grads = unpack(gs, parts, clips, taps, group_count, width, wide)
        return (out, gin, conv_grad.transpose(1, 0, 2), *grads)
    out, act, slope, *rest = forward(lengths, group, frames, weights, hidden, ft, taps, group_count)
    saved = (act, slope.reshape(act.shape), *rest)
    gs, *parts = backward(lengths, group, out_grad, saved, ups, downs, small, ft, taps, group_count)
    gin = unpack(gs, None, clips, taps, group_count, width, wide)
    dup, ddown, lines, ug = parts
    owner = lambda v, axis: lax.psum_scatter(v, axes, scatter_dimension=axis, tiled=True)
    lines = owner(lines, 2)
    return (
        out, gin, lines[:, :taps], lines[:, CONV_BIAS], lines[:, SCALE : SCALE + group_count],
        lines[:, SHIFT : SHIFT + group_count], owner(dup, 1), owner(ug[:, 0], 1), owner(ddown, 1),
        lines[:, DOWN_BIAS], lines[:, GAIN],
    )


def solution(mesh):
    split = ("dp", "fsdp")
    clip = P(split, None, None)
    first, middle, last = P(None, split), P(None, split, None), P(None, None, split)
    in_specs = (clip, P(split), P(split), last, first, last, last, middle, first, middle, first, first, clip)
    out_specs = (clip, clip, last, first, last, last, middle, first, middle, first, first)
    run = functools.partial(body, mesh.shape["dp"], mesh.shape["fsdp"])
    return jax.shard_map(run, mesh=mesh, in_specs=in_specs, out_specs=out_specs, check_vma=False)
```

```python
import functools
import math
import jax
import jax.numpy as jnp
from jax import lax
from jax.experimental import pallas as pl
from jax.experimental.pallas import tpu as pltpu
from jax.sharding import PartitionSpec as P

F32 = jnp.float32
BF16 = jnp.bfloat16
EPSILON = 1e-06
TAPS, CONV_BIAS, SCALE, SHIFT, DOWN_BIAS, GAIN, ROWS = 0, 7, 8, 10, 12, 13, 16
A_TAPS, A_BIAS, A_SCALE, A_SHIFT, A_DOWN, A_GAIN = 0, 7, 8, 9, 10, 11
HALO = 3
LANES = 128
VMEM_LIMIT = 64 * 1024 * 1024 - 128 * 1024
NN = (((1,), (0,)), ((), ()))
NT = (((1,), (1,)), ((), ()))
TN = (((0,), (0,)), ((), ()))
DMA = pltpu.SemaphoreType.DMA


def mm(a, b, dims):
    return lax.dot_general(a, b, dims, preferred_element_type=F32)


def gelu_pair(before):
    u = before * math.sqrt(0.5)
    phi = 0.5 + 0.5 * lax.erf(u)
    bell = jnp.exp2(u * u * (-math.log2(math.e))) * (1.0 / math.sqrt(math.pi))
    return before * phi, phi + u * bell


def per_clip(values, clips, width):
    rows = lax.broadcasted_iota(jnp.int32, (clips, width), 0)
    out = jnp.zeros((clips, width), jnp.int32)
    for c in range(clips):
        out = jnp.where(rows == c, values[c], out)
    return out


def prepare(small, lens, groups, s8, len8, group_count):
    clips, width = len8.shape
    for r in range(14):
        s8[r] = jnp.broadcast_to(small[r : r + 1, :], (clips, width))
    member = per_clip(groups, clips, width)
    len8[...] = per_clip(lens, clips, width)
    gain = jnp.zeros((clips, width), F32)
    shift = jnp.zeros((clips, width), F32)
    for g in range(group_count):
        chosen = jnp.where(member == g, 1.0, 0.0)
        gain = gain + chosen * s8[SCALE + g]
        shift = shift + chosen * s8[SHIFT + g]
    s8[SCALE] = gain
    s8[SHIFT] = shift


def keep_frames(v, t0, len8, other=0.0):
    t = lax.broadcasted_iota(jnp.int32, v.shape, 0) + t0
    return jnp.where(t < len8[...][None], v, other)


def spread_clips(block, t0, dst, d0, frames):
    clips = block.shape[0]
    for c in range(clips):
        for t in range(0, frames, 16):
            v = block[c, pl.ds(t0 + t, 16), :].astype(F32)
            for l in range(dst.shape[0]):
                dst[l, pl.ds((d0 + t) * clips + c, 16, stride=clips), :] = v[:, l * LANES : (l + 1) * LANES]


def collect_clips(src, block, frames):
    clips = block.shape[0]
    for c in range(clips):
        for t in range(0, frames, 16):
            for l in range(src.shape[0]):
                v = src[l, pl.ds(t * clips + c, 16, stride=clips), :]
                block[c, t : t + 16, l * LANES : (l + 1) * LANES] = v.astype(block.dtype)


def rows_of(src, start, n):
    return jnp.concatenate([src[l, pl.ds(start, n), :] for l in range(src.shape[0])], axis=-1)


def put_rows(dst, start, v):
    for l in range(dst.shape[0]):
        dst[l, pl.ds(start, v.shape[0]), :] = v[:, l * LANES : (l + 1) * LANES]


def fold(v):
    return jnp.sum(v, axis=0)


def smem():
    return pl.BlockSpec(memory_space=pltpu.SMEM)


def vmem():
    return pl.BlockSpec(memory_space=pltpu.VMEM)


def hbm():
    return pl.BlockSpec(memory_space=pl.ANY)


def whole(*dims):
    return pl.BlockSpec(dims, lambda i: (0,) * len(dims), pipeline_mode=pl.Buffered(1))


def shape(dims, dtype=F32):
    return jax.ShapeDtypeStruct(dims, dtype)


MESH = pl.DeviceIdType.MESH
PACK = 20


class Place:
    def __init__(self, deep, side):
        self.deep, self.side = deep, side
        self.z = lax.axis_index("dp")
        f = lax.axis_index("fsdp")
        self.f = f
        self.core = lax.rem(f, 2)
        chip = f // 2
        self.low = lax.rem(chip, side)
        self.high = chip // side
        self.first = jnp.where(self.core == 0, self.high, self.low)
        self.second = jnp.where(self.core == 0, self.low, self.high)

    def chip_of(self, first, second):
        high = jnp.where(self.core == 0, first, second)
        low = jnp.where(self.core == 0, second, first)
        return high, low

    def fsdp_of(self, first, second):
        high, low = self.chip_of(first, second)
        return (high * self.side + low) * 2 + self.core

    def z_peer(self, p):
        return {"dp": lax.rem(self.z + p, self.deep)}

    def first_peer(self, p):
        return {"fsdp": self.fsdp_of(lax.rem(self.first + p, self.side), self.second)}

    def second_peer(self, p):
        return {"fsdp": self.fsdp_of(self.first, lax.rem(self.second + p, self.side))}

    def core_peer(self):
        return {"fsdp": self.f + 1 - 2 * self.core}

    def greet(self):
        barrier = pltpu.get_barrier_semaphore()
        peers = [self.z_peer(p) for p in range(1, self.deep)]
        peers += [self.first_peer(p) for p in range(1, self.side)]
        peers += [self.second_peer(p) for p in range(1, self.side)]
        peers.append(self.core_peer())
        for peer in peers:
            pl.semaphore_signal(barrier, inc=1, device_id=peer, device_id_type=MESH)
        pl.semaphore_wait(barrier, len(peers))


def send(src, dst, send_sem, recv_sem, peer):
    return pltpu.make_async_remote_copy(
        src_ref=src, dst_ref=dst, send_sem=send_sem, recv_sem=recv_sem, device_id=peer, device_id_type=MESH
    )


def run(copies):
    for c in copies:
        c.start()


def done(copies):
    for c in copies:
        c.wait()


def weight_route(place, own, full, sems):
    zs, zr, fs, fr, ss, sr, cs, cr = sems
    deep, side, core = place.deep, place.side, place.core

    def held(p, q):
        high, low = place.chip_of(lax.rem(place.first + p, side), lax.rem(place.second + q, side))
        return full.at[:, high, low, core]

    mine = full.at[place.z, place.high, place.low, core]
    along_z = [send(own, mine, zs.at[p - 1], zr.at[p - 1], place.z_peer(p)) for p in range(1, deep)]
    along_first = [
        send(held(0, 0), held(0, 0), fs.at[p - 1], fr.at[p - 1], place.first_peer(p)) for p in range(1, side)
    ]
    along_second = []
    for j in range(side):
        high, low = place.chip_of(j, place.second)
        line = full.at[:, high, low, core]
        for p in range(1, side):
            n = j * (side - 1) + p - 1
            along_second.append(send(line, line, ss.at[n], sr.at[n], place.second_peer(p)))
    across = lambda p, q: send(held(p, q), held(p, q), cs.at[p * side + q], cr.at[p * side + q], place.core_peer())
    over = [[across(0, 0)], [across(p, 0) for p in range(1, side)],
            [across(p, q) for q in range(1, side) for p in range(side)]]
    return [along_z, along_first, along_second], over


def gather_sems(count, deep, side):
    one = [deep - 1, deep - 1, side - 1, side - 1, side * (side - 1), side * (side - 1), side * side, side * side]
    return [DMA((count, n)) for n in one]


def place_small(place, shards, pack, group_count, taps):
    conv_w, conv_b, scale, shift, up_b, down_b, gain = shards
    width = conv_b.shape[1]
    lane = lax.broadcasted_iota(jnp.int32, (width, LANES), 1)
    row = lax.broadcasted_iota(jnp.int32, (width, LANES), 0)
    spot = jnp.where(lane == row + place.f * width, 1.0, 0.0).astype(BF16)
    wide = up_b.shape[1]
    span = wide * LANES // width
    lane = lax.broadcasted_iota(jnp.int32, (wide, span), 1)
    row = lax.broadcasted_iota(jnp.int32, (wide, span), 0)
    spread = jnp.where(lane == row + place.f * wide, 1.0, 0.0).astype(BF16)
    pack[...] = jnp.zeros(pack.shape, F32)
    for b in range(2):
        o = b * PACK
        for k in range(taps):
            pack[o + k : o + k + 1, :] = mm(conv_w[k, b : b + 1, :], spot, NN)
        pack[o + SCALE : o + SCALE + group_count, :] = mm(scale[b], spot, NN)
        pack[o + SHIFT : o + SHIFT + group_count, :] = mm(shift[b], spot, NN)
        for src, at in ((conv_b, CONV_BIAS), (down_b, DOWN_BIAS), (gain, GAIN)):
            pack[o + at : o + at + 1, :] = mm(src[b : b + 1, :], spot, NN)
        bias = mm(up_b[b : b + 1, :], spread, NN)
        for q in range(span // LANES):
            pack[o + 14 + q : o + 15 + q, :] = bias[:, q * LANES : (q + 1) * LANES]


class Gather:
    def __init__(self, shards, up_full, down_full, small_full, upb_full, refs, deep, side, group_count, taps):
        (self.pack, self.zbuf, self.first_in, self.first_sum, self.second_in, self.second_sum, self.core_in,
         self.local_sems, self.small_s, self.small_r) = refs[:10]
        sems = refs[10:]
        self.place = place = Place(deep, side)
        self.small_full, self.upb_full, self.shards = small_full, upb_full, shards
        self.group_count, self.taps = group_count, taps
        up_w, down_w = shards[4], shards[6]
        self.full = (up_full, down_full)
        self.routes, self.local = [], []
        for n, (own, full) in enumerate(
            ((up_w.at[0], up_full.at[0]), (down_w.at[0], down_full.at[0]), (up_w.at[1], up_full.at[1]), (down_w.at[1], down_full.at[1]))
        ):
            self.routes.append(weight_route(place, own, full, [s.at[n] for s in sems]))
            spot = full.at[place.z, place.high, place.low, place.core]
            self.local.append(pltpu.make_async_copy(own, spot, self.local_sems.at[n]))
        stages = [
            [(self.zbuf.at[place.z], self.zbuf.at[place.z], place.z_peer(p)) for p in range(1, deep)],
            [(self.zbuf, self.first_in.at[p - 1], place.first_peer(p)) for p in range(1, side)],
            [(self.first_sum, self.second_in.at[p - 1], place.second_peer(p)) for p in range(1, side)],
            [(self.second_sum, self.core_in, place.core_peer())],
        ]
        n = 0
        self.small = []
        for stage in stages:
            copies = []
            for src, dst, peer in stage:
                copies.append(send(src, dst, self.small_s.at[n], self.small_r.at[n], peer))
                n += 1
            self.small.append(copies)

    def begin(self, n):
        run(self.routes[n][0][0])
        self.local[n].start()

    def after_z(self, n):
        along, over = self.routes[n]
        self.local[n].wait()
        done(along[0])
        run(along[1])
        run(over[0])

    def after_first(self, n):
        along, over = self.routes[n]
        done(along[1])
        run(along[2])
        run(over[1])

    def after_second(self, n):
        along, over = self.routes[n]
        done(along[2])
        run(over[2])

    def end(self, n):
        for copies in self.routes[n][1]:
            done(copies)

    def early(self, spread, ready, conv, tiles):
        place = self.place
        place.greet()
        self.begin(0)
        conv_w, conv_b, scale, shift, _, up_b, _, down_b, gain = self.shards
        place_small(place, (conv_w, conv_b, scale, shift, up_b, down_b, gain), self.pack, self.group_count, self.taps)
        self.zbuf[place.z] = self.pack[...]
        run(self.small[0])
        self.begin(1)
        spread()
        done(self.small[0])
        run(self.small[1])
        self.after_z(0)
        done(self.small[1])
        total = self.zbuf[...]
        for p in range(1, place.side):
            total = total + self.first_in[p - 1]
        self.first_sum[...] = total
        run(self.small[2])
        done(self.small[2])
        total = self.first_sum[...]
        for p in range(1, place.side):
            total = total + self.second_in[p - 1]
        self.second_sum[...] = total
        run(self.small[3])
        self.after_first(0)
        self.after_z(1)
        self.begin(2)
        self.begin(3)
        done(self.small[3])
        self.finish_small()
        ready()
        conv(0, 3 * tiles // 4)
        self.after_second(0)
        self.after_first(1)
        conv(3 * tiles // 4, tiles)
        self.end(0)

    def finish_small(self):
        total = self.second_sum[...] + self.core_in[...]
        deep = self.place.deep
        per = self.upb_full.shape[2] // deep
        self.small_full[...] = jnp.zeros(self.small_full.shape, F32)
        for b in range(2):
            o = b * PACK
            for z in range(deep):
                self.small_full[b, 0:14, z * LANES : (z + 1) * LANES] = total[z, o : o + 14, :]
                for q in range(per // LANES):
                    at = z * per + q * LANES
                    self.upb_full[b, :, at : at + LANES] = total[z, o + 14 + q : o + 15 + q, :]

    def late(self, i, tiles):
        @pl.when(i == tiles // 4)
        def _():
            self.after_z(2)
            self.after_z(3)

        @pl.when(i == 3 * tiles // 4)
        def _():
            self.after_second(1)

        @pl.when(i == tiles)
        def _():
            self.end(1)

        @pl.when(i == tiles + tiles // 4)
        def _():
            self.after_first(2)
            self.after_first(3)

        @pl.when(i == 2 * tiles)
        def _():
            for n in (2, 3):
                self.after_second(n)
            for n in (2, 3):
                self.end(n)


def gather_scratch(deep, side):
    buf = pltpu.VMEM((deep, 2 * PACK, LANES), F32)
    many = pltpu.VMEM((side - 1, deep, 2 * PACK, LANES), F32)
    n = deep - 1 + 2 * (side - 1) + 1
    return [pltpu.VMEM((2 * PACK, LANES), F32), buf, many, buf, many, buf, buf, DMA((4,)), DMA((n,)), DMA((n,))] + gather_sems(
        4, deep, side
    )


def conv_norm(masked, f0, frames, s8, normed, inv, shaped, taps, n0=0, step=4):
    clips, width = s8.shape[1:]
    for j in range(0, frames, step):
        mixed = s8[CONV_BIAS][None]
        for k in range(taps):
            mixed = mixed + s8[TAPS + k][None] * masked[pl.ds(f0 + j + k, step)]
        center = mixed - jnp.mean(mixed, axis=-1, keepdims=True)
        inv_std = lax.rsqrt(jnp.mean(center * center, axis=-1, keepdims=True) + EPSILON)
        norm = center * inv_std
        normed[pl.ds(n0 + f0 + j, step)] = norm
        inv[pl.ds(f0 + j, step)] = jnp.broadcast_to(inv_std, (step, clips, LANES))
        rows = norm * s8[SCALE][None] + s8[SHIFT][None]
        at = pl.multiple_of((f0 + j) * clips, step * clips)
        shaped[pl.ds(at, step * clips), :] = rows.reshape(step * clips, width).astype(BF16)


def up_gelu(shaped, up_cols, u8, act, r0, slope, s0, rows, hidden, cols=256, sub=16):
    left = shaped[pl.ds(r0, rows), :]
    for n in range(0, hidden, cols):
        before = mm(left, up_cols(n, n + cols), NN)
        for r in range(0, rows, sub):
            piece = before[r : r + sub].reshape(sub // 8, 8, cols) + u8[:, n : n + cols][None]
            a, s = gelu_pair(piece.reshape(sub, cols))
            act[pl.ds(r0 + r, sub), n : n + cols] = a.astype(BF16)
            slope[pl.ds(s0 + r, sub), n : n + cols] = s.astype(slope.dtype)


def forward_kernel(
    lens, groups, frames, small_full, upb_full, up_full, down_full, out, act_out, slope, normed_out, inv_out, shaped_out, masked_out,
    stream, masked0, masked1, normed, inv, shaped, first_rows, act, s8, u8, len8, save_sem, act_sem, row_sem, *, ft, taps, group_count,
):
    i = pl.program_id(0)
    clips, frame_count, width = frames.shape
    hidden = act.shape[1]
    tiles = frame_count // ft
    rows = ft * clips

    def up_cols(b):
        return lambda lo, hi: up_full[b, :, lo:hi]

    body = pl.ds(HALO, frame_count)
    save = lambda n, src, dst: pltpu.make_async_copy(src, dst, save_sem.at[n])
    saves0 = [
        save(0, masked0.at[body], masked_out.at[0]), save(1, normed, normed_out.at[0]),
        save(2, inv, inv_out.at[0]), save(3, shaped, shaped_out.at[0]),
    ]
    save_masked1 = save(4, masked1.at[body], masked_out.at[1])
    tail = lambda b, j: pltpu.make_async_copy(
        act.at[pl.ds(pl.multiple_of(j * rows, rows), rows)],
        act_out.at[b, pl.ds(pl.multiple_of(j * rows, rows), rows)], act_sem.at[j])

    def row_saves(j):
        f = pl.ds(j * ft, ft)
        r = pl.ds(pl.multiple_of(j * rows, rows), rows)
        return [
            pltpu.make_async_copy(normed.at[f], normed_out.at[1, f], row_sem.at[0, j]),
            pltpu.make_async_copy(inv.at[f], inv_out.at[1, f], row_sem.at[1, j]),
            pltpu.make_async_copy(shaped.at[r], shaped_out.at[1, r], row_sem.at[2, j]),
        ]

    @pl.when(i == 0)
    def _():
        zeros = jnp.zeros((HALO, clips, width), F32)
        for m in (masked0, masked1):
            m[0:HALO] = zeros
            m[HALO + frame_count :] = zeros
        len8[...] = per_clip(lens, clips, width)

        def spread(n, carry):
            t0 = pl.multiple_of(n * 16, 16)
            spread_clips(frames, t0, stream, 0, 16)
            v = rows_of(stream, 0, 16 * clips)
            at = pl.multiple_of(t0 * clips, 16 * clips)
            first_rows[pl.ds(at, 16 * clips), :] = v.astype(BF16)
            masked0[pl.ds(HALO + t0, 16)] = keep_frames(v.reshape(16, clips, width), t0, len8)
            return carry
        lax.fori_loop(0, frame_count // 16, spread, 0)
        for b in range(2):
            prepare(small_full.at[b], lens, groups, s8.at[b], len8, group_count)
            u8[b] = jnp.broadcast_to(upb_full[b, 0:1, :], u8.shape[1:])

        def conv0(n, carry):
            conv_norm(masked0, n * ft, ft, s8.at[0], normed, inv, shaped, taps)
            return carry
        lax.fori_loop(0, tiles, conv0, 0)
        for c in saves0:
            c.start()

    @pl.when(i < tiles)
    def _():
        r0 = pl.multiple_of(i * rows, rows)
        up_gelu(shaped, up_cols(0), u8.at[0], act, r0, slope, 0, rows, hidden)
        tail(0, i).start()

    @pl.when((i >= tiles) & (i < 2 * tiles))
    def _():
        j = i - tiles
        f0 = j * ft
        r0 = pl.multiple_of(j * rows, rows)
        branch = mm(act[pl.ds(r0, rows), :], down_full[0], NN)
        for t in range(0, ft, 4):
            b = branch[t * clips : (t + 4) * clips].reshape(4, clips, width) + s8[0, DOWN_BIAS][None]
            total = masked0[pl.ds(HALO + f0 + t, 4)] + s8[0, GAIN][None] * b
            masked1[pl.ds(HALO + f0 + t, 4)] = keep_frames(total, f0 + t, len8)
        tail(0, j).wait()

    @pl.when(i == 2 * tiles)
    def _():
        for c in saves0:
            c.wait()
        save_masked1.start()

    @pl.when(i >= 2 * tiles)
    def _():
        j = i - 2 * tiles
        f0 = j * ft
        r0 = pl.multiple_of(j * rows, rows)
        conv_norm(masked1, f0, ft, s8.at[1], normed, inv, shaped, taps)
        for c in row_saves(j):
            c.start()
        up_gelu(shaped, up_cols(1), u8.at[1], act, r0, slope, 0, rows, hidden)
        tail(1, j).start()
        branch = mm(act[pl.ds(r0, rows), :], down_full[1], NN)
        last_block(branch, masked1, f0, r0, ft, s8.at[1], len8, first_rows, stream, out)

    @pl.when(i == 3 * tiles - 1)
    def _():
        save_masked1.wait()
        for j in range(tiles):
            tail(1, j).wait()
            for c in row_saves(j):
                c.wait()


def last_block(branch, masked1, f0, r0, ft, s8, len8, first_rows, stream, out):
    clips, width = len8.shape
    for t in range(0, ft, 4):
        b = branch[t * clips : (t + 4) * clips].reshape(4, clips, width) + s8[DOWN_BIAS][None]
        total = masked1[pl.ds(HALO + f0 + t, 4)] + s8[GAIN][None] * b
        at = pl.multiple_of(r0 + t * clips, 4 * clips)
        first = first_rows[pl.ds(at, 4 * clips), :].astype(F32).reshape(4, clips, width)
        put_rows(stream, t * clips, keep_frames(total, f0 + t, len8, first).reshape(4 * clips, width))
    collect_clips(stream, out, ft)


def forward(lens, groups, frames, weights, hidden, ft, taps, group_count):
    clips, fc, d = frames.shape
    h = hidden
    n, r = fc // ft, ft * clips
    R = fc * clips
    slope_at = lambda i: jnp.where(i < n, i, jnp.where(i < 2 * n, n - 1, i - n))
    return pl.pallas_call(
        functools.partial(forward_kernel, ft=ft, taps=taps, group_count=group_count),
        name="forward",
        grid=(3 * n,),
        in_specs=[smem(), smem(), whole(clips, fc, d)] + [vmem()] * 4,
        out_specs=[
            pl.BlockSpec((clips, ft, d), lambda i: (0, jnp.maximum(i - 2 * n, 0), 0)), hbm(),
            pl.BlockSpec((r, h), lambda i: (slope_at(i), 0)), hbm(), hbm(), hbm(), hbm(),
        ],
        out_shape=[
            shape((clips, fc, d), BF16), shape((2, R, h), BF16), shape((2 * R, h), BF16), shape((2, fc, clips, d)),
            shape((2, fc, clips, LANES)), shape((2, R, d), BF16), shape((2, fc, clips, d)),
        ],
        scratch_shapes=[
            pltpu.VMEM((d // LANES, max(r, 16 * clips), LANES), F32),
            pltpu.VMEM((fc + 2 * HALO, clips, d), F32), pltpu.VMEM((fc + 2 * HALO, clips, d), F32),
            pltpu.VMEM((fc, clips, d), F32), pltpu.VMEM((fc, clips, LANES), F32), pltpu.VMEM((R, d), BF16),
            pltpu.VMEM((R, d), BF16), pltpu.VMEM((R, h), BF16),
            pltpu.VMEM((2, 14, clips, d), F32), pltpu.VMEM((2, clips, h), F32), pltpu.VMEM((clips, d), jnp.int32),
            DMA((5,)), DMA((n,)), DMA((3, n)),
        ],
        compiler_params=pltpu.CompilerParams(vmem_limit_bytes=VMEM_LIMIT),
    )(lens, groups, frames, *weights)


class Scatter:
    def __init__(self, place, term, bufs, sems):
        self.place, self.term = place, term
        self.core_in, self.second_in, self.first_in, self.z_in = bufs
        self.sems = sems

    def line(self, first, second):
        high, low = self.place.chip_of(first, second)
        return self.term.at[:, high, low, self.place.core]

    def spot(self, z, first, second):
        high, low = self.place.chip_of(first, second)
        return (z, high, low)

    def core_copies(self):
        at = self.place
        return [send(self.term.at[:, :, :, 1 - at.core], self.core_in, self.sems[0].at[0], self.sems[1].at[0], at.core_peer())]

    def second_copies(self, p):
        at = self.place
        to = lax.rem(at.second + p, at.side)
        n = (p - 1) * at.side
        return [
            send(self.line(f, to), self.second_in.at[p - 1, f], self.sems[2].at[n + f], self.sems[3].at[n + f], at.second_peer(p))
            for f in range(at.side)
        ]

    def first_copy(self, p):
        at = self.place
        to = lax.rem(at.first + p, at.side)
        return send(self.line(to, at.second), self.first_in.at[p - 1], self.sems[4].at[p - 1], self.sems[5].at[p - 1], at.first_peer(p))

    def z_copy(self, p):
        at = self.place
        to = lax.rem(at.z + p, at.deep)
        high, low = at.chip_of(at.first, at.second)
        return send(self.term.at[to, high, low, at.core], self.z_in.at[p - 1], self.sems[6].at[p - 1], self.sems[7].at[p - 1], at.z_peer(p))

    def part1(self, z, first, second):
        z, high, low = self.spot(z, first, second)
        return self.term[z, high, low, self.place.core].astype(F32) + self.core_in[z, high, low].astype(F32)

    def part2(self, z, first):
        total = self.part1(z, first, self.place.second)
        for p in range(1, self.place.side):
            total = total + self.second_in[p - 1, first, z].astype(F32)
        return total

    def part3(self, z):
        total = self.part2(z, self.place.first)
        for p in range(1, self.place.side):
            total = total + self.first_in[p - 1, z].astype(F32)
        return total

    def put(self, z, first, second, total):
        z, high, low = self.spot(z, first, second)
        self.term[z, high, low, self.place.core] = total.astype(BF16)

    def core_start(self):
        run(self.core_copies())

    def second_start(self):
        at = self.place
        done(self.core_copies())
        for p in range(1, at.side):
            to = lax.rem(at.second + p, at.side)
            copies = self.second_copies(p)
            for first in range(at.side):
                def one(z, carry):
                    self.put(z, first, to, self.part1(z, first, to))
                    return carry
                lax.fori_loop(0, at.deep, one, 0)
                copies[first].start()

    def first_start(self):
        at = self.place
        for p in range(1, at.side):
            done(self.second_copies(p))
        for p in range(1, at.side):
            to = lax.rem(at.first + p, at.side)
            def one(z, carry):
                self.put(z, to, at.second, self.part2(z, to))
                return carry
            lax.fori_loop(0, at.deep, one, 0)
            self.first_copy(p).start()

    def z_start(self):
        at = self.place
        done([self.first_copy(p) for p in range(1, at.side)])
        for p in range(1, at.deep):
            to = lax.rem(at.z + p, at.deep)
            self.put(to, at.first, at.second, self.part3(to))
            self.z_copy(p).start()

    def finish(self, out):
        at = self.place
        done([self.z_copy(p) for p in range(1, at.deep)])
        total = self.part3(at.z)
        for p in range(1, at.deep):
            total = total + self.z_in[p - 1].astype(F32)
        out[...] = total


def scatter_bufs(deep, side, rows, cols):
    v = lambda *lead: pltpu.VMEM(lead + (rows, cols), BF16)
    return [v(deep, side, side), v(side - 1, side, deep), v(side - 1, deep), v(deep - 1)]


def scatter_sems(count, deep, side):
    return [DMA((count, n)) for n in (1, 1, side * (side - 1), side * (side - 1), side - 1, side - 1, deep - 1, deep - 1)]


def pack_small(small, upb, b, terms, deep):
    per = upb.shape[1] // deep
    o = b * PACK
    for z in range(deep):
        terms[z, o : o + 14, :] = small[0:14, z * LANES : (z + 1) * LANES]
        for q in range(per // LANES):
            at = z * per + q * LANES
            terms[z, o + 14 + q : o + 15 + q, :] = upb[:, at : at + LANES]


def sum_small(place, terms, z_in, bufs, out, s, r):
    n = 0
    copies = []
    for p in range(1, place.deep):
        to = lax.rem(place.z + p, place.deep)
        copies.append(send(terms.at[to], z_in.at[p - 1], s.at[n], r.at[n], place.z_peer(p)))
        n += 1
    run(copies)
    yield
    done(copies)
    total = terms[place.z]
    for p in range(1, place.deep):
        total = total + z_in[p - 1]
    stages = [[place.core_peer()], [place.second_peer(p) for p in range(1, place.side)],
              [place.first_peer(p) for p in range(1, place.side)]]
    for (here, into), peers in zip(bufs, stages):
        here[...] = total
        copies = []
        for p, peer in enumerate(peers):
            copies.append(send(here, into.at[p], s.at[n], r.at[n], peer))
            n += 1
        run(copies)
        yield
        done(copies)
        for p in range(len(peers)):
            total = total + into[p]
    out[...] = total


def small_bufs(deep, side):
    many = lambda *n: pltpu.VMEM(n + (2 * PACK, LANES), F32)
    n = deep - 1 + 2 * (side - 1) + 1
    return [many(deep), many(deep - 1), many(), many(1), many(), many(side - 1), many(), many(side - 1), DMA((n,)), DMA((n,))]


class Sums:
    def __init__(self, refs, up_term, down_term, up_part, down_part, small_part, small_grad, upb_grad, deep, side, parts):
        self.place = Place(deep, side)
        self.terms, self.z_in = refs[:2]
        self.bufs = [refs[2:4], refs[4:6], refs[6:8]]
        self.small_s, self.small_r = refs[8:10]
        refs = refs[10:]
        sems = refs[-8:]
        self.small_part, self.small_grad, self.upb_grad = small_part, small_grad, upb_grad
        self.parts = parts
        cols = up_part.shape[2] // parts
        self.jobs = []
        for b in (1, 0):
            views = []
            for p in range(parts):
                c = pl.ds(p * cols, cols)
                views.append((up_term.at[b, :, :, :, :, :, c], up_part.at[b, :, c]))
            views.append((down_term.at[b], down_part.at[b]))
            for term, out in views:
                n = len(self.jobs)
                self.jobs.append((Scatter(self.place, term, refs[4 * n : 4 * n + 4], [s.at[n] for s in sems]), out))

    def do(self, n, what):
        job, out = self.jobs[n]
        if what == "finish":
            job.finish(out)
        else:
            getattr(job, what)()

    def at(self, i, half, span):
        parts, per = self.parts, self.parts + 1
        whats = ("core_start", "second_start", "first_start", "z_start", "finish")
        when = []
        for p in range(parts - 1):
            t = 2 * (p + 1)
            when.append((t, t + 1, t + 3, t + 5, 2 * parts + 6))
        t = 2 * parts
        when.append((t, t + 2, t + 5, t + 8, t + 12))
        when.append((t, t + 3, t + 9, t + 12, t + 16))
        plan = []
        for order, what in enumerate(whats):
            for n in range(2 * per):
                slot = when[n % per][order] + 2 * span * (n // per)
                if slot < 4 * span and slot % 2 == half:
                    plan.append((slot // 2, n, what))
        for now in sorted({p[0] for p in plan}):
            @pl.when(i == now)
            def _():
                for step, n, what in plan:
                    if step == now:
                        self.do(n, what)

    def after(self, i, span):
        @pl.when(i == 2 * span - 1)
        def _():
            self.terms[...] = jnp.zeros(self.terms.shape, F32)
            for b in range(2):
                pack_small(self.small_grad.at[b], self.upb_grad.at[b], b, self.terms, self.place.deep)
            steps = sum_small(self.place, self.terms, self.z_in, self.bufs, self.small_part, self.small_s, self.small_r)
            last = 2 * (self.parts + 1) - 1
            next(steps)
            next(steps)
            self.do(last, "z_start")
            self.do(last - 1, "finish")
            next(steps)
            next(steps)
            self.do(last, "finish")
            for _ in steps:
                pass


def sums_scratch(deep, side, urows, drows, d, h, parts):
    ub, db = scatter_bufs(deep, side, urows, h // parts), scatter_bufs(deep, side, drows, d)
    return small_bufs(deep, side) + 2 * (parts * ub + db) + scatter_sems(2 * (parts + 1), deep, side)


def norm_back(gs, normed, n0, inv, i0, s8, gm, gm0, acc, frames, step=4):
    clips, width = s8.shape[1:]
    a_scale, a_shift, a_bias = acc[A_SCALE], acc[A_SHIFT], acc[A_BIAS]
    for j in range(0, frames, step):
        g = gs[j * clips : (j + step) * clips].reshape(step, clips, width)
        norm = normed[pl.ds(n0 + j, step)]
        gn = g * norm
        a_scale = a_scale + fold(gn)
        a_shift = a_shift + fold(g)
        gg = g * s8[SCALE][None]
        mean = jnp.mean(gg, axis=-1, keepdims=True)
        mean_norm = jnp.mean(gn * s8[SCALE][None], axis=-1, keepdims=True)
        inv_std = jnp.concatenate([inv[pl.ds(i0 + j, step)]] * (width // LANES), axis=-1)
        grad = inv_std * (gg - mean - norm * mean_norm)
        a_bias = a_bias + fold(grad)
        gm[pl.ds(gm0 + j, step)] = grad
    acc[A_SCALE], acc[A_SHIFT], acc[A_BIAS] = a_scale, a_shift, a_bias


def conv_back(gm, gm0, s8, masked, m0, gs, g0, t0, out, acc, frames, len8, taps, step=8):
    clips, width = len8.shape
    half = taps // 2
    for l in range(width // LANES):
        cols = slice(l * LANES, (l + 1) * LANES)
        sums = [acc[A_TAPS + k, :, cols] for k in range(taps)]
        for j in range(0, frames, step):
            here = masked[pl.ds(m0 + j, step), :, cols]
            total = None
            for k in range(taps):
                piece = gm[pl.ds(gm0 + j + half - k, step), :, cols]
                term = s8[TAPS + k, :, cols][None] * piece
                total = term if total is None else total + term
                sums[k] = sums[k] + fold(piece * here)
            t = lax.broadcasted_iota(jnp.int32, total.shape, 0) + (t0 + j)
            total = jnp.where(t < len8[:, cols][None], total, 0.0)
            total = gs[pl.ds(g0 + j, step), :, cols] + total
            gs[pl.ds(g0 + j, step), :, cols] = total
            if out is not None:
                out[l, j * clips : (j + step) * clips, :] = total.reshape(step * clips, LANES)
        for k in range(taps):
            acc[A_TAPS + k, :, cols] = sums[k]


def finish_small(acc, upb_acc, groups, s8, small_grad, upb_grad, group_count):
    clips, width = acc.shape[1:]
    member = per_clip(groups, clips, width)
    line = lambda v: jnp.sum(v, axis=0, keepdims=True)
    rows = [line(acc[A_TAPS + k]) for k in range(7)]
    rows.append(line(acc[A_BIAS]))
    for base in (A_SCALE, A_SHIFT):
        for g in range(group_count):
            rows.append(line(jnp.where(member == g, acc[base], 0.0)))
    rows.append(line(acc[A_DOWN]))
    rows.append(line((acc[A_GAIN] + s8[DOWN_BIAS] * acc[A_DOWN]) / s8[GAIN]))
    for r, row in enumerate(rows):
        small_grad[r : r + 1, :] = row
    for r in range(len(rows), small_grad.shape[0]):
        small_grad[r : r + 1, :] = jnp.zeros((1, width), F32)
    upb_grad[...] = line(upb_acc[...])


def backward_kernel(
    lens, groups, og, act, slope, normed, inv, shaped, masked, up, down, small, gs_out, dup, ddown, small_grad, upb_grad,
    gs, gb, gbef, gm, lanes, s8, len8, acc, upb_acc, *, ft, tiles, parts, taps, group_count,
):
    i = pl.program_id(0)
    frame_count, clips, width = gs.shape
    hidden = gbef.shape[1]
    cols = hidden // parts
    rows = ft * clips
    total_rows = frame_count * clips
    base = 2 * ft
    span = parts + tiles + 2
    step = lax.rem(i, span)
    b = 1 - i // span

    @pl.when(step == 0)
    def _():
        prepare(small.at[b], lens, groups, s8, len8, group_count)
        acc[...] = jnp.zeros(acc.shape, F32)

    @pl.when(i == 0)
    def _():
        gm[pl.ds(0, base)] = jnp.zeros((base, clips, width), F32)
        gm[pl.ds(base + frame_count, HALO)] = jnp.zeros((HALO, clips, width), F32)
        spread_grad(og, lanes, gs, 0)

    @pl.when(step == 0)
    def _():
        acc[A_DOWN] = branch_grad(gs, 0, s8, len8, gb)

    @pl.when(step < parts)
    def _():
        c0 = pl.multiple_of(step * cols, cols)
        at = pl.ds(c0, cols)
        lower = down[0, at, :]
        term = mm(act[0], gb[...], TN)
        ddown[b, at, :] = term
        acc[A_GAIN] += fold((term * lower.astype(F32)).reshape(cols // 8, 8, width))
        before_grad(gb, lower, slope.at[0], slice(None), gbef, at, upb_acc, total_rows)
        dup[b, :, at] = mm(shaped[0], gbef[:, at], TN)

    j = step - parts

    @pl.when((j >= 0) & (j < tiles))
    def _():
        r0 = pl.multiple_of(j * rows, rows)
        grad = mm(gbef[pl.ds(r0, rows), :], up[0], NT)
        norm_back(grad, normed.at[0], 0, inv.at[0], 0, s8, gm, base + j * ft, acc, ft)

    @pl.when(j >= 2)
    def _():
        f0 = (j - 2) * ft
        conv_back(gm, base + f0, s8, masked.at[0], 0, gs, f0, f0, gs_out, acc, ft, len8, taps)

    @pl.when(step == span - 1)
    def _():
        finish_small(acc, upb_acc, groups, s8, small_grad.at[b], upb_grad.at[b], group_count)


def spread_grad(og, lanes, gs, g0):
    clips, frame_count, width = og.shape

    def one(n, carry):
        t0 = pl.multiple_of(n * 16, 16)
        spread_clips(og, t0, lanes, 0, 16)
        gs[pl.ds(g0 + t0, 16)] = rows_of(lanes, 0, 16 * clips).reshape(16, clips, width)
        return carry
    lax.fori_loop(0, frame_count // 16, one, 0)


def branch_grad(gs, g0, s8, len8, gb):
    clips, width = len8.shape
    frame_count = gb.shape[0] // clips

    def one(n, a_down):
        t0 = n * 4
        gvb = s8[GAIN][None] * keep_frames(gs[pl.ds(g0 + t0, 4)], t0, len8)
        at = pl.multiple_of(t0 * clips, 4 * clips)
        gb[pl.ds(at, 4 * clips), :] = gvb.reshape(4 * clips, width).astype(BF16)
        return a_down + fold(gvb)
    return lax.fori_loop(0, frame_count // 4, one, jnp.zeros((clips, width), F32), unroll=4)


def before_grad(gb, lower, slope, slope_cols, gbef, at, upb_acc, rows, chunk=1024, sub=16):
    cols = lower.shape[0]
    total = jnp.zeros((8, cols), F32)
    for c in range(0, rows, chunk):
        ga = mm(gb[c : c + chunk, :], lower, NT)
        for r in range(0, chunk, sub):
            gr = ga[r : r + sub] * slope[c + r : c + r + sub, slope_cols].astype(F32)
            total = total + fold(gr.reshape(sub // 8, 8, cols))
            gbef[c + r : c + r + sub, at] = gr.astype(BF16)
    upb_acc[:, at] = total


def backward(lens, groups, og, saved, ups, downs, small, ft, taps, group_count):
    act, slope, normed, inv, shaped, masked = saved
    clips, fc, d = og.shape
    h = ups.shape[2]
    R, r, n = fc * clips, ft * clips, fc // ft
    parts = 6
    cols = h // parts
    span = parts + n + 2
    block = lambda i: 1 - i // span
    part = lambda i: jnp.minimum(lax.rem(i, span), parts - 1)
    tile = lambda i: jnp.clip(lax.rem(i, span) - parts, 0, n - 1)
    late = lambda i: jnp.clip(lax.rem(i, span) - parts - 2, 0, n - 1)
    last = lambda i: jnp.clip(i - span - parts - 2, 0, n - 1)
    sums = [(2, d, h), (2, h, d), (2, ROWS, d), (2, 1, h)]
    return pl.pallas_call(
        functools.partial(backward_kernel, ft=ft, tiles=n, parts=parts, taps=taps, group_count=group_count),
        name="backward",
        grid=(2 * span,),
        in_specs=[
            smem(), smem(), whole(clips, fc, d),
            pl.BlockSpec((1, R, cols), lambda i: (block(i), 0, part(i))),
            pl.BlockSpec((1, R, cols), lambda i: (block(i), 0, part(i))),
            pl.BlockSpec((1, ft, clips, d), lambda i: (block(i), tile(i), 0, 0)),
            pl.BlockSpec((1, ft, clips, LANES), lambda i: (block(i), tile(i), 0, 0)),
            pl.BlockSpec((1, R, d), lambda i: (block(i), 0, 0), pipeline_mode=pl.Buffered(1)),
            pl.BlockSpec((1, ft, clips, d), lambda i: (block(i), late(i), 0, 0)),
            pl.BlockSpec((1, d, h), lambda i: (block(i), 0, 0)),
            pl.BlockSpec((1, h, d), lambda i: (block(i), 0, 0)),
            whole(2, ROWS, d),
        ],
        out_specs=[pl.BlockSpec((d // LANES, r, LANES), lambda i: (0, last(i), 0))] + [whole(*v) for v in sums],
        out_shape=[shape((d // LANES, R, LANES))] + [shape(v) for v in sums],
        scratch_shapes=[
            pltpu.VMEM((fc, clips, d), F32), pltpu.VMEM((R, d), BF16), pltpu.VMEM((R, h), BF16),
            pltpu.VMEM((fc + 2 * ft + HALO, clips, d), F32), pltpu.VMEM((d // LANES, 16 * clips, LANES), F32),
            pltpu.VMEM((14, clips, d), F32), pltpu.VMEM((clips, d), jnp.int32),
            pltpu.VMEM((12, clips, d), F32), pltpu.VMEM((clips, h), F32),
        ],
        compiler_params=pltpu.CompilerParams(vmem_limit_bytes=VMEM_LIMIT),
    )(lens, groups, og, act, slope, normed, inv, shaped, masked, ups, downs, small)


def step_kernel(*refs, deep, side, ft, parts, taps, group_count):
    lens, groups, frames, og = refs[:4]
    shards = refs[4:13]
    out, gs_out, up_part, down_part, small_part, act_far, slope_far = refs[13:20]
    (io, stream, masked0, masked1, normed, inv, shaped, first_rows, act, slope, gb, s8, u8, len8, acc, upb_acc) = refs[20:36]
    small_full, upb_full, small_grad, upb_grad, up_full, down_full, up_term, down_term = refs[36:44]
    io_sem, act_sem, slope_sem, act_back_sem, slope_back_sem, gs_sem = refs[44:50]
    gather_refs, sum_refs = refs[50:68], refs[68:]

    i = pl.program_id(0)
    clips, frame_count, width = io.shape
    hidden = act.shape[1]
    tiles = frame_count // ft
    rows = ft * clips
    cols = hidden // parts
    span = parts + tiles + 1
    body = pl.ds(HALO, frame_count)

    load = lambda n, src: pltpu.make_async_copy(src, io, io_sem.at[n])
    tile_rows = lambda j: pl.ds(pl.multiple_of(j * rows, rows), rows)
    part_at = lambda p: pl.ds(pl.multiple_of(p * cols, cols), cols)

    def spills(j):
        r = tile_rows(j)
        return [
            pltpu.make_async_copy(act.at[r], act_far.at[r], act_sem.at[j]),
            pltpu.make_async_copy(slope.at[r], slope_far.at[r], slope_sem.at[j]),
        ]

    def act_back(p):
        return pltpu.make_async_copy(act_far.at[:, part_at(p)], act.at[:, part_at(p)], act_back_sem.at[p])

    def slope_back(j):
        return pltpu.make_async_copy(slope_far.at[tile_rows(j)], slope.at[tile_rows(j)], slope_back_sem.at[j])

    def up_cols(b):
        return lambda lo, hi: up_full[b, :, :, :, :, :, lo:hi].reshape(width, hi - lo)

    def spread():
        load(0, frames).wait()

        def one(n, carry):
            t0 = pl.multiple_of(n * 16, 16)
            spread_clips(io, t0, stream, 0, 16)
            v = rows_of(stream, 0, 16 * clips)
            at = pl.multiple_of(t0 * clips, 16 * clips)
            first_rows[pl.ds(at, 16 * clips), :] = v.astype(BF16)
            masked0[pl.ds(HALO + t0, 16)] = keep_frames(v.reshape(16, clips, width), t0, len8)
            return carry
        lax.fori_loop(0, frame_count // 16, one, 0)
        load(1, og).start()

    def conv0(lo, hi):
        def one(n, carry):
            conv_norm(masked0, n * ft, ft, s8.at[0], normed.at[0], inv.at[0], shaped, taps, HALO)
            return carry
        lax.fori_loop(lo, hi, one, 0)

    def ready():
        for b in range(2):
            prepare(small_full.at[b], lens, groups, s8.at[b], len8, group_count)
            u8[b] = jnp.broadcast_to(upb_full[b, 0:1, :], u8.shape[1:])

    @pl.when(i == 0)
    def _():
        load(0, frames).start()
        zeros = jnp.zeros((HALO, clips, width), F32)
        for m in (masked0, masked1, normed.at[0], normed.at[1]):
            m[0:HALO] = zeros
            m[HALO + frame_count : HALO + frame_count + HALO] = zeros
        len8[...] = per_clip(lens, clips, width)
        Gather(shards, up_full, down_full, small_full, upb_full, gather_refs, deep, side, group_count, taps).early(
            spread, ready, conv0, tiles)

    Gather(shards, up_full, down_full, small_full, upb_full, gather_refs, deep, side, group_count, taps).late(i, tiles)

    @pl.when(i < tiles)
    def _():
        r0 = pl.multiple_of(i * rows, rows)
        up_gelu(shaped, up_cols(0), u8.at[0], act, r0, slope, r0, rows, hidden)
        run(spills(i))

    @pl.when((i >= tiles) & (i < 2 * tiles))
    def _():
        j = i - tiles
        f0 = j * ft
        r0 = pl.multiple_of(j * rows, rows)
        branch = mm(act[pl.ds(r0, rows), :], down_full[0].reshape(hidden, width), NN)
        for t in range(0, ft, 4):
            b = branch[t * clips : (t + 4) * clips].reshape(4, clips, width) + s8[0, DOWN_BIAS][None]
            total = masked0[pl.ds(HALO + f0 + t, 4)] + s8[0, GAIN][None] * b
            masked1[pl.ds(HALO + f0 + t, 4)] = keep_frames(total, f0 + t, len8)

    @pl.when((i >= 2 * tiles) & (i < 3 * tiles))
    def _():
        j = i - 2 * tiles
        f0 = j * ft
        r0 = pl.multiple_of(j * rows, rows)
        done(spills(j))
        conv_norm(masked1, f0, ft, s8.at[1], normed.at[1], inv.at[1], shaped, taps, HALO)
        up_gelu(shaped, up_cols(1), u8.at[1], act, r0, slope, r0, rows, hidden)
        branch = mm(act[pl.ds(r0, rows), :], down_full[1].reshape(hidden, width), NN)
        last_block(branch, masked1, f0, r0, ft, s8.at[1], len8, first_rows, stream, out)

    k = i - 3 * tiles
    step = lax.rem(jnp.maximum(k, 0), span)
    b = jnp.where(k < span, 1, 0)

    @pl.when(k == 0)
    def _():
        load(1, og).wait()
        spread_grad(io, stream, masked0, HALO)

    @pl.when(k == span)
    def _():
        def one(n, carry):
            t0 = n * 4
            at = pl.multiple_of(t0 * clips, 4 * clips)
            v = normed[0, pl.ds(HALO + t0, 4)] * s8[0, SCALE][None] + s8[0, SHIFT][None]
            shaped[pl.ds(at, 4 * clips), :] = v.reshape(4 * clips, width).astype(BF16)
            first = first_rows[pl.ds(at, 4 * clips), :].astype(F32).reshape(4, clips, width)
            masked1[pl.ds(HALO + t0, 4)] = keep_frames(first, t0, len8)
            return carry
        lax.fori_loop(0, frame_count // 4, one, 0, unroll=4)
        for j in range(tiles):
            slope_back(j).wait()

    @pl.when((k >= 0) & (step == 0))
    def _():
        acc[...] = jnp.zeros(acc.shape, F32)
        acc[A_DOWN] = branch_grad(masked0, HALO, s8.at[b], len8, gb)

    sums = Sums(sum_refs, up_term, down_term, up_part, down_part, small_part, small_grad, upb_grad, deep, side, parts)
    sums.at(k, 0, span)

    @pl.when((k >= span) & (step < parts))
    def _():
        act_back(step).wait()

    @pl.when((k >= 0) & (step < parts))
    def _():
        at = part_at(step)
        drows, urows = down_full.shape[5], up_full.shape[5]
        per = drows // 16
        spots = []
        for m in range(cols // 16):
            row = step * (cols // 16) + m
            e = row // per
            z, chip = e // (2 * side * side), e // 2
            sub = pl.ds(pl.multiple_of((row - e * per) * 16, 16), 16)
            spots.append((b, z, lax.rem(chip // side, side), lax.rem(chip, side), lax.rem(e, 2), sub))
        lower = jnp.concatenate([down_full[spot] for spot in spots], axis=0)
        term = mm(act[:, at], gb[...], TN)
        for m, spot in enumerate(spots):
            down_term[spot] = term[m * 16 : (m + 1) * 16].astype(BF16)
        acc[A_GAIN] += fold((term * lower.astype(F32)).reshape(cols // 8, 8, width))
        before_grad(gb, lower, slope, at, slope, at, upb_acc, frame_count * clips)
        term = mm(shaped[...], slope[:, at], TN).astype(BF16)
        up_term[b, :, :, :, :, :, at] = term.reshape(deep, side, side, 2, urows, cols)

    @pl.when((k >= 0) & (k < parts))
    def _():
        act_back(step).start()

    j = step - parts

    @pl.when((j >= 0) & (j < tiles))
    def _():
        r0 = pl.multiple_of(j * rows, rows)
        grad = mm(slope[pl.ds(r0, rows), :], up_full[b].reshape(width, hidden), NT)
        norm_back(grad, normed.at[b], HALO + j * ft, inv.at[b], j * ft, s8.at[b], normed.at[b], HALO + j * ft, acc, ft)

    @pl.when((k < span) & (j >= 0) & (j < tiles))
    def _():
        slope_back(j).start()

    sums.at(k, 1, span)
    gs_copy = lambda f0, n: pltpu.make_async_copy(masked0.at[pl.ds(HALO + f0, ft)], gs_out.at[pl.ds(f0, ft)], gs_sem.at[n])

    @pl.when(j >= 1)
    def _():
        f0 = (j - 1) * ft
        conv_back(
            normed.at[b], HALO + f0, s8.at[b], masked1, HALO + f0, masked0, HALO + f0, f0, None, acc, ft, len8, taps)

    @pl.when((k >= span) & (j >= 1))
    def _():
        gs_copy((j - 1) * ft, j - 1).start()

    @pl.when((k >= 0) & (step == span - 1))
    def _():
        finish_small(acc, upb_acc, groups, s8.at[b], small_grad.at[b], upb_grad.at[b], group_count)

    sums.after(k, span)

    @pl.when(k == 2 * span - 1)
    def _():
        for n in range(tiles):
            gs_copy(n * ft, n).wait()


def whole_step(deep, side, lens, groups, frames, og, weights, ft, taps, group_count):
    clips, fc, d = frames.shape
    h = weights[4].shape[2]
    urows, drows = weights[4].shape[1], weights[6].shape[1]
    R, r, n = fc * clips, ft * clips, fc // ft
    parts = 3
    span = parts + n + 1
    dims = (2, deep, side, side, 2)
    rows = lambda dtype, *lead: pltpu.VMEM(lead + (d,), dtype)
    halo = fc + 2 * HALO
    return pl.pallas_call(
        functools.partial(step_kernel, deep=deep, side=side, ft=ft, parts=parts, taps=taps, group_count=group_count),
        name="step",
        grid=(3 * n + 2 * span,),
        in_specs=[smem(), smem(), hbm(), hbm()] + [vmem()] * 9,
        out_specs=[
            pl.BlockSpec((clips, ft, d), lambda i: (0, jnp.clip(i - 2 * n, 0, n - 1), 0)),
            hbm(), vmem(), vmem(), vmem(), hbm(), hbm(),
        ],
        out_shape=[
            shape((clips, fc, d), BF16), shape((fc, clips, d)), shape((2, urows, h)), shape((2, drows, d)),
            shape((2 * PACK, LANES)), shape((R, h), BF16), shape((R, h), BF16),
        ],
        scratch_shapes=[
            rows(BF16, clips, fc), pltpu.VMEM((d // LANES, max(r, 16 * clips), LANES), F32),
            rows(F32, halo, clips), rows(F32, halo, clips), rows(F32, 2, halo, clips), pltpu.VMEM((2, fc, clips, LANES), F32),
            rows(BF16, R), rows(BF16, R), pltpu.VMEM((R, h), BF16), pltpu.VMEM((R, h), BF16), rows(BF16, R),
            rows(F32, 2, 14, clips), pltpu.VMEM((2, clips, h), F32), rows(jnp.int32, clips), rows(F32, 12, clips),
            pltpu.VMEM((clips, h), F32),
            rows(F32, 2, ROWS), pltpu.VMEM((2, 1, h), F32), rows(F32, 2, ROWS), pltpu.VMEM((2, 1, h), F32),
            pltpu.VMEM(dims + (urows, h), BF16), rows(BF16, *dims, drows), pltpu.VMEM(dims + (urows, h), BF16), rows(BF16, *dims, drows),
            DMA((2,)), DMA((n,)), DMA((n,)), DMA((parts,)), DMA((n,)), DMA((n,)),
        ] + gather_scratch(deep, side) + sums_scratch(deep, side, urows, drows, d, h, parts),
        compiler_params=pltpu.CompilerParams(vmem_limit_bytes=VMEM_LIMIT, collective_id=0, has_side_effects=True),
    )(lens, groups, frames, og, *weights)


def unpack_kernel(gs, up_in, down_in, small, gin, conv_w, conv_b, scale, shift, up_w, up_b, down_w, down_b, gain):
    clips, frames, _ = gin.shape
    for c in range(clips):
        for t in range(0, frames, 16):
            gin[c, t : t + 16, :] = gs[pl.ds(t * clips + c, 16, stride=clips), :]

    @pl.when((pl.program_id(0) == 0) & (pl.program_id(1) == 0))
    def _():
        unpack_parts(up_in, down_in, small, conv_w, conv_b, scale, shift, up_w, up_b, down_w, down_b, gain)


def unpack_parts(up_in, down_in, small, conv_w, conv_b, scale, shift, up_w, up_b, down_w, down_b, gain):
    f = lax.axis_index("fsdp")
    width = conv_b.shape[1]
    wide = up_b.shape[1]
    span = wide * LANES // width
    turned = pltpu.roll(small[...], lax.rem(LANES - f * width, LANES), 1)
    for b in range(2):
        o = b * PACK
        for k in range(conv_w.shape[0]):
            conv_w[k, b : b + 1, :] = turned[o + k : o + k + 1, :width]
        conv_b[b : b + 1, :] = turned[o + CONV_BIAS : o + CONV_BIAS + 1, :width]
        scale[b] = turned[o + SCALE : o + SCALE + scale.shape[1], :width]
        shift[b] = turned[o + SHIFT : o + SHIFT + shift.shape[1], :width]
        down_b[b : b + 1, :] = turned[o + DOWN_BIAS : o + DOWN_BIAS + 1, :width]
        gain[b : b + 1, :] = turned[o + GAIN : o + GAIN + 1, :width]
        bias = jnp.concatenate([small[o + 14 + q : o + 15 + q, :] for q in range(span // LANES)], axis=1)
        bias = pltpu.roll(jnp.broadcast_to(bias, (8, span)), lax.rem(span - f * wide, span), 1)
        up_b[b : b + 1, :] = bias[0:1, :wide]
    up_w[...] = up_in[...]
    down_w[...] = down_in[...]


def unpack_far(gs, clips):
    split, R, lanes = gs.shape
    fc = R // clips
    ft = 32
    return pl.pallas_call(
        lambda src, dst: collect_clips(src, dst, ft),
        name="unpack",
        grid=(fc // ft,),
        in_specs=[pl.BlockSpec((split, ft * clips, lanes), lambda i: (0, i, 0))],
        out_specs=pl.BlockSpec((clips, ft, split * lanes), lambda i: (0, i, 0)),
        out_shape=shape((clips, fc, split * lanes)),
    )(gs)


def unpack(gs, parts, taps, group_count, width, wide):
    fc, clips, d = gs.shape
    ft = 128
    fixed = lambda *dims: pl.BlockSpec(dims, lambda i, l: (0,) * len(dims), pipeline_mode=pl.Buffered(1))
    up_in, down_in, small = parts
    outs = [(taps, 2, width), (2, width), (2, group_count, width), (2, group_count, width), up_in.shape, (2, wide),
            down_in.shape, (2, width), (2, width)]
    return pl.pallas_call(
        unpack_kernel,
        name="unpack",
        grid=(fc // ft, d // LANES),
        in_specs=[pl.BlockSpec((ft * clips, LANES), lambda i, l: (i, l))] + [fixed(*v.shape) for v in parts],
        out_specs=[pl.BlockSpec((clips, ft, LANES), lambda i, l: (0, i, l))] + [fixed(*v) for v in outs],
        out_shape=[shape((clips, fc, d))] + [shape(v) for v in outs],
    )(gs.reshape(fc * clips, d), up_in, down_in, small)


def body(deep, fan, frames, group, lengths, conv_w, conv_b, scale, shift, up_w, up_b, down_w, down_b, gain, out_grad):
    side = math.isqrt(fan // 2)
    clips = frames.shape[0]
    taps, group_count, hidden = conv_w.shape[1], scale.shape[1], up_w.shape[2]
    width, wide = conv_b.shape[1], up_b.shape[1]
    axes = ("dp", "fsdp")
    near = width * fan == LANES and up_w.shape[1] % 16 == 0 and down_w.shape[1] % 16 == 0
    ft = 32
    if near:
        weights = (conv_w.transpose(1, 0, 2), conv_b, scale, shift, up_w, up_b, down_w, down_b, gain)
    else:
        whole_of = lambda v, axis: lax.all_gather(v, axes, axis=axis, tiled=True)
        ups, downs = whole_of(up_w, 1), whole_of(down_w, 1)
        lines = jnp.concatenate(
            [conv_w, conv_b[:, None], scale, shift, down_b[:, None], gain[:, None], jnp.zeros((2, 2, width), BF16)], axis=1
        )
        small = whole_of(lines, 2).astype(F32)
        upb = whole_of(up_b, 1).astype(F32)[:, None]
        weights = (small, upb, ups, downs)
    if near:
        out, gs, *parts, _, _ = whole_step(deep, side, lengths, group, frames, out_grad, weights, 64, taps, group_count)
        gin, conv_grad, *grads = unpack(gs, parts, taps, group_count, width, wide)
        return (out, gin, conv_grad.transpose(1, 0, 2), *grads)
    out, act, slope, *rest = forward(lengths, group, frames, weights, hidden, ft, taps, group_count)
    saved = (act, slope.reshape(act.shape), *rest)
    gs, *parts = backward(lengths, group, out_grad, saved, ups, downs, small, ft, taps, group_count)
    gin = unpack_far(gs, clips)
    dup, ddown, lines, ug = parts
    owner = lambda v, axis: lax.psum_scatter(v, axes, scatter_dimension=axis, tiled=True)
    lines = owner(lines, 2)
    return (
        out, gin, lines[:, :taps], lines[:, CONV_BIAS], lines[:, SCALE : SCALE + group_count],
        lines[:, SHIFT : SHIFT + group_count], owner(dup, 1), owner(ug[:, 0], 1), owner(ddown, 1),
        lines[:, DOWN_BIAS], lines[:, GAIN],
    )


def solution(mesh):
    split = ("dp", "fsdp")
    clip = P(split, None, None)
    first, middle, last = P(None, split), P(None, split, None), P(None, None, split)
    in_specs = (clip, P(split), P(split), last, first, last, last, middle, first, middle, first, first, clip)
    out_specs = (clip, clip, last, first, last, last, middle, first, middle, first, first)
    run = functools.partial(body, mesh.shape["dp"], mesh.shape["fsdp"])
    return jax.shard_map(run, mesh=mesh, in_specs=in_specs, out_specs=out_specs, check_vma=False)
```

```python
import functools
import math
import jax
import jax.numpy as jnp
from jax import lax
from jax.experimental import pallas as pl
from jax.experimental.pallas import tpu as pltpu
from jax.sharding import PartitionSpec as P

F32 = jnp.float32
BF16 = jnp.bfloat16
EPSILON = 1e-06
TAPS, CONV_BIAS, SCALE, SHIFT, DOWN_BIAS, GAIN, ROWS = 0, 7, 8, 10, 12, 13, 16
A_TAPS, A_BIAS, A_SCALE, A_SHIFT, A_DOWN, A_GAIN = 0, 7, 8, 9, 10, 11
HALO = 3
LANES = 128
VMEM_LIMIT = 64 * 1024 * 1024 - 128 * 1024
NN = (((1,), (0,)), ((), ()))
NT = (((1,), (1,)), ((), ()))
TN = (((0,), (0,)), ((), ()))
DMA = pltpu.SemaphoreType.DMA


def mm(a, b, dims):
    return lax.dot_general(a, b, dims, preferred_element_type=F32)


def gelu_pair(before):
    u = before * math.sqrt(0.5)
    phi = 0.5 + 0.5 * lax.erf(u)
    bell = jnp.exp2(u * u * (-math.log2(math.e))) * (1.0 / math.sqrt(math.pi))
    return before * phi, phi + u * bell


def per_clip(values, clips, width):
    rows = lax.broadcasted_iota(jnp.int32, (clips, width), 0)
    out = jnp.zeros((clips, width), jnp.int32)
    for c in range(clips):
        out = jnp.where(rows == c, values[c], out)
    return out


def prepare(small, lens, groups, s8, len8, group_count):
    clips, width = len8.shape
    for r in range(14):
        s8[r] = jnp.broadcast_to(small[r : r + 1, :], (clips, width))
    member = per_clip(groups, clips, width)
    len8[...] = per_clip(lens, clips, width)
    gain = jnp.zeros((clips, width), F32)
    shift = jnp.zeros((clips, width), F32)
    for g in range(group_count):
        chosen = jnp.where(member == g, 1.0, 0.0)
        gain = gain + chosen * s8[SCALE + g]
        shift = shift + chosen * s8[SHIFT + g]
    s8[SCALE] = gain
    s8[SHIFT] = shift


def keep_frames(v, t0, len8, other=0.0):
    t = lax.broadcasted_iota(jnp.int32, v.shape, 0) + t0
    return jnp.where(t < len8[...][None], v, other)


def swap_frames(block, t0, frames):
    return jnp.swapaxes(block[:, pl.ds(t0, frames), :].astype(F32), 0, 1)


def fold(v):
    return jnp.sum(v, axis=0)


def smem():
    return pl.BlockSpec(memory_space=pltpu.SMEM)


def vmem():
    return pl.BlockSpec(memory_space=pltpu.VMEM)


def hbm():
    return pl.BlockSpec(memory_space=pl.ANY)


def whole(*dims):
    return pl.BlockSpec(dims, lambda i: (0,) * len(dims), pipeline_mode=pl.Buffered(1))


def shape(dims, dtype=F32):
    return jax.ShapeDtypeStruct(dims, dtype)


MESH = pl.DeviceIdType.MESH
PACK = 20


class Place:
    def __init__(self, deep, side):
        self.deep, self.side = deep, side
        self.z = lax.axis_index("dp")
        f = lax.axis_index("fsdp")
        self.f = f
        self.core = lax.rem(f, 2)
        chip = f // 2
        self.low = lax.rem(chip, side)
        self.high = chip // side
        self.first = jnp.where(self.core == 0, self.high, self.low)
        self.second = jnp.where(self.core == 0, self.low, self.high)

    def chip_of(self, first, second):
        high = jnp.where(self.core == 0, first, second)
        low = jnp.where(self.core == 0, second, first)
        return high, low

    def fsdp_of(self, first, second):
        high, low = self.chip_of(first, second)
        return (high * self.side + low) * 2 + self.core

    def z_peer(self, p):
        return {"dp": lax.rem(self.z + p, self.deep)}

    def first_peer(self, p):
        return {"fsdp": self.fsdp_of(lax.rem(self.first + p, self.side), self.second)}

    def second_peer(self, p):
        return {"fsdp": self.fsdp_of(self.first, lax.rem(self.second + p, self.side))}

    def core_peer(self):
        return {"fsdp": self.f + 1 - 2 * self.core}

    def greet(self):
        barrier = pltpu.get_barrier_semaphore()
        peers = [self.z_peer(p) for p in range(1, self.deep)]
        peers += [self.first_peer(p) for p in range(1, self.side)]
        peers += [self.second_peer(p) for p in range(1, self.side)]
        peers.append(self.core_peer())
        for peer in peers:
            pl.semaphore_signal(barrier, inc=1, device_id=peer, device_id_type=MESH)
        pl.semaphore_wait(barrier, len(peers))


def send(src, dst, send_sem, recv_sem, peer):
    return pltpu.make_async_remote_copy(
        src_ref=src, dst_ref=dst, send_sem=send_sem, recv_sem=recv_sem, device_id=peer, device_id_type=MESH
    )


def run(copies):
    for c in copies:
        c.start()


def done(copies):
    for c in copies:
        c.wait()


def weight_route(place, own, full, sems):
    zs, zr, fs, fr, ss, sr, cs, cr = sems
    deep, side, core = place.deep, place.side, place.core

    def held(p, q):
        high, low = place.chip_of(lax.rem(place.first + p, side), lax.rem(place.second + q, side))
        return full.at[:, high, low, core]

    mine = full.at[place.z, place.high, place.low, core]
    along_z = [send(own, mine, zs.at[p - 1], zr.at[p - 1], place.z_peer(p)) for p in range(1, deep)]
    along_first = [
        send(held(0, 0), held(0, 0), fs.at[p - 1], fr.at[p - 1], place.first_peer(p)) for p in range(1, side)
    ]
    along_second = []
    for j in range(side):
        high, low = place.chip_of(j, place.second)
        line = full.at[:, high, low, core]
        for p in range(1, side):
            n = j * (side - 1) + p - 1
            along_second.append(send(line, line, ss.at[n], sr.at[n], place.second_peer(p)))
    across = lambda p, q: send(held(p, q), held(p, q), cs.at[p * side + q], cr.at[p * side + q], place.core_peer())
    over = [[across(0, 0)], [across(p, 0) for p in range(1, side)],
            [across(p, q) for q in range(1, side) for p in range(side)]]
    return [along_z, along_first, along_second], over


def gather_sems(count, deep, side):
    one = [deep - 1, deep - 1, side - 1, side - 1, side * (side - 1), side * (side - 1), side * side, side * side]
    return [DMA((count, n)) for n in one]


def place_small(place, shards, pack, group_count, taps):
    conv_w, conv_b, scale, shift, up_b, down_b, gain = shards
    width = conv_b.shape[1]
    lane = lax.broadcasted_iota(jnp.int32, (width, LANES), 1)
    row = lax.broadcasted_iota(jnp.int32, (width, LANES), 0)
    spot = jnp.where(lane == row + place.f * width, 1.0, 0.0).astype(BF16)
    wide = up_b.shape[1]
    span = wide * LANES // width
    lane = lax.broadcasted_iota(jnp.int32, (wide, span), 1)
    row = lax.broadcasted_iota(jnp.int32, (wide, span), 0)
    spread = jnp.where(lane == row + place.f * wide, 1.0, 0.0).astype(BF16)
    pack[...] = jnp.zeros(pack.shape, F32)
    for b in range(2):
        o = b * PACK
        for k in range(taps):
            pack[o + k : o + k + 1, :] = mm(conv_w[k, b : b + 1, :], spot, NN)
        pack[o + SCALE : o + SCALE + group_count, :] = mm(scale[b], spot, NN)
        pack[o + SHIFT : o + SHIFT + group_count, :] = mm(shift[b], spot, NN)
        for src, at in ((conv_b, CONV_BIAS), (down_b, DOWN_BIAS), (gain, GAIN)):
            pack[o + at : o + at + 1, :] = mm(src[b : b + 1, :], spot, NN)
        bias = mm(up_b[b : b + 1, :], spread, NN)
        for q in range(span // LANES):
            pack[o + 14 + q : o + 15 + q, :] = bias[:, q * LANES : (q + 1) * LANES]


class Gather:
    def __init__(self, shards, up_full, down_full, small_full, upb_full, refs, deep, side, group_count, taps):
        (self.pack, self.zbuf, self.first_in, self.first_sum, self.second_in, self.second_sum, self.core_in,
         self.local_sems, self.small_s, self.small_r) = refs[:10]
        sems = refs[10:]
        self.place = place = Place(deep, side)
        self.small_full, self.upb_full, self.shards = small_full, upb_full, shards
        self.group_count, self.taps = group_count, taps
        up_w, down_w = shards[4], shards[6]
        self.full = (up_full, down_full)
        self.routes, self.local = [], []
        for n, (own, full) in enumerate(
            ((up_w.at[0], up_full.at[0]), (down_w.at[0], down_full.at[0]), (up_w.at[1], up_full.at[1]), (down_w.at[1], down_full.at[1]))
        ):
            self.routes.append(weight_route(place, own, full, [s.at[n] for s in sems]))
            spot = full.at[place.z, place.high, place.low, place.core]
            self.local.append(pltpu.make_async_copy(own, spot, self.local_sems.at[n]))
        stages = [
            [(self.zbuf.at[place.z], self.zbuf.at[place.z], place.z_peer(p)) for p in range(1, deep)],
            [(self.zbuf, self.first_in.at[p - 1], place.first_peer(p)) for p in range(1, side)],
            [(self.first_sum, self.second_in.at[p - 1], place.second_peer(p)) for p in range(1, side)],
            [(self.second_sum, self.core_in, place.core_peer())],
        ]
        n = 0
        self.small = []
        for stage in stages:
            copies = []
            for src, dst, peer in stage:
                copies.append(send(src, dst, self.small_s.at[n], self.small_r.at[n], peer))
                n += 1
            self.small.append(copies)

    def begin(self, n):
        run(self.routes[n][0][0])
        self.local[n].start()

    def after_z(self, n):
        along, over = self.routes[n]
        self.local[n].wait()
        done(along[0])
        run(along[1])
        run(over[0])

    def after_first(self, n):
        along, over = self.routes[n]
        done(along[1])
        run(along[2])
        run(over[1])

    def after_second(self, n):
        along, over = self.routes[n]
        done(along[2])
        run(over[2])

    def end(self, n):
        for copies in self.routes[n][1]:
            done(copies)

    def early(self, spread, ready, conv, tiles):
        place = self.place
        place.greet()
        self.begin(0)
        conv_w, conv_b, scale, shift, _, up_b, _, down_b, gain = self.shards
        place_small(place, (conv_w, conv_b, scale, shift, up_b, down_b, gain), self.pack, self.group_count, self.taps)
        self.zbuf[place.z] = self.pack[...]
        run(self.small[0])
        self.begin(1)
        spread()
        done(self.small[0])
        run(self.small[1])
        self.after_z(0)
        done(self.small[1])
        total = self.zbuf[...]
        for p in range(1, place.side):
            total = total + self.first_in[p - 1]
        self.first_sum[...] = total
        run(self.small[2])
        done(self.small[2])
        total = self.first_sum[...]
        for p in range(1, place.side):
            total = total + self.second_in[p - 1]
        self.second_sum[...] = total
        run(self.small[3])
        self.after_first(0)
        self.after_z(1)
        self.begin(2)
        self.begin(3)
        done(self.small[3])
        self.finish_small()
        ready()
        conv(0, tiles // 2)
        self.after_second(0)
        self.after_first(1)
        conv(tiles // 2, 3 * tiles // 4)
        self.after_z(2)
        conv(3 * tiles // 4, tiles)
        self.end(0)

    def finish_small(self):
        total = self.second_sum[...] + self.core_in[...]
        deep = self.place.deep
        per = self.upb_full.shape[2] // deep
        self.small_full[...] = jnp.zeros(self.small_full.shape, F32)
        for b in range(2):
            o = b * PACK
            for z in range(deep):
                self.small_full[b, 0:14, z * LANES : (z + 1) * LANES] = total[z, o : o + 14, :]
                for q in range(per // LANES):
                    at = z * per + q * LANES
                    self.upb_full[b, :, at : at + LANES] = total[z, o + 14 + q : o + 15 + q, :]

    def late(self, i, tiles):
        @pl.when(i == tiles // 4)
        def _():
            self.after_z(3)
            self.after_second(1)

        @pl.when(i == tiles // 2)
        def _():
            self.after_first(2)

        @pl.when(i == 3 * tiles // 4)
        def _():
            self.after_first(3)

        @pl.when(i == tiles)
        def _():
            self.end(1)

        @pl.when(i == 2 * tiles - 1)
        def _():
            self.after_second(2)

        @pl.when(i == 2 * tiles)
        def _():
            self.after_second(3)
            for n in (2, 3):
                self.end(n)


def gather_scratch(deep, side):
    buf = pltpu.VMEM((deep, 2 * PACK, LANES), F32)
    many = pltpu.VMEM((side - 1, deep, 2 * PACK, LANES), F32)
    n = deep - 1 + 2 * (side - 1) + 1
    return [pltpu.VMEM((2 * PACK, LANES), F32), buf, many, buf, many, buf, buf, DMA((4,)), DMA((n,)), DMA((n,))] + gather_sems(
        4, deep, side
    )


def conv_norm(masked, f0, frames, s8, normed, inv, shaped, taps, n0=0, step=4):
    clips, width = s8.shape[1:]
    for j in range(0, frames, step):
        mixed = s8[CONV_BIAS][None]
        for k in range(taps):
            mixed = mixed + s8[TAPS + k][None] * masked[pl.ds(f0 + j + k, step)]
        center = mixed - jnp.mean(mixed, axis=-1, keepdims=True)
        inv_std = lax.rsqrt(jnp.mean(center * center, axis=-1, keepdims=True) + EPSILON)
        norm = center * inv_std
        normed[pl.ds(n0 + f0 + j, step)] = norm
        inv[pl.ds(f0 + j, step)] = jnp.broadcast_to(inv_std, (step, clips, LANES))
        rows = norm * s8[SCALE][None] + s8[SHIFT][None]
        at = pl.multiple_of((f0 + j) * clips, step * clips)
        shaped[pl.ds(at, step * clips), :] = rows.reshape(step * clips, width).astype(BF16)


def up_gelu(shaped, up_cols, u8, act, r0, slope, s0, rows, hidden, cols=256, sub=16):
    left = shaped[pl.ds(r0, rows), :]
    for n in range(0, hidden, cols):
        before = mm(left, up_cols(n, n + cols), NN)
        for r in range(0, rows, sub):
            piece = before[r : r + sub].reshape(sub // 8, 8, cols) + u8[:, n : n + cols][None]
            a, s = gelu_pair(piece.reshape(sub, cols))
            act[pl.ds(r0 + r, sub), n : n + cols] = a.astype(BF16)
            slope[pl.ds(s0 + r, sub), n : n + cols] = s.astype(slope.dtype)


def forward_kernel(
    lens, groups, frames, small_full, upb_full, up_full, down_full, out, act_out, slope, normed_out, inv_out, shaped_out, masked_out,
    masked0, masked1, normed, inv, shaped, first_rows, act, s8, u8, len8, save_sem, act_sem, row_sem, *, ft, taps, group_count,
):
    i = pl.program_id(0)
    clips, frame_count, width = frames.shape
    hidden = act.shape[1]
    tiles = frame_count // ft
    rows = ft * clips

    def up_cols(b):
        return lambda lo, hi: up_full[b, :, lo:hi]

    body = pl.ds(HALO, frame_count)
    save = lambda n, src, dst: pltpu.make_async_copy(src, dst, save_sem.at[n])
    saves0 = [
        save(0, masked0.at[body], masked_out.at[0]), save(1, normed, normed_out.at[0]),
        save(2, inv, inv_out.at[0]), save(3, shaped, shaped_out.at[0]),
    ]
    save_masked1 = save(4, masked1.at[body], masked_out.at[1])
    tail = lambda b, j: pltpu.make_async_copy(
        act.at[pl.ds(pl.multiple_of(j * rows, rows), rows)],
        act_out.at[b, pl.ds(pl.multiple_of(j * rows, rows), rows)], act_sem.at[j])

    def row_saves(j):
        f = pl.ds(j * ft, ft)
        r = pl.ds(pl.multiple_of(j * rows, rows), rows)
        return [
            pltpu.make_async_copy(normed.at[f], normed_out.at[1, f], row_sem.at[0, j]),
            pltpu.make_async_copy(inv.at[f], inv_out.at[1, f], row_sem.at[1, j]),
            pltpu.make_async_copy(shaped.at[r], shaped_out.at[1, r], row_sem.at[2, j]),
        ]

    @pl.when(i == 0)
    def _():
        zeros = jnp.zeros((HALO, clips, width), F32)
        for m in (masked0, masked1):
            m[0:HALO] = zeros
            m[HALO + frame_count :] = zeros
        len8[...] = per_clip(lens, clips, width)

        def spread(n, carry):
            t0 = pl.multiple_of(n * 16, 16)
            v = swap_frames(frames, t0, 16)
            at = pl.multiple_of(t0 * clips, 16 * clips)
            first_rows[pl.ds(at, 16 * clips), :] = v.reshape(16 * clips, width).astype(BF16)
            masked0[pl.ds(HALO + t0, 16)] = keep_frames(v, t0, len8)
            return carry
        lax.fori_loop(0, frame_count // 16, spread, 0)
        for b in range(2):
            prepare(small_full.at[b], lens, groups, s8.at[b], len8, group_count)
            u8[b] = jnp.broadcast_to(upb_full[b, 0:1, :], u8.shape[1:])

        def conv0(n, carry):
            conv_norm(masked0, n * ft, ft, s8.at[0], normed, inv, shaped, taps)
            return carry
        lax.fori_loop(0, tiles, conv0, 0)
        for c in saves0:
            c.start()

    @pl.when(i < tiles)
    def _():
        r0 = pl.multiple_of(i * rows, rows)
        up_gelu(shaped, up_cols(0), u8.at[0], act, r0, slope, 0, rows, hidden)
        tail(0, i).start()

    @pl.when((i >= tiles) & (i < 2 * tiles))
    def _():
        j = i - tiles
        f0 = j * ft
        r0 = pl.multiple_of(j * rows, rows)
        branch = mm(act[pl.ds(r0, rows), :], down_full[0], NN)
        for t in range(0, ft, 4):
            b = branch[t * clips : (t + 4) * clips].reshape(4, clips, width) + s8[0, DOWN_BIAS][None]
            total = masked0[pl.ds(HALO + f0 + t, 4)] + s8[0, GAIN][None] * b
            masked1[pl.ds(HALO + f0 + t, 4)] = keep_frames(total, f0 + t, len8)
        tail(0, j).wait()

    @pl.when(i == 2 * tiles)
    def _():
        for c in saves0:
            c.wait()
        save_masked1.start()

    @pl.when(i >= 2 * tiles)
    def _():
        j = i - 2 * tiles
        f0 = j * ft
        r0 = pl.multiple_of(j * rows, rows)
        conv_norm(masked1, f0, ft, s8.at[1], normed, inv, shaped, taps)
        for c in row_saves(j):
            c.start()
        up_gelu(shaped, up_cols(1), u8.at[1], act, r0, slope, 0, rows, hidden)
        tail(1, j).start()
        branch = mm(act[pl.ds(r0, rows), :], down_full[1], NN)
        last_block(branch, masked1, f0, r0, ft, s8.at[1], len8, first_rows, out)

    @pl.when(i == 3 * tiles - 1)
    def _():
        save_masked1.wait()
        for j in range(tiles):
            tail(1, j).wait()
            for c in row_saves(j):
                c.wait()


def last_block(branch, masked1, f0, r0, ft, s8, len8, first_rows, out, step=16):
    clips, width = len8.shape
    for t in range(0, ft, step):
        b = branch[t * clips : (t + step) * clips].reshape(step, clips, width) + s8[DOWN_BIAS][None]
        total = masked1[pl.ds(HALO + f0 + t, step)] + s8[GAIN][None] * b
        at = pl.multiple_of(r0 + t * clips, step * clips)
        first = first_rows[pl.ds(at, step * clips), :].astype(F32).reshape(step, clips, width)
        out[:, t : t + step, :] = jnp.swapaxes(keep_frames(total, f0 + t, len8, first), 0, 1).astype(BF16)


def forward(lens, groups, frames, weights, hidden, ft, taps, group_count):
    clips, fc, d = frames.shape
    h = hidden
    n, r = fc // ft, ft * clips
    R = fc * clips
    slope_at = lambda i: jnp.where(i < n, i, jnp.where(i < 2 * n, n - 1, i - n))
    return pl.pallas_call(
        functools.partial(forward_kernel, ft=ft, taps=taps, group_count=group_count),
        name="forward",
        grid=(3 * n,),
        in_specs=[smem(), smem(), whole(clips, fc, d)] + [vmem()] * 4,
        out_specs=[
            pl.BlockSpec((clips, ft, d), lambda i: (0, jnp.maximum(i - 2 * n, 0), 0)), hbm(),
            pl.BlockSpec((r, h), lambda i: (slope_at(i), 0)), hbm(), hbm(), hbm(), hbm(),
        ],
        out_shape=[
            shape((clips, fc, d), BF16), shape((2, R, h), BF16), shape((2 * R, h), BF16), shape((2, fc, clips, d)),
            shape((2, fc, clips, LANES)), shape((2, R, d), BF16), shape((2, fc, clips, d)),
        ],
        scratch_shapes=[
            pltpu.VMEM((fc + 2 * HALO, clips, d), F32), pltpu.VMEM((fc + 2 * HALO, clips, d), F32),
            pltpu.VMEM((fc, clips, d), F32), pltpu.VMEM((fc, clips, LANES), F32), pltpu.VMEM((R, d), BF16),
            pltpu.VMEM((R, d), BF16), pltpu.VMEM((R, h), BF16),
            pltpu.VMEM((2, 14, clips, d), F32), pltpu.VMEM((2, clips, h), F32), pltpu.VMEM((clips, d), jnp.int32),
            DMA((5,)), DMA((n,)), DMA((3, n)),
        ],
        compiler_params=pltpu.CompilerParams(vmem_limit_bytes=VMEM_LIMIT),
    )(lens, groups, frames, *weights)


class Scatter:
    def __init__(self, place, term, bufs, sems):
        self.place, self.term = place, term
        self.core_in, self.second_in, self.first_in, self.z_in = bufs
        self.sems = sems

    def line(self, first, second):
        high, low = self.place.chip_of(first, second)
        return self.term.at[:, high, low, self.place.core]

    def spot(self, z, first, second):
        high, low = self.place.chip_of(first, second)
        return (z, high, low)

    def core_copies(self):
        at = self.place
        return [send(self.term.at[:, :, :, 1 - at.core], self.core_in, self.sems[0].at[0], self.sems[1].at[0], at.core_peer())]

    def second_copies(self, p):
        at = self.place
        to = lax.rem(at.second + p, at.side)
        n = (p - 1) * at.side
        return [
            send(self.line(f, to), self.second_in.at[p - 1, f], self.sems[2].at[n + f], self.sems[3].at[n + f], at.second_peer(p))
            for f in range(at.side)
        ]

    def first_copy(self, p):
        at = self.place
        to = lax.rem(at.first + p, at.side)
        return send(self.line(to, at.second), self.first_in.at[p - 1], self.sems[4].at[p - 1], self.sems[5].at[p - 1], at.first_peer(p))

    def z_copy(self, p):
        at = self.place
        to = lax.rem(at.z + p, at.deep)
        high, low = at.chip_of(at.first, at.second)
        return send(self.term.at[to, high, low, at.core], self.z_in.at[p - 1], self.sems[6].at[p - 1], self.sems[7].at[p - 1], at.z_peer(p))

    def part1(self, z, first, second):
        z, high, low = self.spot(z, first, second)
        return self.term[z, high, low, self.place.core].astype(F32) + self.core_in[z, high, low].astype(F32)

    def part2(self, z, first):
        total = self.part1(z, first, self.place.second)
        for p in range(1, self.place.side):
            total = total + self.second_in[p - 1, first, z].astype(F32)
        return total

    def part3(self, z):
        total = self.part2(z, self.place.first)
        for p in range(1, self.place.side):
            total = total + self.first_in[p - 1, z].astype(F32)
        return total

    def put(self, z, first, second, total):
        z, high, low = self.spot(z, first, second)
        self.term[z, high, low, self.place.core] = total.astype(BF16)

    def core_start(self):
        run(self.core_copies())

    def second_start(self):
        at = self.place
        done(self.core_copies())
        for p in range(1, at.side):
            to = lax.rem(at.second + p, at.side)
            copies = self.second_copies(p)
            for first in range(at.side):
                def one(z, carry):
                    self.put(z, first, to, self.part1(z, first, to))
                    return carry
                lax.fori_loop(0, at.deep, one, 0)
                copies[first].start()

    def first_start(self):
        at = self.place
        for p in range(1, at.side):
            done(self.second_copies(p))
        for p in range(1, at.side):
            to = lax.rem(at.first + p, at.side)
            def one(z, carry):
                self.put(z, to, at.second, self.part2(z, to))
                return carry
            lax.fori_loop(0, at.deep, one, 0)
            self.first_copy(p).start()

    def z_start(self):
        at = self.place
        done([self.first_copy(p) for p in range(1, at.side)])
        for p in range(1, at.deep):
            to = lax.rem(at.z + p, at.deep)
            self.put(to, at.first, at.second, self.part3(to))
            self.z_copy(p).start()

    def finish(self, out):
        at = self.place
        done([self.z_copy(p) for p in range(1, at.deep)])
        total = self.part3(at.z)
        for p in range(1, at.deep):
            total = total + self.z_in[p - 1].astype(F32)
        out[...] = total


def scatter_bufs(deep, side, rows, cols):
    v = lambda *lead: pltpu.VMEM(lead + (rows, cols), BF16)
    return [v(deep, side, side), v(side - 1, side, deep), v(side - 1, deep), v(deep - 1)]


def scatter_sems(count, deep, side):
    return [DMA((count, n)) for n in (1, 1, side * (side - 1), side * (side - 1), side - 1, side - 1, deep - 1, deep - 1)]


def pack_small(small, upb, b, terms, deep):
    per = upb.shape[1] // deep
    o = b * PACK
    for z in range(deep):
        terms[z, o : o + 14, :] = small[0:14, z * LANES : (z + 1) * LANES]
        for q in range(per // LANES):
            at = z * per + q * LANES
            terms[z, o + 14 + q : o + 15 + q, :] = upb[:, at : at + LANES]


def sum_small(place, terms, z_in, bufs, out, s, r):
    n = 0
    copies = []
    for p in range(1, place.deep):
        to = lax.rem(place.z + p, place.deep)
        copies.append(send(terms.at[to], z_in.at[p - 1], s.at[n], r.at[n], place.z_peer(p)))
        n += 1
    run(copies)
    yield
    done(copies)
    total = terms[place.z]
    for p in range(1, place.deep):
        total = total + z_in[p - 1]
    stages = [[place.core_peer()], [place.second_peer(p) for p in range(1, place.side)],
              [place.first_peer(p) for p in range(1, place.side)]]
    for (here, into), peers in zip(bufs, stages):
        here[...] = total
        copies = []
        for p, peer in enumerate(peers):
            copies.append(send(here, into.at[p], s.at[n], r.at[n], peer))
            n += 1
        run(copies)
        yield
        done(copies)
        for p in range(len(peers)):
            total = total + into[p]
    out[...] = total


def small_bufs(deep, side):
    many = lambda *n: pltpu.VMEM(n + (2 * PACK, LANES), F32)
    n = deep - 1 + 2 * (side - 1) + 1
    return [many(deep), many(deep - 1), many(), many(1), many(), many(side - 1), many(), many(side - 1), DMA((n,)), DMA((n,))]


class Sums:
    def __init__(self, refs, up_term, down_term, up_part, down_part, small_part, small_grad, upb_grad, deep, side, parts):
        self.place = Place(deep, side)
        self.terms, self.z_in = refs[:2]
        self.bufs = [refs[2:4], refs[4:6], refs[6:8]]
        self.small_s, self.small_r = refs[8:10]
        refs = refs[10:]
        sems = refs[-8:]
        self.small_part, self.small_grad, self.upb_grad = small_part, small_grad, upb_grad
        self.parts = parts
        cols = up_part.shape[2] // parts
        self.jobs = []
        for b in (1, 0):
            views = []
            for p in range(parts):
                c = pl.ds(p * cols, cols)
                views.append((up_term.at[b, :, :, :, :, :, c], up_part.at[b, :, c]))
            views.append((down_term.at[b], down_part.at[b]))
            for term, out in views:
                n = len(self.jobs)
                self.jobs.append((Scatter(self.place, term, refs[4 * n : 4 * n + 4], [s.at[n] for s in sems]), out))

    def do(self, n, what):
        job, out = self.jobs[n]
        if what == "finish":
            job.finish(out)
        else:
            getattr(job, what)()

    def at(self, i, half, span):
        parts, per = self.parts, self.parts + 1
        whats = ("core_start", "second_start", "first_start", "z_start", "finish")
        when = []
        top = 2 * parts
        for p in range(parts - 1):
            t = 2 * (p + 1)
            when.append((t, t + 1, t + 3 if p < parts - 2 else top + 3, top + 3 if p < parts - 2 else top + 6, top + 9))
        when.append((top, top + 3, top + 6, top + 9, top + 12))
        when.append((top, top + 3, top + 10, top + 13, top + 16))
        plan = []
        for order, what in enumerate(whats):
            for n in range(2 * per):
                slot = when[n % per][order] + 2 * span * (n // per)
                if slot < 4 * span and slot % 2 == half:
                    plan.append((slot // 2, n, what))
        for now in sorted({p[0] for p in plan}):
            @pl.when(i == now)
            def _():
                for step, n, what in plan:
                    if step == now:
                        self.do(n, what)

    def after(self, i, span):
        @pl.when(i == 2 * span - 1)
        def _():
            self.terms[...] = jnp.zeros(self.terms.shape, F32)
            for b in range(2):
                pack_small(self.small_grad.at[b], self.upb_grad.at[b], b, self.terms, self.place.deep)
            steps = sum_small(self.place, self.terms, self.z_in, self.bufs, self.small_part, self.small_s, self.small_r)
            last = 2 * (self.parts + 1) - 1
            next(steps)
            self.do(last, "first_start")
            next(steps)
            self.do(last - 1, "finish")
            next(steps)
            self.do(last, "z_start")
            next(steps)
            self.do(last, "finish")
            for _ in steps:
                pass


def sums_scratch(deep, side, urows, drows, d, h, parts):
    ub, db = scatter_bufs(deep, side, urows, h // parts), scatter_bufs(deep, side, drows, d)
    return small_bufs(deep, side) + 2 * (parts * ub + db) + scatter_sems(2 * (parts + 1), deep, side)


def norm_back(gs, normed, n0, inv, i0, s8, gm, gm0, acc, frames, step=4):
    clips, width = s8.shape[1:]
    a_scale, a_shift, a_bias = acc[A_SCALE], acc[A_SHIFT], acc[A_BIAS]
    for j in range(0, frames, step):
        g = gs[j * clips : (j + step) * clips].reshape(step, clips, width)
        norm = normed[pl.ds(n0 + j, step)]
        gn = g * norm
        a_scale = a_scale + fold(gn)
        a_shift = a_shift + fold(g)
        gg = g * s8[SCALE][None]
        mean = jnp.mean(gg, axis=-1, keepdims=True)
        mean_norm = jnp.mean(gn * s8[SCALE][None], axis=-1, keepdims=True)
        inv_std = jnp.concatenate([inv[pl.ds(i0 + j, step)]] * (width // LANES), axis=-1)
        grad = inv_std * (gg - mean - norm * mean_norm)
        a_bias = a_bias + fold(grad)
        gm[pl.ds(gm0 + j, step)] = grad
    acc[A_SCALE], acc[A_SHIFT], acc[A_BIAS] = a_scale, a_shift, a_bias


def conv_back(gm, gm0, s8, masked, m0, gs, g0, t0, out, acc, frames, len8, taps, step=8):
    clips, width = len8.shape
    half = taps // 2
    for l in range(width // LANES):
        cols = slice(l * LANES, (l + 1) * LANES)
        sums = [acc[A_TAPS + k, :, cols] for k in range(taps)]
        for j in range(0, frames, step):
            here = masked[pl.ds(m0 + j, step), :, cols]
            total = None
            for k in range(taps):
                piece = gm[pl.ds(gm0 + j + half - k, step), :, cols]
                term = s8[TAPS + k, :, cols][None] * piece
                total = term if total is None else total + term
                sums[k] = sums[k] + fold(piece * here)
            t = lax.broadcasted_iota(jnp.int32, total.shape, 0) + (t0 + j)
            total = jnp.where(t < len8[:, cols][None], total, 0.0)
            total = gs[pl.ds(g0 + j, step), :, cols] + total
            gs[pl.ds(g0 + j, step), :, cols] = total
            if out is not None:
                out[j : j + step, :, cols] = total
        for k in range(taps):
            acc[A_TAPS + k, :, cols] = sums[k]


def finish_small(acc, upb_acc, groups, s8, small_grad, upb_grad, group_count):
    clips, width = acc.shape[1:]
    member = per_clip(groups, clips, width)
    line = lambda v: jnp.sum(v, axis=0, keepdims=True)
    rows = [line(acc[A_TAPS + k]) for k in range(7)]
    rows.append(line(acc[A_BIAS]))
    for base in (A_SCALE, A_SHIFT):
        for g in range(group_count):
            rows.append(line(jnp.where(member == g, acc[base], 0.0)))
    rows.append(line(acc[A_DOWN]))
    rows.append(line((acc[A_GAIN] + s8[DOWN_BIAS] * acc[A_DOWN]) / s8[GAIN]))
    for r, row in enumerate(rows):
        small_grad[r : r + 1, :] = row
    for r in range(len(rows), small_grad.shape[0]):
        small_grad[r : r + 1, :] = jnp.zeros((1, width), F32)
    upb_grad[...] = line(upb_acc[...])


def backward_kernel(
    lens, groups, og, act, slope, normed, inv, shaped, masked, up, down, small, gs_out, dup, ddown, small_grad, upb_grad,
    gs, gb, gbef, gm, s8, len8, acc, upb_acc, *, ft, tiles, parts, taps, group_count,
):
    i = pl.program_id(0)
    frame_count, clips, width = gs.shape
    hidden = gbef.shape[1]
    cols = hidden // parts
    rows = ft * clips
    total_rows = frame_count * clips
    base = 2 * ft
    span = parts + tiles + 2
    step = lax.rem(i, span)
    b = 1 - i // span

    @pl.when(step == 0)
    def _():
        prepare(small.at[b], lens, groups, s8, len8, group_count)
        acc[...] = jnp.zeros(acc.shape, F32)

    @pl.when(i == 0)
    def _():
        gm[pl.ds(0, base)] = jnp.zeros((base, clips, width), F32)
        gm[pl.ds(base + frame_count, HALO)] = jnp.zeros((HALO, clips, width), F32)
        spread_grad(og, gs, 0)

    @pl.when(step == 0)
    def _():
        acc[A_DOWN] = branch_grad(gs, 0, s8, len8, gb)

    @pl.when(step < parts)
    def _():
        c0 = pl.multiple_of(step * cols, cols)
        at = pl.ds(c0, cols)
        lower = down[0, at, :]
        term = mm(act[0], gb[...], TN)
        ddown[b, at, :] = term
        acc[A_GAIN] += fold((term * lower.astype(F32)).reshape(cols // 8, 8, width))
        before_grad(gb, lower, slope.at[0], slice(None), gbef, at, upb_acc, total_rows)
        dup[b, :, at] = mm(shaped[0], gbef[:, at], TN)

    j = step - parts

    @pl.when((j >= 0) & (j < tiles))
    def _():
        r0 = pl.multiple_of(j * rows, rows)
        grad = mm(gbef[pl.ds(r0, rows), :], up[0], NT)
        norm_back(grad, normed.at[0], 0, inv.at[0], 0, s8, gm, base + j * ft, acc, ft)

    @pl.when(j >= 2)
    def _():
        f0 = (j - 2) * ft
        conv_back(gm, base + f0, s8, masked.at[0], 0, gs, f0, f0, gs_out, acc, ft, len8, taps)

    @pl.when(step == span - 1)
    def _():
        finish_small(acc, upb_acc, groups, s8, small_grad.at[b], upb_grad.at[b], group_count)


def spread_grad(og, gs, g0):
    def one(n, carry):
        t0 = pl.multiple_of(n * 16, 16)
        gs[pl.ds(g0 + t0, 16)] = swap_frames(og, t0, 16)
        return carry
    lax.fori_loop(0, og.shape[1] // 16, one, 0)


def branch_grad(gs, g0, s8, len8, gb):
    clips, width = len8.shape
    frame_count = gb.shape[0] // clips

    def one(n, a_down):
        t0 = n * 4
        gvb = s8[GAIN][None] * keep_frames(gs[pl.ds(g0 + t0, 4)], t0, len8)
        at = pl.multiple_of(t0 * clips, 4 * clips)
        gb[pl.ds(at, 4 * clips), :] = gvb.reshape(4 * clips, width).astype(BF16)
        return a_down + fold(gvb)
    return lax.fori_loop(0, frame_count // 4, one, jnp.zeros((clips, width), F32), unroll=4)


def before_grad(gb, lower, slope, slope_cols, gbef, at, upb_acc, rows, chunk=1024, sub=16):
    cols = lower.shape[0]
    total = jnp.zeros((8, cols), F32)
    for c in range(0, rows, chunk):
        ga = mm(gb[c : c + chunk, :], lower, NT)
        for r in range(0, chunk, sub):
            gr = ga[r : r + sub] * slope[c + r : c + r + sub, slope_cols].astype(F32)
            total = total + fold(gr.reshape(sub // 8, 8, cols))
            gbef[c + r : c + r + sub, at] = gr.astype(BF16)
    upb_acc[:, at] = total


def backward(lens, groups, og, saved, ups, downs, small, ft, taps, group_count):
    act, slope, normed, inv, shaped, masked = saved
    clips, fc, d = og.shape
    h = ups.shape[2]
    R, r, n = fc * clips, ft * clips, fc // ft
    parts = 6
    cols = h // parts
    span = parts + n + 2
    block = lambda i: 1 - i // span
    part = lambda i: jnp.minimum(lax.rem(i, span), parts - 1)
    tile = lambda i: jnp.clip(lax.rem(i, span) - parts, 0, n - 1)
    late = lambda i: jnp.clip(lax.rem(i, span) - parts - 2, 0, n - 1)
    last = lambda i: jnp.clip(i - span - parts - 2, 0, n - 1)
    sums = [(2, d, h), (2, h, d), (2, ROWS, d), (2, 1, h)]
    return pl.pallas_call(
        functools.partial(backward_kernel, ft=ft, tiles=n, parts=parts, taps=taps, group_count=group_count),
        name="backward",
        grid=(2 * span,),
        in_specs=[
            smem(), smem(), whole(clips, fc, d),
            pl.BlockSpec((1, R, cols), lambda i: (block(i), 0, part(i))),
            pl.BlockSpec((1, R, cols), lambda i: (block(i), 0, part(i))),
            pl.BlockSpec((1, ft, clips, d), lambda i: (block(i), tile(i), 0, 0)),
            pl.BlockSpec((1, ft, clips, LANES), lambda i: (block(i), tile(i), 0, 0)),
            pl.BlockSpec((1, R, d), lambda i: (block(i), 0, 0), pipeline_mode=pl.Buffered(1)),
            pl.BlockSpec((1, ft, clips, d), lambda i: (block(i), late(i), 0, 0)),
            pl.BlockSpec((1, d, h), lambda i: (block(i), 0, 0)),
            pl.BlockSpec((1, h, d), lambda i: (block(i), 0, 0)),
            whole(2, ROWS, d),
        ],
        out_specs=[pl.BlockSpec((ft, clips, d), lambda i: (last(i), 0, 0))] + [whole(*v) for v in sums],
        out_shape=[shape((fc, clips, d))] + [shape(v) for v in sums],
        scratch_shapes=[
            pltpu.VMEM((fc, clips, d), F32), pltpu.VMEM((R, d), BF16), pltpu.VMEM((R, h), BF16),
            pltpu.VMEM((fc + 2 * ft + HALO, clips, d), F32),
            pltpu.VMEM((14, clips, d), F32), pltpu.VMEM((clips, d), jnp.int32),
            pltpu.VMEM((12, clips, d), F32), pltpu.VMEM((clips, h), F32),
        ],
        compiler_params=pltpu.CompilerParams(vmem_limit_bytes=VMEM_LIMIT),
    )(lens, groups, og, act, slope, normed, inv, shaped, masked, ups, downs, small)


def step_kernel(*refs, deep, side, ft, parts, taps, group_count):
    lens, groups, frames, og = refs[:4]
    shards = refs[4:13]
    out, gs_out, up_part, down_part, small_part, act_far, slope_far = refs[13:20]
    (io, masked0, masked1, normed, inv, shaped, first_rows, act, slope, gb, s8, u8, len8, acc, upb_acc) = refs[20:35]
    small_full, upb_full, small_grad, upb_grad, up_full, down_full, up_term, down_term = refs[35:43]
    io_sem, act_sem, slope_sem, act_back_sem, slope_back_sem, gs_sem = refs[43:49]
    gather_refs, sum_refs = refs[49:67], refs[67:]

    i = pl.program_id(0)
    clips, frame_count, width = io.shape
    hidden = act.shape[1]
    tiles = frame_count // ft
    rows = ft * clips
    cols = hidden // parts
    span = parts + tiles + 1
    body = pl.ds(HALO, frame_count)

    load = lambda n, src: pltpu.make_async_copy(src, io, io_sem.at[n])
    tile_rows = lambda j: pl.ds(pl.multiple_of(j * rows, rows), rows)
    part_at = lambda p: pl.ds(pl.multiple_of(p * cols, cols), cols)

    def spills(j):
        r = tile_rows(j)
        return [
            pltpu.make_async_copy(act.at[r], act_far.at[r], act_sem.at[j]),
            pltpu.make_async_copy(slope.at[r], slope_far.at[r], slope_sem.at[j]),
        ]

    def act_back(p):
        return pltpu.make_async_copy(act_far.at[:, part_at(p)], act.at[:, part_at(p)], act_back_sem.at[p])

    def slope_back(j):
        return pltpu.make_async_copy(slope_far.at[tile_rows(j)], slope.at[tile_rows(j)], slope_back_sem.at[j])

    def up_cols(b):
        return lambda lo, hi: up_full[b, :, :, :, :, :, lo:hi].reshape(width, hi - lo)

    def spread():
        load(0, frames).wait()

        def one(n, carry):
            t0 = pl.multiple_of(n * 16, 16)
            v = swap_frames(io, t0, 16)
            at = pl.multiple_of(t0 * clips, 16 * clips)
            first_rows[pl.ds(at, 16 * clips), :] = v.reshape(16 * clips, width).astype(BF16)
            masked0[pl.ds(HALO + t0, 16)] = keep_frames(v, t0, len8)
            return carry
        lax.fori_loop(0, frame_count // 16, one, 0)
        load(1, og).start()

    def conv0(lo, hi):
        def one(n, carry):
            conv_norm(masked0, n * ft, ft, s8.at[0], normed.at[0], inv.at[0], shaped, taps, HALO)
            return carry
        lax.fori_loop(lo, hi, one, 0)

    def ready():
        for b in range(2):
            prepare(small_full.at[b], lens, groups, s8.at[b], len8, group_count)
            u8[b] = jnp.broadcast_to(upb_full[b, 0:1, :], u8.shape[1:])

    @pl.when(i == 0)
    def _():
        load(0, frames).start()
        zeros = jnp.zeros((HALO, clips, width), F32)
        for m in (masked0, masked1, normed.at[0], normed.at[1]):
            m[0:HALO] = zeros
            m[HALO + frame_count : HALO + frame_count + HALO] = zeros
        len8[...] = per_clip(lens, clips, width)
        Gather(shards, up_full, down_full, small_full, upb_full, gather_refs, deep, side, group_count, taps).early(
            spread, ready, conv0, tiles)

    Gather(shards, up_full, down_full, small_full, upb_full, gather_refs, deep, side, group_count, taps).late(i, tiles)

    @pl.when(i < tiles)
    def _():
        r0 = pl.multiple_of(i * rows, rows)
        up_gelu(shaped, up_cols(0), u8.at[0], act, r0, slope, r0, rows, hidden)
        run(spills(i))

    @pl.when((i >= tiles) & (i < 2 * tiles))
    def _():
        j = i - tiles
        f0 = j * ft
        r0 = pl.multiple_of(j * rows, rows)
        branch = mm(act[pl.ds(r0, rows), :], down_full[0].reshape(hidden, width), NN)
        for t in range(0, ft, 4):
            b = branch[t * clips : (t + 4) * clips].reshape(4, clips, width) + s8[0, DOWN_BIAS][None]
            total = masked0[pl.ds(HALO + f0 + t, 4)] + s8[0, GAIN][None] * b
            masked1[pl.ds(HALO + f0 + t, 4)] = keep_frames(total, f0 + t, len8)

    @pl.when((i >= 2 * tiles) & (i < 3 * tiles))
    def _():
        j = i - 2 * tiles
        f0 = j * ft
        r0 = pl.multiple_of(j * rows, rows)
        done(spills(j))
        conv_norm(masked1, f0, ft, s8.at[1], normed.at[1], inv.at[1], shaped, taps, HALO)
        up_gelu(shaped, up_cols(1), u8.at[1], act, r0, slope, r0, rows, hidden)
        branch = mm(act[pl.ds(r0, rows), :], down_full[1].reshape(hidden, width), NN)
        last_block(branch, masked1, f0, r0, ft, s8.at[1], len8, first_rows, out)

    k = i - 3 * tiles
    step = lax.rem(jnp.maximum(k, 0), span)
    b = jnp.where(k < span, 1, 0)

    @pl.when(k == 0)
    def _():
        load(1, og).wait()
        spread_grad(io, masked0, HALO)

    @pl.when(k == span)
    def _():
        def one(n, carry):
            t0 = n * 4
            at = pl.multiple_of(t0 * clips, 4 * clips)
            v = normed[0, pl.ds(HALO + t0, 4)] * s8[0, SCALE][None] + s8[0, SHIFT][None]
            shaped[pl.ds(at, 4 * clips), :] = v.reshape(4 * clips, width).astype(BF16)
            first = first_rows[pl.ds(at, 4 * clips), :].astype(F32).reshape(4, clips, width)
            masked1[pl.ds(HALO + t0, 4)] = keep_frames(first, t0, len8)
            return carry
        lax.fori_loop(0, frame_count // 4, one, 0, unroll=4)
        for j in range(tiles):
            slope_back(j).wait()

    @pl.when((k >= 0) & (step == 0))
    def _():
        acc[...] = jnp.zeros(acc.shape, F32)
        acc[A_DOWN] = branch_grad(masked0, HALO, s8.at[b], len8, gb)

    sums = Sums(sum_refs, up_term, down_term, up_part, down_part, small_part, small_grad, upb_grad, deep, side, parts)
    sums.at(k, 0, span)

    @pl.when((k >= span) & (step < parts))
    def _():
        act_back(step).wait()

    @pl.when((k >= 0) & (step < parts))
    def _():
        at = part_at(step)
        drows, urows = down_full.shape[5], up_full.shape[5]
        per = drows // 16
        spots = []
        for m in range(cols // 16):
            row = step * (cols // 16) + m
            e = row // per
            z, chip = e // (2 * side * side), e // 2
            sub = pl.ds(pl.multiple_of((row - e * per) * 16, 16), 16)
            spots.append((b, z, lax.rem(chip // side, side), lax.rem(chip, side), lax.rem(e, 2), sub))
        lower = jnp.concatenate([down_full[spot] for spot in spots], axis=0)
        term = mm(act[:, at], gb[...], TN)
        for m, spot in enumerate(spots):
            down_term[spot] = term[m * 16 : (m + 1) * 16].astype(BF16)
        acc[A_GAIN] += fold((term * lower.astype(F32)).reshape(cols // 8, 8, width))
        before_grad(gb, lower, slope, at, slope, at, upb_acc, frame_count * clips)
        term = mm(shaped[...], slope[:, at], TN).astype(BF16)
        up_term[b, :, :, :, :, :, at] = term.reshape(deep, side, side, 2, urows, cols)

    @pl.when((k >= 0) & (k < parts))
    def _():
        act_back(step).start()

    j = step - parts

    @pl.when((j >= 0) & (j < tiles))
    def _():
        r0 = pl.multiple_of(j * rows, rows)
        grad = mm(slope[pl.ds(r0, rows), :], up_full[b].reshape(width, hidden), NT)
        norm_back(grad, normed.at[b], HALO + j * ft, inv.at[b], j * ft, s8.at[b], normed.at[b], HALO + j * ft, acc, ft)

    @pl.when((k < span) & (j >= 0) & (j < tiles))
    def _():
        slope_back(j).start()

    sums.at(k, 1, span)
    gs_copy = lambda f0, n: pltpu.make_async_copy(masked0.at[pl.ds(HALO + f0, ft)], gs_out.at[pl.ds(f0, ft)], gs_sem.at[n])

    @pl.when(j >= 1)
    def _():
        f0 = (j - 1) * ft
        conv_back(
            normed.at[b], HALO + f0, s8.at[b], masked1, HALO + f0, masked0, HALO + f0, f0, None, acc, ft, len8, taps)

    @pl.when((k >= span) & (j >= 1))
    def _():
        gs_copy((j - 1) * ft, j - 1).start()

    @pl.when((k >= 0) & (step == span - 1))
    def _():
        finish_small(acc, upb_acc, groups, s8.at[b], small_grad.at[b], upb_grad.at[b], group_count)

    sums.after(k, span)

    @pl.when(k == 2 * span - 1)
    def _():
        for n in range(tiles):
            gs_copy(n * ft, n).wait()


def whole_step(deep, side, lens, groups, frames, og, weights, ft, taps, group_count):
    clips, fc, d = frames.shape
    h = weights[4].shape[2]
    urows, drows = weights[4].shape[1], weights[6].shape[1]
    R, r, n = fc * clips, ft * clips, fc // ft
    parts = 3
    span = parts + n + 1
    dims = (2, deep, side, side, 2)
    rows = lambda dtype, *lead: pltpu.VMEM(lead + (d,), dtype)
    halo = fc + 2 * HALO
    return pl.pallas_call(
        functools.partial(step_kernel, deep=deep, side=side, ft=ft, parts=parts, taps=taps, group_count=group_count),
        name="step",
        grid=(3 * n + 2 * span,),
        in_specs=[smem(), smem(), hbm(), hbm()] + [vmem()] * 9,
        out_specs=[
            pl.BlockSpec((clips, ft, d), lambda i: (0, jnp.clip(i - 2 * n, 0, n - 1), 0)),
            hbm(), vmem(), vmem(), vmem(), hbm(), hbm(),
        ],
        out_shape=[
            shape((clips, fc, d), BF16), shape((fc, clips, d)), shape((2, urows, h)), shape((2, drows, d)),
            shape((2 * PACK, LANES)), shape((R, h), BF16), shape((R, h), BF16),
        ],
        scratch_shapes=[
            rows(BF16, clips, fc),
            rows(F32, halo, clips), rows(F32, halo, clips), rows(F32, 2, halo, clips), pltpu.VMEM((2, fc, clips, LANES), F32),
            rows(BF16, R), rows(BF16, R), pltpu.VMEM((R, h), BF16), pltpu.VMEM((R, h), BF16), rows(BF16, R),
            rows(F32, 2, 14, clips), pltpu.VMEM((2, clips, h), F32), rows(jnp.int32, clips), rows(F32, 12, clips),
            pltpu.VMEM((clips, h), F32),
            rows(F32, 2, ROWS), pltpu.VMEM((2, 1, h), F32), rows(F32, 2, ROWS), pltpu.VMEM((2, 1, h), F32),
            pltpu.VMEM(dims + (urows, h), BF16), rows(BF16, *dims, drows), pltpu.VMEM(dims + (urows, h), BF16), rows(BF16, *dims, drows),
            DMA((2,)), DMA((n,)), DMA((n,)), DMA((parts,)), DMA((n,)), DMA((n,)),
        ] + gather_scratch(deep, side) + sums_scratch(deep, side, urows, drows, d, h, parts),
        compiler_params=pltpu.CompilerParams(vmem_limit_bytes=VMEM_LIMIT, collective_id=0, has_side_effects=True),
    )(lens, groups, frames, og, *weights)


def swap_rows(src, dst):
    for t in range(0, src.shape[0], 8):
        dst[:, t : t + 8, :] = jnp.swapaxes(src[t : t + 8], 0, 1)


def unpack_kernel(gs, up_in, down_in, small, gin, conv_w, conv_b, scale, shift, up_w, up_b, down_w, down_b, gain):
    swap_rows(gs, gin)

    @pl.when(pl.program_id(0) == 0)
    def _():
        unpack_parts(up_in, down_in, small, conv_w, conv_b, scale, shift, up_w, up_b, down_w, down_b, gain)


def unpack_parts(up_in, down_in, small, conv_w, conv_b, scale, shift, up_w, up_b, down_w, down_b, gain):
    f = lax.axis_index("fsdp")
    width = conv_b.shape[1]
    wide = up_b.shape[1]
    span = wide * LANES // width
    turned = pltpu.roll(small[...], lax.rem(LANES - f * width, LANES), 1)
    for b in range(2):
        o = b * PACK
        for k in range(conv_w.shape[0]):
            conv_w[k, b : b + 1, :] = turned[o + k : o + k + 1, :width]
        conv_b[b : b + 1, :] = turned[o + CONV_BIAS : o + CONV_BIAS + 1, :width]
        scale[b] = turned[o + SCALE : o + SCALE + scale.shape[1], :width]
        shift[b] = turned[o + SHIFT : o + SHIFT + shift.shape[1], :width]
        down_b[b : b + 1, :] = turned[o + DOWN_BIAS : o + DOWN_BIAS + 1, :width]
        gain[b : b + 1, :] = turned[o + GAIN : o + GAIN + 1, :width]
        bias = jnp.concatenate([small[o + 14 + q : o + 15 + q, :] for q in range(span // LANES)], axis=1)
        bias = pltpu.roll(jnp.broadcast_to(bias, (8, span)), lax.rem(span - f * wide, span), 1)
        up_b[b : b + 1, :] = bias[0:1, :wide]
    up_w[...] = up_in[...]
    down_w[...] = down_in[...]


def unpack_far(gs):
    fc, clips, d = gs.shape
    ft = 64
    return pl.pallas_call(
        swap_rows,
        name="unpack",
        grid=(fc // ft,),
        in_specs=[pl.BlockSpec((ft, clips, d), lambda i: (i, 0, 0))],
        out_specs=pl.BlockSpec((clips, ft, d), lambda i: (0, i, 0)),
        out_shape=shape((clips, fc, d)),
    )(gs)


def unpack(gs, parts, taps, group_count, width, wide):
    fc, clips, d = gs.shape
    ft = 64
    up_in, down_in, small = parts
    outs = [(taps, 2, width), (2, width), (2, group_count, width), (2, group_count, width), up_in.shape, (2, wide),
            down_in.shape, (2, width), (2, width)]
    return pl.pallas_call(
        unpack_kernel,
        name="unpack",
        grid=(fc // ft,),
        in_specs=[pl.BlockSpec((ft, clips, d), lambda i: (i, 0, 0))] + [whole(*v.shape) for v in parts],
        out_specs=[pl.BlockSpec((clips, ft, d), lambda i: (0, i, 0))] + [whole(*v) for v in outs],
        out_shape=[shape((clips, fc, d))] + [shape(v) for v in outs],
    )(gs, up_in, down_in, small)


def body(deep, fan, frames, group, lengths, conv_w, conv_b, scale, shift, up_w, up_b, down_w, down_b, gain, out_grad):
    side = math.isqrt(fan // 2)
    clips = frames.shape[0]
    taps, group_count, hidden = conv_w.shape[1], scale.shape[1], up_w.shape[2]
    width, wide = conv_b.shape[1], up_b.shape[1]
    axes = ("dp", "fsdp")
    near = width * fan == LANES and up_w.shape[1] % 16 == 0 and down_w.shape[1] % 16 == 0
    ft = 32
    if near:
        weights = (conv_w.transpose(1, 0, 2), conv_b, scale, shift, up_w, up_b, down_w, down_b, gain)
    else:
        whole_of = lambda v, axis: lax.all_gather(v, axes, axis=axis, tiled=True)
        ups, downs = whole_of(up_w, 1), whole_of(down_w, 1)
        lines = jnp.concatenate(
            [conv_w, conv_b[:, None], scale, shift, down_b[:, None], gain[:, None], jnp.zeros((2, 2, width), BF16)], axis=1
        )
        small = whole_of(lines, 2).astype(F32)
        upb = whole_of(up_b, 1).astype(F32)[:, None]
        weights = (small, upb, ups, downs)
    if near:
        out, gs, *parts, _, _ = whole_step(deep, side, lengths, group, frames, out_grad, weights, 64, taps, group_count)
        gin, conv_grad, *grads = unpack(gs, parts, taps, group_count, width, wide)
        return (out, gin, conv_grad.transpose(1, 0, 2), *grads)
    out, act, slope, *rest = forward(lengths, group, frames, weights, hidden, ft, taps, group_count)
    saved = (act, slope.reshape(act.shape), *rest)
    gs, *parts = backward(lengths, group, out_grad, saved, ups, downs, small, ft, taps, group_count)
    gin = unpack_far(gs)
    dup, ddown, lines, ug = parts
    owner = lambda v, axis: lax.psum_scatter(v, axes, scatter_dimension=axis, tiled=True)
    lines = owner(lines, 2)
    return (
        out, gin, lines[:, :taps], lines[:, CONV_BIAS], lines[:, SCALE : SCALE + group_count],
        lines[:, SHIFT : SHIFT + group_count], owner(dup, 1), owner(ug[:, 0], 1), owner(ddown, 1),
        lines[:, DOWN_BIAS], lines[:, GAIN],
    )


def solution(mesh):
    split = ("dp", "fsdp")
    clip = P(split, None, None)
    first, middle, last = P(None, split), P(None, split, None), P(None, None, split)
    in_specs = (clip, P(split), P(split), last, first, last, last, middle, first, middle, first, first, clip)
    out_specs = (clip, clip, last, first, last, last, middle, first, middle, first, first)
    run = functools.partial(body, mesh.shape["dp"], mesh.shape["fsdp"])
    return jax.shard_map(run, mesh=mesh, in_specs=in_specs, out_specs=out_specs, check_vma=False)
```

```python
import functools
import math
import jax
import jax.numpy as jnp
from jax import lax
from jax.experimental import pallas as pl
from jax.experimental.pallas import tpu as pltpu
from jax.sharding import PartitionSpec as P

F32 = jnp.float32
BF16 = jnp.bfloat16
EPSILON = 1e-06
TAPS, CONV_BIAS, SCALE, SHIFT, DOWN_BIAS, GAIN, ROWS = 0, 7, 8, 10, 12, 13, 16
A_TAPS, A_BIAS, A_SCALE, A_SHIFT, A_DOWN, A_GAIN = 0, 7, 8, 9, 10, 11
HALO = 3
LANES = 128
VMEM_LIMIT = 64 * 1024 * 1024 - 128 * 1024
NN = (((1,), (0,)), ((), ()))
NT = (((1,), (1,)), ((), ()))
TN = (((0,), (0,)), ((), ()))
DMA = pltpu.SemaphoreType.DMA


def mm(a, b, dims):
    return lax.dot_general(a, b, dims, preferred_element_type=F32)


def gelu_pair(before):
    u = before * math.sqrt(0.5)
    phi = 0.5 + 0.5 * lax.erf(u)
    bell = jnp.exp2(u * u * (-math.log2(math.e))) * (1.0 / math.sqrt(math.pi))
    return before * phi, phi + u * bell


def per_clip(values, clips, width):
    rows = lax.broadcasted_iota(jnp.int32, (clips, width), 0)
    out = jnp.zeros((clips, width), jnp.int32)
    for c in range(clips):
        out = jnp.where(rows == c, values[c], out)
    return out


def prepare(small, lens, groups, s8, len8, group_count):
    clips, width = len8.shape
    for r in range(14):
        s8[r] = jnp.broadcast_to(small[r : r + 1, :], (clips, width))
    member = per_clip(groups, clips, width)
    len8[...] = per_clip(lens, clips, width)
    gain = jnp.zeros((clips, width), F32)
    shift = jnp.zeros((clips, width), F32)
    for g in range(group_count):
        chosen = jnp.where(member == g, 1.0, 0.0)
        gain = gain + chosen * s8[SCALE + g]
        shift = shift + chosen * s8[SHIFT + g]
    s8[SCALE] = gain
    s8[SHIFT] = shift


def keep_frames(v, t0, len8, other=0.0):
    t = lax.broadcasted_iota(jnp.int32, v.shape, 0) + t0
    return jnp.where(t < len8[...][None], v, other)


def swap_frames(block, t0, frames):
    return jnp.swapaxes(block[:, pl.ds(t0, frames), :].astype(F32), 0, 1)


def fold(v):
    return jnp.sum(v, axis=0)


def smem():
    return pl.BlockSpec(memory_space=pltpu.SMEM)


def vmem():
    return pl.BlockSpec(memory_space=pltpu.VMEM)


def hbm():
    return pl.BlockSpec(memory_space=pl.ANY)


def whole(*dims):
    return pl.BlockSpec(dims, lambda i: (0,) * len(dims), pipeline_mode=pl.Buffered(1))


def shape(dims, dtype=F32):
    return jax.ShapeDtypeStruct(dims, dtype)


MESH = pl.DeviceIdType.MESH
PACK = 24


class Place:
    def __init__(self, deep, side):
        self.deep, self.side = deep, side
        self.z = lax.axis_index("dp")
        f = lax.axis_index("fsdp")
        self.f = f
        self.core = lax.rem(f, 2)
        chip = f // 2
        self.low = lax.rem(chip, side)
        self.high = chip // side
        self.first = jnp.where(self.core == 0, self.high, self.low)
        self.second = jnp.where(self.core == 0, self.low, self.high)

    def chip_of(self, first, second):
        high = jnp.where(self.core == 0, first, second)
        low = jnp.where(self.core == 0, second, first)
        return high, low

    def fsdp_of(self, first, second):
        high, low = self.chip_of(first, second)
        return (high * self.side + low) * 2 + self.core

    def z_peer(self, p):
        return {"dp": lax.rem(self.z + p, self.deep)}

    def first_peer(self, p):
        return {"fsdp": self.fsdp_of(lax.rem(self.first + p, self.side), self.second)}

    def second_peer(self, p):
        return {"fsdp": self.fsdp_of(self.first, lax.rem(self.second + p, self.side))}

    def core_peer(self):
        return {"fsdp": self.f + 1 - 2 * self.core}

    def greet(self):
        barrier = pltpu.get_barrier_semaphore()
        peers = [self.z_peer(p) for p in range(1, self.deep)]
        peers += [self.first_peer(p) for p in range(1, self.side)]
        peers += [self.second_peer(p) for p in range(1, self.side)]
        peers.append(self.core_peer())
        for peer in peers:
            pl.semaphore_signal(barrier, inc=1, device_id=peer, device_id_type=MESH)
        pl.semaphore_wait(barrier, len(peers))


def send(src, dst, send_sem, recv_sem, peer):
    return pltpu.make_async_remote_copy(
        src_ref=src, dst_ref=dst, send_sem=send_sem, recv_sem=recv_sem, device_id=peer, device_id_type=MESH
    )


def run(copies):
    for c in copies:
        c.start()


def done(copies):
    for c in copies:
        c.wait()


def weight_route(place, own, full, sems):
    zs, zr, fs, fr, ss, sr, cs, cr = sems
    deep, side, core = place.deep, place.side, place.core

    def held(p, q):
        high, low = place.chip_of(lax.rem(place.first + p, side), lax.rem(place.second + q, side))
        return full.at[:, high, low, core]

    mine = full.at[place.z, place.high, place.low, core]
    along_z = [send(own, mine, zs.at[p - 1], zr.at[p - 1], place.z_peer(p)) for p in range(1, deep)]
    along_first = [
        send(held(0, 0), held(0, 0), fs.at[p - 1], fr.at[p - 1], place.first_peer(p)) for p in range(1, side)
    ]
    along_second = []
    for j in range(side):
        high, low = place.chip_of(j, place.second)
        line = full.at[:, high, low, core]
        for p in range(1, side):
            n = j * (side - 1) + p - 1
            along_second.append(send(line, line, ss.at[n], sr.at[n], place.second_peer(p)))
    across = lambda p, q: send(held(p, q), held(p, q), cs.at[p * side + q], cr.at[p * side + q], place.core_peer())
    over = [[across(0, 0)], [across(p, 0) for p in range(1, side)],
            [across(p, q) for q in range(1, side) for p in range(side)]]
    return [along_z, along_first, along_second], over


def gather_sems(count, deep, side):
    one = [deep - 1, deep - 1, side - 1, side - 1, side * (side - 1), side * (side - 1), side * side, side * side]
    return [DMA((count, n)) for n in one]


def place_small(place, shards, pack, group_count, taps):
    conv_w, conv_b, scale, shift, up_b, down_b, gain = shards
    width = conv_b.shape[1]
    lane = lax.broadcasted_iota(jnp.int32, (width, LANES), 1)
    row = lax.broadcasted_iota(jnp.int32, (width, LANES), 0)
    spot = jnp.where(lane == row + place.f * width, 1.0, 0.0).astype(BF16)
    wide = up_b.shape[1]
    span = wide * LANES // width
    lane = lax.broadcasted_iota(jnp.int32, (wide, span), 1)
    row = lax.broadcasted_iota(jnp.int32, (wide, span), 0)
    spread = jnp.where(lane == row + place.f * wide, 1.0, 0.0).astype(BF16)
    pack[...] = jnp.zeros(pack.shape, F32)
    for b in range(2):
        o = b * PACK
        for k in range(taps):
            pack[o + k : o + k + 1, :] = mm(conv_w[k, b : b + 1, :], spot, NN)
        pack[o + SCALE : o + SCALE + group_count, :] = mm(scale[b], spot, NN)
        pack[o + SHIFT : o + SHIFT + group_count, :] = mm(shift[b], spot, NN)
        for src, at in ((conv_b, CONV_BIAS), (down_b, DOWN_BIAS), (gain, GAIN)):
            pack[o + at : o + at + 1, :] = mm(src[b : b + 1, :], spot, NN)
        bias = mm(up_b[b : b + 1, :], spread, NN)
        for q in range(span // LANES):
            pack[o + 14 + q : o + 15 + q, :] = bias[:, q * LANES : (q + 1) * LANES]


class Gather:
    def __init__(self, shards, up_full, down_full, small_full, upb_full, refs, deep, side, group_count, taps):
        (self.pack, self.zbuf, self.first_in, self.first_sum, self.second_in, self.second_sum, self.core_in,
         self.local_sems, self.small_s, self.small_r) = refs[:10]
        sems = refs[10:]
        self.place = place = Place(deep, side)
        self.small_full, self.upb_full, self.shards = small_full, upb_full, shards
        self.group_count, self.taps = group_count, taps
        up_w, down_w = shards[4], shards[6]
        self.full = (up_full, down_full)
        self.routes, self.local = [], []
        for n, (own, full) in enumerate(
            ((up_w.at[0], up_full.at[0]), (down_w.at[0], down_full.at[0]), (up_w.at[1], up_full.at[1]), (down_w.at[1], down_full.at[1]))
        ):
            self.routes.append(weight_route(place, own, full, [s.at[n] for s in sems]))
            spot = full.at[place.z, place.high, place.low, place.core]
            self.local.append(pltpu.make_async_copy(own, spot, self.local_sems.at[n]))
        stages = [
            [(self.zbuf.at[place.z], self.zbuf.at[place.z], place.z_peer(p)) for p in range(1, deep)],
            [(self.zbuf, self.first_in.at[p - 1], place.first_peer(p)) for p in range(1, side)],
            [(self.first_sum, self.second_in.at[p - 1], place.second_peer(p)) for p in range(1, side)],
            [(self.second_sum, self.core_in, place.core_peer())],
        ]
        n = 0
        self.small = []
        for stage in stages:
            copies = []
            for src, dst, peer in stage:
                copies.append(send(src, dst, self.small_s.at[n], self.small_r.at[n], peer))
                n += 1
            self.small.append(copies)

    def begin(self, n):
        run(self.routes[n][0][0])
        self.local[n].start()

    def after_z(self, n):
        along, over = self.routes[n]
        self.local[n].wait()
        done(along[0])
        run(along[1])
        run(over[0])

    def after_first(self, n):
        along, over = self.routes[n]
        done(along[1])
        run(along[2])
        run(over[1])

    def after_second(self, n):
        along, over = self.routes[n]
        done(along[2])
        run(over[2])

    def end(self, n):
        for copies in self.routes[n][1]:
            done(copies)

    def early(self, spread, ready, conv, tiles):
        place = self.place
        conv_w, conv_b, scale, shift, _, up_b, _, down_b, gain = self.shards
        place_small(place, (conv_w, conv_b, scale, shift, up_b, down_b, gain), self.pack, self.group_count, self.taps)
        self.zbuf[place.z] = self.pack[...].astype(BF16)
        place.greet()
        run(self.small[0])
        self.begin(0)
        self.begin(1)
        spread()
        done(self.small[0])
        run(self.small[1])
        self.after_z(0)
        done(self.small[1])
        total = self.zbuf[...].astype(F32)
        for p in range(1, place.side):
            total = total + self.first_in[p - 1].astype(F32)
        self.first_sum[...] = total.astype(BF16)
        run(self.small[2])
        done(self.small[2])
        total = self.first_sum[...].astype(F32)
        for p in range(1, place.side):
            total = total + self.second_in[p - 1].astype(F32)
        self.second_sum[...] = total.astype(BF16)
        run(self.small[3])
        self.after_first(0)
        self.begin(2)
        self.begin(3)
        done(self.small[3])
        self.finish_small()
        ready()
        conv(0, tiles // 4)
        self.after_z(1)
        conv(tiles // 4, 3 * tiles // 4)
        self.after_second(0)
        self.after_first(1)
        self.after_z(2)
        conv(3 * tiles // 4, tiles)
        self.end(0)

    def finish_small(self):
        total = self.second_sum[...].astype(F32) + self.core_in[...].astype(F32)
        deep = self.place.deep
        per = self.upb_full.shape[2] // deep
        self.small_full[...] = jnp.zeros(self.small_full.shape, F32)
        for b in range(2):
            o = b * PACK
            for z in range(deep):
                self.small_full[b, 0:14, z * LANES : (z + 1) * LANES] = total[z, o : o + 14, :]
                for q in range(per // LANES):
                    at = z * per + q * LANES
                    self.upb_full[b, :, at : at + LANES] = total[z, o + 14 + q : o + 15 + q, :]

    def late(self, i, tiles):
        @pl.when(i == tiles // 4)
        def _():
            self.after_z(3)

        @pl.when(i == 3 * tiles // 4)
        def _():
            self.after_second(1)
            self.after_first(2)

        @pl.when(i == tiles)
        def _():
            self.end(1)

        @pl.when(i == tiles + tiles // 4)
        def _():
            self.after_first(3)

        @pl.when(i == 2 * tiles - 1)
        def _():
            self.after_second(2)

        @pl.when(i == 2 * tiles)
        def _():
            self.after_second(3)
            for n in (2, 3):
                self.end(n)


def gather_scratch(deep, side):
    buf = pltpu.VMEM((deep, 2 * PACK, LANES), BF16)
    many = pltpu.VMEM((side - 1, deep, 2 * PACK, LANES), BF16)
    n = deep - 1 + 2 * (side - 1) + 1
    return [pltpu.VMEM((2 * PACK, LANES), F32), buf, many, buf, many, buf, buf, DMA((4,)), DMA((n,)), DMA((n,))] + gather_sems(
        4, deep, side
    )


def conv_norm(masked, f0, frames, s8, normed, inv, shaped, taps, n0=0, step=4):
    clips, width = s8.shape[1:]
    for j in range(0, frames, step):
        mixed = s8[CONV_BIAS][None]
        for k in range(taps):
            mixed = mixed + s8[TAPS + k][None] * masked[pl.ds(f0 + j + k, step)]
        center = mixed - jnp.mean(mixed, axis=-1, keepdims=True)
        inv_std = lax.rsqrt(jnp.mean(center * center, axis=-1, keepdims=True) + EPSILON)
        norm = center * inv_std
        normed[pl.ds(n0 + f0 + j, step)] = norm
        inv[pl.ds(f0 + j, step)] = jnp.broadcast_to(inv_std, (step, clips, LANES))
        rows = norm * s8[SCALE][None] + s8[SHIFT][None]
        at = pl.multiple_of((f0 + j) * clips, step * clips)
        shaped[pl.ds(at, step * clips), :] = rows.reshape(step * clips, width).astype(BF16)


def up_gelu(shaped, up_cols, u8, act, r0, slope, s0, rows, hidden, cols=256, sub=16):
    left = shaped[pl.ds(r0, rows), :]
    for n in range(0, hidden, cols):
        before = mm(left, up_cols(n, n + cols), NN)
        for r in range(0, rows, sub):
            piece = before[r : r + sub].reshape(sub // 8, 8, cols) + u8[:, n : n + cols][None]
            a, s = gelu_pair(piece.reshape(sub, cols))
            act[pl.ds(r0 + r, sub), n : n + cols] = a.astype(BF16)
            slope[pl.ds(s0 + r, sub), n : n + cols] = s.astype(slope.dtype)


def forward_kernel(
    lens, groups, frames, small_full, upb_full, up_full, down_full, out, act_out, slope, normed_out, inv_out, shaped_out, masked_out,
    masked0, masked1, normed, inv, shaped, first_rows, act, s8, u8, len8, save_sem, act_sem, row_sem, *, ft, taps, group_count,
):
    i = pl.program_id(0)
    clips, frame_count, width = frames.shape
    hidden = act.shape[1]
    tiles = frame_count // ft
    rows = ft * clips

    def up_cols(b):
        return lambda lo, hi: up_full[b, :, lo:hi]

    body = pl.ds(HALO, frame_count)
    save = lambda n, src, dst: pltpu.make_async_copy(src, dst, save_sem.at[n])
    saves0 = [
        save(0, masked0.at[body], masked_out.at[0]), save(1, normed, normed_out.at[0]),
        save(2, inv, inv_out.at[0]), save(3, shaped, shaped_out.at[0]),
    ]
    save_masked1 = save(4, masked1.at[body], masked_out.at[1])
    tail = lambda b, j: pltpu.make_async_copy(
        act.at[pl.ds(pl.multiple_of(j * rows, rows), rows)],
        act_out.at[b, pl.ds(pl.multiple_of(j * rows, rows), rows)], act_sem.at[j])

    def row_saves(j):
        f = pl.ds(j * ft, ft)
        r = pl.ds(pl.multiple_of(j * rows, rows), rows)
        return [
            pltpu.make_async_copy(normed.at[f], normed_out.at[1, f], row_sem.at[0, j]),
            pltpu.make_async_copy(inv.at[f], inv_out.at[1, f], row_sem.at[1, j]),
            pltpu.make_async_copy(shaped.at[r], shaped_out.at[1, r], row_sem.at[2, j]),
        ]

    @pl.when(i == 0)
    def _():
        zeros = jnp.zeros((HALO, clips, width), F32)
        for m in (masked0, masked1):
            m[0:HALO] = zeros
            m[HALO + frame_count :] = zeros
        len8[...] = per_clip(lens, clips, width)

        def spread(n, carry):
            t0 = pl.multiple_of(n * 16, 16)
            v = swap_frames(frames, t0, 16)
            at = pl.multiple_of(t0 * clips, 16 * clips)
            first_rows[pl.ds(at, 16 * clips), :] = v.reshape(16 * clips, width).astype(BF16)
            masked0[pl.ds(HALO + t0, 16)] = keep_frames(v, t0, len8)
            return carry
        lax.fori_loop(0, frame_count // 16, spread, 0)
        for b in range(2):
            prepare(small_full.at[b], lens, groups, s8.at[b], len8, group_count)
            u8[b] = jnp.broadcast_to(upb_full[b, 0:1, :], u8.shape[1:])

        def conv0(n, carry):
            conv_norm(masked0, n * ft, ft, s8.at[0], normed, inv, shaped, taps)
            return carry
        lax.fori_loop(0, tiles, conv0, 0)
        for c in saves0:
            c.start()

    @pl.when(i < tiles)
    def _():
        r0 = pl.multiple_of(i * rows, rows)
        up_gelu(shaped, up_cols(0), u8.at[0], act, r0, slope, 0, rows, hidden)
        tail(0, i).start()

    @pl.when((i >= tiles) & (i < 2 * tiles))
    def _():
        j = i - tiles
        f0 = j * ft
        r0 = pl.multiple_of(j * rows, rows)
        branch = mm(act[pl.ds(r0, rows), :], down_full[0], NN)
        for t in range(0, ft, 4):
            b = branch[t * clips : (t + 4) * clips].reshape(4, clips, width) + s8[0, DOWN_BIAS][None]
            total = masked0[pl.ds(HALO + f0 + t, 4)] + s8[0, GAIN][None] * b
            masked1[pl.ds(HALO + f0 + t, 4)] = keep_frames(total, f0 + t, len8)
        tail(0, j).wait()

    @pl.when(i == 2 * tiles)
    def _():
        for c in saves0:
            c.wait()
        save_masked1.start()

    @pl.when(i >= 2 * tiles)
    def _():
        j = i - 2 * tiles
        f0 = j * ft
        r0 = pl.multiple_of(j * rows, rows)
        conv_norm(masked1, f0, ft, s8.at[1], normed, inv, shaped, taps)
        for c in row_saves(j):
            c.start()
        up_gelu(shaped, up_cols(1), u8.at[1], act, r0, slope, 0, rows, hidden)
        tail(1, j).start()
        branch = mm(act[pl.ds(r0, rows), :], down_full[1], NN)
        last_block(branch, masked1, f0, r0, ft, s8.at[1], len8, first_rows, out)

    @pl.when(i == 3 * tiles - 1)
    def _():
        save_masked1.wait()
        for j in range(tiles):
            tail(1, j).wait()
            for c in row_saves(j):
                c.wait()


def last_block(branch, masked1, f0, r0, ft, s8, len8, first_rows, out, step=16):
    clips, width = len8.shape
    for t in range(0, ft, step):
        b = branch[t * clips : (t + step) * clips].reshape(step, clips, width) + s8[DOWN_BIAS][None]
        total = masked1[pl.ds(HALO + f0 + t, step)] + s8[GAIN][None] * b
        at = pl.multiple_of(r0 + t * clips, step * clips)
        first = first_rows[pl.ds(at, step * clips), :].astype(F32).reshape(step, clips, width)
        out[:, t : t + step, :] = jnp.swapaxes(keep_frames(total, f0 + t, len8, first), 0, 1).astype(BF16)


def forward(lens, groups, frames, weights, hidden, ft, taps, group_count):
    clips, fc, d = frames.shape
    h = hidden
    n, r = fc // ft, ft * clips
    R = fc * clips
    slope_at = lambda i: jnp.where(i < n, i, jnp.where(i < 2 * n, n - 1, i - n))
    return pl.pallas_call(
        functools.partial(forward_kernel, ft=ft, taps=taps, group_count=group_count),
        name="forward",
        grid=(3 * n,),
        in_specs=[smem(), smem(), whole(clips, fc, d)] + [vmem()] * 4,
        out_specs=[
            pl.BlockSpec((clips, ft, d), lambda i: (0, jnp.maximum(i - 2 * n, 0), 0)), hbm(),
            pl.BlockSpec((r, h), lambda i: (slope_at(i), 0)), hbm(), hbm(), hbm(), hbm(),
        ],
        out_shape=[
            shape((clips, fc, d), BF16), shape((2, R, h), BF16), shape((2 * R, h), BF16), shape((2, fc, clips, d)),
            shape((2, fc, clips, LANES)), shape((2, R, d), BF16), shape((2, fc, clips, d)),
        ],
        scratch_shapes=[
            pltpu.VMEM((fc + 2 * HALO, clips, d), F32), pltpu.VMEM((fc + 2 * HALO, clips, d), F32),
            pltpu.VMEM((fc, clips, d), F32), pltpu.VMEM((fc, clips, LANES), F32), pltpu.VMEM((R, d), BF16),
            pltpu.VMEM((R, d), BF16), pltpu.VMEM((R, h), BF16),
            pltpu.VMEM((2, 14, clips, d), F32), pltpu.VMEM((2, clips, h), F32), pltpu.VMEM((clips, d), jnp.int32),
            DMA((5,)), DMA((n,)), DMA((3, n)),
        ],
        compiler_params=pltpu.CompilerParams(vmem_limit_bytes=VMEM_LIMIT),
    )(lens, groups, frames, *weights)


class Scatter:
    def __init__(self, place, term, bufs, sems):
        self.place, self.term = place, term
        self.core_in, self.second_in, self.first_in, self.z_in = bufs
        self.sems = sems

    def line(self, first, second):
        high, low = self.place.chip_of(first, second)
        return self.term.at[:, high, low, self.place.core]

    def spot(self, z, first, second):
        high, low = self.place.chip_of(first, second)
        return (z, high, low)

    def core_copies(self):
        at = self.place
        return [send(self.term.at[:, :, :, 1 - at.core], self.core_in, self.sems[0].at[0], self.sems[1].at[0], at.core_peer())]

    def second_copies(self, p):
        at = self.place
        to = lax.rem(at.second + p, at.side)
        n = (p - 1) * at.side
        return [
            send(self.line(f, to), self.second_in.at[p - 1, f], self.sems[2].at[n + f], self.sems[3].at[n + f], at.second_peer(p))
            for f in range(at.side)
        ]

    def first_copy(self, p):
        at = self.place
        to = lax.rem(at.first + p, at.side)
        return send(self.line(to, at.second), self.first_in.at[p - 1], self.sems[4].at[p - 1], self.sems[5].at[p - 1], at.first_peer(p))

    def z_copy(self, p):
        at = self.place
        to = lax.rem(at.z + p, at.deep)
        high, low = at.chip_of(at.first, at.second)
        return send(self.term.at[to, high, low, at.core], self.z_in.at[p - 1], self.sems[6].at[p - 1], self.sems[7].at[p - 1], at.z_peer(p))

    def part1(self, z, first, second):
        z, high, low = self.spot(z, first, second)
        return self.term[z, high, low, self.place.core].astype(F32) + self.core_in[z, high, low].astype(F32)

    def part2(self, z, first):
        total = self.part1(z, first, self.place.second)
        for p in range(1, self.place.side):
            total = total + self.second_in[p - 1, first, z].astype(F32)
        return total

    def part3(self, z):
        total = self.part2(z, self.place.first)
        for p in range(1, self.place.side):
            total = total + self.first_in[p - 1, z].astype(F32)
        return total

    def put(self, z, first, second, total):
        z, high, low = self.spot(z, first, second)
        self.term[z, high, low, self.place.core] = total.astype(BF16)

    def core_start(self):
        run(self.core_copies())

    def second_start(self):
        at = self.place
        done(self.core_copies())
        for p in range(1, at.side):
            to = lax.rem(at.second + p, at.side)
            copies = self.second_copies(p)
            for first in range(at.side):
                def one(z, carry):
                    self.put(z, first, to, self.part1(z, first, to))
                    return carry
                lax.fori_loop(0, at.deep, one, 0)
                copies[first].start()

    def first_start(self):
        at = self.place
        for p in range(1, at.side):
            done(self.second_copies(p))
        for p in range(1, at.side):
            to = lax.rem(at.first + p, at.side)
            def one(z, carry):
                self.put(z, to, at.second, self.part2(z, to))
                return carry
            lax.fori_loop(0, at.deep, one, 0)
            self.first_copy(p).start()

    def z_start(self):
        at = self.place
        done([self.first_copy(p) for p in range(1, at.side)])
        for p in range(1, at.deep):
            to = lax.rem(at.z + p, at.deep)
            self.put(to, at.first, at.second, self.part3(to))
            self.z_copy(p).start()

    def finish(self, out):
        at = self.place
        done([self.z_copy(p) for p in range(1, at.deep)])
        total = self.part3(at.z)
        for p in range(1, at.deep):
            total = total + self.z_in[p - 1].astype(F32)
        out[...] = total


def scatter_bufs(deep, side, rows, cols):
    v = lambda *lead: pltpu.VMEM(lead + (rows, cols), BF16)
    return [v(deep, side, side), v(side - 1, side, deep), v(side - 1, deep), v(deep - 1)]


def scatter_sems(count, deep, side):
    return [DMA((count, n)) for n in (1, 1, side * (side - 1), side * (side - 1), side - 1, side - 1, deep - 1, deep - 1)]


def pack_small(small, upb, b, terms, deep):
    per = upb.shape[1] // deep
    o = b * PACK
    for z in range(deep):
        terms[z, o : o + 14, :] = small[0:14, z * LANES : (z + 1) * LANES]
        for q in range(per // LANES):
            at = z * per + q * LANES
            terms[z, o + 14 + q : o + 15 + q, :] = upb[:, at : at + LANES]


def sum_small(place, terms, z_in, bufs, out, s, r):
    n = 0
    copies = []
    for p in range(1, place.deep):
        to = lax.rem(place.z + p, place.deep)
        copies.append(send(terms.at[to], z_in.at[p - 1], s.at[n], r.at[n], place.z_peer(p)))
        n += 1
    run(copies)
    yield
    done(copies)
    total = terms[place.z]
    for p in range(1, place.deep):
        total = total + z_in[p - 1]
    stages = [[place.core_peer()], [place.second_peer(p) for p in range(1, place.side)],
              [place.first_peer(p) for p in range(1, place.side)]]
    for (here, into), peers in zip(bufs, stages):
        here[...] = total
        copies = []
        for p, peer in enumerate(peers):
            copies.append(send(here, into.at[p], s.at[n], r.at[n], peer))
            n += 1
        run(copies)
        yield
        done(copies)
        for p in range(len(peers)):
            total = total + into[p]
    out[...] = total


def small_bufs(deep, side):
    many = lambda *n: pltpu.VMEM(n + (2 * PACK, LANES), F32)
    n = deep - 1 + 2 * (side - 1) + 1
    return [many(deep), many(deep - 1), many(), many(1), many(), many(side - 1), many(), many(side - 1), DMA((n,)), DMA((n,))]


class Sums:
    def __init__(self, refs, up_term, down_term, up_part, down_part, small_part, small_grad, upb_grad, deep, side, parts):
        self.place = Place(deep, side)
        self.terms, self.z_in = refs[:2]
        self.bufs = [refs[2:4], refs[4:6], refs[6:8]]
        self.small_s, self.small_r = refs[8:10]
        refs = refs[10:]
        sems = refs[-8:]
        self.small_part, self.small_grad, self.upb_grad = small_part, small_grad, upb_grad
        self.parts = parts
        cols = up_part.shape[2] // parts
        self.jobs = []
        for b in (1, 0):
            views = []
            for p in range(parts):
                c = pl.ds(p * cols, cols)
                views.append((up_term.at[b, :, :, :, :, :, c], up_part.at[b, :, c]))
            views.append((down_term.at[b], down_part.at[b]))
            for term, out in views:
                n = len(self.jobs)
                self.jobs.append((Scatter(self.place, term, refs[4 * n : 4 * n + 4], [s.at[n] for s in sems]), out))

    def do(self, n, what):
        job, out = self.jobs[n]
        if what == "finish":
            job.finish(out)
        else:
            getattr(job, what)()

    def at(self, i, half, span):
        parts, per = self.parts, self.parts + 1
        whats = ("core_start", "second_start", "first_start", "z_start", "finish")
        when = []
        top = 2 * parts
        for p in range(parts - 1):
            t = 2 * (p + 1)
            when.append((t, t + 1, t + 3 if p < parts - 2 else top + 3, top + 3 if p < parts - 2 else top + 6, top + 9))
        when.append((top, top + 3, top + 6, top + 9, top + 12))
        when.append((top, top + 3, top + 10, top + 13, top + 16))
        plan = []
        for order, what in enumerate(whats):
            for n in range(2 * per):
                slot = when[n % per][order] + 2 * span * (n // per)
                if slot < 4 * span and slot % 2 == half:
                    plan.append((slot // 2, n, what))
        for now in sorted({p[0] for p in plan}):
            @pl.when(i == now)
            def _():
                for step, n, what in plan:
                    if step == now:
                        self.do(n, what)

    def after(self, i, span):
        @pl.when(i == 2 * span - 1)
        def _():
            self.terms[...] = jnp.zeros(self.terms.shape, F32)
            for b in range(2):
                pack_small(self.small_grad.at[b], self.upb_grad.at[b], b, self.terms, self.place.deep)
            steps = sum_small(self.place, self.terms, self.z_in, self.bufs, self.small_part, self.small_s, self.small_r)
            last = 2 * (self.parts + 1) - 1
            next(steps)
            self.do(last, "first_start")
            next(steps)
            self.do(last - 1, "finish")
            next(steps)
            self.do(last, "z_start")
            next(steps)
            self.do(last, "finish")
            for _ in steps:
                pass


def sums_scratch(deep, side, urows, drows, d, h, parts):
    ub, db = scatter_bufs(deep, side, urows, h // parts), scatter_bufs(deep, side, drows, d)
    return small_bufs(deep, side) + 2 * (parts * ub + db) + scatter_sems(2 * (parts + 1), deep, side)


def norm_back(gs, normed, n0, inv, i0, s8, gm, gm0, acc, frames, step=4):
    clips, width = s8.shape[1:]
    a_scale, a_shift, a_bias = acc[A_SCALE], acc[A_SHIFT], acc[A_BIAS]
    for j in range(0, frames, step):
        g = gs[j * clips : (j + step) * clips].reshape(step, clips, width)
        norm = normed[pl.ds(n0 + j, step)]
        gn = g * norm
        a_scale = a_scale + fold(gn)
        a_shift = a_shift + fold(g)
        gg = g * s8[SCALE][None]
        mean = jnp.mean(gg, axis=-1, keepdims=True)
        mean_norm = jnp.mean(gn * s8[SCALE][None], axis=-1, keepdims=True)
        inv_std = jnp.concatenate([inv[pl.ds(i0 + j, step)]] * (width // LANES), axis=-1)
        grad = inv_std * (gg - mean - norm * mean_norm)
        a_bias = a_bias + fold(grad)
        gm[pl.ds(gm0 + j, step)] = grad
    acc[A_SCALE], acc[A_SHIFT], acc[A_BIAS] = a_scale, a_shift, a_bias


def conv_back(gm, gm0, s8, masked, m0, gs, g0, t0, out, acc, frames, len8, taps, step=8):
    clips, width = len8.shape
    half = taps // 2
    for l in range(width // LANES):
        cols = slice(l * LANES, (l + 1) * LANES)
        sums = [acc[A_TAPS + k, :, cols] for k in range(taps)]
        for j in range(0, frames, step):
            here = masked[pl.ds(m0 + j, step), :, cols]
            total = None
            for k in range(taps):
                piece = gm[pl.ds(gm0 + j + half - k, step), :, cols]
                term = s8[TAPS + k, :, cols][None] * piece
                total = term if total is None else total + term
                sums[k] = sums[k] + fold(piece * here)
            t = lax.broadcasted_iota(jnp.int32, total.shape, 0) + (t0 + j)
            total = jnp.where(t < len8[:, cols][None], total, 0.0)
            total = gs[pl.ds(g0 + j, step), :, cols] + total
            gs[pl.ds(g0 + j, step), :, cols] = total
            if out is not None:
                out[j : j + step, :, cols] = total
        for k in range(taps):
            acc[A_TAPS + k, :, cols] = sums[k]


def finish_small(acc, upb_acc, groups, s8, small_grad, upb_grad, group_count):
    clips, width = acc.shape[1:]
    member = per_clip(groups, clips, width)
    line = lambda v: jnp.sum(v, axis=0, keepdims=True)
    rows = [line(acc[A_TAPS + k]) for k in range(7)]
    rows.append(line(acc[A_BIAS]))
    for base in (A_SCALE, A_SHIFT):
        for g in range(group_count):
            rows.append(line(jnp.where(member == g, acc[base], 0.0)))
    rows.append(line(acc[A_DOWN]))
    rows.append(line((acc[A_GAIN] + s8[DOWN_BIAS] * acc[A_DOWN]) / s8[GAIN]))
    for r, row in enumerate(rows):
        small_grad[r : r + 1, :] = row
    for r in range(len(rows), small_grad.shape[0]):
        small_grad[r : r + 1, :] = jnp.zeros((1, width), F32)
    upb_grad[...] = line(upb_acc[...])


def backward_kernel(
    lens, groups, og, act, slope, normed, inv, shaped, masked, up, down, small, gs_out, dup, ddown, small_grad, upb_grad,
    gs, gb, gbef, gm, s8, len8, acc, upb_acc, *, ft, tiles, parts, taps, group_count,
):
    i = pl.program_id(0)
    frame_count, clips, width = gs.shape
    hidden = gbef.shape[1]
    cols = hidden // parts
    rows = ft * clips
    total_rows = frame_count * clips
    base = 2 * ft
    span = parts + tiles + 2
    step = lax.rem(i, span)
    b = 1 - i // span

    @pl.when(step == 0)
    def _():
        prepare(small.at[b], lens, groups, s8, len8, group_count)
        acc[...] = jnp.zeros(acc.shape, F32)

    @pl.when(i == 0)
    def _():
        gm[pl.ds(0, base)] = jnp.zeros((base, clips, width), F32)
        gm[pl.ds(base + frame_count, HALO)] = jnp.zeros((HALO, clips, width), F32)
        spread_grad(og, gs, 0)

    @pl.when(step == 0)
    def _():
        acc[A_DOWN] = branch_grad(gs, 0, s8, len8, gb)

    @pl.when(step < parts)
    def _():
        c0 = pl.multiple_of(step * cols, cols)
        at = pl.ds(c0, cols)
        lower = down[0, at, :]
        term = mm(act[0], gb[...], TN)
        ddown[b, at, :] = term
        acc[A_GAIN] += fold((term * lower.astype(F32)).reshape(cols // 8, 8, width))
        before_grad(gb, lower, slope.at[0], slice(None), gbef, at, upb_acc, total_rows)
        dup[b, :, at] = mm(shaped[0], gbef[:, at], TN)

    j = step - parts

    @pl.when((j >= 0) & (j < tiles))
    def _():
        r0 = pl.multiple_of(j * rows, rows)
        grad = mm(gbef[pl.ds(r0, rows), :], up[0], NT)
        norm_back(grad, normed.at[0], 0, inv.at[0], 0, s8, gm, base + j * ft, acc, ft)

    @pl.when(j >= 2)
    def _():
        f0 = (j - 2) * ft
        conv_back(gm, base + f0, s8, masked.at[0], 0, gs, f0, f0, gs_out, acc, ft, len8, taps)

    @pl.when(step == span - 1)
    def _():
        finish_small(acc, upb_acc, groups, s8, small_grad.at[b], upb_grad.at[b], group_count)


def spread_grad(og, gs, g0):
    def one(n, carry):
        t0 = pl.multiple_of(n * 16, 16)
        gs[pl.ds(g0 + t0, 16)] = swap_frames(og, t0, 16)
        return carry
    lax.fori_loop(0, og.shape[1] // 16, one, 0)


def branch_grad(gs, g0, s8, len8, gb):
    clips, width = len8.shape
    frame_count = gb.shape[0] // clips

    def one(n, a_down):
        t0 = n * 4
        gvb = s8[GAIN][None] * keep_frames(gs[pl.ds(g0 + t0, 4)], t0, len8)
        at = pl.multiple_of(t0 * clips, 4 * clips)
        gb[pl.ds(at, 4 * clips), :] = gvb.reshape(4 * clips, width).astype(BF16)
        return a_down + fold(gvb)
    return lax.fori_loop(0, frame_count // 4, one, jnp.zeros((clips, width), F32), unroll=4)


def before_grad(gb, lower, slope, slope_cols, gbef, at, upb_acc, rows, chunk=1024, sub=16):
    cols = lower.shape[0]
    total = jnp.zeros((8, cols), F32)
    for c in range(0, rows, chunk):
        ga = mm(gb[c : c + chunk, :], lower, NT)
        for r in range(0, chunk, sub):
            gr = ga[r : r + sub] * slope[c + r : c + r + sub, slope_cols].astype(F32)
            total = total + fold(gr.reshape(sub // 8, 8, cols))
            gbef[c + r : c + r + sub, at] = gr.astype(BF16)
    upb_acc[:, at] = total


def backward(lens, groups, og, saved, ups, downs, small, ft, taps, group_count):
    act, slope, normed, inv, shaped, masked = saved
    clips, fc, d = og.shape
    h = ups.shape[2]
    R, r, n = fc * clips, ft * clips, fc // ft
    parts = 6
    cols = h // parts
    span = parts + n + 2
    block = lambda i: 1 - i // span
    part = lambda i: jnp.minimum(lax.rem(i, span), parts - 1)
    tile = lambda i: jnp.clip(lax.rem(i, span) - parts, 0, n - 1)
    late = lambda i: jnp.clip(lax.rem(i, span) - parts - 2, 0, n - 1)
    last = lambda i: jnp.clip(i - span - parts - 2, 0, n - 1)
    sums = [(2, d, h), (2, h, d), (2, ROWS, d), (2, 1, h)]
    return pl.pallas_call(
        functools.partial(backward_kernel, ft=ft, tiles=n, parts=parts, taps=taps, group_count=group_count),
        name="backward",
        grid=(2 * span,),
        in_specs=[
            smem(), smem(), whole(clips, fc, d),
            pl.BlockSpec((1, R, cols), lambda i: (block(i), 0, part(i))),
            pl.BlockSpec((1, R, cols), lambda i: (block(i), 0, part(i))),
            pl.BlockSpec((1, ft, clips, d), lambda i: (block(i), tile(i), 0, 0)),
            pl.BlockSpec((1, ft, clips, LANES), lambda i: (block(i), tile(i), 0, 0)),
            pl.BlockSpec((1, R, d), lambda i: (block(i), 0, 0), pipeline_mode=pl.Buffered(1)),
            pl.BlockSpec((1, ft, clips, d), lambda i: (block(i), late(i), 0, 0)),
            pl.BlockSpec((1, d, h), lambda i: (block(i), 0, 0)),
            pl.BlockSpec((1, h, d), lambda i: (block(i), 0, 0)),
            whole(2, ROWS, d),
        ],
        out_specs=[pl.BlockSpec((ft, clips, d), lambda i: (last(i), 0, 0))] + [whole(*v) for v in sums],
        out_shape=[shape((fc, clips, d))] + [shape(v) for v in sums],
        scratch_shapes=[
            pltpu.VMEM((fc, clips, d), F32), pltpu.VMEM((R, d), BF16), pltpu.VMEM((R, h), BF16),
            pltpu.VMEM((fc + 2 * ft + HALO, clips, d), F32),
            pltpu.VMEM((14, clips, d), F32), pltpu.VMEM((clips, d), jnp.int32),
            pltpu.VMEM((12, clips, d), F32), pltpu.VMEM((clips, h), F32),
        ],
        compiler_params=pltpu.CompilerParams(vmem_limit_bytes=VMEM_LIMIT),
    )(lens, groups, og, act, slope, normed, inv, shaped, masked, ups, downs, small)


def step_kernel(*refs, deep, side, ft, parts, taps, group_count):
    lens, groups, frames, og = refs[:4]
    shards = refs[4:13]
    out, gs_out, up_part, down_part, small_part, act_far, slope_far = refs[13:20]
    (io, masked0, masked1, normed, inv, shaped, first_rows, act, slope, gb, s8, u8, len8, acc, upb_acc) = refs[20:35]
    small_full, upb_full, small_grad, upb_grad, up_full, down_full, up_term, down_term = refs[35:43]
    io_sem, act_sem, slope_sem, act_back_sem, slope_back_sem, gs_sem = refs[43:49]
    gather_refs, sum_refs = refs[49:67], refs[67:]

    i = pl.program_id(0)
    clips, frame_count, width = io.shape
    hidden = act.shape[1]
    tiles = frame_count // ft
    rows = ft * clips
    cols = hidden // parts
    span = parts + tiles + 1
    body = pl.ds(HALO, frame_count)

    load = lambda n, src: pltpu.make_async_copy(src, io, io_sem.at[n])
    tile_rows = lambda j: pl.ds(pl.multiple_of(j * rows, rows), rows)
    part_at = lambda p: pl.ds(pl.multiple_of(p * cols, cols), cols)

    def spills(j):
        r = tile_rows(j)
        return [
            pltpu.make_async_copy(act.at[r], act_far.at[r], act_sem.at[j]),
            pltpu.make_async_copy(slope.at[r], slope_far.at[r], slope_sem.at[j]),
        ]

    def act_back(p):
        return pltpu.make_async_copy(act_far.at[:, part_at(p)], act.at[:, part_at(p)], act_back_sem.at[p])

    def slope_back(j):
        return pltpu.make_async_copy(slope_far.at[tile_rows(j)], slope.at[tile_rows(j)], slope_back_sem.at[j])

    def up_cols(b):
        return lambda lo, hi: up_full[b, :, :, :, :, :, lo:hi].reshape(width, hi - lo)

    def spread():
        load(0, frames).wait()

        def one(n, carry):
            t0 = pl.multiple_of(n * 16, 16)
            v = swap_frames(io, t0, 16)
            at = pl.multiple_of(t0 * clips, 16 * clips)
            first_rows[pl.ds(at, 16 * clips), :] = v.reshape(16 * clips, width).astype(BF16)
            masked0[pl.ds(HALO + t0, 16)] = keep_frames(v, t0, len8)
            return carry
        lax.fori_loop(0, frame_count // 16, one, 0)
        load(1, og).start()

    def conv0(lo, hi):
        def one(n, carry):
            conv_norm(masked0, n * ft, ft, s8.at[0], normed.at[0], inv.at[0], shaped, taps, HALO)
            return carry
        lax.fori_loop(lo, hi, one, 0)

    def ready():
        for b in range(2):
            prepare(small_full.at[b], lens, groups, s8.at[b], len8, group_count)
            u8[b] = jnp.broadcast_to(upb_full[b, 0:1, :], u8.shape[1:])

    @pl.when(i == 0)
    def _():
        load(0, frames).start()
        zeros = jnp.zeros((HALO, clips, width), F32)
        for m in (masked0, masked1, normed.at[0], normed.at[1]):
            m[0:HALO] = zeros
            m[HALO + frame_count : HALO + frame_count + HALO] = zeros
        len8[...] = per_clip(lens, clips, width)
        Gather(shards, up_full, down_full, small_full, upb_full, gather_refs, deep, side, group_count, taps).early(
            spread, ready, conv0, tiles)

    Gather(shards, up_full, down_full, small_full, upb_full, gather_refs, deep, side, group_count, taps).late(i, tiles)

    @pl.when(i < tiles)
    def _():
        r0 = pl.multiple_of(i * rows, rows)
        up_gelu(shaped, up_cols(0), u8.at[0], act, r0, slope, r0, rows, hidden)
        run(spills(i))

    @pl.when((i >= tiles) & (i < 2 * tiles))
    def _():
        j = i - tiles
        f0 = j * ft
        r0 = pl.multiple_of(j * rows, rows)
        branch = mm(act[pl.ds(r0, rows), :], down_full[0].reshape(hidden, width), NN)
        for t in range(0, ft, 4):
            b = branch[t * clips : (t + 4) * clips].reshape(4, clips, width) + s8[0, DOWN_BIAS][None]
            total = masked0[pl.ds(HALO + f0 + t, 4)] + s8[0, GAIN][None] * b
            masked1[pl.ds(HALO + f0 + t, 4)] = keep_frames(total, f0 + t, len8)

    @pl.when((i >= 2 * tiles) & (i < 3 * tiles))
    def _():
        j = i - 2 * tiles
        f0 = j * ft
        r0 = pl.multiple_of(j * rows, rows)
        done(spills(j))
        conv_norm(masked1, f0, ft, s8.at[1], normed.at[1], inv.at[1], shaped, taps, HALO)
        up_gelu(shaped, up_cols(1), u8.at[1], act, r0, slope, r0, rows, hidden)
        branch = mm(act[pl.ds(r0, rows), :], down_full[1].reshape(hidden, width), NN)
        last_block(branch, masked1, f0, r0, ft, s8.at[1], len8, first_rows, out)

    k = i - 3 * tiles
    step = lax.rem(jnp.maximum(k, 0), span)
    b = jnp.where(k < span, 1, 0)

    @pl.when(k == 0)
    def _():
        load(1, og).wait()
        spread_grad(io, masked0, HALO)

    @pl.when(k == span)
    def _():
        def one(n, carry):
            t0 = n * 4
            at = pl.multiple_of(t0 * clips, 4 * clips)
            v = normed[0, pl.ds(HALO + t0, 4)] * s8[0, SCALE][None] + s8[0, SHIFT][None]
            shaped[pl.ds(at, 4 * clips), :] = v.reshape(4 * clips, width).astype(BF16)
            first = first_rows[pl.ds(at, 4 * clips), :].astype(F32).reshape(4, clips, width)
            masked1[pl.ds(HALO + t0, 4)] = keep_frames(first, t0, len8)
            return carry
        lax.fori_loop(0, frame_count // 4, one, 0, unroll=4)
        for j in range(tiles):
            slope_back(j).wait()

    @pl.when((k >= 0) & (step == 0))
    def _():
        acc[...] = jnp.zeros(acc.shape, F32)
        acc[A_DOWN] = branch_grad(masked0, HALO, s8.at[b], len8, gb)

    sums = Sums(sum_refs, up_term, down_term, up_part, down_part, small_part, small_grad, upb_grad, deep, side, parts)
    sums.at(k, 0, span)

    @pl.when((k >= span) & (step < parts))
    def _():
        act_back(step).wait()

    @pl.when((k >= 0) & (step < parts))
    def _():
        at = part_at(step)
        drows, urows = down_full.shape[5], up_full.shape[5]
        per = drows // 16
        spots = []
        for m in range(cols // 16):
            row = step * (cols // 16) + m
            e = row // per
            z, chip = e // (2 * side * side), e // 2
            sub = pl.ds(pl.multiple_of((row - e * per) * 16, 16), 16)
            spots.append((b, z, lax.rem(chip // side, side), lax.rem(chip, side), lax.rem(e, 2), sub))
        lower = jnp.concatenate([down_full[spot] for spot in spots], axis=0)
        term = mm(act[:, at], gb[...], TN)
        for m, spot in enumerate(spots):
            down_term[spot] = term[m * 16 : (m + 1) * 16].astype(BF16)
        acc[A_GAIN] += fold((term * lower.astype(F32)).reshape(cols // 8, 8, width))
        before_grad(gb, lower, slope, at, slope, at, upb_acc, frame_count * clips)
        term = mm(shaped[...], slope[:, at], TN).astype(BF16)
        up_term[b, :, :, :, :, :, at] = term.reshape(deep, side, side, 2, urows, cols)

    @pl.when((k >= 0) & (k < parts))
    def _():
        act_back(step).start()

    j = step - parts

    @pl.when((j >= 0) & (j < tiles))
    def _():
        r0 = pl.multiple_of(j * rows, rows)
        grad = mm(slope[pl.ds(r0, rows), :], up_full[b].reshape(width, hidden), NT)
        norm_back(grad, normed.at[b], HALO + j * ft, inv.at[b], j * ft, s8.at[b], normed.at[b], HALO + j * ft, acc, ft)

    @pl.when((k < span) & (j >= 0) & (j < tiles))
    def _():
        slope_back(j).start()

    sums.at(k, 1, span)
    gs_copy = lambda f0, n: pltpu.make_async_copy(masked0.at[pl.ds(HALO + f0, ft)], gs_out.at[pl.ds(f0, ft)], gs_sem.at[n])

    @pl.when(j >= 1)
    def _():
        f0 = (j - 1) * ft
        conv_back(
            normed.at[b], HALO + f0, s8.at[b], masked1, HALO + f0, masked0, HALO + f0, f0, None, acc, ft, len8, taps)

    @pl.when((k >= span) & (j >= 1))
    def _():
        gs_copy((j - 1) * ft, j - 1).start()

    @pl.when((k >= 0) & (step == span - 1))
    def _():
        finish_small(acc, upb_acc, groups, s8.at[b], small_grad.at[b], upb_grad.at[b], group_count)

    sums.after(k, span)

    @pl.when(k == 2 * span - 1)
    def _():
        for n in range(tiles):
            gs_copy(n * ft, n).wait()


def whole_step(deep, side, lens, groups, frames, og, weights, ft, taps, group_count):
    clips, fc, d = frames.shape
    h = weights[4].shape[2]
    urows, drows = weights[4].shape[1], weights[6].shape[1]
    R, r, n = fc * clips, ft * clips, fc // ft
    parts = 3
    span = parts + n + 1
    dims = (2, deep, side, side, 2)
    rows = lambda dtype, *lead: pltpu.VMEM(lead + (d,), dtype)
    halo = fc + 2 * HALO
    return pl.pallas_call(
        functools.partial(step_kernel, deep=deep, side=side, ft=ft, parts=parts, taps=taps, group_count=group_count),
        name="step",
        grid=(3 * n + 2 * span,),
        in_specs=[smem(), smem(), hbm(), hbm()] + [vmem()] * 9,
        out_specs=[
            pl.BlockSpec((clips, ft, d), lambda i: (0, jnp.clip(i - 2 * n, 0, n - 1), 0)),
            hbm(), vmem(), vmem(), vmem(), hbm(), hbm(),
        ],
        out_shape=[
            shape((clips, fc, d), BF16), shape((fc, clips, d)), shape((2, urows, h)), shape((2, drows, d)),
            shape((2 * PACK, LANES)), shape((R, h), BF16), shape((R, h), BF16),
        ],
        scratch_shapes=[
            rows(BF16, clips, fc),
            rows(F32, halo, clips), rows(F32, halo, clips), rows(F32, 2, halo, clips), pltpu.VMEM((2, fc, clips, LANES), F32),
            rows(BF16, R), rows(BF16, R), pltpu.VMEM((R, h), BF16), pltpu.VMEM((R, h), BF16), rows(BF16, R),
            rows(F32, 2, 14, clips), pltpu.VMEM((2, clips, h), F32), rows(jnp.int32, clips), rows(F32, 12, clips),
            pltpu.VMEM((clips, h), F32),
            rows(F32, 2, ROWS), pltpu.VMEM((2, 1, h), F32), rows(F32, 2, ROWS), pltpu.VMEM((2, 1, h), F32),
            pltpu.VMEM(dims + (urows, h), BF16), rows(BF16, *dims, drows), pltpu.VMEM(dims + (urows, h), BF16), rows(BF16, *dims, drows),
            DMA((2,)), DMA((n,)), DMA((n,)), DMA((parts,)), DMA((n,)), DMA((n,)),
        ] + gather_scratch(deep, side) + sums_scratch(deep, side, urows, drows, d, h, parts),
        compiler_params=pltpu.CompilerParams(vmem_limit_bytes=VMEM_LIMIT, collective_id=0, has_side_effects=True),
    )(lens, groups, frames, og, *weights)


def swap_rows(src, dst):
    for t in range(0, src.shape[0], 8):
        dst[:, t : t + 8, :] = jnp.swapaxes(src[t : t + 8], 0, 1)


def unpack_kernel(gs, up_in, down_in, small, gin, conv_w, conv_b, scale, shift, up_w, up_b, down_w, down_b, gain):
    swap_rows(gs, gin)

    @pl.when(pl.program_id(0) == 0)
    def _():
        unpack_parts(up_in, down_in, small, conv_w, conv_b, scale, shift, up_w, up_b, down_w, down_b, gain)


def unpack_parts(up_in, down_in, small, conv_w, conv_b, scale, shift, up_w, up_b, down_w, down_b, gain):
    f = lax.axis_index("fsdp")
    width = conv_b.shape[1]
    wide = up_b.shape[1]
    span = wide * LANES // width
    turned = pltpu.roll(small[...], lax.rem(LANES - f * width, LANES), 1)
    for b in range(2):
        o = b * PACK
        for k in range(conv_w.shape[0]):
            conv_w[k, b : b + 1, :] = turned[o + k : o + k + 1, :width]
        conv_b[b : b + 1, :] = turned[o + CONV_BIAS : o + CONV_BIAS + 1, :width]
        scale[b] = turned[o + SCALE : o + SCALE + scale.shape[1], :width]
        shift[b] = turned[o + SHIFT : o + SHIFT + shift.shape[1], :width]
        down_b[b : b + 1, :] = turned[o + DOWN_BIAS : o + DOWN_BIAS + 1, :width]
        gain[b : b + 1, :] = turned[o + GAIN : o + GAIN + 1, :width]
        bias = jnp.concatenate([small[o + 14 + q : o + 15 + q, :] for q in range(span // LANES)], axis=1)
        bias = pltpu.roll(jnp.broadcast_to(bias, (8, span)), lax.rem(span - f * wide, span), 1)
        up_b[b : b + 1, :] = bias[0:1, :wide]
    up_w[...] = up_in[...]
    down_w[...] = down_in[...]


def unpack_far(gs):
    fc, clips, d = gs.shape
    ft = 64
    return pl.pallas_call(
        swap_rows,
        name="unpack",
        grid=(fc // ft,),
        in_specs=[pl.BlockSpec((ft, clips, d), lambda i: (i, 0, 0))],
        out_specs=pl.BlockSpec((clips, ft, d), lambda i: (0, i, 0)),
        out_shape=shape((clips, fc, d)),
    )(gs)


def unpack(gs, parts, taps, group_count, width, wide):
    fc, clips, d = gs.shape
    ft = 64
    up_in, down_in, small = parts
    outs = [(taps, 2, width), (2, width), (2, group_count, width), (2, group_count, width), up_in.shape, (2, wide),
            down_in.shape, (2, width), (2, width)]
    return pl.pallas_call(
        unpack_kernel,
        name="unpack",
        grid=(fc // ft,),
        in_specs=[pl.BlockSpec((ft, clips, d), lambda i: (i, 0, 0))] + [whole(*v.shape) for v in parts],
        out_specs=[pl.BlockSpec((clips, ft, d), lambda i: (0, i, 0))] + [whole(*v) for v in outs],
        out_shape=[shape((clips, fc, d))] + [shape(v) for v in outs],
    )(gs, up_in, down_in, small)


def body(deep, fan, frames, group, lengths, conv_w, conv_b, scale, shift, up_w, up_b, down_w, down_b, gain, out_grad):
    side = math.isqrt(fan // 2)
    clips = frames.shape[0]
    taps, group_count, hidden = conv_w.shape[1], scale.shape[1], up_w.shape[2]
    width, wide = conv_b.shape[1], up_b.shape[1]
    axes = ("dp", "fsdp")
    near = width * fan == LANES and up_w.shape[1] % 16 == 0 and down_w.shape[1] % 16 == 0
    ft = 32
    if near:
        weights = (conv_w.transpose(1, 0, 2), conv_b, scale, shift, up_w, up_b, down_w, down_b, gain)
    else:
        whole_of = lambda v, axis: lax.all_gather(v, axes, axis=axis, tiled=True)
        ups, downs = whole_of(up_w, 1), whole_of(down_w, 1)
        lines = jnp.concatenate(
            [conv_w, conv_b[:, None], scale, shift, down_b[:, None], gain[:, None], jnp.zeros((2, 2, width), BF16)], axis=1
        )
        small = whole_of(lines, 2).astype(F32)
        upb = whole_of(up_b, 1).astype(F32)[:, None]
        weights = (small, upb, ups, downs)
    if near:
        out, gs, *parts, _, _ = whole_step(deep, side, lengths, group, frames, out_grad, weights, 64, taps, group_count)
        gin, conv_grad, *grads = unpack(gs, parts, taps, group_count, width, wide)
        return (out, gin, conv_grad.transpose(1, 0, 2), *grads)
    out, act, slope, *rest = forward(lengths, group, frames, weights, hidden, ft, taps, group_count)
    saved = (act, slope.reshape(act.shape), *rest)
    gs, *parts = backward(lengths, group, out_grad, saved, ups, downs, small, ft, taps, group_count)
    gin = unpack_far(gs)
    dup, ddown, lines, ug = parts
    owner = lambda v, axis: lax.psum_scatter(v, axes, scatter_dimension=axis, tiled=True)
    lines = owner(lines, 2)
    return (
        out, gin, lines[:, :taps], lines[:, CONV_BIAS], lines[:, SCALE : SCALE + group_count],
        lines[:, SHIFT : SHIFT + group_count], owner(dup, 1), owner(ug[:, 0], 1), owner(ddown, 1),
        lines[:, DOWN_BIAS], lines[:, GAIN],
    )


def solution(mesh):
    split = ("dp", "fsdp")
    clip = P(split, None, None)
    first, middle, last = P(None, split), P(None, split, None), P(None, None, split)
    in_specs = (clip, P(split), P(split), last, first, last, last, middle, first, middle, first, first, clip)
    out_specs = (clip, clip, last, first, last, last, middle, first, middle, first, first)
    run = functools.partial(body, mesh.shape["dp"], mesh.shape["fsdp"])
    return jax.shard_map(run, mesh=mesh, in_specs=in_specs, out_specs=out_specs, check_vma=False)
```

```python
import functools
import math
import jax
import jax.numpy as jnp
from jax import lax
from jax.experimental import pallas as pl
from jax.experimental.pallas import tpu as pltpu
from jax.sharding import PartitionSpec as P

F32 = jnp.float32
BF16 = jnp.bfloat16
EPSILON = 1e-06
TAPS, CONV_BIAS, SCALE, SHIFT, DOWN_BIAS, GAIN, ROWS = 0, 7, 8, 10, 12, 13, 16
A_TAPS, A_BIAS, A_SCALE, A_SHIFT, A_DOWN, A_GAIN = 0, 7, 8, 9, 10, 11
HALO = 3
LANES = 128
VMEM_LIMIT = 64 * 1024 * 1024 - 128 * 1024
NN = (((1,), (0,)), ((), ()))
NT = (((1,), (1,)), ((), ()))
TN = (((0,), (0,)), ((), ()))
DMA = pltpu.SemaphoreType.DMA


def mm(a, b, dims):
    return lax.dot_general(a, b, dims, preferred_element_type=F32)


def gelu_pair(before):
    u = before * math.sqrt(0.5)
    phi = 0.5 + 0.5 * lax.erf(u)
    bell = jnp.exp2(u * u * (-math.log2(math.e))) * (1.0 / math.sqrt(math.pi))
    return before * phi, phi + u * bell


def per_clip(values, clips, width):
    rows = lax.broadcasted_iota(jnp.int32, (clips, width), 0)
    out = jnp.zeros((clips, width), jnp.int32)
    for c in range(clips):
        out = jnp.where(rows == c, values[c], out)
    return out


def prepare(small, lens, groups, s8, len8, group_count):
    clips, width = len8.shape
    for r in range(14):
        s8[r] = jnp.broadcast_to(small[r : r + 1, :], (clips, width))
    member = per_clip(groups, clips, width)
    len8[...] = per_clip(lens, clips, width)
    gain = jnp.zeros((clips, width), F32)
    shift = jnp.zeros((clips, width), F32)
    for g in range(group_count):
        chosen = jnp.where(member == g, 1.0, 0.0)
        gain = gain + chosen * s8[SCALE + g]
        shift = shift + chosen * s8[SHIFT + g]
    s8[SCALE] = gain
    s8[SHIFT] = shift


def keep_frames(v, t0, len8, other=0.0):
    t = lax.broadcasted_iota(jnp.int32, v.shape, 0) + t0
    return jnp.where(t < len8[...][None], v, other)


def swap_frames(block, t0, frames):
    return jnp.swapaxes(block[:, pl.ds(t0, frames), :].astype(F32), 0, 1)


def fold(v):
    return jnp.sum(v, axis=0)


def smem():
    return pl.BlockSpec(memory_space=pltpu.SMEM)


def vmem():
    return pl.BlockSpec(memory_space=pltpu.VMEM)


def hbm():
    return pl.BlockSpec(memory_space=pl.ANY)


def whole(*dims):
    return pl.BlockSpec(dims, lambda i: (0,) * len(dims), pipeline_mode=pl.Buffered(1))


def shape(dims, dtype=F32):
    return jax.ShapeDtypeStruct(dims, dtype)


MESH = pl.DeviceIdType.MESH
PACK = 24


class Place:
    def __init__(self, deep, side):
        self.deep, self.side = deep, side
        self.z = lax.axis_index("dp")
        f = lax.axis_index("fsdp")
        self.f = f
        self.core = lax.rem(f, 2)
        chip = f // 2
        self.low = lax.rem(chip, side)
        self.high = chip // side
        self.first = jnp.where(self.core == 0, self.high, self.low)
        self.second = jnp.where(self.core == 0, self.low, self.high)

    def chip_of(self, first, second):
        high = jnp.where(self.core == 0, first, second)
        low = jnp.where(self.core == 0, second, first)
        return high, low

    def fsdp_of(self, first, second):
        high, low = self.chip_of(first, second)
        return (high * self.side + low) * 2 + self.core

    def z_peer(self, p):
        return {"dp": lax.rem(self.z + p, self.deep)}

    def first_peer(self, p):
        return {"fsdp": self.fsdp_of(lax.rem(self.first + p, self.side), self.second)}

    def second_peer(self, p):
        return {"fsdp": self.fsdp_of(self.first, lax.rem(self.second + p, self.side))}

    def plane_peers(self):
        ends = [(p, q) for p in range(self.side) for q in range(self.side) if p or q]
        return [{"fsdp": self.fsdp_of(lax.rem(self.first + p, self.side), lax.rem(self.second + q, self.side))} for p, q in ends]

    def core_peer(self):
        return {"fsdp": self.f + 1 - 2 * self.core}

    def greet(self):
        barrier = pltpu.get_barrier_semaphore()
        peers = [self.z_peer(p) for p in range(1, self.deep)]
        peers += self.plane_peers()
        peers.append(self.core_peer())
        for peer in peers:
            pl.semaphore_signal(barrier, inc=1, device_id=peer, device_id_type=MESH)
        pl.semaphore_wait(barrier, len(peers))


def send(src, dst, send_sem, recv_sem, peer):
    return pltpu.make_async_remote_copy(
        src_ref=src, dst_ref=dst, send_sem=send_sem, recv_sem=recv_sem, device_id=peer, device_id_type=MESH
    )


def run(copies):
    for c in copies:
        c.start()


def done(copies):
    for c in copies:
        c.wait()


def weight_route(place, own, full, sems):
    zs, zr, fs, fr, ss, sr, cs, cr = sems
    deep, side, core = place.deep, place.side, place.core

    def held(p, q):
        high, low = place.chip_of(lax.rem(place.first + p, side), lax.rem(place.second + q, side))
        return full.at[:, high, low, core]

    mine = full.at[place.z, place.high, place.low, core]
    along_z = [send(own, mine, zs.at[p - 1], zr.at[p - 1], place.z_peer(p)) for p in range(1, deep)]
    along_first = [
        send(held(0, 0), held(0, 0), fs.at[p - 1], fr.at[p - 1], place.first_peer(p)) for p in range(1, side)
    ]
    along_second = []
    for j in range(side):
        high, low = place.chip_of(j, place.second)
        line = full.at[:, high, low, core]
        for p in range(1, side):
            n = j * (side - 1) + p - 1
            along_second.append(send(line, line, ss.at[n], sr.at[n], place.second_peer(p)))
    across = lambda p, q: send(held(p, q), held(p, q), cs.at[p * side + q], cr.at[p * side + q], place.core_peer())
    over = [[across(0, 0)], [across(p, 0) for p in range(1, side)],
            [across(p, q) for q in range(1, side) for p in range(side)]]
    return [along_z, along_first, along_second], over


def gather_sems(count, deep, side):
    one = [deep - 1, deep - 1, side - 1, side - 1, side * (side - 1), side * (side - 1), side * side, side * side]
    return [DMA((count, n)) for n in one]


def place_small(place, shards, pack, group_count, taps):
    conv_w, conv_b, scale, shift, up_b, down_b, gain = shards
    width = conv_b.shape[1]
    lane = lax.broadcasted_iota(jnp.int32, (width, LANES), 1)
    row = lax.broadcasted_iota(jnp.int32, (width, LANES), 0)
    spot = jnp.where(lane == row + place.f * width, 1.0, 0.0).astype(BF16)
    wide = up_b.shape[1]
    span = wide * LANES // width
    lane = lax.broadcasted_iota(jnp.int32, (wide, span), 1)
    row = lax.broadcasted_iota(jnp.int32, (wide, span), 0)
    spread = jnp.where(lane == row + place.f * wide, 1.0, 0.0).astype(BF16)
    pack[...] = jnp.zeros(pack.shape, F32)
    for b in range(2):
        o = b * PACK
        for k in range(taps):
            pack[o + k : o + k + 1, :] = mm(conv_w[k, b : b + 1, :], spot, NN)
        pack[o + SCALE : o + SCALE + group_count, :] = mm(scale[b], spot, NN)
        pack[o + SHIFT : o + SHIFT + group_count, :] = mm(shift[b], spot, NN)
        for src, at in ((conv_b, CONV_BIAS), (down_b, DOWN_BIAS), (gain, GAIN)):
            pack[o + at : o + at + 1, :] = mm(src[b : b + 1, :], spot, NN)
        bias = mm(up_b[b : b + 1, :], spread, NN)
        for q in range(span // LANES):
            pack[o + 14 + q : o + 15 + q, :] = bias[:, q * LANES : (q + 1) * LANES]


class Gather:
    def __init__(self, shards, up_full, down_full, small_full, upb_full, refs, deep, side, group_count, taps):
        (self.pack, self.zbuf, self.first_in, self.first_sum, self.second_in, self.second_sum, self.core_in,
         self.local_sems, self.small_s, self.small_r) = refs[:10]
        sems = refs[10:]
        self.place = place = Place(deep, side)
        self.small_full, self.upb_full, self.shards = small_full, upb_full, shards
        self.group_count, self.taps = group_count, taps
        up_w, down_w = shards[4], shards[6]
        self.full = (up_full, down_full)
        self.routes, self.local = [], []
        for n, (own, full) in enumerate(
            ((up_w.at[0], up_full.at[0]), (down_w.at[0], down_full.at[0]), (up_w.at[1], up_full.at[1]), (down_w.at[1], down_full.at[1]))
        ):
            self.routes.append(weight_route(place, own, full, [s.at[n] for s in sems]))
            spot = full.at[place.z, place.high, place.low, place.core]
            self.local.append(pltpu.make_async_copy(own, spot, self.local_sems.at[n]))
        stages = [
            [(self.zbuf.at[place.z], self.zbuf.at[place.z], place.z_peer(p)) for p in range(1, deep)],
            [(self.zbuf, self.first_in.at[p - 1], place.first_peer(p)) for p in range(1, side)],
            [(self.first_sum, self.second_in.at[p - 1], place.second_peer(p)) for p in range(1, side)],
            [(self.second_sum, self.core_in, place.core_peer())],
        ]
        n = 0
        self.small = []
        for stage in stages:
            copies = []
            for src, dst, peer in stage:
                copies.append(send(src, dst, self.small_s.at[n], self.small_r.at[n], peer))
                n += 1
            self.small.append(copies)

    def begin(self, n):
        run(self.routes[n][0][0])
        self.local[n].start()

    def after_z(self, n):
        along, over = self.routes[n]
        self.local[n].wait()
        done(along[0])
        run(along[1])
        run(over[0])

    def after_first(self, n):
        along, over = self.routes[n]
        done(along[1])
        run(along[2])
        run(over[1])

    def after_second(self, n):
        along, over = self.routes[n]
        done(along[2])
        run(over[2])

    def end(self, n):
        for copies in self.routes[n][1]:
            done(copies)

    def early(self, spread, ready, conv, tiles):
        place = self.place
        conv_w, conv_b, scale, shift, _, up_b, _, down_b, gain = self.shards
        place_small(place, (conv_w, conv_b, scale, shift, up_b, down_b, gain), self.pack, self.group_count, self.taps)
        self.zbuf[place.z] = self.pack[...].astype(BF16)
        place.greet()
        run(self.small[0])
        self.begin(0)
        self.begin(1)
        spread()
        done(self.small[0])
        run(self.small[1])
        self.after_z(0)
        done(self.small[1])
        total = self.zbuf[...].astype(F32)
        for p in range(1, place.side):
            total = total + self.first_in[p - 1].astype(F32)
        self.first_sum[...] = total.astype(BF16)
        run(self.small[2])
        done(self.small[2])
        total = self.first_sum[...].astype(F32)
        for p in range(1, place.side):
            total = total + self.second_in[p - 1].astype(F32)
        self.second_sum[...] = total.astype(BF16)
        run(self.small[3])
        self.after_first(0)
        self.begin(2)
        self.begin(3)
        done(self.small[3])
        self.finish_small()
        ready()
        conv(0, tiles // 4)
        self.after_z(1)
        conv(tiles // 4, 3 * tiles // 4)
        self.after_second(0)
        self.after_first(1)
        self.after_z(2)
        conv(3 * tiles // 4, tiles)
        self.end(0)

    def finish_small(self):
        total = self.second_sum[...].astype(F32) + self.core_in[...].astype(F32)
        deep = self.place.deep
        per = self.upb_full.shape[2] // deep
        self.small_full[...] = jnp.zeros(self.small_full.shape, F32)
        for b in range(2):
            o = b * PACK
            for z in range(deep):
                self.small_full[b, 0:14, z * LANES : (z + 1) * LANES] = total[z, o : o + 14, :]
                for q in range(per // LANES):
                    at = z * per + q * LANES
                    self.upb_full[b, :, at : at + LANES] = total[z, o + 14 + q : o + 15 + q, :]

    def late(self, i, tiles):
        @pl.when(i == tiles // 4)
        def _():
            self.after_z(3)

        @pl.when(i == 3 * tiles // 4)
        def _():
            self.after_second(1)
            self.after_first(2)

        @pl.when(i == tiles)
        def _():
            self.end(1)

        @pl.when(i == tiles + tiles // 4)
        def _():
            self.after_first(3)

        @pl.when(i == 2 * tiles - 1)
        def _():
            self.after_second(2)

        @pl.when(i == 2 * tiles)
        def _():
            self.after_second(3)
            for n in (2, 3):
                self.end(n)


def gather_scratch(deep, side):
    buf = pltpu.VMEM((deep, 2 * PACK, LANES), BF16)
    many = pltpu.VMEM((side - 1, deep, 2 * PACK, LANES), BF16)
    n = deep - 1 + 2 * (side - 1) + 1
    return [pltpu.VMEM((2 * PACK, LANES), F32), buf, many, buf, many, buf, buf, DMA((4,)), DMA((n,)), DMA((n,))] + gather_sems(
        4, deep, side
    )


def conv_norm(masked, f0, frames, s8, normed, inv, shaped, taps, n0=0, step=4):
    clips, width = s8.shape[1:]
    for j in range(0, frames, step):
        mixed = s8[CONV_BIAS][None]
        for k in range(taps):
            mixed = mixed + s8[TAPS + k][None] * masked[pl.ds(f0 + j + k, step)]
        center = mixed - jnp.mean(mixed, axis=-1, keepdims=True)
        inv_std = lax.rsqrt(jnp.mean(center * center, axis=-1, keepdims=True) + EPSILON)
        norm = center * inv_std
        normed[pl.ds(n0 + f0 + j, step)] = norm
        inv[pl.ds(f0 + j, step)] = jnp.broadcast_to(inv_std, (step, clips, LANES))
        rows = norm * s8[SCALE][None] + s8[SHIFT][None]
        at = pl.multiple_of((f0 + j) * clips, step * clips)
        shaped[pl.ds(at, step * clips), :] = rows.reshape(step * clips, width).astype(BF16)


def up_gelu(shaped, up_cols, u8, act, r0, slope, s0, rows, hidden, cols=256, sub=16):
    left = shaped[pl.ds(r0, rows), :]
    for n in range(0, hidden, cols):
        before = mm(left, up_cols(n, n + cols), NN)
        for r in range(0, rows, sub):
            piece = before[r : r + sub].reshape(sub // 8, 8, cols) + u8[:, n : n + cols][None]
            a, s = gelu_pair(piece.reshape(sub, cols))
            act[pl.ds(r0 + r, sub), n : n + cols] = a.astype(BF16)
            slope[pl.ds(s0 + r, sub), n : n + cols] = s.astype(slope.dtype)


def forward_kernel(
    lens, groups, frames, small_full, upb_full, up_full, down_full, out, act_out, slope, normed_out, inv_out, shaped_out, masked_out,
    masked0, masked1, normed, inv, shaped, first_rows, act, s8, u8, len8, save_sem, act_sem, row_sem, *, ft, taps, group_count,
):
    i = pl.program_id(0)
    clips, frame_count, width = frames.shape
    hidden = act.shape[1]
    tiles = frame_count // ft
    rows = ft * clips

    def up_cols(b):
        return lambda lo, hi: up_full[b, :, lo:hi]

    body = pl.ds(HALO, frame_count)
    save = lambda n, src, dst: pltpu.make_async_copy(src, dst, save_sem.at[n])
    saves0 = [
        save(0, masked0.at[body], masked_out.at[0]), save(1, normed, normed_out.at[0]),
        save(2, inv, inv_out.at[0]), save(3, shaped, shaped_out.at[0]),
    ]
    save_masked1 = save(4, masked1.at[body], masked_out.at[1])
    tail = lambda b, j: pltpu.make_async_copy(
        act.at[pl.ds(pl.multiple_of(j * rows, rows), rows)],
        act_out.at[b, pl.ds(pl.multiple_of(j * rows, rows), rows)], act_sem.at[j])

    def row_saves(j):
        f = pl.ds(j * ft, ft)
        r = pl.ds(pl.multiple_of(j * rows, rows), rows)
        return [
            pltpu.make_async_copy(normed.at[f], normed_out.at[1, f], row_sem.at[0, j]),
            pltpu.make_async_copy(inv.at[f], inv_out.at[1, f], row_sem.at[1, j]),
            pltpu.make_async_copy(shaped.at[r], shaped_out.at[1, r], row_sem.at[2, j]),
        ]

    @pl.when(i == 0)
    def _():
        zeros = jnp.zeros((HALO, clips, width), F32)
        for m in (masked0, masked1):
            m[0:HALO] = zeros
            m[HALO + frame_count :] = zeros
        len8[...] = per_clip(lens, clips, width)

        def spread(n, carry):
            t0 = pl.multiple_of(n * 16, 16)
            v = swap_frames(frames, t0, 16)
            at = pl.multiple_of(t0 * clips, 16 * clips)
            first_rows[pl.ds(at, 16 * clips), :] = v.reshape(16 * clips, width).astype(BF16)
            masked0[pl.ds(HALO + t0, 16)] = keep_frames(v, t0, len8)
            return carry
        lax.fori_loop(0, frame_count // 16, spread, 0)
        for b in range(2):
            prepare(small_full.at[b], lens, groups, s8.at[b], len8, group_count)
            u8[b] = jnp.broadcast_to(upb_full[b, 0:1, :], u8.shape[1:])

        def conv0(n, carry):
            conv_norm(masked0, n * ft, ft, s8.at[0], normed, inv, shaped, taps)
            return carry
        lax.fori_loop(0, tiles, conv0, 0)
        for c in saves0:
            c.start()

    @pl.when(i < tiles)
    def _():
        r0 = pl.multiple_of(i * rows, rows)
        up_gelu(shaped, up_cols(0), u8.at[0], act, r0, slope, 0, rows, hidden)
        tail(0, i).start()

    @pl.when((i >= tiles) & (i < 2 * tiles))
    def _():
        j = i - tiles
        f0 = j * ft
        r0 = pl.multiple_of(j * rows, rows)
        branch = mm(act[pl.ds(r0, rows), :], down_full[0], NN)
        for t in range(0, ft, 4):
            b = branch[t * clips : (t + 4) * clips].reshape(4, clips, width) + s8[0, DOWN_BIAS][None]
            total = masked0[pl.ds(HALO + f0 + t, 4)] + s8[0, GAIN][None] * b
            masked1[pl.ds(HALO + f0 + t, 4)] = keep_frames(total, f0 + t, len8)
        tail(0, j).wait()

    @pl.when(i == 2 * tiles)
    def _():
        for c in saves0:
            c.wait()
        save_masked1.start()

    @pl.when(i >= 2 * tiles)
    def _():
        j = i - 2 * tiles
        f0 = j * ft
        r0 = pl.multiple_of(j * rows, rows)
        conv_norm(masked1, f0, ft, s8.at[1], normed, inv, shaped, taps)
        for c in row_saves(j):
            c.start()
        up_gelu(shaped, up_cols(1), u8.at[1], act, r0, slope, 0, rows, hidden)
        tail(1, j).start()
        branch = mm(act[pl.ds(r0, rows), :], down_full[1], NN)
        last_block(branch, masked1, f0, r0, ft, s8.at[1], len8, first_rows, out)

    @pl.when(i == 3 * tiles - 1)
    def _():
        save_masked1.wait()
        for j in range(tiles):
            tail(1, j).wait()
            for c in row_saves(j):
                c.wait()


def last_block(branch, masked1, f0, r0, ft, s8, len8, first_rows, out, step=16):
    clips, width = len8.shape
    for t in range(0, ft, step):
        b = branch[t * clips : (t + step) * clips].reshape(step, clips, width) + s8[DOWN_BIAS][None]
        total = masked1[pl.ds(HALO + f0 + t, step)] + s8[GAIN][None] * b
        at = pl.multiple_of(r0 + t * clips, step * clips)
        first = first_rows[pl.ds(at, step * clips), :].astype(F32).reshape(step, clips, width)
        out[:, t : t + step, :] = jnp.swapaxes(keep_frames(total, f0 + t, len8, first), 0, 1).astype(BF16)


def forward(lens, groups, frames, weights, hidden, ft, taps, group_count):
    clips, fc, d = frames.shape
    h = hidden
    n, r = fc // ft, ft * clips
    R = fc * clips
    slope_at = lambda i: jnp.where(i < n, i, jnp.where(i < 2 * n, n - 1, i - n))
    return pl.pallas_call(
        functools.partial(forward_kernel, ft=ft, taps=taps, group_count=group_count),
        name="forward",
        grid=(3 * n,),
        in_specs=[smem(), smem(), whole(clips, fc, d)] + [vmem()] * 4,
        out_specs=[
            pl.BlockSpec((clips, ft, d), lambda i: (0, jnp.maximum(i - 2 * n, 0), 0)), hbm(),
            pl.BlockSpec((r, h), lambda i: (slope_at(i), 0)), hbm(), hbm(), hbm(), hbm(),
        ],
        out_shape=[
            shape((clips, fc, d), BF16), shape((2, R, h), BF16), shape((2 * R, h), BF16), shape((2, fc, clips, d)),
            shape((2, fc, clips, LANES)), shape((2, R, d), BF16), shape((2, fc, clips, d)),
        ],
        scratch_shapes=[
            pltpu.VMEM((fc + 2 * HALO, clips, d), F32), pltpu.VMEM((fc + 2 * HALO, clips, d), F32),
            pltpu.VMEM((fc, clips, d), F32), pltpu.VMEM((fc, clips, LANES), F32), pltpu.VMEM((R, d), BF16),
            pltpu.VMEM((R, d), BF16), pltpu.VMEM((R, h), BF16),
            pltpu.VMEM((2, 14, clips, d), F32), pltpu.VMEM((2, clips, h), F32), pltpu.VMEM((clips, d), jnp.int32),
            DMA((5,)), DMA((n,)), DMA((3, n)),
        ],
        compiler_params=pltpu.CompilerParams(vmem_limit_bytes=VMEM_LIMIT),
    )(lens, groups, frames, *weights)


class Scatter:
    def __init__(self, place, term, bufs, sems):
        self.place, self.term = place, term
        self.core_in, self.second_in, self.first_in, self.z_in = bufs
        self.sems = sems

    def line(self, first, second):
        high, low = self.place.chip_of(first, second)
        return self.term.at[:, high, low, self.place.core]

    def spot(self, z, first, second):
        high, low = self.place.chip_of(first, second)
        return (z, high, low)

    def core_copies(self):
        at = self.place
        return [send(self.term.at[:, :, :, 1 - at.core], self.core_in, self.sems[0].at[0], self.sems[1].at[0], at.core_peer())]

    def second_copies(self, p):
        at = self.place
        to = lax.rem(at.second + p, at.side)
        n = (p - 1) * at.side
        return [
            send(self.line(f, to), self.second_in.at[p - 1, f], self.sems[2].at[n + f], self.sems[3].at[n + f], at.second_peer(p))
            for f in range(at.side)
        ]

    def first_copy(self, p):
        at = self.place
        to = lax.rem(at.first + p, at.side)
        return send(self.line(to, at.second), self.first_in.at[p - 1], self.sems[4].at[p - 1], self.sems[5].at[p - 1], at.first_peer(p))

    def z_copy(self, p):
        at = self.place
        to = lax.rem(at.z + p, at.deep)
        high, low = at.chip_of(at.first, at.second)
        return send(self.term.at[to, high, low, at.core], self.z_in.at[p - 1], self.sems[6].at[p - 1], self.sems[7].at[p - 1], at.z_peer(p))

    def part1(self, z, first, second):
        z, high, low = self.spot(z, first, second)
        return self.term[z, high, low, self.place.core].astype(F32) + self.core_in[z, high, low].astype(F32)

    def part2(self, z, first):
        total = self.part1(z, first, self.place.second)
        for p in range(1, self.place.side):
            total = total + self.second_in[p - 1, first, z].astype(F32)
        return total

    def part3(self, z):
        total = self.part2(z, self.place.first)
        for p in range(1, self.place.side):
            total = total + self.first_in[p - 1, z].astype(F32)
        return total

    def put(self, z, first, second, total):
        z, high, low = self.spot(z, first, second)
        self.term[z, high, low, self.place.core] = total.astype(BF16)

    def core_start(self):
        run(self.core_copies())

    def second_start(self):
        at = self.place
        done(self.core_copies())
        for p in range(1, at.side):
            to = lax.rem(at.second + p, at.side)
            copies = self.second_copies(p)
            for first in range(at.side):
                def one(z, carry):
                    self.put(z, first, to, self.part1(z, first, to))
                    return carry
                lax.fori_loop(0, at.deep, one, 0)
                copies[first].start()

    def first_start(self):
        at = self.place
        for p in range(1, at.side):
            done(self.second_copies(p))
        for p in range(1, at.side):
            to = lax.rem(at.first + p, at.side)
            def one(z, carry):
                self.put(z, to, at.second, self.part2(z, to))
                return carry
            lax.fori_loop(0, at.deep, one, 0)
            self.first_copy(p).start()

    def z_start(self):
        at = self.place
        done([self.first_copy(p) for p in range(1, at.side)])
        for p in range(1, at.deep):
            to = lax.rem(at.z + p, at.deep)
            self.put(to, at.first, at.second, self.part3(to))
            self.z_copy(p).start()

    def finish(self, out):
        at = self.place
        done([self.z_copy(p) for p in range(1, at.deep)])
        total = self.part3(at.z)
        for p in range(1, at.deep):
            total = total + self.z_in[p - 1].astype(F32)
        out[...] = total


def scatter_bufs(deep, side, rows, cols):
    v = lambda *lead: pltpu.VMEM(lead + (rows, cols), BF16)
    return [v(deep, side, side), v(side - 1, side, deep), v(side - 1, deep), v(deep - 1)]


def scatter_sems(count, deep, side):
    return [DMA((count, n)) for n in (1, 1, side * (side - 1), side * (side - 1), side - 1, side - 1, deep - 1, deep - 1)]


def pack_small(small, upb, b, terms, deep):
    per = upb.shape[1] // deep
    o = b * PACK
    for z in range(deep):
        terms[z, o : o + 14, :] = small[0:14, z * LANES : (z + 1) * LANES]
        for q in range(per // LANES):
            at = z * per + q * LANES
            terms[z, o + 14 + q : o + 15 + q, :] = upb[:, at : at + LANES]


def sum_small(place, terms, z_in, bufs, out, s, r):
    n = 0
    copies = []
    for p in range(1, place.deep):
        to = lax.rem(place.z + p, place.deep)
        copies.append(send(terms.at[to], z_in.at[p - 1], s.at[n], r.at[n], place.z_peer(p)))
        n += 1
    run(copies)
    yield
    done(copies)
    total = terms[place.z]
    for p in range(1, place.deep):
        total = total + z_in[p - 1]
    stages = [[place.core_peer()], place.plane_peers()]
    for (here, into), peers in zip(bufs, stages):
        here[...] = total
        copies = []
        for p, peer in enumerate(peers):
            copies.append(send(here, into.at[p], s.at[n], r.at[n], peer))
            n += 1
        run(copies)
        yield
        done(copies)
        for p in range(len(peers)):
            total = total + into[p]
    out[...] = total


def small_bufs(deep, side):
    many = lambda *n: pltpu.VMEM(n + (2 * PACK, LANES), F32)
    others = side * side - 1
    n = deep + others
    return [many(deep), many(deep - 1), many(), many(1), many(), many(others), DMA((n,)), DMA((n,))]


class Sums:
    def __init__(self, refs, up_term, down_term, up_part, down_part, small_part, small_grad, upb_grad, deep, side, parts):
        self.place = Place(deep, side)
        self.terms, self.z_in = refs[:2]
        self.bufs = [refs[2:4], refs[4:6]]
        self.small_s, self.small_r = refs[6:8]
        refs = refs[8:]
        sems = refs[-8:]
        self.small_part, self.small_grad, self.upb_grad = small_part, small_grad, upb_grad
        self.parts = parts
        cols = up_part.shape[2] // parts
        self.jobs = []
        for b in (1, 0):
            views = []
            for p in range(parts):
                c = pl.ds(p * cols, cols)
                views.append((up_term.at[b, :, :, :, :, :, c], up_part.at[b, :, c]))
            views.append((down_term.at[b], down_part.at[b]))
            for term, out in views:
                n = len(self.jobs)
                self.jobs.append((Scatter(self.place, term, refs[4 * n : 4 * n + 4], [s.at[n] for s in sems]), out))

    def do(self, n, what):
        job, out = self.jobs[n]
        if what == "finish":
            job.finish(out)
        else:
            getattr(job, what)()

    def at(self, i, half, span):
        parts, per = self.parts, self.parts + 1
        whats = ("core_start", "second_start", "first_start", "z_start", "finish")
        when = []
        top = 2 * parts
        for p in range(parts - 1):
            t = 2 * (p + 1)
            when.append((t, t + 1, t + 3 if p < parts - 2 else top + 3, top + 3 if p < parts - 2 else top + 6, top + 9))
        when.append((top, top + 3, top + 6, top + 9, top + 12))
        when.append((top, top + 3, top + 10, top + 13, top + 16))
        plan = []
        for order, what in enumerate(whats):
            for n in range(2 * per):
                slot = when[n % per][order] + 2 * span * (n // per)
                if slot < 4 * span and slot % 2 == half:
                    plan.append((slot // 2, n, what))
        for now in sorted({p[0] for p in plan}):
            @pl.when(i == now)
            def _():
                for step, n, what in plan:
                    if step == now:
                        self.do(n, what)

    def after(self, i, span):
        @pl.when(i == 2 * span - 1)
        def _():
            self.terms[...] = jnp.zeros(self.terms.shape, F32)
            for b in range(2):
                pack_small(self.small_grad.at[b], self.upb_grad.at[b], b, self.terms, self.place.deep)
            steps = sum_small(self.place, self.terms, self.z_in, self.bufs, self.small_part, self.small_s, self.small_r)
            last = 2 * (self.parts + 1) - 1
            next(steps)
            self.do(last, "first_start")
            next(steps)
            self.do(last - 1, "finish")
            next(steps)
            self.do(last, "z_start")
            self.do(last, "finish")
            for _ in steps:
                pass


def sums_scratch(deep, side, urows, drows, d, h, parts):
    ub, db = scatter_bufs(deep, side, urows, h // parts), scatter_bufs(deep, side, drows, d)
    return small_bufs(deep, side) + 2 * (parts * ub + db) + scatter_sems(2 * (parts + 1), deep, side)


def norm_back(gs, normed, n0, inv, i0, s8, gm, gm0, acc, frames, step=4):
    clips, width = s8.shape[1:]
    a_scale, a_shift, a_bias = acc[A_SCALE], acc[A_SHIFT], acc[A_BIAS]
    for j in range(0, frames, step):
        g = gs[j * clips : (j + step) * clips].reshape(step, clips, width)
        norm = normed[pl.ds(n0 + j, step)]
        gn = g * norm
        a_scale = a_scale + fold(gn)
        a_shift = a_shift + fold(g)
        gg = g * s8[SCALE][None]
        mean = jnp.mean(gg, axis=-1, keepdims=True)
        mean_norm = jnp.mean(gn * s8[SCALE][None], axis=-1, keepdims=True)
        inv_std = jnp.concatenate([inv[pl.ds(i0 + j, step)]] * (width // LANES), axis=-1)
        grad = inv_std * (gg - mean - norm * mean_norm)
        a_bias = a_bias + fold(grad)
        gm[pl.ds(gm0 + j, step)] = grad
    acc[A_SCALE], acc[A_SHIFT], acc[A_BIAS] = a_scale, a_shift, a_bias


def conv_back(gm, gm0, s8, masked, m0, gs, g0, t0, out, acc, frames, len8, taps, step=8):
    clips, width = len8.shape
    half = taps // 2
    for l in range(width // LANES):
        cols = slice(l * LANES, (l + 1) * LANES)
        sums = [acc[A_TAPS + k, :, cols] for k in range(taps)]
        for j in range(0, frames, step):
            here = masked[pl.ds(m0 + j, step), :, cols]
            total = None
            for k in range(taps):
                piece = gm[pl.ds(gm0 + j + half - k, step), :, cols]
                term = s8[TAPS + k, :, cols][None] * piece
                total = term if total is None else total + term
                sums[k] = sums[k] + fold(piece * here)
            t = lax.broadcasted_iota(jnp.int32, total.shape, 0) + (t0 + j)
            total = jnp.where(t < len8[:, cols][None], total, 0.0)
            total = gs[pl.ds(g0 + j, step), :, cols] + total
            gs[pl.ds(g0 + j, step), :, cols] = total
            if out is not None:
                out[j : j + step, :, cols] = total
        for k in range(taps):
            acc[A_TAPS + k, :, cols] = sums[k]


def finish_small(acc, upb_acc, groups, s8, small_grad, upb_grad, group_count):
    clips, width = acc.shape[1:]
    member = per_clip(groups, clips, width)
    line = lambda v: jnp.sum(v, axis=0, keepdims=True)
    rows = [line(acc[A_TAPS + k]) for k in range(7)]
    rows.append(line(acc[A_BIAS]))
    for base in (A_SCALE, A_SHIFT):
        for g in range(group_count):
            rows.append(line(jnp.where(member == g, acc[base], 0.0)))
    rows.append(line(acc[A_DOWN]))
    rows.append(line((acc[A_GAIN] + s8[DOWN_BIAS] * acc[A_DOWN]) / s8[GAIN]))
    for r, row in enumerate(rows):
        small_grad[r : r + 1, :] = row
    for r in range(len(rows), small_grad.shape[0]):
        small_grad[r : r + 1, :] = jnp.zeros((1, width), F32)
    upb_grad[...] = line(upb_acc[...])


def backward_kernel(
    lens, groups, og, act, slope, normed, inv, shaped, masked, up, down, small, gs_out, dup, ddown, small_grad, upb_grad,
    gs, gb, gbef, gm, s8, len8, acc, upb_acc, *, ft, tiles, parts, taps, group_count,
):
    i = pl.program_id(0)
    frame_count, clips, width = gs.shape
    hidden = gbef.shape[1]
    cols = hidden // parts
    rows = ft * clips
    total_rows = frame_count * clips
    base = 2 * ft
    span = parts + tiles + 2
    step = lax.rem(i, span)
    b = 1 - i // span

    @pl.when(step == 0)
    def _():
        prepare(small.at[b], lens, groups, s8, len8, group_count)
        acc[...] = jnp.zeros(acc.shape, F32)

    @pl.when(i == 0)
    def _():
        gm[pl.ds(0, base)] = jnp.zeros((base, clips, width), F32)
        gm[pl.ds(base + frame_count, HALO)] = jnp.zeros((HALO, clips, width), F32)
        spread_grad(og, gs, 0)

    @pl.when(step == 0)
    def _():
        acc[A_DOWN] = branch_grad(gs, 0, s8, len8, gb)

    @pl.when(step < parts)
    def _():
        c0 = pl.multiple_of(step * cols, cols)
        at = pl.ds(c0, cols)
        lower = down[0, at, :]
        term = mm(act[0], gb[...], TN)
        ddown[b, at, :] = term
        acc[A_GAIN] += fold((term * lower.astype(F32)).reshape(cols // 8, 8, width))
        before_grad(gb, lower, slope.at[0], slice(None), gbef, at, upb_acc, total_rows)
        dup[b, :, at] = mm(shaped[0], gbef[:, at], TN)

    j = step - parts

    @pl.when((j >= 0) & (j < tiles))
    def _():
        r0 = pl.multiple_of(j * rows, rows)
        grad = mm(gbef[pl.ds(r0, rows), :], up[0], NT)
        norm_back(grad, normed.at[0], 0, inv.at[0], 0, s8, gm, base + j * ft, acc, ft)

    @pl.when(j >= 2)
    def _():
        f0 = (j - 2) * ft
        conv_back(gm, base + f0, s8, masked.at[0], 0, gs, f0, f0, gs_out, acc, ft, len8, taps)

    @pl.when(step == span - 1)
    def _():
        finish_small(acc, upb_acc, groups, s8, small_grad.at[b], upb_grad.at[b], group_count)


def spread_grad(og, gs, g0):
    def one(n, carry):
        t0 = pl.multiple_of(n * 16, 16)
        gs[pl.ds(g0 + t0, 16)] = swap_frames(og, t0, 16)
        return carry
    lax.fori_loop(0, og.shape[1] // 16, one, 0)


def branch_grad(gs, g0, s8, len8, gb):
    clips, width = len8.shape
    frame_count = gb.shape[0] // clips

    def one(n, a_down):
        t0 = n * 4
        gvb = s8[GAIN][None] * keep_frames(gs[pl.ds(g0 + t0, 4)], t0, len8)
        at = pl.multiple_of(t0 * clips, 4 * clips)
        gb[pl.ds(at, 4 * clips), :] = gvb.reshape(4 * clips, width).astype(BF16)
        return a_down + fold(gvb)
    return lax.fori_loop(0, frame_count // 4, one, jnp.zeros((clips, width), F32), unroll=4)


def before_grad(gb, lower, slope, slope_cols, gbef, at, upb_acc, rows, chunk=1024, sub=16):
    cols = lower.shape[0]
    total = jnp.zeros((8, cols), F32)
    for c in range(0, rows, chunk):
        ga = mm(gb[c : c + chunk, :], lower, NT)
        for r in range(0, chunk, sub):
            gr = ga[r : r + sub] * slope[c + r : c + r + sub, slope_cols].astype(F32)
            total = total + fold(gr.reshape(sub // 8, 8, cols))
            gbef[c + r : c + r + sub, at] = gr.astype(BF16)
    upb_acc[:, at] = total


def backward(lens, groups, og, saved, ups, downs, small, ft, taps, group_count):
    act, slope, normed, inv, shaped, masked = saved
    clips, fc, d = og.shape
    h = ups.shape[2]
    R, r, n = fc * clips, ft * clips, fc // ft
    parts = 6
    cols = h // parts
    span = parts + n + 2
    block = lambda i: 1 - i // span
    part = lambda i: jnp.minimum(lax.rem(i, span), parts - 1)
    tile = lambda i: jnp.clip(lax.rem(i, span) - parts, 0, n - 1)
    late = lambda i: jnp.clip(lax.rem(i, span) - parts - 2, 0, n - 1)
    last = lambda i: jnp.clip(i - span - parts - 2, 0, n - 1)
    sums = [(2, d, h), (2, h, d), (2, ROWS, d), (2, 1, h)]
    return pl.pallas_call(
        functools.partial(backward_kernel, ft=ft, tiles=n, parts=parts, taps=taps, group_count=group_count),
        name="backward",
        grid=(2 * span,),
        in_specs=[
            smem(), smem(), whole(clips, fc, d),
            pl.BlockSpec((1, R, cols), lambda i: (block(i), 0, part(i))),
            pl.BlockSpec((1, R, cols), lambda i: (block(i), 0, part(i))),
            pl.BlockSpec((1, ft, clips, d), lambda i: (block(i), tile(i), 0, 0)),
            pl.BlockSpec((1, ft, clips, LANES), lambda i: (block(i), tile(i), 0, 0)),
            pl.BlockSpec((1, R, d), lambda i: (block(i), 0, 0), pipeline_mode=pl.Buffered(1)),
            pl.BlockSpec((1, ft, clips, d), lambda i: (block(i), late(i), 0, 0)),
            pl.BlockSpec((1, d, h), lambda i: (block(i), 0, 0)),
            pl.BlockSpec((1, h, d), lambda i: (block(i), 0, 0)),
            whole(2, ROWS, d),
        ],
        out_specs=[pl.BlockSpec((ft, clips, d), lambda i: (last(i), 0, 0))] + [whole(*v) for v in sums],
        out_shape=[shape((fc, clips, d))] + [shape(v) for v in sums],
        scratch_shapes=[
            pltpu.VMEM((fc, clips, d), F32), pltpu.VMEM((R, d), BF16), pltpu.VMEM((R, h), BF16),
            pltpu.VMEM((fc + 2 * ft + HALO, clips, d), F32),
            pltpu.VMEM((14, clips, d), F32), pltpu.VMEM((clips, d), jnp.int32),
            pltpu.VMEM((12, clips, d), F32), pltpu.VMEM((clips, h), F32),
        ],
        compiler_params=pltpu.CompilerParams(vmem_limit_bytes=VMEM_LIMIT),
    )(lens, groups, og, act, slope, normed, inv, shaped, masked, ups, downs, small)


def step_kernel(*refs, deep, side, ft, parts, taps, group_count):
    lens, groups, frames, og = refs[:4]
    shards = refs[4:13]
    out, gs_out, up_part, down_part, small_part, act_far, slope_far = refs[13:20]
    (io, masked0, masked1, normed, inv, shaped, first_rows, act, slope, gb, s8, u8, len8, acc, upb_acc) = refs[20:35]
    small_full, upb_full, small_grad, upb_grad, up_full, down_full, up_term, down_term = refs[35:43]
    io_sem, act_sem, slope_sem, act_back_sem, slope_back_sem, gs_sem = refs[43:49]
    gather_refs, sum_refs = refs[49:67], refs[67:]

    i = pl.program_id(0)
    clips, frame_count, width = io.shape
    hidden = act.shape[1]
    tiles = frame_count // ft
    rows = ft * clips
    cols = hidden // parts
    span = parts + tiles + 1
    body = pl.ds(HALO, frame_count)

    load = lambda n, src: pltpu.make_async_copy(src, io, io_sem.at[n])
    tile_rows = lambda j: pl.ds(pl.multiple_of(j * rows, rows), rows)
    part_at = lambda p: pl.ds(pl.multiple_of(p * cols, cols), cols)

    def spills(j):
        r = tile_rows(j)
        return [
            pltpu.make_async_copy(act.at[r], act_far.at[r], act_sem.at[j]),
            pltpu.make_async_copy(slope.at[r], slope_far.at[r], slope_sem.at[j]),
        ]

    def act_back(p):
        return pltpu.make_async_copy(act_far.at[:, part_at(p)], act.at[:, part_at(p)], act_back_sem.at[p])

    def slope_back(j):
        return pltpu.make_async_copy(slope_far.at[tile_rows(j)], slope.at[tile_rows(j)], slope_back_sem.at[j])

    def up_cols(b):
        return lambda lo, hi: up_full[b, :, :, :, :, :, lo:hi].reshape(width, hi - lo)

    def spread():
        load(0, frames).wait()

        def one(n, carry):
            t0 = pl.multiple_of(n * 16, 16)
            v = swap_frames(io, t0, 16)
            at = pl.multiple_of(t0 * clips, 16 * clips)
            first_rows[pl.ds(at, 16 * clips), :] = v.reshape(16 * clips, width).astype(BF16)
            masked0[pl.ds(HALO + t0, 16)] = keep_frames(v, t0, len8)
            return carry
        lax.fori_loop(0, frame_count // 16, one, 0)
        load(1, og).start()

    def conv0(lo, hi):
        def one(n, carry):
            conv_norm(masked0, n * ft, ft, s8.at[0], normed.at[0], inv.at[0], shaped, taps, HALO)
            return carry
        lax.fori_loop(lo, hi, one, 0)

    def ready():
        for b in range(2):
            prepare(small_full.at[b], lens, groups, s8.at[b], len8, group_count)
            u8[b] = jnp.broadcast_to(upb_full[b, 0:1, :], u8.shape[1:])

    @pl.when(i == 0)
    def _():
        load(0, frames).start()
        zeros = jnp.zeros((HALO, clips, width), F32)
        for m in (masked0, masked1, normed.at[0], normed.at[1]):
            m[0:HALO] = zeros
            m[HALO + frame_count : HALO + frame_count + HALO] = zeros
        len8[...] = per_clip(lens, clips, width)
        Gather(shards, up_full, down_full, small_full, upb_full, gather_refs, deep, side, group_count, taps).early(
            spread, ready, conv0, tiles)

    Gather(shards, up_full, down_full, small_full, upb_full, gather_refs, deep, side, group_count, taps).late(i, tiles)

    @pl.when(i < tiles)
    def _():
        r0 = pl.multiple_of(i * rows, rows)
        up_gelu(shaped, up_cols(0), u8.at[0], act, r0, slope, r0, rows, hidden)
        run(spills(i))

    @pl.when((i >= tiles) & (i < 2 * tiles))
    def _():
        j = i - tiles
        f0 = j * ft
        r0 = pl.multiple_of(j * rows, rows)
        branch = mm(act[pl.ds(r0, rows), :], down_full[0].reshape(hidden, width), NN)
        for t in range(0, ft, 4):
            b = branch[t * clips : (t + 4) * clips].reshape(4, clips, width) + s8[0, DOWN_BIAS][None]
            total = masked0[pl.ds(HALO + f0 + t, 4)] + s8[0, GAIN][None] * b
            masked1[pl.ds(HALO + f0 + t, 4)] = keep_frames(total, f0 + t, len8)

    @pl.when((i >= 2 * tiles) & (i < 3 * tiles))
    def _():
        j = i - 2 * tiles
        f0 = j * ft
        r0 = pl.multiple_of(j * rows, rows)
        done(spills(j))
        conv_norm(masked1, f0, ft, s8.at[1], normed.at[1], inv.at[1], shaped, taps, HALO)
        up_gelu(shaped, up_cols(1), u8.at[1], act, r0, slope, r0, rows, hidden)
        branch = mm(act[pl.ds(r0, rows), :], down_full[1].reshape(hidden, width), NN)
        last_block(branch, masked1, f0, r0, ft, s8.at[1], len8, first_rows, out)

    k = i - 3 * tiles
    step = lax.rem(jnp.maximum(k, 0), span)
    b = jnp.where(k < span, 1, 0)

    @pl.when(k == 0)
    def _():
        load(1, og).wait()
        spread_grad(io, masked0, HALO)

    @pl.when(k == span)
    def _():
        def one(n, carry):
            t0 = n * 4
            at = pl.multiple_of(t0 * clips, 4 * clips)
            v = normed[0, pl.ds(HALO + t0, 4)] * s8[0, SCALE][None] + s8[0, SHIFT][None]
            shaped[pl.ds(at, 4 * clips), :] = v.reshape(4 * clips, width).astype(BF16)
            first = first_rows[pl.ds(at, 4 * clips), :].astype(F32).reshape(4, clips, width)
            masked1[pl.ds(HALO + t0, 4)] = keep_frames(first, t0, len8)
            return carry
        lax.fori_loop(0, frame_count // 4, one, 0, unroll=4)
        for j in range(tiles):
            slope_back(j).wait()

    @pl.when((k >= 0) & (step == 0))
    def _():
        acc[...] = jnp.zeros(acc.shape, F32)
        acc[A_DOWN] = branch_grad(masked0, HALO, s8.at[b], len8, gb)

    sums = Sums(sum_refs, up_term, down_term, up_part, down_part, small_part, small_grad, upb_grad, deep, side, parts)
    sums.at(k, 0, span)

    @pl.when((k >= span) & (step < parts))
    def _():
        act_back(step).wait()

    @pl.when((k >= 0) & (step < parts))
    def _():
        at = part_at(step)
        drows, urows = down_full.shape[5], up_full.shape[5]
        per = drows // 16
        spots = []
        for m in range(cols // 16):
            row = step * (cols // 16) + m
            e = row // per
            z, chip = e // (2 * side * side), e // 2
            sub = pl.ds(pl.multiple_of((row - e * per) * 16, 16), 16)
            spots.append((b, z, lax.rem(chip // side, side), lax.rem(chip, side), lax.rem(e, 2), sub))
        lower = jnp.concatenate([down_full[spot] for spot in spots], axis=0)
        term = mm(act[:, at], gb[...], TN)
        for m, spot in enumerate(spots):
            down_term[spot] = term[m * 16 : (m + 1) * 16].astype(BF16)
        acc[A_GAIN] += fold((term * lower.astype(F32)).reshape(cols // 8, 8, width))
        before_grad(gb, lower, slope, at, slope, at, upb_acc, frame_count * clips)
        term = mm(shaped[...], slope[:, at], TN).astype(BF16)
        up_term[b, :, :, :, :, :, at] = term.reshape(deep, side, side, 2, urows, cols)

    @pl.when((k >= 0) & (k < parts))
    def _():
        act_back(step).start()

    j = step - parts

    @pl.when((j >= 0) & (j < tiles))
    def _():
        r0 = pl.multiple_of(j * rows, rows)
        grad = mm(slope[pl.ds(r0, rows), :], up_full[b].reshape(width, hidden), NT)
        norm_back(grad, normed.at[b], HALO + j * ft, inv.at[b], j * ft, s8.at[b], normed.at[b], HALO + j * ft, acc, ft)

    @pl.when((k < span) & (j >= 0) & (j < tiles))
    def _():
        slope_back(j).start()

    sums.at(k, 1, span)
    gs_copy = lambda f0, n: pltpu.make_async_copy(masked0.at[pl.ds(HALO + f0, ft)], gs_out.at[pl.ds(f0, ft)], gs_sem.at[n])

    @pl.when(j >= 1)
    def _():
        f0 = (j - 1) * ft
        conv_back(
            normed.at[b], HALO + f0, s8.at[b], masked1, HALO + f0, masked0, HALO + f0, f0, None, acc, ft, len8, taps)

    @pl.when((k >= span) & (j >= 1))
    def _():
        gs_copy((j - 1) * ft, j - 1).start()

    @pl.when((k >= 0) & (step == span - 1))
    def _():
        finish_small(acc, upb_acc, groups, s8.at[b], small_grad.at[b], upb_grad.at[b], group_count)

    sums.after(k, span)

    @pl.when(k == 2 * span - 1)
    def _():
        for n in range(tiles):
            gs_copy(n * ft, n).wait()


def whole_step(deep, side, lens, groups, frames, og, weights, ft, taps, group_count):
    clips, fc, d = frames.shape
    h = weights[4].shape[2]
    urows, drows = weights[4].shape[1], weights[6].shape[1]
    R, r, n = fc * clips, ft * clips, fc // ft
    parts = 3
    span = parts + n + 1
    dims = (2, deep, side, side, 2)
    rows = lambda dtype, *lead: pltpu.VMEM(lead + (d,), dtype)
    halo = fc + 2 * HALO
    return pl.pallas_call(
        functools.partial(step_kernel, deep=deep, side=side, ft=ft, parts=parts, taps=taps, group_count=group_count),
        name="step",
        grid=(3 * n + 2 * span,),
        in_specs=[smem(), smem(), hbm(), hbm()] + [vmem()] * 9,
        out_specs=[
            pl.BlockSpec((clips, ft, d), lambda i: (0, jnp.clip(i - 2 * n, 0, n - 1), 0)),
            hbm(), vmem(), vmem(), vmem(), hbm(), hbm(),
        ],
        out_shape=[
            shape((clips, fc, d), BF16), shape((fc, clips, d)), shape((2, urows, h)), shape((2, drows, d)),
            shape((2 * PACK, LANES)), shape((R, h), BF16), shape((R, h), BF16),
        ],
        scratch_shapes=[
            rows(BF16, clips, fc),
            rows(F32, halo, clips), rows(F32, halo, clips), rows(F32, 2, halo, clips), pltpu.VMEM((2, fc, clips, LANES), F32),
            rows(BF16, R), rows(BF16, R), pltpu.VMEM((R, h), BF16), pltpu.VMEM((R, h), BF16), rows(BF16, R),
            rows(F32, 2, 14, clips), pltpu.VMEM((2, clips, h), F32), rows(jnp.int32, clips), rows(F32, 12, clips),
            pltpu.VMEM((clips, h), F32),
            rows(F32, 2, ROWS), pltpu.VMEM((2, 1, h), F32), rows(F32, 2, ROWS), pltpu.VMEM((2, 1, h), F32),
            pltpu.VMEM(dims + (urows, h), BF16), rows(BF16, *dims, drows), pltpu.VMEM(dims + (urows, h), BF16), rows(BF16, *dims, drows),
            DMA((2,)), DMA((n,)), DMA((n,)), DMA((parts,)), DMA((n,)), DMA((n,)),
        ] + gather_scratch(deep, side) + sums_scratch(deep, side, urows, drows, d, h, parts),
        compiler_params=pltpu.CompilerParams(vmem_limit_bytes=VMEM_LIMIT, collective_id=0, has_side_effects=True),
    )(lens, groups, frames, og, *weights)


def swap_rows(src, dst):
    for t in range(0, src.shape[0], 8):
        dst[:, t : t + 8, :] = jnp.swapaxes(src[t : t + 8], 0, 1)


def unpack_kernel(gs, up_in, down_in, small, gin, conv_w, conv_b, scale, shift, up_w, up_b, down_w, down_b, gain):
    swap_rows(gs, gin)

    @pl.when(pl.program_id(0) == 0)
    def _():
        unpack_parts(up_in, down_in, small, conv_w, conv_b, scale, shift, up_w, up_b, down_w, down_b, gain)


def unpack_parts(up_in, down_in, small, conv_w, conv_b, scale, shift, up_w, up_b, down_w, down_b, gain):
    f = lax.axis_index("fsdp")
    width = conv_b.shape[1]
    wide = up_b.shape[1]
    span = wide * LANES // width
    turned = pltpu.roll(small[...], lax.rem(LANES - f * width, LANES), 1)
    for b in range(2):
        o = b * PACK
        for k in range(conv_w.shape[0]):
            conv_w[k, b : b + 1, :] = turned[o + k : o + k + 1, :width]
        conv_b[b : b + 1, :] = turned[o + CONV_BIAS : o + CONV_BIAS + 1, :width]
        scale[b] = turned[o + SCALE : o + SCALE + scale.shape[1], :width]
        shift[b] = turned[o + SHIFT : o + SHIFT + shift.shape[1], :width]
        down_b[b : b + 1, :] = turned[o + DOWN_BIAS : o + DOWN_BIAS + 1, :width]
        gain[b : b + 1, :] = turned[o + GAIN : o + GAIN + 1, :width]
        bias = jnp.concatenate([small[o + 14 + q : o + 15 + q, :] for q in range(span // LANES)], axis=1)
        bias = pltpu.roll(jnp.broadcast_to(bias, (8, span)), lax.rem(span - f * wide, span), 1)
        up_b[b : b + 1, :] = bias[0:1, :wide]
    up_w[...] = up_in[...]
    down_w[...] = down_in[...]


def unpack_far(gs):
    fc, clips, d = gs.shape
    ft = 64
    return pl.pallas_call(
        swap_rows,
        name="unpack",
        grid=(fc // ft,),
        in_specs=[pl.BlockSpec((ft, clips, d), lambda i: (i, 0, 0))],
        out_specs=pl.BlockSpec((clips, ft, d), lambda i: (0, i, 0)),
        out_shape=shape((clips, fc, d)),
    )(gs)


def unpack(gs, parts, taps, group_count, width, wide):
    fc, clips, d = gs.shape
    ft = 64
    up_in, down_in, small = parts
    outs = [(taps, 2, width), (2, width), (2, group_count, width), (2, group_count, width), up_in.shape, (2, wide),
            down_in.shape, (2, width), (2, width)]
    return pl.pallas_call(
        unpack_kernel,
        name="unpack",
        grid=(fc // ft,),
        in_specs=[pl.BlockSpec((ft, clips, d), lambda i: (i, 0, 0))] + [whole(*v.shape) for v in parts],
        out_specs=[pl.BlockSpec((clips, ft, d), lambda i: (0, i, 0))] + [whole(*v) for v in outs],
        out_shape=[shape((clips, fc, d))] + [shape(v) for v in outs],
    )(gs, up_in, down_in, small)


def body(deep, fan, frames, group, lengths, conv_w, conv_b, scale, shift, up_w, up_b, down_w, down_b, gain, out_grad):
    side = math.isqrt(fan // 2)
    clips = frames.shape[0]
    taps, group_count, hidden = conv_w.shape[1], scale.shape[1], up_w.shape[2]
    width, wide = conv_b.shape[1], up_b.shape[1]
    axes = ("dp", "fsdp")
    near = width * fan == LANES and up_w.shape[1] % 16 == 0 and down_w.shape[1] % 16 == 0
    ft = 32
    if near:
        weights = (conv_w.transpose(1, 0, 2), conv_b, scale, shift, up_w, up_b, down_w, down_b, gain)
    else:
        whole_of = lambda v, axis: lax.all_gather(v, axes, axis=axis, tiled=True)
        ups, downs = whole_of(up_w, 1), whole_of(down_w, 1)
        lines = jnp.concatenate(
            [conv_w, conv_b[:, None], scale, shift, down_b[:, None], gain[:, None], jnp.zeros((2, 2, width), BF16)], axis=1
        )
        small = whole_of(lines, 2).astype(F32)
        upb = whole_of(up_b, 1).astype(F32)[:, None]
        weights = (small, upb, ups, downs)
    if near:
        out, gs, *parts, _, _ = whole_step(deep, side, lengths, group, frames, out_grad, weights, 64, taps, group_count)
        gin, conv_grad, *grads = unpack(gs, parts, taps, group_count, width, wide)
        return (out, gin, conv_grad.transpose(1, 0, 2), *grads)
    out, act, slope, *rest = forward(lengths, group, frames, weights, hidden, ft, taps, group_count)
    saved = (act, slope.reshape(act.shape), *rest)
    gs, *parts = backward(lengths, group, out_grad, saved, ups, downs, small, ft, taps, group_count)
    gin = unpack_far(gs)
    dup, ddown, lines, ug = parts
    owner = lambda v, axis: lax.psum_scatter(v, axes, scatter_dimension=axis, tiled=True)
    lines = owner(lines, 2)
    return (
        out, gin, lines[:, :taps], lines[:, CONV_BIAS], lines[:, SCALE : SCALE + group_count],
        lines[:, SHIFT : SHIFT + group_count], owner(dup, 1), owner(ug[:, 0], 1), owner(ddown, 1),
        lines[:, DOWN_BIAS], lines[:, GAIN],
    )


def solution(mesh):
    split = ("dp", "fsdp")
    clip = P(split, None, None)
    first, middle, last = P(None, split), P(None, split, None), P(None, None, split)
    in_specs = (clip, P(split), P(split), last, first, last, last, middle, first, middle, first, first, clip)
    out_specs = (clip, clip, last, first, last, last, middle, first, middle, first, first)
    run = functools.partial(body, mesh.shape["dp"], mesh.shape["fsdp"])
    return jax.shard_map(run, mesh=mesh, in_specs=in_specs, out_specs=out_specs, check_vma=False)
```
